32 devices in a mesh: context: 4 (over y, x), expert: 8 (over z, core).
Axes of the slice: x: 2, y: 2, z: 4, core: 2. Of those that a mesh axis runs over, the one named last changes fastest.
Arguments:
- tokens: bfloat16 [8, 1024, 2048], P('expert', 'context'), may hold values from -6 to 6
- cotangent: bfloat16 [8, 1024, 2048], P('expert', 'context'), may hold values from -6 to 6
- lengths: int32 [8], P('expert'), may hold values from 257 to 1024, as said below
- expert_ids: int32 [8, 1024, 8], P('expert', 'context'), may hold values from 0 to 15, all different within a row; in each aligned block of 256 rows (0 to 255, 256 to 511, ..., all dimensions but the last counted through in order) at most 144 rows name the same one
- query_weight: bfloat16 [2048, 2048], P(('context', 'expert')), may hold values from -0.125 to 0.125
- key_weight: bfloat16 [2048, 2048], P(('context', 'expert')), may hold values from -0.125 to 0.125
- value_weight: bfloat16 [2048, 2048], P(('context', 'expert')), may hold values from -0.125 to 0.125
- out_weight: bfloat16 [2048, 2048], P(('context', 'expert')), may hold values from -0.5 to 0.5
- router_weight: bfloat16 [2048, 16], P(('context', 'expert')), may hold values from -0.0625 to 0.0625
- first_gain: bfloat16 [2048], P(('context', 'expert')), may hold values from 0.5 to 1.5
- second_gain: bfloat16 [2048], P(('context', 'expert')), may hold values from 0.5 to 1.5
- query_gain: bfloat16 [2048], P(('context', 'expert')), may hold values from 0.5 to 1.5
- key_gain: bfloat16 [2048], P(('context', 'expert')), may hold values from 0.5 to 1.5
- gate_weight: bfloat16 [16, 2048, 1024], P('expert', None, 'context'), may hold values from -0.125 to 0.125
- up_weight: bfloat16 [16, 2048, 1024], P('expert', None, 'context'), may hold values from -0.125 to 0.125
- down_weight: bfloat16 [16, 1024, 2048], P('expert', 'context'), may hold values from -4 to 4
Outputs:
- layer_out: bfloat16 [8, 1024, 2048], P('expert', 'context')
- input_grad: bfloat16 [8, 1024, 2048], P('expert', 'context')
- query_grad: float32 [2048, 2048], P(('context', 'expert'))
- key_grad: float32 [2048, 2048], P(('context', 'expert'))
- value_grad: float32 [2048, 2048], P(('context', 'expert'))
- out_grad: float32 [2048, 2048], P(('context', 'expert'))
- router_grad: float32 [2048, 16], P(('context', 'expert'))
- first_gain_grad: float32 [2048], P(('context', 'expert'))
- second_gain_grad: float32 [2048], P(('context', 'expert'))
- query_gain_grad: float32 [2048], P(('context', 'expert'))
- key_gain_grad: float32 [2048], P(('context', 'expert'))
- gate_grad: float32 [16, 2048, 1024], P('expert', None, 'context')
- up_grad: float32 [16, 2048, 1024], P('expert', None, 'context')
- down_grad: float32 [16, 1024, 2048], P('expert', 'context')
The draws below stay inside these ranges and needn't reach their ends.
Inputs may be any that keep to these rules, and one draw needn't show every extreme that they name: `lengths`: the longest sequence has exactly 1024 positions. `expert_ids`: each token names 8 different experts. Among the tokens of one device's block, no expert is named more than 144 times, and some expert reaches 144.
All inputs are finite; a program needn't handle non-finite values.
Results may differ from the reference program's by a relative error of at most 0.02.
Values may be sent and summed in bfloat16 or wider, within the bound.
A program may use at most 384 MiB of HBM per device.

```python
import math
import jax
import jax.numpy as jnp
import numpy as np
from jax import lax

D = 2048
HEADS = 16
HD = 128
FF = 1024
TOP = 8
TOK_DEV = 256
EXPERTS = 16
LEN = 1024
SEQS = 8
CAP = 144


def draw_lengths(key, part):
    first_key, second_key = jax.random.split(key)
    values = jax.random.randint(first_key, (SEQS,), LEN // 4 + 1, LEN + 1)
    longest = jax.random.randint(second_key, (), 0, SEQS)
    return jnp.where(jnp.arange(SEQS) == longest, LEN, values).astype(jnp.int32)


def block_levels(stream_key, shape, cuts, low, largest):
    def one(axis_at, shards_of):
        heights = jax.random.uniform(jax.random.fold_in(jax.random.fold_in(stream_key, 6), axis_at), (shards_of,), jnp.float32, low / len(cuts), largest / len(cuts))
        return jnp.repeat(jnp.exp(heights), shape[axis_at] // shards_of).reshape((-1,) + (1,) * (len(shape) - axis_at - 1))

    factor_of = one(*cuts[0])
    for cut in cuts[1:]:
        factor_of = factor_of * one(*cut)
    return factor_of


def routed_block(stream_key, own, number, rows, count, top, limit, lean):
    ranking = jax.random.permutation(stream_key, count)
    crowded, usual = load_shares(count, rows * top, limit, lean, True), load_shares(count, rows * top, limit, lean, False)
    places = jnp.arange(count)

    def named(sizes, turn):
        used = int((sizes > 0).sum())
        fixed = max(1, used // 4)
        shifted = fixed + (places - fixed + turn * (used - fixed)) % max(1, count - fixed)
        return jnp.zeros((count,), jnp.int32).at[ranking[jnp.where(places < fixed, places, shifted)]].set(jnp.asarray(sizes, jnp.int32))

    sizes = jnp.where(number % 4 == 0, named(crowded, number // 4), named(usual, number - number // 4 - 1))
    mixed = jax.random.permutation(jax.random.fold_in(own, 3), count)
    donor, sink = mixed[0:count // 2 * 2:2], mixed[1:count // 2 * 2:2]
    margin = jnp.minimum(sizes[donor] - 1, limit - sizes[sink]) // 2
    margin = jnp.where((donor == ranking[0]) | (sink == ranking[0]) | (sizes[sink] == 0), 0, jnp.maximum(margin, 0))
    shifted = jax.random.randint(jax.random.fold_in(own, 4), (count // 2,), 0, 1 << 20) % (margin + 1)
    sizes = sizes.at[donor].add(-shifted).at[sink].add(shifted)
    items = jnp.searchsorted(jnp.cumsum(sizes), jnp.arange(rows * top), side="right").astype(jnp.int32)
    grid = items.reshape(top, rows).T
    grid = grid[jax.random.permutation(jax.random.fold_in(own, 1), rows)]
    turn = jax.random.randint(jax.random.fold_in(own, 2), (rows, 1), 0, top)
    return jnp.take_along_axis(grid, (jnp.arange(top)[None, :] + turn) % top, axis=1)


def load_shares(count, total, most, skew, full):
    weights = [(1 << 20) // math.isqrt(standing ** skew) + 1 for standing in range(1, count + 1)]
    largest = most if full else min(most, max(-(-total // count), total * weights[0] // sum(weights)))
    least = 1 if total - largest >= count - 1 else 0
    given, rest = [largest] + [least] * (count - 1), total - largest - least * (count - 1)
    while rest > 0:
        movable = [i for i in range(1, count) if given[i] < largest] or [i for i in range(1, count) if given[i] < most]
        pool, left = sum([weights[i] for i in movable]), rest
        for i in movable:
            addition = min(most - given[i], max(1, left * weights[i] // pool), rest)
            given[i] = given[i] + addition
            rest = rest - addition
    return np.array(given)


def scatter_about(rng, dims, width, bound, cuts=(), kind=jnp.bfloat16):
    level = block_levels(rng, dims, cuts, -0.22, 0.18) if cuts else 1.0
    values = jax.random.normal(rng, dims, jnp.float32) * width * level
    return jnp.minimum(jnp.maximum(values, -bound), bound).astype(kind)


def setup_inputs(seed: int = 0) -> dict:
    key_of = jax.random.split(jax.random.key(seed), 17)
    tokens = scatter_about(key_of[0], (SEQS, LEN, D), 1.0, 6.0, ((0, 8), (1, 4)))
    cotangent = scatter_about(key_of[1], (SEQS, LEN, D), 1.0, 6.0, ((0, 8), (1, 4)))
    lengths = draw_lengths(jax.random.fold_in(key_of[16], 71), 0)
    expert_ids_keys = jax.random.split(jax.random.fold_in(key_of[3], 1), SEQS * LEN // TOK_DEV)
    expert_ids_turns = jax.random.permutation(jax.random.fold_in(key_of[3], 3), SEQS * LEN // TOK_DEV)
    expert_ids = jax.vmap(lambda own, number: routed_block(jax.random.fold_in(key_of[3], 2), own, number, TOK_DEV, EXPERTS, TOP, CAP, 1))(expert_ids_keys, expert_ids_turns).reshape((SEQS, LEN, TOP))
    query_weight = scatter_about(key_of[4], (D, D), D ** -0.5, 0.125, ((0, 32),))
    key_weight = scatter_about(key_of[5], (D, D), D ** -0.5, 0.125, ((0, 32),))
    value_weight = scatter_about(key_of[6], (D, D), D ** -0.5, 0.125, ((0, 32),))
    out_weight = scatter_about(key_of[7], (D, D), (D // 16) ** -0.5, 0.5, ((0, 32),))
    router_weight = scatter_about(key_of[8], (D, EXPERTS), (4 * D) ** -0.5, 0.0625, ((0, 32),))
    first_gain = jnp.clip(1.0 + 0.1 * jax.random.normal(key_of[9], (D,), jnp.float32), 0.5, 1.5).astype(jnp.bfloat16)
    second_gain = jnp.clip(1.0 + 0.1 * jax.random.normal(key_of[10], (D,), jnp.float32), 0.5, 1.5).astype(jnp.bfloat16)
    query_gain = jnp.clip(1.0 + 0.1 * jax.random.normal(key_of[11], (D,), jnp.float32), 0.5, 1.5).astype(jnp.bfloat16)
    key_gain = jnp.clip(1.0 + 0.1 * jax.random.normal(key_of[12], (D,), jnp.float32), 0.5, 1.5).astype(jnp.bfloat16)
    gate_weight = scatter_about(key_of[13], (EXPERTS, D, FF), D ** -0.5, 0.125, ((0, 8), (2, 4)))
    up_weight = scatter_about(key_of[14], (EXPERTS, D, FF), D ** -0.5, 0.125, ((0, 8), (2, 4)))
    down_weight = scatter_about(key_of[15], (EXPERTS, FF, D), (max(FF // 512, 1)) ** -0.5, 4.0, ((0, 8), (1, 4)))
    return dict(tokens=tokens, cotangent=cotangent, lengths=lengths, expert_ids=expert_ids, query_weight=query_weight, key_weight=key_weight, value_weight=value_weight, out_weight=out_weight, router_weight=router_weight, first_gain=first_gain, second_gain=second_gain, query_gain=query_gain, key_gain=key_gain, gate_weight=gate_weight, up_weight=up_weight, down_weight=down_weight)


EPSILON = 1e-06
ROPE_THETA = 10000.0
NEG_FILL = -1e+30

@jax.custom_vjp
def low(v):
    return lax.optimization_barrier(v.astype(jnp.bfloat16)).astype(jnp.float32)

@jax.custom_vjp
def low_back(v):
    return v

def low_keep(v):
    return (low(v), None)

def low_pass(kept, grad):
    return (grad,)

def back_keep(v):
    return (v, None)

def back_low(kept, grad):
    return (low(grad),)
low.defvjp(low_keep, low_pass)
low_back.defvjp(back_keep, back_low)

def matmul(left, right):
    return jnp.dot(left, right, precision=lax.Precision.HIGHEST, preferred_element_type=jnp.float32)

def rms_norm(values, gain):
    factor = lax.rsqrt(lax.optimization_barrier(jnp.mean(values * values, axis=-1, keepdims=True)) + EPSILON)
    return values * factor * gain

def softmax_rows(scores):
    peak = lax.optimization_barrier(jnp.max(scores, axis=-1, keepdims=True))
    expo = jnp.exp(scores - peak)
    return expo / lax.optimization_barrier(jnp.sum(expo, axis=-1, keepdims=True))

def rotary_tables():
    half_dim = HD // 2
    frequency = jnp.exp(-jnp.log(ROPE_THETA) * jnp.arange(half_dim, dtype=jnp.float32) / half_dim)
    angles = jnp.arange(LEN, dtype=jnp.float32)[:, None] * frequency[None, :]
    return (jnp.cos(angles), jnp.sin(angles))

def rotate(values, cosine, sine):
    half_dim = HD // 2
    first = values[..., :half_dim]
    second = values[..., half_dim:]
    cos_rows = cosine[:, None, :]
    sin_rows = sine[:, None, :]
    return jnp.concatenate([first * cos_rows - second * sin_rows, second * cos_rows + first * sin_rows], axis=-1)

def attend_one(packed):
    query, keys, values, valid = packed
    scores = jnp.einsum('qhd,khd->hqk', query, keys, precision=lax.Precision.HIGHEST) * (1.0 / jnp.sqrt(jnp.float32(HD)))
    scores = low_back(scores)
    scores = jnp.where(valid[None, None, :], scores, NEG_FILL)
    weights = low(softmax_rows(scores))
    return jnp.einsum('hqk,khd->qhd', weights, values, precision=lax.Precision.HIGHEST)

def expert_one(packed):
    rows, gate_matrix, up_matrix, down_matrix = packed
    gate_pre = low_back(matmul(rows, gate_matrix))
    up_pre = low_back(matmul(rows, up_matrix))
    hidden = low(gate_pre * jax.nn.sigmoid(gate_pre) * up_pre)
    return low(low_back(matmul(hidden, down_matrix)))

def reference(tokens, cotangent, lengths, expert_ids, query_weight, key_weight, value_weight, out_weight, router_weight, first_gain, second_gain, query_gain, key_gain, gate_weight, up_weight, down_weight):
    key_valid = jnp.arange(LEN, dtype=jnp.int32)[None, :] < lengths[:, None]
    row_valid = key_valid.astype(jnp.float32).reshape(-1, 1)
    cosine, sine = rotary_tables()
    ids_flat = expert_ids.reshape(-1, TOP)
    blocks = SEQS * LEN // TOK_DEV
    pair_experts = expert_ids.reshape(blocks, TOK_DEV * TOP)
    pick_table = (pair_experts[:, :, None] == jnp.arange(EXPERTS, dtype=jnp.int32)[None, None, :]).astype(jnp.int32)
    ranks = lax.optimization_barrier(jnp.sum((jnp.cumsum(pick_table, axis=1) - pick_table) * pick_table, axis=2))
    block_index = jnp.arange(blocks, dtype=jnp.int32)[:, None]
    dest = (pair_experts * (blocks * CAP) + block_index * CAP + ranks).reshape(-1).astype(jnp.int32)

    def forward(inputs, query_matrix, key_matrix, value_matrix, out_matrix, router_matrix, gain_one, gain_two, gain_queries, gain_keys, gate_matrix, up_matrix, down_matrix):
        flat = inputs.reshape(-1, D)
        normed_one = low(rms_norm(flat, gain_one))
        query_raw = low_back(matmul(normed_one, query_matrix))
        key_raw = low_back(matmul(normed_one, key_matrix))
        value_low = low(low_back(matmul(normed_one, value_matrix)))
        query_low = low(rotate(rms_norm(query_raw, gain_queries).reshape(SEQS, LEN, HEADS, HD), cosine, sine))
        key_low = low(rotate(rms_norm(key_raw, gain_keys).reshape(SEQS, LEN, HEADS, HD), cosine, sine))
        attended = lax.map(jax.checkpoint(attend_one), (query_low, key_low, value_low.reshape(SEQS, LEN, HEADS, HD), key_valid))
        attended_low = low(low_back(attended.reshape(-1, D)))
        hidden_state = flat + low_back(matmul(attended_low, out_matrix))
        normed_two = low(rms_norm(hidden_state, gain_two))
        logits = low_back(matmul(normed_two, router_matrix))
        router_probs = softmax_rows(logits)
        gates = jnp.take_along_axis(router_probs, ids_flat, axis=1)
        pair_rows = low_back(jnp.repeat(normed_two, TOP, axis=0))
        buffer = jnp.zeros((EXPERTS * blocks * CAP, D), jnp.float32).at[dest].add(pair_rows)
        buffer = buffer.reshape(EXPERTS, blocks * CAP, D)
        expert_out = lax.map(expert_one, (buffer, gate_matrix, up_matrix, down_matrix))
        pair_out = expert_out.reshape(-1, D)[dest].reshape(-1, TOP, D)
        mixed = lax.optimization_barrier(jnp.sum(gates[:, :, None] * pair_out, axis=1))
        return (row_valid * (hidden_state + mixed)).reshape(SEQS, LEN, D)
    floats = [array.astype(jnp.float32) for array in (tokens, query_weight, key_weight, value_weight, out_weight, router_weight, first_gain, second_gain, query_gain, key_gain, gate_weight, up_weight, down_weight)]
    result, pullback = jax.vjp(forward, *floats)
    grads = pullback(cotangent.astype(jnp.float32))
    return (result.astype(jnp.bfloat16), grads[0].astype(jnp.bfloat16), grads[1], grads[2], grads[3], grads[4], grads[5], grads[6], grads[7], grads[8], grads[9], grads[10], grads[11], grads[12])
```

```python
import functools
import math

import jax
import jax.numpy as jnp
from jax import lax
from jax.experimental import pallas as pl
from jax.experimental.pallas import tpu as pltpu
from jax.sharding import Mesh
from jax.sharding import PartitionSpec as P

HEADS = 16
HD = 128
EPSILON = 1e-06
ROPE_THETA = 10000.0
NEG_FILL = -1e30

CTX = ("ca", "cb")
EXP = ("ring", "core")
ALL = CTX + EXP


MESH = pl.DeviceIdType.MESH


def turn(name, by):
    size = lax.axis_size(name)
    return lax.rem(lax.axis_index(name) + by, size)


def await_bytes(ref, sem):
    pltpu.make_async_copy(ref, ref, sem).wait()


def greet(peers):
    barrier = pltpu.get_barrier_semaphore()
    for peer in peers:
        pl.semaphore_signal(barrier, inc=1, device_id=peer, device_id_type=MESH)
    pl.semaphore_wait(barrier, len(peers))


RING, SIDE_B, SIDE_A, FIRST, SECOND, CORE_OWN, CORE_B, CORE_A, CORE_FIRST, CORE_SECOND = range(10)


def spread_kernel(count, *refs):
    ring = lax.axis_size("ring")
    shards, ids, outs, ids_out = refs[:count], refs[count], refs[count + 1 : 2 * count + 1], refs[2 * count + 1]
    send, got_ring, got_b, got_a, got, place, ids_send, ids_got, ids_place = refs[2 * count + 2 :]
    a, b, r, c = (lax.axis_index(n) for n in ALL)
    na, nb, nc = turn("ca", 1), turn("cb", 1), turn("core", 1)
    to_a, to_b, to_core = {"ca": na}, {"cb": nb}, {"core": nc}
    greet([to_a, to_b, to_core] + [{"ring": turn("ring", k)} for k in range(1, ring)])

    def push(src, dst, ssem, rsem, to):
        pltpu.make_async_remote_copy(
            src_ref=src, dst_ref=dst, send_sem=ssem, recv_sem=rsem, device_id=to, device_id_type=MESH
        ).start()

    def half(ref, which):
        rows, cols = ref.shape[-2:]
        if rows * 8 < cols:
            return ref.at[..., pl.ds(which * (cols // 2), cols // 2)]
        return ref.at[..., pl.ds(which * (rows // 2), rows // 2), :]

    def halves(ref, which):
        rows, cols = ref.shape[-2:]
        if rows * 8 < cols:
            return ref.at[:, :, pl.ds(which * (cols // 2), cols // 2)]
        return ref.at[:, pl.ds(which * (rows // 2), rows // 2), :]

    for w in range(count):
        out = outs[w]
        pltpu.make_async_copy(shards[w], out.at[a, b, r, c], place.at[w]).start()
    pltpu.make_async_copy(ids, ids_out.at[r, c], ids_place).start()
    push(ids, ids_out.at[r, c], ids_send.at[ring], ids_got.at[ring], to_core)
    for w in reversed(range(count)):
        out = outs[w]
        for k in range(1, ring):
            push(shards[w], out.at[a, b, r, c], send.at[w, RING], got_ring.at[w, k], {"ring": turn("ring", k)})
        push(shards[w], out.at[a, b, r, c], send.at[w, SIDE_B], got_b.at[w, 0], to_b)
        push(shards[w], out.at[a, b, r, c], send.at[w, SIDE_A], got_a.at[w, 0], to_a)
        push(shards[w], out.at[a, b, r, c], send.at[w, CORE_OWN], got.at[w, CORE_OWN], to_core)
    for k in range(1, ring):
        push(ids, ids_out.at[r, c], ids_send.at[k], ids_got.at[k], {"ring": turn("ring", k)})

    def sides(w):
        out = outs[w]

        def one(k, carry):
            at = lax.rem(r + ring - k, ring)
            block = out.at[a, b, at, c]
            await_bytes(block, got_ring.at[w, k])
            push(block, block, send.at[w, SIDE_B], got_b.at[w, k], to_b)
            push(block, block, send.at[w, SIDE_A], got_a.at[w, k], to_a)
            push(block, block, send.at[w, CORE_OWN], got.at[w, CORE_OWN], to_core)
            return carry

        lax.fori_loop(1, ring, one, 0)

    def diagonal(w):
        out = outs[w]

        def one(k, carry):
            at = lax.rem(r + ring - k, ring)
            block = out.at[a, nb, at, c]
            await_bytes(block, got_b.at[w, k])
            push(half(block, 0), half(block, 0), send.at[w, FIRST], got.at[w, FIRST], to_a)
            push(block, block, send.at[w, CORE_B], got.at[w, CORE_B], to_core)
            block = out.at[na, b, at, c]
            await_bytes(block, got_a.at[w, k])
            push(half(block, 1), half(block, 1), send.at[w, SECOND], got.at[w, SECOND], to_b)
            push(block, block, send.at[w, CORE_A], got.at[w, CORE_A], to_core)
            return carry

        lax.fori_loop(0, ring, one, 0)

    def last(w):
        block = outs[w].at[na, nb, :, c]
        for which, kind, core_kind in ((0, FIRST, CORE_FIRST), (1, SECOND, CORE_SECOND)):
            part = halves(block, which)
            await_bytes(part, got.at[w, kind])
            push(part, part, send.at[w, core_kind], got.at[w, core_kind], to_core)

    order = list(reversed(range(count)))
    for step in range(count + 2):
        if step < count:
            sides(order[step])
        if 0 <= step - 1 < count:
            diagonal(order[step - 1])
        if 0 <= step - 2 < count:
            last(order[step - 2])

    def ids_on(k, carry):
        block = ids_out.at[lax.rem(r + ring - k, ring), c]
        await_bytes(block, ids_got.at[k])
        push(block, block, ids_send.at[ring], ids_got.at[ring], to_core)
        return carry

    lax.fori_loop(1, ring, ids_on, 0)
    for w in range(count):
        out = outs[w]
        pltpu.make_async_copy(shards[w], out.at[a, b, r, c], place.at[w]).wait()
        mine = lambda p, q: out.at[p, q, :, c]
        await_bytes(out.at[a, b, pl.ds(0, ring - 1), c], send.at[w, RING])
        for kind in (SIDE_B, SIDE_A, CORE_OWN, CORE_B, CORE_A):
            await_bytes(mine(a, b), send.at[w, kind])
        for which, kind in ((0, FIRST), (1, SECOND), (0, CORE_FIRST), (1, CORE_SECOND)):
            await_bytes(halves(mine(a, b), which), send.at[w, kind])
        for kind, p, q in ((CORE_OWN, a, b), (CORE_B, a, nb), (CORE_A, na, b)):
            await_bytes(out.at[p, q, :, nc], got.at[w, kind])
        for which, kind in ((0, CORE_FIRST), (1, CORE_SECOND)):
            await_bytes(halves(out.at[na, nb, :, nc], which), got.at[w, kind])
    pltpu.make_async_copy(ids, ids_out.at[r, c], ids_place).wait()
    for k in range(1, ring):
        await_bytes(ids, ids_send.at[k])
    await_bytes(ids_out.at[:, c], ids_send.at[ring])
    await_bytes(ids_out.at[:, nc], ids_got.at[ring])


def spread(shards, ids):
    count, ring = len(shards), lax.axis_size("ring")
    square = (lax.axis_size("ca"), lax.axis_size("cb"), ring, 2)
    dma = pltpu.SemaphoreType.DMA
    outs = pl.pallas_call(
        functools.partial(spread_kernel, count),
        out_shape=[jax.ShapeDtypeStruct(square + s.shape, s.dtype) for s in shards]
        + [jax.ShapeDtypeStruct((ring, 2) + ids.shape, ids.dtype)],
        in_specs=[pl.BlockSpec(memory_space=pltpu.VMEM)] * (count + 1),
        out_specs=[pl.BlockSpec(memory_space=pl.ANY)] * (count + 1),
        scratch_shapes=[
            dma((count, 10)), dma((count, ring)), dma((count, ring)), dma((count, ring)), dma((count, 10)), dma((count,)),
            dma((ring + 1,)), dma((ring + 1,)), dma,
        ],
        compiler_params=pltpu.CompilerParams(collective_id=0, has_side_effects=True),
        name="spread",
    )(*shards, ids)
    return outs[:count], outs[count]


def collect_kernel(count, *refs):
    ring = lax.axis_size("ring")
    parts, outs = refs[:count], refs[count : 2 * count]
    scratch = refs[2 * count :]
    a, b, r, c = (lax.axis_index(n) for n in ALL)
    na, nb, nc = turn("ca", 1), turn("cb", 1), turn("core", 1)
    to_a, to_b, to_core = {"ca": na}, {"cb": nb}, {"core": nc}
    send, got, ring_send, ring_got, load = scratch[-5:]
    bufs = [scratch[9 * w : 9 * w + 9] for w in range(count)]
    greet([to_a, to_b, to_core] + [{"ring": turn("ring", k)} for k in range(1, ring)])

    def push(src, dst, ssem, rsem, to):
        pltpu.make_async_remote_copy(
            src_ref=src, dst_ref=dst, send_sem=ssem, recv_sem=rsem, device_id=to, device_id_type=MESH
        ).start()

    def half(ref, which):
        rows, cols = ref.shape[-2:]
        lead = (slice(None),) * (len(ref.shape) - 2)
        if cols > 128:
            return ref.at[(*lead, slice(None), pl.ds(which * (cols // 2), cols // 2))]
        return ref.at[(*lead, pl.ds(which * (rows // 2), rows // 2), slice(None))]

    def loads(w):
        own_a, own_b = bufs[w][0:2]
        return (
            pltpu.make_async_copy(half(parts[w].at[a], 0), own_a, load.at[w, 0]),
            pltpu.make_async_copy(half(parts[w].at[:, b], 1), own_b, load.at[w, 1]),
        )

    def first(w):
        for copy in loads(w):
            copy.start()
        in_a, in_b = bufs[w][2:4]
        push(half(parts[w].at[na], 0), in_a, send.at[w, 0], got.at[w, 0], to_a)
        push(half(parts[w].at[:, nb], 1), in_b, send.at[w, 1], got.at[w, 1], to_b)

    def add(into, other):
        def one(k, carry):
            into[:, k] = (into[:, k].astype(jnp.float32) + other[:, k].astype(jnp.float32)).astype(into.dtype)
            return carry

        lax.fori_loop(0, ring, one, 0)

    def second(w):
        own_a, own_b, in_a, in_b, in_a2, in_b2 = bufs[w][:6]
        for copy in loads(w):
            copy.wait()
        await_bytes(in_a, got.at[w, 0])
        add(own_a, in_a)
        push(own_a.at[nb], in_a2, send.at[w, 2], got.at[w, 2], to_b)
        await_bytes(in_b, got.at[w, 1])
        add(own_b, in_b)
        push(own_b.at[na], in_b2, send.at[w, 3], got.at[w, 3], to_a)

    def third(w):
        own_a, own_b, _, _, in_a2, in_b2, total, in_ring = bufs[w][:8]
        await_bytes(in_a2, got.at[w, 2])
        await_bytes(in_b2, got.at[w, 3])

        def one(k, carry):
            sums = [
                own[own_at, k].astype(jnp.float32) + more[k].astype(jnp.float32)
                for own, own_at, more in ((own_a, b, in_a2), (own_b, a, in_b2))
            ]
            for which in range(2):
                half(total.at[k], which)[...] = sums[which].astype(total.dtype)
            return carry

        lax.fori_loop(0, ring, one, 0)
        for k in range(1, ring):
            at = turn("ring", k)
            push(total.at[at], in_ring.at[k - 1], ring_send.at[w, k - 1], ring_got.at[w, k - 1], {"ring": at})

    def fourth(w):
        total, in_ring, final = bufs[w][6:9]
        for k in range(1, ring):
            await_bytes(in_ring.at[k - 1], ring_got.at[w, k - 1])
        if final.shape[0] == 2:
            rows = final.shape[1]
            for core in range(2):
                at = pl.ds(core * rows, rows)
                value = total[r, at, :].astype(jnp.float32)
                for k in range(ring - 1):
                    value = value + in_ring[k, at, :].astype(jnp.float32)
                final[core] = value
            cols = final.shape[2]
            there = outs[w].at[:, pl.ds(pl.multiple_of(c * cols, cols), cols)]
            push(final.at[nc], there, send.at[w, 4], got.at[w, 4], to_core)
            pltpu.make_async_copy(final.at[c], there, load.at[w, 2]).start()
        else:
            value = total[r].astype(jnp.float32)
            for k in range(ring - 1):
                value = value + in_ring[k].astype(jnp.float32)
            outs[w][...] = value

    def finish(w):
        own_a, own_b, in_a, in_b, in_a2, in_b2, total, in_ring, final = bufs[w]
        await_bytes(in_a, send.at[w, 0])
        await_bytes(in_b, send.at[w, 1])
        await_bytes(in_a2, send.at[w, 2])
        await_bytes(in_b2, send.at[w, 3])
        for k in range(1, ring):
            await_bytes(in_ring.at[k - 1], ring_send.at[w, k - 1])
        if final.shape[0] == 2:
            await_bytes(final.at[0], send.at[w, 4])
            await_bytes(final.at[0], got.at[w, 4])
            await_bytes(final.at[0], load.at[w, 2])

    first(0)
    for step in range(count + 3):
        if step + 1 < count:
            first(step + 1)
        if step < count:
            second(step)
        if 0 <= step - 1 < count:
            third(step - 1)
        if 0 <= step - 2 < count:
            fourth(step - 2)
    for w in range(count):
        finish(w)


def collect(parts, small):
    count, ring = len(parts) + 1, lax.axis_size("ring")
    chips = lax.axis_size("ca") * lax.axis_size("cb") * ring
    square = (lax.axis_size("ca"), lax.axis_size("cb"), ring)
    views = [p.reshape(square + (p.shape[0] // chips, p.shape[1])) for p in parts]
    views = [small.reshape(square + small.shape[1:])] + views
    shapes, scratch = [], []
    for v in views:
        rows, cols = v.shape[3:]
        piece = (rows, cols // 2) if cols > 128 else (rows // 2, cols)
        big = cols > 128
        vm = lambda *shape: pltpu.VMEM(shape, v.dtype)
        scratch += [vm(2, ring, *piece)] * 4 + [vm(ring, *piece)] * 2
        scratch += [vm(ring, rows, cols), vm(ring - 1, rows, cols)]
        scratch += [pltpu.VMEM((2, rows // 2, cols) if big else (1, 8, 128), jnp.float32)]
        shapes.append(jax.ShapeDtypeStruct((rows // 2, 2 * cols) if big else (rows, cols), jnp.float32))
    dma = pltpu.SemaphoreType.DMA
    outs = pl.pallas_call(
        functools.partial(collect_kernel, count),
        out_shape=shapes,
        in_specs=[pl.BlockSpec(memory_space=pl.ANY)] * count,
        out_specs=[pl.BlockSpec(memory_space=pltpu.VMEM)] * count,
        scratch_shapes=scratch
        + [dma((count, 5)), dma((count, 5)), dma((count, ring - 1)), dma((count, ring - 1)), dma((count, 3))],
        compiler_params=pltpu.CompilerParams(collective_id=1, has_side_effects=True, vmem_limit_bytes=60 << 20),
        name="collect",
    )(*views)
    return outs[1:], outs[0]


def matmul(left, right):
    return jnp.dot(left, right, preferred_element_type=jnp.float32)


def times_transposed(left, right):
    return lax.dot_general(
        left, right, (((1,), (1,)), ((), ())), preferred_element_type=jnp.float32
    )


def transposed_times(left, right):
    return lax.dot_general(
        left, right, (((0,), (0,)), ((), ())), preferred_element_type=jnp.float32
    )


def norm_rows(values, gain):
    factor = lax.rsqrt(jnp.mean(values * values, axis=-1, keepdims=True) + EPSILON)
    return (values * factor * gain, factor)


def norm_back(grad, values, factor, gain):
    weighted = grad * gain
    inner = jnp.mean(weighted * values, axis=-1, keepdims=True)
    return (factor * weighted - values * factor**3 * inner, jnp.sum(grad * values * factor, axis=0))


def rotary_tables(positions, head_dim):
    half_dim = head_dim // 2
    frequency = jnp.exp(-math.log(ROPE_THETA) * jnp.arange(half_dim, dtype=jnp.float32) / half_dim)
    angles = positions.astype(jnp.float32)[:, None] * frequency[None, :]
    return (jnp.cos(angles), jnp.sin(angles))


def rotate(values, cosine, sine, direction):
    half_dim = values.shape[-1] // 2
    first = values[..., :half_dim]
    second = values[..., half_dim:]
    cos_rows = cosine[:, None, :]
    sin_rows = direction * sine[:, None, :]
    return jnp.concatenate(
        [first * cos_rows - second * sin_rows, second * cos_rows + first * sin_rows], axis=-1
    )


def to_heads(values):
    return lax.all_to_all(values, CTX, split_axis=1, concat_axis=0, tiled=True)


def to_rows(values):
    return lax.all_to_all(values, CTX, split_axis=0, concat_axis=1, tiled=True)


def local(
    tokens, cotangent, lengths, expert_ids, query_weight, key_weight, value_weight, out_weight,
    router_weight, first_gain, second_gain, query_gain, key_gain, gate_weight, up_weight, down_weight,
):
    token_count = tokens.shape[1]
    model_width = tokens.shape[2]
    head_dim = HD
    top_count = expert_ids.shape[2]
    experts = router_weight.shape[1]
    local_experts = gate_weight.shape[0]
    ctx_size = lax.axis_size(CTX)
    sources = lax.axis_size(EXP)
    capacity = max(2, -(-(token_count * top_count * 9) // (experts * 8)))
    score_scale = 1.0 / math.sqrt(head_dim)
    seq_len = token_count * ctx_size
    own_heads = HEADS // ctx_size

    rows_each = query_weight.shape[0]
    packed = jnp.concatenate(
        [g.reshape(-1) for g in (first_gain, second_gain, query_gain, key_gain)] + [router_weight.reshape(-1)]
    )
    small = jnp.pad(packed, (0, -packed.size % 2048)).reshape(-1, 128)
    ids_low = expert_ids[0].astype(jnp.bfloat16).reshape(-1, 128)
    gathered, ids_all = spread([query_weight, key_weight, value_weight, out_weight, small], ids_low)
    full_query, full_key, full_value, full_out = (w.reshape(model_width, -1) for w in gathered[:4])
    smalls = gathered[4].reshape(-1, small.size)
    gains = [smalls[:, i * rows_each : (i + 1) * rows_each].reshape(-1).astype(jnp.float32) for i in range(4)]
    gain_first, gain_second, gain_queries, gain_keys = gains
    full_router = smalls[:, 4 * rows_each : packed.size].reshape(model_width, experts)
    ids_all = ids_all.reshape(sources, token_count, top_count).astype(jnp.int32)
    inputs = tokens[0].astype(jnp.float32)
    length = lengths[0]
    positions = lax.axis_index(CTX) * token_count + jnp.arange(token_count, dtype=jnp.int32)
    row_valid = positions < length
    row_valid = row_valid.astype(jnp.float32)[:, None]
    key_valid = jnp.arange(seq_len, dtype=jnp.int32) < length
    grad_total_low = (cotangent[0].astype(jnp.float32) * row_valid).astype(jnp.bfloat16)
    grad_total = grad_total_low.astype(jnp.float32)

    g_all = lax.all_gather(grad_total_low, EXP, axis=0)
    gate_all, up_all, down_all = (
        lax.all_gather(gate_weight, CTX, axis=2, tiled=True),
        lax.all_gather(up_weight, CTX, axis=2, tiled=True),
        lax.all_gather(down_weight, CTX, axis=1, tiled=True),
    )

    cosine, sine = rotary_tables(positions, head_dim)
    normed_one, factor_one = norm_rows(inputs, gain_first)
    normed_one_low = normed_one.astype(jnp.bfloat16)
    query_raw = matmul(normed_one_low, full_query)
    key_raw = matmul(normed_one_low, full_key)
    value_low = matmul(normed_one_low, full_value).astype(jnp.bfloat16)
    query_normed, query_factor = norm_rows(query_raw, gain_queries)
    key_normed, key_factor = norm_rows(key_raw, gain_keys)
    by_head = lambda v: v.reshape(token_count, HEADS, head_dim)
    query_low = rotate(by_head(query_normed), cosine, sine, 1.0).astype(jnp.bfloat16)
    key_low = rotate(by_head(key_normed), cosine, sine, 1.0).astype(jnp.bfloat16)
    flat = lambda v: v.reshape(v.shape[0], -1)
    heads_of = lambda v: v.reshape(seq_len, own_heads, head_dim)
    q, k, v = (heads_of(to_heads(flat(a))) for a in (query_low, key_low, value_low))

    def scores_of():
        s = jnp.einsum("qhd,khd->hqk", q, k, preferred_element_type=jnp.float32) * score_scale
        return jnp.where(key_valid[None, None, :], s, NEG_FILL)

    scores = scores_of()
    peak = jnp.max(scores, axis=-1, keepdims=True)
    log_total = peak + jnp.log(jnp.sum(jnp.exp(scores - peak), axis=-1, keepdims=True))
    softmax_low = jnp.exp(scores - log_total).astype(jnp.bfloat16)
    attended = jnp.einsum("hqk,khd->qhd", softmax_low, v, preferred_element_type=jnp.float32)
    attended_low = to_rows(flat(attended.astype(jnp.bfloat16)))
    hidden_state = inputs + matmul(attended_low, full_out)
    normed_two, factor_two = norm_rows(hidden_state, gain_second)
    normed_two_low = normed_two.astype(jnp.bfloat16)

    n2_all = lax.all_gather(normed_two_low, EXP, axis=0)
    first_expert = lax.axis_index(EXP) * local_experts
    own_experts = first_expert + jnp.arange(local_experts, dtype=jnp.int32)
    mask = jnp.any(ids_all[:, None, :, :] == own_experts[None, :, None, None], axis=-1)
    before = (jnp.arange(token_count)[:, None] < jnp.arange(token_count)[None, :]).astype(jnp.bfloat16)
    ranks = jnp.einsum("seu,ut->set", mask.astype(jnp.bfloat16), before, preferred_element_type=jnp.float32)
    slots = jnp.arange(capacity, dtype=jnp.float32)
    hot = (mask[:, :, None, :] & (ranks[:, :, None, :] == slots[None, None, :, None])).astype(jnp.bfloat16)
    logits = matmul(n2_all.reshape(-1, model_width), full_router)
    probs = jax.nn.softmax(logits, axis=-1)
    own_probs = lax.dynamic_slice_in_dim(probs, first_expert, local_experts, 1).reshape(sources, token_count, local_experts)
    hot32 = hot.astype(jnp.float32)
    row_gate = jnp.sum(hot32 * own_probs.transpose(0, 2, 1)[:, :, None, :], axis=-1)
    x = jnp.einsum("sect,std->escd", hot, n2_all, preferred_element_type=jnp.float32).astype(jnp.bfloat16)
    g_rows = jnp.einsum("sect,std->escd", hot, g_all, preferred_element_type=jnp.float32)
    row_gate = row_gate.transpose(1, 0, 2)[..., None]
    de = (g_rows * row_gate).astype(jnp.bfloat16)
    ee = lambda eq, a, b: jnp.einsum(eq, a, b, preferred_element_type=jnp.float32)
    gp = ee("escd,edf->escf", x, gate_all)
    up = ee("escd,edf->escf", x, up_all)
    sig = jax.nn.sigmoid(gp)
    hid = (gp * sig * up).astype(jnp.bfloat16)
    eo = ee("escf,efd->escd", hid, down_all).astype(jnp.bfloat16)
    dgate_rows = jnp.sum(g_rows * eo.astype(jnp.float32), axis=-1)
    mixed_rows = (row_gate * eo.astype(jnp.float32)).astype(jnp.bfloat16)
    mixed_part = jnp.einsum("sect,escd->std", hot, mixed_rows, preferred_element_type=jnp.float32)
    mixed = lax.psum_scatter(mixed_part.astype(jnp.bfloat16).reshape(-1, model_width), EXP, scatter_dimension=0, tiled=True)
    layer_out = (row_valid * (hidden_state + mixed.astype(jnp.float32))).astype(jnp.bfloat16)

    dhid = ee("escd,efd->escf", de, down_all)
    dgp = (dhid * up * sig * (1.0 + gp * (1.0 - sig))).astype(jnp.bfloat16)
    dup = (dhid * gp * sig).astype(jnp.bfloat16)
    down_part = ee("escf,escd->efd", hid, de)
    gate_part = ee("escd,escf->edf", x, dgp)
    up_part = ee("escd,escf->edf", x, dup)
    dpair = (ee("escf,edf->escd", dgp, gate_all) + ee("escf,edf->escd", dup, up_all)).astype(jnp.bfloat16)
    rs_ctx = lambda v, a: lax.psum_scatter(v.astype(jnp.bfloat16), CTX, scatter_dimension=a, tiled=True).astype(jnp.float32)
    gate_grad, up_grad, down_grad = rs_ctx(gate_part, 2), rs_ctx(up_part, 2), rs_ctx(down_part, 1)

    dprobs_own = jnp.sum(hot32 * dgate_rows.transpose(1, 0, 2)[..., None], axis=2)
    dprobs_own = dprobs_own.transpose(0, 2, 1).reshape(-1, local_experts)
    onto = (jnp.arange(experts)[None, :] == own_experts[:, None]).astype(jnp.float32)
    dprobs = jnp.sum(dprobs_own[:, :, None] * onto[None], axis=1)
    dlogit_low = (probs * (dprobs - jnp.sum(dprobs * probs, axis=-1, keepdims=True))).astype(jnp.bfloat16)
    router_part = transposed_times(n2_all.reshape(-1, model_width), dlogit_low)
    dn2_part = jnp.einsum("sect,escd->std", hot, dpair, preferred_element_type=jnp.float32).reshape(-1, model_width)
    dn2_part = dn2_part + times_transposed(dlogit_low, full_router)
    dn2 = lax.psum_scatter(dn2_part.astype(jnp.bfloat16), EXP, scatter_dimension=0, tiled=True).astype(jnp.float32)

    dh_norm, gain_second_part = norm_back(dn2, hidden_state, factor_two, gain_second)
    grad_hidden = grad_total + dh_norm
    dh_low = grad_hidden.astype(jnp.bfloat16)
    out_part = transposed_times(attended_low, dh_low)
    d_att = heads_of(to_heads(times_transposed(dh_low, full_out).astype(jnp.bfloat16)))
    soft = jnp.exp(scores_of() - log_total)
    dp = jnp.einsum("qhd,khd->hqk", d_att, v, preferred_element_type=jnp.float32)
    dv = jnp.einsum("hqk,qhd->khd", soft.astype(jnp.bfloat16), d_att, preferred_element_type=jnp.float32)
    inner = jnp.sum(dp * soft, axis=-1, keepdims=True)
    ds = (soft * (dp - inner)).astype(jnp.bfloat16)
    dq = jnp.einsum("hqk,khd->qhd", ds, k, preferred_element_type=jnp.float32) * score_scale
    dk = jnp.einsum("hqk,qhd->khd", ds, q, preferred_element_type=jnp.float32) * score_scale
    dq, dk, dv = (to_rows(flat(a.astype(jnp.bfloat16))) for a in (dq, dk, dv))
    unrotate = lambda a: rotate(by_head(a.astype(jnp.float32)), cosine, sine, -1.0).reshape(token_count, model_width)
    dk_raw, gain_keys_part = norm_back(unrotate(dk), key_raw, key_factor, gain_keys)
    dq_raw, gain_queries_part = norm_back(unrotate(dq), query_raw, query_factor, gain_queries)
    dk_low, dq_low, dv_low = dk_raw.astype(jnp.bfloat16), dq_raw.astype(jnp.bfloat16), dv
    dn1 = times_transposed(dq_low, full_query) + times_transposed(dk_low, full_key)
    dn1 = dn1 + times_transposed(dv_low, full_value)
    input_norm, gain_first_part = norm_back(dn1, inputs, factor_one, gain_first)
    input_grad = (grad_hidden + input_norm).astype(jnp.bfloat16)
    core = lax.axis_index("core")
    swap = lambda v: lax.ppermute(v, "core", [(0, 1), (1, 0)])

    def columns_of_core(v):
        v = v.reshape(token_count, 2, -1)
        return jnp.concatenate([lax.dynamic_index_in_dim(v, core, 1, False), swap(lax.dynamic_index_in_dim(v, 1 - core, 1, False))], axis=0)

    both = lambda v: jnp.concatenate([v, swap(v)], axis=0)
    n1_both, att_both = both(normed_one_low), both(attended_low)
    parts = [
        transposed_times(l, columns_of_core(r)).astype(jnp.bfloat16)
        for l, r in ((att_both, dh_low), (n1_both, dq_low), (n1_both, dk_low), (n1_both, dv_low))
    ]
    split = lambda v: v.reshape(ctx_size * sources // 2, 2, -1)
    small_parts = jnp.concatenate(
        [split(v) for v in (gain_first_part, gain_second_part, gain_queries_part, gain_keys_part, router_part)], axis=2
    )
    small_parts = jnp.pad(small_parts, ((0, 0), (0, 0), (0, -small_parts.shape[2] % 2048)))
    small_parts = lax.dynamic_index_in_dim(small_parts, core, 1, False) + swap(lax.dynamic_index_in_dim(small_parts, 1 - core, 1, False))
    weight_grads, small_grads = collect(parts, small_parts.reshape(ctx_size * sources // 2, -1, 128))
    weight_grads = list(weight_grads[1:]) + [weight_grads[0]]
    small_grads = small_grads.reshape(-1)
    gain_grads = [small_grads[i * rows_each : (i + 1) * rows_each] for i in range(4)]
    router_grad = small_grads[4 * rows_each : packed.size].reshape(rows_each, experts)
    return (layer_out[None], input_grad[None], *weight_grads, router_grad, *gain_grads, gate_grad, up_grad, down_grad)


def solution(mesh):
    ctx, exp = mesh.devices.shape
    fine = Mesh(mesh.devices.reshape(2, ctx // 2, exp // 2, 2), ("ca", "cb", "ring", "core"))
    rows = P(EXP, CTX, None)
    flat2, flat1 = P(ALL, None), P(ALL)
    placed = (rows, rows, P(EXP), rows) + (flat2,) * 5 + (flat1,) * 4 + (P(EXP, None, CTX),) * 2 + (P(EXP, CTX, None),)
    outs = (rows, rows) + (flat2,) * 5 + (flat1,) * 4 + (P(EXP, None, CTX),) * 2 + (P(EXP, CTX, None),)
    return jax.shard_map(local, mesh=fine, in_specs=placed, out_specs=outs, check_vma=False)
```

```python
import functools
import math

import jax
import jax.numpy as jnp
from jax import lax
from jax.experimental import pallas as pl
from jax.experimental.pallas import tpu as pltpu
from jax.sharding import Mesh
from jax.sharding import PartitionSpec as P

HEADS = 16
HD = 128
EPSILON = 1e-06
ROPE_THETA = 10000.0
NEG_FILL = -1e30

CTX = ("ca", "cb")
EXP = ("ring", "core")
ALL = CTX + EXP


MESH = pl.DeviceIdType.MESH


def turn(name, by):
    size = lax.axis_size(name)
    return lax.rem(lax.axis_index(name) + by, size)


def await_bytes(ref, sem):
    pltpu.make_async_copy(ref, ref, sem).wait()


def greet(peers):
    barrier = pltpu.get_barrier_semaphore()
    for peer in peers:
        pl.semaphore_signal(barrier, inc=1, device_id=peer, device_id_type=MESH)
    pl.semaphore_wait(barrier, len(peers))


def push(src, dst, ssem, rsem, to):
    pltpu.make_async_remote_copy(
        src_ref=src, dst_ref=dst, send_sem=ssem, recv_sem=rsem, device_id=to, device_id_type=MESH
    ).start()


RING, SIDE_B, SIDE_A, FIRST, SECOND, CORE_OWN, CORE_B, CORE_A, CORE_FIRST, CORE_SECOND = range(10)


def spread_kernel(count, *refs):
    ring = lax.axis_size("ring")
    shards, ids, outs, ids_out = refs[:count], refs[count], refs[count + 1 : 2 * count + 1], refs[2 * count + 1]
    send, got_ring, got_b, got_a, got, place, ids_send, ids_got, ids_place = refs[2 * count + 2 :]
    a, b, r, c = (lax.axis_index(n) for n in ALL)
    na, nb, nc = turn("ca", 1), turn("cb", 1), turn("core", 1)
    to_a, to_b, to_core = {"ca": na}, {"cb": nb}, {"core": nc}
    greet([to_a, to_b, to_core] + [{"ring": turn("ring", k)} for k in range(1, ring)])

    def half(ref, which):
        rows, cols = ref.shape[-2:]
        if rows * 8 < cols:
            return ref.at[..., pl.ds(which * (cols // 2), cols // 2)]
        return ref.at[..., pl.ds(which * (rows // 2), rows // 2), :]

    def halves(ref, which):
        rows, cols = ref.shape[-2:]
        if rows * 8 < cols:
            return ref.at[:, :, pl.ds(which * (cols // 2), cols // 2)]
        return ref.at[:, pl.ds(which * (rows // 2), rows // 2), :]

    for w in range(count):
        out = outs[w]
        pltpu.make_async_copy(shards[w], out.at[a, b, r, c], place.at[w]).start()
    pltpu.make_async_copy(ids, ids_out.at[r, c], ids_place).start()
    push(ids, ids_out.at[r, c], ids_send.at[ring], ids_got.at[ring], to_core)
    for w in reversed(range(count)):
        out = outs[w]
        for k in range(1, ring):
            push(shards[w], out.at[a, b, r, c], send.at[w, RING], got_ring.at[w, k], {"ring": turn("ring", k)})
        push(shards[w], out.at[a, b, r, c], send.at[w, SIDE_B], got_b.at[w, 0], to_b)
        push(shards[w], out.at[a, b, r, c], send.at[w, SIDE_A], got_a.at[w, 0], to_a)
        push(shards[w], out.at[a, b, r, c], send.at[w, CORE_OWN], got.at[w, CORE_OWN], to_core)
    for k in range(1, ring):
        push(ids, ids_out.at[r, c], ids_send.at[k], ids_got.at[k], {"ring": turn("ring", k)})

    def sides(w):
        out = outs[w]

        def one(k, carry):
            at = lax.rem(r + ring - k, ring)
            block = out.at[a, b, at, c]
            await_bytes(block, got_ring.at[w, k])
            push(block, block, send.at[w, SIDE_B], got_b.at[w, k], to_b)
            push(block, block, send.at[w, SIDE_A], got_a.at[w, k], to_a)
            push(block, block, send.at[w, CORE_OWN], got.at[w, CORE_OWN], to_core)
            return carry

        lax.fori_loop(1, ring, one, 0)

    def diagonal(w):
        out = outs[w]

        def one(k, carry):
            at = lax.rem(r + ring - k, ring)
            block = out.at[a, nb, at, c]
            await_bytes(block, got_b.at[w, k])
            push(half(block, 0), half(block, 0), send.at[w, FIRST], got.at[w, FIRST], to_a)
            push(block, block, send.at[w, CORE_B], got.at[w, CORE_B], to_core)
            block = out.at[na, b, at, c]
            await_bytes(block, got_a.at[w, k])
            push(half(block, 1), half(block, 1), send.at[w, SECOND], got.at[w, SECOND], to_b)
            push(block, block, send.at[w, CORE_A], got.at[w, CORE_A], to_core)
            return carry

        lax.fori_loop(0, ring, one, 0)

    def last(w):
        block = outs[w].at[na, nb, :, c]
        for which, kind, core_kind in ((0, FIRST, CORE_FIRST), (1, SECOND, CORE_SECOND)):
            part = halves(block, which)
            await_bytes(part, got.at[w, kind])
            push(part, part, send.at[w, core_kind], got.at[w, core_kind], to_core)

    order = list(reversed(range(count)))
    for step in range(count + 2):
        if step < count:
            sides(order[step])
        if 0 <= step - 1 < count:
            diagonal(order[step - 1])
        if 0 <= step - 2 < count:
            last(order[step - 2])

    def ids_on(k, carry):
        block = ids_out.at[lax.rem(r + ring - k, ring), c]
        await_bytes(block, ids_got.at[k])
        push(block, block, ids_send.at[ring], ids_got.at[ring], to_core)
        return carry

    lax.fori_loop(1, ring, ids_on, 0)
    for w in range(count):
        out = outs[w]
        pltpu.make_async_copy(shards[w], out.at[a, b, r, c], place.at[w]).wait()
        mine = lambda p, q: out.at[p, q, :, c]
        await_bytes(out.at[a, b, pl.ds(0, ring - 1), c], send.at[w, RING])
        for kind in (SIDE_B, SIDE_A, CORE_OWN, CORE_B, CORE_A):
            await_bytes(mine(a, b), send.at[w, kind])
        for which, kind in ((0, FIRST), (1, SECOND), (0, CORE_FIRST), (1, CORE_SECOND)):
            await_bytes(halves(mine(a, b), which), send.at[w, kind])
        for kind, p, q in ((CORE_OWN, a, b), (CORE_B, a, nb), (CORE_A, na, b)):
            await_bytes(out.at[p, q, :, nc], got.at[w, kind])
        for which, kind in ((0, CORE_FIRST), (1, CORE_SECOND)):
            await_bytes(halves(out.at[na, nb, :, nc], which), got.at[w, kind])
    pltpu.make_async_copy(ids, ids_out.at[r, c], ids_place).wait()
    for k in range(1, ring):
        await_bytes(ids, ids_send.at[k])
    await_bytes(ids_out.at[:, c], ids_send.at[ring])
    await_bytes(ids_out.at[:, nc], ids_got.at[ring])


def spread(shards, ids):
    count, ring = len(shards), lax.axis_size("ring")
    square = (lax.axis_size("ca"), lax.axis_size("cb"), ring, 2)
    dma = pltpu.SemaphoreType.DMA
    outs = pl.pallas_call(
        functools.partial(spread_kernel, count),
        out_shape=[jax.ShapeDtypeStruct(square + s.shape, s.dtype) for s in shards]
        + [jax.ShapeDtypeStruct((ring, 2) + ids.shape, ids.dtype)],
        in_specs=[pl.BlockSpec(memory_space=pltpu.VMEM)] * (count + 1),
        out_specs=[pl.BlockSpec(memory_space=pl.ANY)] * (count + 1),
        scratch_shapes=[
            dma((count, 10)), dma((count, ring)), dma((count, ring)), dma((count, ring)), dma((count, 10)), dma((count,)),
            dma((ring + 1,)), dma((ring + 1,)), dma,
        ],
        compiler_params=pltpu.CompilerParams(collective_id=0, has_side_effects=True),
        cost_estimate=pl.CostEstimate(flops=150_000_000_000, bytes_accessed=300_000_000, transcendentals=0),
        name="spread",
    )(*shards, ids)
    return outs[:count], outs[count]


def collect_kernel(count, *refs):
    ring = lax.axis_size("ring")
    parts, outs = refs[:count], refs[count : 2 * count]
    scratch = refs[2 * count :]
    a, b, r, c = (lax.axis_index(n) for n in ALL)
    na, nb, nc = turn("ca", 1), turn("cb", 1), turn("core", 1)
    to_a, to_b, to_core = {"ca": na}, {"cb": nb}, {"core": nc}
    send, got, ring_send, ring_got, load = scratch[-5:]
    bufs = [scratch[9 * w : 9 * w + 9] for w in range(count)]
    greet([to_a, to_b, to_core] + [{"ring": turn("ring", k)} for k in range(1, ring)])

    def half(ref, which):
        rows, cols = ref.shape[-2:]
        lead = (slice(None),) * (len(ref.shape) - 2)
        if cols > 128:
            return ref.at[(*lead, slice(None), pl.ds(which * (cols // 2), cols // 2))]
        return ref.at[(*lead, pl.ds(which * (rows // 2), rows // 2), slice(None))]

    def loads(w):
        own_a, own_b = bufs[w][0:2]
        return (
            pltpu.make_async_copy(half(parts[w].at[a], 0), own_a, load.at[w, 0]),
            pltpu.make_async_copy(half(parts[w].at[:, b], 1), own_b, load.at[w, 1]),
        )

    def first(w):
        for copy in loads(w):
            copy.start()
        in_a, in_b = bufs[w][2:4]
        push(half(parts[w].at[na], 0), in_a, send.at[w, 0], got.at[w, 0], to_a)
        push(half(parts[w].at[:, nb], 1), in_b, send.at[w, 1], got.at[w, 1], to_b)

    def add(into, other):
        def one(k, carry):
            into[:, k] = (into[:, k].astype(jnp.float32) + other[:, k].astype(jnp.float32)).astype(into.dtype)
            return carry

        lax.fori_loop(0, ring, one, 0)

    def second(w):
        own_a, own_b, in_a, in_b, in_a2, in_b2 = bufs[w][:6]
        for copy in loads(w):
            copy.wait()
        await_bytes(in_a, got.at[w, 0])
        add(own_a, in_a)
        push(own_a.at[nb], in_a2, send.at[w, 2], got.at[w, 2], to_b)
        await_bytes(in_b, got.at[w, 1])
        add(own_b, in_b)
        push(own_b.at[na], in_b2, send.at[w, 3], got.at[w, 3], to_a)

    def third(w):
        own_a, own_b, _, _, in_a2, in_b2, total, in_ring = bufs[w][:8]
        await_bytes(in_a2, got.at[w, 2])
        await_bytes(in_b2, got.at[w, 3])

        def one(k, carry):
            sums = [
                own[own_at, k].astype(jnp.float32) + more[k].astype(jnp.float32)
                for own, own_at, more in ((own_a, b, in_a2), (own_b, a, in_b2))
            ]
            for which in range(2):
                half(total.at[k], which)[...] = sums[which].astype(total.dtype)
            return carry

        lax.fori_loop(0, ring, one, 0)
        for k in range(1, ring):
            at = turn("ring", k)
            push(total.at[at], in_ring.at[k - 1], ring_send.at[w, k - 1], ring_got.at[w, k - 1], {"ring": at})

    def fourth(w):
        total, in_ring, final = bufs[w][6:9]
        for k in range(1, ring):
            await_bytes(in_ring.at[k - 1], ring_got.at[w, k - 1])
        if final.shape[0] == 2:
            rows = final.shape[1]
            for core in range(2):
                at = pl.ds(core * rows, rows)
                value = total[r, at, :].astype(jnp.float32)
                for k in range(ring - 1):
                    value = value + in_ring[k, at, :].astype(jnp.float32)
                final[core] = value
            cols = final.shape[2]
            there = outs[w].at[:, pl.ds(pl.multiple_of(c * cols, cols), cols)]
            push(final.at[nc], there, send.at[w, 4], got.at[w, 4], to_core)
            pltpu.make_async_copy(final.at[c], there, load.at[w, 2]).start()
        else:
            value = total[r].astype(jnp.float32)
            for k in range(ring - 1):
                value = value + in_ring[k].astype(jnp.float32)
            outs[w][...] = value

    def finish(w):
        own_a, own_b, in_a, in_b, in_a2, in_b2, total, in_ring, final = bufs[w]
        await_bytes(in_a, send.at[w, 0])
        await_bytes(in_b, send.at[w, 1])
        await_bytes(in_a2, send.at[w, 2])
        await_bytes(in_b2, send.at[w, 3])
        for k in range(1, ring):
            await_bytes(in_ring.at[k - 1], ring_send.at[w, k - 1])
        if final.shape[0] == 2:
            await_bytes(final.at[0], send.at[w, 4])
            await_bytes(final.at[0], got.at[w, 4])
            await_bytes(final.at[0], load.at[w, 2])

    first(0)
    for step in range(count + 3):
        if step + 1 < count:
            first(step + 1)
        if step < count:
            second(step)
        if 0 <= step - 1 < count:
            third(step - 1)
        if 0 <= step - 2 < count:
            fourth(step - 2)
    for w in range(count):
        finish(w)


def collect(parts, small):
    count, ring = len(parts) + 1, lax.axis_size("ring")
    chips = lax.axis_size("ca") * lax.axis_size("cb") * ring
    square = (lax.axis_size("ca"), lax.axis_size("cb"), ring)
    views = [p.reshape(square + (p.shape[0] // chips, p.shape[1])) for p in parts]
    views = [small.reshape(square + small.shape[1:])] + views
    shapes, scratch = [], []
    for v in views:
        rows, cols = v.shape[3:]
        piece = (rows, cols // 2) if cols > 128 else (rows // 2, cols)
        big = cols > 128
        vm = lambda *shape: pltpu.VMEM(shape, v.dtype)
        scratch += [vm(2, ring, *piece)] * 4 + [vm(ring, *piece)] * 2
        scratch += [vm(ring, rows, cols), vm(ring - 1, rows, cols)]
        scratch += [pltpu.VMEM((2, rows // 2, cols) if big else (1, 8, 128), jnp.float32)]
        shapes.append(jax.ShapeDtypeStruct((rows // 2, 2 * cols) if big else (rows, cols), jnp.float32))
    dma = pltpu.SemaphoreType.DMA
    outs = pl.pallas_call(
        functools.partial(collect_kernel, count),
        out_shape=shapes,
        in_specs=[pl.BlockSpec(memory_space=pl.ANY)] * count,
        out_specs=[pl.BlockSpec(memory_space=pltpu.VMEM)] * count,
        scratch_shapes=scratch
        + [dma((count, 5)), dma((count, 5)), dma((count, ring - 1)), dma((count, ring - 1)), dma((count, 3))],
        compiler_params=pltpu.CompilerParams(collective_id=1, has_side_effects=True, vmem_limit_bytes=60 << 20),
        cost_estimate=pl.CostEstimate(flops=160000000000, bytes_accessed=320000000, transcendentals=0),
        name="collect",
    )(*views)
    return outs[1:], outs[0]


def dispatch_kernel(down, *refs):
    ring, count = lax.axis_size("ring"), len(down)
    rows, weights, rows_out, weights_out = refs[0], refs[1 : count + 1], refs[count + 1], refs[count + 2 : 2 * count + 2]
    held_rows, held = refs[2 * count + 2], refs[2 * count + 3 : 3 * count + 3]
    load, place, send_ring, got_ring, core_sem, send_side, got_side, send_diag, got_diag = refs[3 * count + 3 :]
    a, b, r, c = (lax.axis_index(n) for n in ALL)
    na, nb, nc = turn("ca", 1), turn("cb", 1), turn("core", 1)
    to_a, to_b, to_core = {"ca": na}, {"cb": nb}, {"core": nc}
    greet([to_a, to_b, to_core] + [{"ring": turn("ring", k)} for k in range(1, ring)])

    def slot(w, e, p, q):
        units = weights[w].shape[1 if down[w] else 2]
        at = pl.ds(pl.multiple_of((2 * p + q) * units, units), units)
        return weights_out[w].at[e, at, :] if down[w] else weights_out[w].at[e, :, at]

    fetch_rows = pltpu.make_async_copy(rows, held_rows, load.at[count])
    fetch_rows.start()
    fetches = [pltpu.make_async_copy(weights[w], held[w], load.at[w]) for w in range(count)]
    for fetch in fetches:
        fetch.start()
    fetch_rows.wait()
    pltpu.make_async_copy(held_rows, rows_out.at[r, c], place.at[count]).start()
    to_next, to_last = {"ring": turn("ring", 1)}, {"ring": turn("ring", ring - 1)}

    def along(step):
        return (
            ((r + 1 < ring) & (r >= step), r >= step + 1, lax.rem(r + ring - step, ring), lax.rem(r + ring - 1 - step, ring), to_next, 0),
            ((r >= 1) & (r + step < ring), r + 1 + step < ring, lax.rem(r + step, ring), lax.rem(r + 1 + step, ring), to_last, 1),
        )

    def send_along(step):
        for sent, _, block, _, to, side in along(step):

            @pl.when(sent)
            def _(block=block, to=to, side=side):
                src = held_rows if step == 0 else rows_out.at[block, c]
                push(src, rows_out.at[block, c], send_ring.at[side, step], got_ring.at[side, step], to)

    send_along(0)
    push(held_rows, rows_out.at[r, c], core_sem.at[0], core_sem.at[1], to_core)
    for w in range(count):
        fetches[w].wait()
        for e in range(weights[w].shape[0]):
            mine, here = held[w].at[e], slot(w, e, a, b)
            push(mine, here, send_side.at[w, 0, e], got_side.at[w, 0, e], to_b)
            push(mine, here, send_side.at[w, 1, e], got_side.at[w, 1, e], to_a)
            pltpu.make_async_copy(mine, here, place.at[w]).start()

    for step in range(ring - 1):
        for _, comes, _, block, _, side in along(step):

            @pl.when(comes)
            def _(block=block, side=side):
                await_bytes(rows_out.at[block, c], got_ring.at[side, step])

        if step + 1 < ring - 1:
            send_along(step + 1)
        for _, comes, _, block, _, side in along(step):

            @pl.when(comes)
            def _(block=block):
                here = rows_out.at[block, c]
                push(here, here, core_sem.at[0], core_sem.at[1], to_core)

    for w in range(count):
        experts = weights[w].shape[0]
        for e in range(experts):
            from_b, from_a = slot(w, e, a, nb), slot(w, e, na, b)
            await_bytes(from_b, got_side.at[w, 0, e])
            await_bytes(from_a, got_side.at[w, 1, e])
            if 2 * e < experts:
                push(from_b, from_b, send_diag.at[w, e], got_diag.at[w, e], to_a)
            else:
                push(from_a, from_a, send_diag.at[w, e], got_diag.at[w, e], to_b)

    await_bytes(held_rows, place.at[count])
    for step in range(ring - 1):
        for sent, _, _, _, _, side in along(step):

            @pl.when(sent)
            def _(side=side):
                await_bytes(held_rows, send_ring.at[side, step])

    await_bytes(rows_out.at[:, c], core_sem.at[0])
    await_bytes(rows_out.at[:, nc], core_sem.at[1])
    for w in range(count):
        await_bytes(held[w], place.at[w])
        for e in range(weights[w].shape[0]):
            await_bytes(held[w].at[e], send_side.at[w, 0, e])
            await_bytes(held[w].at[e], send_side.at[w, 1, e])
            await_bytes(held[w].at[e], send_diag.at[w, e])
            await_bytes(slot(w, e, na, nb), got_diag.at[w, e])


def dispatch(rows, weights, down):
    ring, chips = lax.axis_size("ring"), lax.axis_size("ca") * lax.axis_size("cb")
    experts, count = max([w.shape[0] for w in weights], default=1), len(weights)
    full = [(w.shape[0], w.shape[1] * (chips if d else 1), w.shape[2] * (1 if d else chips)) for w, d in zip(weights, down)]
    dma = pltpu.SemaphoreType.DMA
    outs = pl.pallas_call(
        functools.partial(dispatch_kernel, tuple(down)),
        out_shape=[jax.ShapeDtypeStruct((ring, 2) + rows.shape, rows.dtype)]
        + [jax.ShapeDtypeStruct(shape, rows.dtype) for shape in full],
        in_specs=[pl.BlockSpec(memory_space=pl.ANY)] * (count + 1),
        out_specs=[pl.BlockSpec(memory_space=pl.ANY)] * (count + 1),
        scratch_shapes=[pltpu.VMEM(v.shape, v.dtype) for v in (rows, *weights)]
        + [
            dma((1 + count,)), dma((1 + count,)), dma((2, ring)), dma((2, ring)), dma((2,)),
            dma((max(count, 1), 2, experts)), dma((max(count, 1), 2, experts)), dma((max(count, 1), experts)), dma((max(count, 1), experts)),
        ],
        compiler_params=pltpu.CompilerParams(collective_id=2, has_side_effects=True),
        cost_estimate=pl.CostEstimate(flops=80_000_000_000, bytes_accessed=100_000_000, transcendentals=0),
        name="dispatch",
    )(rows, *weights)
    return outs[0], outs[1:]


def give_back_kernel(part, out, own, core_in, ring_in, load, core_send, core_got, ring_send, ring_got):
    ring = lax.axis_size("ring")
    r, c, nc = lax.axis_index("ring"), lax.axis_index("core"), turn("core", 1)
    greet([{"core": nc}] + [{"ring": turn("ring", k)} for k in range(1, ring)])
    order = list(range(1, ring)) + [0]
    block_of = lambda k: lax.rem(r + k, ring)
    for k in order:
        push(part.at[block_of(k), nc], core_in.at[k], core_send.at[k], core_got.at[k], {"core": nc})
        pltpu.make_async_copy(part.at[block_of(k), c], own.at[k], load.at[k]).start()
    rows, cols = own.shape[1:]
    tile = 32
    for k in order:
        await_bytes(own.at[k], load.at[k])
        await_bytes(core_in.at[k], core_got.at[k])
        if k == 0:
            continue

        def add(i, carry):
            at = pl.ds(pl.multiple_of(i * tile, tile), tile)
            own[k, at] = (own[k, at].astype(jnp.float32) + core_in[k, at].astype(jnp.float32)).astype(own.dtype)
            return carry

        lax.fori_loop(0, rows // tile, add, 0)
        push(own.at[k], ring_in.at[k - 1], ring_send.at[k - 1], ring_got.at[k - 1], {"ring": block_of(k)})
    for k in range(1, ring):
        await_bytes(ring_in.at[k - 1], ring_got.at[k - 1])

    def total(i, carry):
        at = pl.ds(pl.multiple_of(i * tile, tile), tile)
        value = own[0, at].astype(jnp.float32) + core_in[0, at].astype(jnp.float32)
        for k in range(ring - 1):
            value = value + ring_in[k, at].astype(jnp.float32)
        out[at, :] = value
        return carry

    lax.fori_loop(0, rows // tile, total, 0)
    for k in order:
        await_bytes(core_in.at[k], core_send.at[k])
        if k:
            await_bytes(ring_in.at[k - 1], ring_send.at[k - 1])


def give_back(part):
    ring, dma = lax.axis_size("ring"), pltpu.SemaphoreType.DMA
    rows, cols = part.shape[1:]
    block = lambda n: pltpu.VMEM((n, rows, cols), part.dtype)
    return pl.pallas_call(
        give_back_kernel,
        out_shape=jax.ShapeDtypeStruct((rows, cols), jnp.float32),
        in_specs=[pl.BlockSpec(memory_space=pl.ANY)],
        out_specs=pl.BlockSpec(memory_space=pltpu.VMEM),
        scratch_shapes=[block(ring), block(ring), block(ring - 1), dma((ring,)), dma((ring,)), dma((ring,)), dma((ring,)), dma((ring,))],
        compiler_params=pltpu.CompilerParams(collective_id=3, has_side_effects=True, vmem_limit_bytes=60 << 20),
        cost_estimate=pl.CostEstimate(flops=100000000000, bytes_accessed=200000000, transcendentals=0),
        name="give_back",
    )(part.reshape(ring, 2, rows, cols))


def matmul(left, right):
    return jnp.dot(left, right, preferred_element_type=jnp.float32)


def times_transposed(left, right):
    return lax.dot_general(
        left, right, (((1,), (1,)), ((), ())), preferred_element_type=jnp.float32
    )


def transposed_times(left, right):
    return lax.dot_general(
        left, right, (((0,), (0,)), ((), ())), preferred_element_type=jnp.float32
    )


def corners():
    return ((0, 1), (1, 0), (1, 1))


def corner(da, db):
    pa, pb = turn("ca", da), turn("cb", db)
    return 2 * pa + pb, {"ca": pa, "cb": pb}


def rows_to_heads(src, dst, send, got, place):
    rows, width = src.shape[0], dst.shape[1]
    me, _ = corner(0, 0)
    there = dst.at[pl.ds(pl.multiple_of(me * rows, rows), rows), :]
    for i, (da, db) in enumerate(corners()):
        peer, to = corner(da, db)
        push(src.at[:, pl.ds(pl.multiple_of(peer * width, width), width)], there, send.at[i], got.at[i], to)
    pltpu.make_async_copy(src.at[:, pl.ds(pl.multiple_of(me * width, width), width)], there, place).start()


def wait_heads(src, dst, got, place):
    rows = src.shape[0]
    here = lambda at: dst.at[pl.ds(pl.multiple_of(at * rows, rows), rows), :]
    await_bytes(here(corner(0, 0)[0]), place)
    for i, (da, db) in enumerate(corners()):
        await_bytes(here(corner(da, db)[0]), got.at[i])


def attend_kernel(scale, q, k, v, keep, o, qh, kh, vh, logs, oh, send, got, place, send_o, got_o, place_o):
    rows, width = q.shape[0], qh.shape[1]
    greet([corner(da, db)[1] for da, db in corners()])
    pairs = ((q, qh), (k, kh), (v, vh))
    for i, (src, dst) in enumerate(pairs):
        rows_to_heads(src, dst, send.at[i], got.at[i], place.at[i])
    for i, (src, dst) in enumerate(pairs):
        wait_heads(src, dst, got.at[i], place.at[i])
    me, _ = corner(0, 0)
    tile = 128
    mine = pl.ds(pl.multiple_of(me * width, width), width)

    def block(at_block):
        def part(i, carry):
            at = pl.ds(pl.multiple_of(at_block * rows + i * tile, tile), tile)
            for h in range(width // HD):
                lanes = pl.ds(h * HD, HD)
                s = times_transposed(qh[at, lanes], kh[:, lanes]) * scale
                s = jnp.where(keep[...] > 0.0, s, NEG_FILL)
                peak = jnp.max(s, axis=-1, keepdims=True)
                p = jnp.exp(s - peak)
                total = jnp.sum(p, axis=-1, keepdims=True)
                logs[h, at, :] = peak + jnp.log(total)
                low = (p * (1.0 / total)).astype(jnp.bfloat16)
                oh[at, lanes] = matmul(low, vh[:, lanes]).astype(jnp.bfloat16)
            return carry

        lax.fori_loop(0, rows // tile, part, 0)

    for i, (da, db) in enumerate(corners()):
        peer, to = corner(da, db)
        block(peer)
        push(oh.at[pl.ds(pl.multiple_of(peer * rows, rows), rows), :], o.at[:, mine], send_o.at[i], got_o.at[i], to)
    block(me)
    pltpu.make_async_copy(oh.at[pl.ds(pl.multiple_of(me * rows, rows), rows), :], o.at[:, mine], place_o).start()
    pltpu.make_async_copy(oh.at[pl.ds(pl.multiple_of(me * rows, rows), rows), :], o.at[:, mine], place_o).wait()
    piece = o.at[:, mine]
    for i in range(3):
        await_bytes(piece, got_o.at[i])
        await_bytes(piece, send_o.at[i])
        for j in range(3):
            await_bytes(piece, send.at[j, i])


def attend(q, k, v, keep, scale):
    rows, width = q.shape
    chips = lax.axis_size("ca") * lax.axis_size("cb")
    heads = jax.ShapeDtypeStruct((rows * chips, width // chips), q.dtype)
    vm, dma = pl.BlockSpec(memory_space=pltpu.VMEM), pltpu.SemaphoreType.DMA
    return pl.pallas_call(
        functools.partial(attend_kernel, scale),
        out_shape=[jax.ShapeDtypeStruct(q.shape, q.dtype), heads, heads, heads]
        + [jax.ShapeDtypeStruct((width // chips // HD, rows * chips, 1), jnp.float32)],
        in_specs=[vm] * 4,
        out_specs=[vm] * 5,
        scratch_shapes=[pltpu.VMEM(heads.shape, q.dtype)]
        + [dma((3, 3)), dma((3, 3)), dma((3,)), dma((3,)), dma((3,)), dma],
        compiler_params=pltpu.CompilerParams(collective_id=4, has_side_effects=True, vmem_limit_bytes=48 << 20),
        cost_estimate=pl.CostEstimate(flops=1_000_000, bytes_accessed=10_000, transcendentals=0),
        name="attend",
    )(q, k, v, keep)


def attend_back_kernel(scale, do, qh, kh, vh, logs, keep, dq, dk, dv, doh, dqh, dkh, dvh, send, got, place, send_g, got_g, place_g):
    rows, width = do.shape[0], qh.shape[1]
    greet([corner(da, db)[1] for da, db in corners()])
    rows_to_heads(do, doh, send, got, place)
    wait_heads(do, doh, got, place)
    me, _ = corner(0, 0)
    tile, total_rows = 128, qh.shape[0]
    grads = ((dqh, dq), (dkh, dk), (dvh, dv))

    def one_head(h):
        lanes = pl.ds(h * HD, HD)

        def part(i, carry):
            dk_sum, dv_sum = carry
            at = pl.ds(pl.multiple_of(i * tile, tile), tile)
            qb, db, kb, vb = qh[at, lanes], doh[at, lanes], kh[:, lanes], vh[:, lanes]
            s = times_transposed(qb, kb) * scale
            s = jnp.where(keep[...] > 0.0, s, NEG_FILL)
            p = jnp.exp(s - logs[h, at, :])
            dp = times_transposed(db, vb)
            ds = (p * (dp - jnp.sum(dp * p, axis=-1, keepdims=True))).astype(jnp.bfloat16)
            dqh[at, lanes] = (matmul(ds, kb) * scale).astype(jnp.bfloat16)
            dk_sum = dk_sum + transposed_times(ds, qb)
            dv_sum = dv_sum + transposed_times(p.astype(jnp.bfloat16), db)
            return dk_sum, dv_sum

        zero = jnp.zeros((total_rows, HD), jnp.float32)
        dk_sum, dv_sum = lax.fori_loop(0, total_rows // tile, part, (zero, zero))
        dkh[:, lanes] = (dk_sum * scale).astype(jnp.bfloat16)
        dvh[:, lanes] = dv_sum.astype(jnp.bfloat16)

    for h in range(width // HD):
        one_head(h)
        lanes = pl.ds(h * HD, HD)
        here = pl.ds(pl.multiple_of(me * width + h * HD, HD), HD)
        for g, (src, dst) in enumerate(grads):
            for i, (da, db) in enumerate(corners()):
                peer, to = corner(da, db)
                push(src.at[pl.ds(pl.multiple_of(peer * rows, rows), rows), lanes], dst.at[:, here], send_g.at[g, i, h], got_g.at[g, i, h], to)
            own = src.at[pl.ds(pl.multiple_of(me * rows, rows), rows), lanes]
            pltpu.make_async_copy(own, dst.at[:, here], place_g.at[g, h]).start()
    piece = dq.at[:, pl.ds(0, HD)]
    for h in range(width // HD):
        for g in range(3):
            await_bytes(piece, place_g.at[g, h])
            for i in range(3):
                await_bytes(piece, send_g.at[g, i, h])
                await_bytes(piece, got_g.at[g, i, h])
    for i in range(3):
        await_bytes(do.at[:, pl.ds(0, width)], send.at[i])


def attend_back(do, qh, kh, vh, logs, keep, scale):
    heads = qh.shape[1] // HD
    vm, dma = pl.BlockSpec(memory_space=pltpu.VMEM), pltpu.SemaphoreType.DMA
    return pl.pallas_call(
        functools.partial(attend_back_kernel, scale),
        out_shape=[jax.ShapeDtypeStruct(do.shape, do.dtype)] * 3,
        in_specs=[vm] * 6,
        out_specs=[vm] * 3,
        scratch_shapes=[pltpu.VMEM(qh.shape, qh.dtype)] * 4
        + [dma((3,)), dma((3,)), dma, dma((3, 3, heads)), dma((3, 3, heads)), dma((3, heads))],
        compiler_params=pltpu.CompilerParams(collective_id=5, has_side_effects=True, vmem_limit_bytes=48 << 20),
        cost_estimate=pl.CostEstimate(flops=50_000_000_000, bytes_accessed=10_000_000, transcendentals=0),
        name="attend_back",
    )(do, qh, kh, vh, logs, keep)


def norm_rows(values, gain):
    factor = lax.rsqrt(jnp.mean(values * values, axis=-1, keepdims=True) + EPSILON)
    return (values * factor * gain, factor)


def norm_back(grad, values, factor, gain):
    weighted = grad * gain
    inner = jnp.mean(weighted * values, axis=-1, keepdims=True)
    return (factor * weighted - values * factor**3 * inner, jnp.sum(grad * values * factor, axis=0))


def rotary_tables(positions, head_dim):
    half_dim = head_dim // 2
    frequency = jnp.exp(-math.log(ROPE_THETA) * jnp.arange(half_dim, dtype=jnp.float32) / half_dim)
    angles = positions.astype(jnp.float32)[:, None] * frequency[None, :]
    return (jnp.cos(angles), jnp.sin(angles))


def rotate(values, cosine, sine, direction):
    half_dim = values.shape[-1] // 2
    first = values[..., :half_dim]
    second = values[..., half_dim:]
    cos_rows = cosine[:, None, :]
    sin_rows = direction * sine[:, None, :]
    return jnp.concatenate(
        [first * cos_rows - second * sin_rows, second * cos_rows + first * sin_rows], axis=-1
    )


def local(
    tokens, cotangent, lengths, expert_ids, query_weight, key_weight, value_weight, out_weight,
    router_weight, first_gain, second_gain, query_gain, key_gain, gate_weight, up_weight, down_weight,
):
    token_count = tokens.shape[1]
    model_width = tokens.shape[2]
    head_dim = HD
    top_count = expert_ids.shape[2]
    experts = router_weight.shape[1]
    local_experts = gate_weight.shape[0]
    ctx_size = lax.axis_size(CTX)
    sources = lax.axis_size(EXP)
    capacity = max(2, -(-(token_count * top_count * 9) // (experts * 8)))
    score_scale = 1.0 / math.sqrt(head_dim)
    seq_len = token_count * ctx_size

    rows_each = query_weight.shape[0]
    packed = jnp.concatenate(
        [g.reshape(-1) for g in (first_gain, second_gain, query_gain, key_gain)] + [router_weight.reshape(-1)]
    )
    small = jnp.pad(packed, (0, -packed.size % 2048)).reshape(-1, 128)
    ids_low = expert_ids[0].astype(jnp.bfloat16).reshape(-1, 128)
    gathered, ids_all = spread([query_weight, key_weight, value_weight, out_weight, small], ids_low)
    full_query, full_key, full_value, full_out = (w.reshape(model_width, -1) for w in gathered[:4])
    smalls = gathered[4].reshape(-1, small.size)
    gains = [smalls[:, i * rows_each : (i + 1) * rows_each].reshape(-1).astype(jnp.float32) for i in range(4)]
    gain_first, gain_second, gain_queries, gain_keys = gains
    full_router = smalls[:, 4 * rows_each : packed.size].reshape(model_width, experts)
    ids_all = ids_all.reshape(sources, token_count, top_count).astype(jnp.int32)
    gate_all, up_all = (lax.all_gather(w, CTX, axis=2, tiled=True) for w in (gate_weight, up_weight))
    down_all = lax.all_gather(down_weight, CTX, axis=1, tiled=True)
    inputs = tokens[0].astype(jnp.float32)
    length = lengths[0]
    positions = lax.axis_index(CTX) * token_count + jnp.arange(token_count, dtype=jnp.int32)
    row_valid = positions < length
    row_valid = row_valid.astype(jnp.float32)[:, None]
    key_valid = jnp.arange(seq_len, dtype=jnp.int32) < length
    grad_total_low = (cotangent[0].astype(jnp.float32) * row_valid).astype(jnp.bfloat16)
    grad_total = grad_total_low.astype(jnp.float32)

    g_all = lax.all_gather(grad_total_low, EXP, axis=0)
    cosine, sine = rotary_tables(positions, head_dim)
    normed_one, factor_one = norm_rows(inputs, gain_first)
    normed_one_low = normed_one.astype(jnp.bfloat16)
    query_raw = matmul(normed_one_low, full_query)
    key_raw = matmul(normed_one_low, full_key)
    value_low = matmul(normed_one_low, full_value).astype(jnp.bfloat16)
    query_normed, query_factor = norm_rows(query_raw, gain_queries)
    key_normed, key_factor = norm_rows(key_raw, gain_keys)
    by_head = lambda v: v.reshape(token_count, HEADS, head_dim)
    query_low = rotate(by_head(query_normed), cosine, sine, 1.0).astype(jnp.bfloat16)
    key_low = rotate(by_head(key_normed), cosine, sine, 1.0).astype(jnp.bfloat16)
    flat = lambda v: v.reshape(v.shape[0], -1)
    keep = key_valid.astype(jnp.float32)[None, :]
    value_low, gate_all = lax.optimization_barrier((value_low, gate_all))
    attended_low, *saved = attend(flat(query_low), flat(key_low), value_low, keep, score_scale)
    hidden_state = inputs + matmul(attended_low, full_out)
    normed_two, factor_two = norm_rows(hidden_state, gain_second)
    normed_two_low = normed_two.astype(jnp.bfloat16)

    n2_sent, up_all = lax.optimization_barrier((normed_two_low, up_all))
    n2_all, _ = dispatch(n2_sent, [], [])
    n2_all = n2_all.reshape(sources, token_count, model_width)
    first_expert = lax.axis_index(EXP) * local_experts
    own_experts = first_expert + jnp.arange(local_experts, dtype=jnp.int32)
    mask = jnp.any(ids_all[:, None, :, :] == own_experts[None, :, None, None], axis=-1)
    before = (jnp.arange(token_count)[:, None] < jnp.arange(token_count)[None, :]).astype(jnp.bfloat16)
    ranks = jnp.einsum("seu,ut->set", mask.astype(jnp.bfloat16), before, preferred_element_type=jnp.float32)
    slots = jnp.arange(capacity, dtype=jnp.float32)
    hot = (mask[:, :, None, :] & (ranks[:, :, None, :] == slots[None, None, :, None])).astype(jnp.bfloat16)
    logits = matmul(n2_all.reshape(-1, model_width), full_router)
    probs = jax.nn.softmax(logits, axis=-1)
    own_probs = lax.dynamic_slice_in_dim(probs, first_expert, local_experts, 1).reshape(sources, token_count, local_experts)
    hot32 = hot.astype(jnp.float32)
    row_gate = jnp.sum(hot32 * own_probs.transpose(0, 2, 1)[:, :, None, :], axis=-1)
    x = jnp.einsum("sect,std->escd", hot, n2_all, preferred_element_type=jnp.float32).astype(jnp.bfloat16)
    row_gate = row_gate.transpose(1, 0, 2)[..., None]
    ee = lambda eq, a, b: jnp.einsum(eq, a, b, preferred_element_type=jnp.float32)
    gp = ee("escd,edf->escf", x, gate_all)
    up = ee("escd,edf->escf", x, up_all)
    up, g_all = lax.optimization_barrier((up, g_all))
    g_rows = jnp.einsum("sect,std->escd", hot, g_all, preferred_element_type=jnp.float32)
    de = (g_rows * row_gate).astype(jnp.bfloat16)
    sig = jax.nn.sigmoid(gp)
    hid = (gp * sig * up).astype(jnp.bfloat16)
    eo = ee("escf,efd->escd", hid, down_all).astype(jnp.bfloat16)
    dgate_rows = jnp.sum(g_rows * eo.astype(jnp.float32), axis=-1)
    mixed_rows = (row_gate * eo.astype(jnp.float32)).astype(jnp.bfloat16)
    mixed_part = jnp.einsum("sect,escd->std", hot, mixed_rows, preferred_element_type=jnp.float32)
    mixed_part = mixed_part.astype(jnp.bfloat16)

    dhid = ee("escd,efd->escf", de, down_all)
    dgp = (dhid * up * sig * (1.0 + gp * (1.0 - sig))).astype(jnp.bfloat16)
    dup = (dhid * gp * sig).astype(jnp.bfloat16)
    down_part = ee("escf,escd->efd", hid, de)
    gate_part = ee("escd,escf->edf", x, dgp)
    up_part = ee("escd,escf->edf", x, dup)
    parts = [v.astype(jnp.bfloat16) for v in (down_part, gate_part, up_part)]
    dgp, dup, *_ = lax.optimization_barrier((dgp, dup, *parts))
    rs_ctx = lambda v, a: lax.psum_scatter(v, CTX, scatter_dimension=a, tiled=True)
    down_grad, gate_grad, up_grad = rs_ctx(parts[0], 1), rs_ctx(parts[1], 2), rs_ctx(parts[2], 2)
    dpair = (ee("escf,edf->escd", dgp, gate_all) + ee("escf,edf->escd", dup, up_all)).astype(jnp.bfloat16)

    dprobs_own = jnp.sum(hot32 * dgate_rows.transpose(1, 0, 2)[..., None], axis=2)
    dprobs_own = dprobs_own.transpose(0, 2, 1).reshape(-1, local_experts)
    onto = (jnp.arange(experts)[None, :] == own_experts[:, None]).astype(jnp.float32)
    dprobs = jnp.sum(dprobs_own[:, :, None] * onto[None], axis=1)
    dlogit_low = (probs * (dprobs - jnp.sum(dprobs * probs, axis=-1, keepdims=True))).astype(jnp.bfloat16)
    router_part = transposed_times(n2_all.reshape(-1, model_width), dlogit_low)
    dn2_part = jnp.einsum("sect,escd->std", hot, dpair, preferred_element_type=jnp.float32).reshape(-1, model_width)
    dn2_part = dn2_part + times_transposed(dlogit_low, full_router)
    dn2_part = dn2_part.astype(jnp.bfloat16).reshape(sources, token_count, model_width)
    dn2_part, down_grad = lax.optimization_barrier((dn2_part, down_grad))
    dn2 = give_back(dn2_part)
    dn2, gate_grad = lax.optimization_barrier((dn2, gate_grad))
    dn2, mixed_part = lax.optimization_barrier((dn2, mixed_part))
    mixed = lax.psum_scatter(mixed_part.reshape(-1, model_width), EXP, scatter_dimension=0, tiled=True)

    dh_norm, gain_second_part = norm_back(dn2, hidden_state, factor_two, gain_second)
    grad_hidden = grad_total + dh_norm
    dh_low = grad_hidden.astype(jnp.bfloat16)
    out_part = transposed_times(attended_low, dh_low)
    d_att = times_transposed(dh_low, full_out).astype(jnp.bfloat16)
    dq, dk, dv = attend_back(d_att, *saved, keep, score_scale)
    dq, up_grad = lax.optimization_barrier((dq, up_grad))
    unrotate = lambda a: rotate(by_head(a.astype(jnp.float32)), cosine, sine, -1.0).reshape(token_count, model_width)
    dk_raw, gain_keys_part = norm_back(unrotate(dk), key_raw, key_factor, gain_keys)
    dq_raw, gain_queries_part = norm_back(unrotate(dq), query_raw, query_factor, gain_queries)
    dk_low, dq_low, dv_low = dk_raw.astype(jnp.bfloat16), dq_raw.astype(jnp.bfloat16), dv
    dn1 = times_transposed(dq_low, full_query) + times_transposed(dk_low, full_key)
    dn1 = dn1 + times_transposed(dv_low, full_value)
    input_norm, gain_first_part = norm_back(dn1, inputs, factor_one, gain_first)
    input_grad = (grad_hidden + input_norm).astype(jnp.bfloat16)
    core = lax.axis_index("core")
    swap = lambda v: lax.ppermute(v, "core", [(0, 1), (1, 0)])

    def columns_of_core(v):
        v = v.reshape(token_count, 2, -1)
        return jnp.concatenate([lax.dynamic_index_in_dim(v, core, 1, False), swap(lax.dynamic_index_in_dim(v, 1 - core, 1, False))], axis=0)

    both = lambda v: jnp.concatenate([v, swap(v)], axis=0)
    n1_both, att_both = both(normed_one_low), both(attended_low)
    parts = [
        transposed_times(l, columns_of_core(r)).astype(jnp.bfloat16)
        for l, r in ((att_both, dh_low), (n1_both, dq_low), (n1_both, dk_low), (n1_both, dv_low))
    ]
    split = lambda v: v.reshape(ctx_size * sources // 2, 2, -1)
    small_parts = jnp.concatenate(
        [split(v) for v in (gain_first_part, gain_second_part, gain_queries_part, gain_keys_part, router_part)], axis=2
    )
    small_parts = jnp.pad(small_parts, ((0, 0), (0, 0), (0, -small_parts.shape[2] % 2048)))
    small_parts = lax.dynamic_index_in_dim(small_parts, core, 1, False) + swap(lax.dynamic_index_in_dim(small_parts, 1 - core, 1, False))
    weight_grads, small_grads = collect(parts, small_parts.reshape(ctx_size * sources // 2, -1, 128))
    weight_grads, mixed, gate_grad, up_grad, down_grad = lax.optimization_barrier(
        (list(weight_grads), mixed, gate_grad, up_grad, down_grad)
    )
    layer_out = (row_valid * (hidden_state + mixed.astype(jnp.float32))).astype(jnp.bfloat16)
    gate_grad, up_grad, down_grad = (v.astype(jnp.float32) for v in (gate_grad, up_grad, down_grad))
    weight_grads = list(weight_grads[1:]) + [weight_grads[0]]
    small_grads = small_grads.reshape(-1)
    gain_grads = [small_grads[i * rows_each : (i + 1) * rows_each] for i in range(4)]
    router_grad = small_grads[4 * rows_each : packed.size].reshape(rows_each, experts)
    return (layer_out[None], input_grad[None], *weight_grads, router_grad, *gain_grads, gate_grad, up_grad, down_grad)


def solution(mesh):
    ctx, exp = mesh.devices.shape
    fine = Mesh(mesh.devices.reshape(2, ctx // 2, exp // 2, 2), ("ca", "cb", "ring", "core"))
    rows = P(EXP, CTX, None)
    flat2, flat1 = P(ALL, None), P(ALL)
    placed = (rows, rows, P(EXP), rows) + (flat2,) * 5 + (flat1,) * 4 + (P(EXP, None, CTX),) * 2 + (P(EXP, CTX, None),)
    outs = (rows, rows) + (flat2,) * 5 + (flat1,) * 4 + (P(EXP, None, CTX),) * 2 + (P(EXP, CTX, None),)
    return jax.shard_map(local, mesh=fine, in_specs=placed, out_specs=outs, check_vma=False)
```

```python
import functools
import math

import jax
import jax.numpy as jnp
from jax import lax
from jax.experimental import pallas as pl
from jax.experimental.pallas import tpu as pltpu
from jax.sharding import Mesh
from jax.sharding import PartitionSpec as P

HEADS = 16
HD = 128
EPSILON = 1e-06
ROPE_THETA = 10000.0
NEG_FILL = -1e30

CTX = ("ca", "cb")
EXP = ("ring", "core")
ALL = CTX + EXP


MESH = pl.DeviceIdType.MESH


def turn(name, by):
    size = lax.axis_size(name)
    return lax.rem(lax.axis_index(name) + by, size)


def await_bytes(ref, sem):
    pltpu.make_async_copy(ref, ref, sem).wait()


def greet(peers):
    barrier = pltpu.get_barrier_semaphore()
    for peer in peers:
        pl.semaphore_signal(barrier, inc=1, device_id=peer, device_id_type=MESH)
    pl.semaphore_wait(barrier, len(peers))


def push(src, dst, ssem, rsem, to):
    pltpu.make_async_remote_copy(
        src_ref=src, dst_ref=dst, send_sem=ssem, recv_sem=rsem, device_id=to, device_id_type=MESH
    ).start()


RING, SIDE_B, SIDE_A, FIRST, SECOND, CORE_OWN, CORE_B, CORE_A, CORE_FIRST, CORE_SECOND = range(10)


def along(step):
    ring, r = lax.axis_size("ring"), lax.axis_index("ring")
    to_next, to_last = {"ring": turn("ring", 1)}, {"ring": turn("ring", ring - 1)}
    return (
        ((r + 1 < ring) & (r >= step), r >= step + 1, lax.rem(r + ring - step, ring), lax.rem(r + ring - 1 - step, ring), to_next, 0),
        ((r >= 1) & (r + step < ring), r + 1 + step < ring, lax.rem(r + step, ring), lax.rem(r + 1 + step, ring), to_last, 1),
    )


def send_along(step, own, block_of, send, got):
    for sent, _, block, _, to, side in along(step):

        @pl.when(sent)
        def _(block=block, to=to, side=side):
            push(own if step == 0 else block_of(block), block_of(block), send.at[side, step], got.at[side, step], to)


def take_along(step, block_of, got, then):
    for _, comes, _, block, _, side in along(step):

        @pl.when(comes)
        def _(block=block, side=side):
            await_bytes(block_of(block), got.at[side, step])

    for _, comes, _, block, _, side in along(step):

        @pl.when(comes)
        def _(block=block):
            then(block)


def sent_along(own, send):
    ring = lax.axis_size("ring")
    for step in range(ring - 1):
        for sent, _, _, _, _, side in along(step):

            @pl.when(sent)
            def _(side=side):
                await_bytes(own, send.at[side, step])


def spread_kernel(count, tables, *refs):
    ring = lax.axis_size("ring")
    ins, refs = refs[: count + tables], refs[count + tables :]
    outs, sems = refs[: count + tables], refs[count + tables :]
    send, send_ring, got_ring, got_b, got_a, got, place, core_sem = sems
    a, b, r, c = (lax.axis_index(n) for n in ALL)
    na, nb, nc = turn("ca", 1), turn("cb", 1), turn("core", 1)
    to_a, to_b, to_core = {"ca": na}, {"cb": nb}, {"core": nc}
    greet([to_a, to_b, to_core] + [{"ring": turn("ring", k)} for k in range(1, ring)])

    def half(ref, which):
        rows, cols = ref.shape[-2:]
        if rows * 8 < cols:
            return ref.at[..., pl.ds(which * (cols // 2), cols // 2)]
        return ref.at[..., pl.ds(which * (rows // 2), rows // 2), :]

    def halves(ref, which):
        rows, cols = ref.shape[-2:]
        if rows * 8 < cols:
            return ref.at[:, :, pl.ds(which * (cols // 2), cols // 2)]
        return ref.at[:, pl.ds(which * (rows // 2), rows // 2), :]

    def place_of(w):
        return (lambda at: outs[w].at[a, b, at, c]) if w < count else (lambda at: outs[w].at[at, c])

    for w in range(count + tables):
        pltpu.make_async_copy(ins[w], place_of(w)(r), place.at[w]).start()
    for w in reversed(range(count)):
        send_along(0, ins[w], place_of(w), send_ring.at[w], got_ring.at[w])
        here = place_of(w)(r)
        push(ins[w], here, send.at[w, SIDE_B], got_b.at[w, r], to_b)
        push(ins[w], here, send.at[w, SIDE_A], got_a.at[w, r], to_a)
        push(ins[w], here, send.at[w, CORE_OWN], got.at[w, CORE_OWN], to_core)
    for t in range(tables):
        push(ins[count + t], place_of(count + t)(r), core_sem.at[t, 0], core_sem.at[t, 1], to_core)

    def sides(w):
        for step in range(ring - 1):

            def on(at):
                block = place_of(w)(at)
                push(block, block, send.at[w, SIDE_B], got_b.at[w, at], to_b)
                push(block, block, send.at[w, SIDE_A], got_a.at[w, at], to_a)
                push(block, block, send.at[w, CORE_OWN], got.at[w, CORE_OWN], to_core)

            take_along(step, place_of(w), got_ring.at[w], on)
            if step + 1 < ring - 1:
                send_along(step + 1, ins[w], place_of(w), send_ring.at[w], got_ring.at[w])

    def diagonal(w):
        out = outs[w]

        def one(k, carry):
            at = lax.rem(r + ring - k, ring)
            block = out.at[a, nb, at, c]
            await_bytes(block, got_b.at[w, at])
            push(half(block, 0), half(block, 0), send.at[w, FIRST], got.at[w, FIRST], to_a)
            push(block, block, send.at[w, CORE_B], got.at[w, CORE_B], to_core)
            block = out.at[na, b, at, c]
            await_bytes(block, got_a.at[w, at])
            push(half(block, 1), half(block, 1), send.at[w, SECOND], got.at[w, SECOND], to_b)
            push(block, block, send.at[w, CORE_A], got.at[w, CORE_A], to_core)
            return carry

        lax.fori_loop(0, ring, one, 0)

    def last(w):
        block = outs[w].at[na, nb, :, c]
        for which, kind, core_kind in ((0, FIRST, CORE_FIRST), (1, SECOND, CORE_SECOND)):
            part = halves(block, which)
            await_bytes(part, got.at[w, kind])
            push(part, part, send.at[w, core_kind], got.at[w, core_kind], to_core)

    def table_step(t, step):
        w = count + t

        def on(at):
            push(place_of(w)(at), place_of(w)(at), core_sem.at[t, 0], core_sem.at[t, 1], to_core)

        if step >= 0:
            take_along(step, place_of(w), got_ring.at[w], on)
        if step + 1 < ring - 1:
            send_along(step + 1, ins[w], place_of(w), send_ring.at[w], got_ring.at[w])

    order = list(reversed(range(count)))
    for step in range(count + 2):
        if step < count:
            sides(order[step])
        if step >= count - 1:
            for t in range(tables):
                table_step(t, step - count)
        if 0 <= step - 1 < count:
            diagonal(order[step - 1])
        if 0 <= step - 2 < count:
            last(order[step - 2])
    for step in range(2, ring - 1):
        for t in range(tables):
            table_step(t, step)

    for w in range(count):
        out = outs[w]
        mine = lambda p, q: out.at[p, q, :, c]
        await_bytes(ins[w], place.at[w])
        sent_along(ins[w], send_ring.at[w])
        for kind in (SIDE_B, SIDE_A, CORE_OWN, CORE_B, CORE_A):
            await_bytes(mine(a, b), send.at[w, kind])
        for which, kind in ((0, FIRST), (1, SECOND), (0, CORE_FIRST), (1, CORE_SECOND)):
            await_bytes(halves(mine(a, b), which), send.at[w, kind])
        for kind, p, q in ((CORE_OWN, a, b), (CORE_B, a, nb), (CORE_A, na, b)):
            await_bytes(out.at[p, q, :, nc], got.at[w, kind])
        for which, kind in ((0, CORE_FIRST), (1, CORE_SECOND)):
            await_bytes(halves(out.at[na, nb, :, nc], which), got.at[w, kind])
    for t in range(tables):
        w = count + t
        await_bytes(ins[w], place.at[w])
        sent_along(ins[w], send_ring.at[w])
        await_bytes(outs[w].at[:, c], core_sem.at[t, 0])
        await_bytes(outs[w].at[:, nc], core_sem.at[t, 1])


def spread(shards, tables):
    count, more, ring = len(shards), len(tables), lax.axis_size("ring")
    square = (lax.axis_size("ca"), lax.axis_size("cb"), ring, 2)
    dma = pltpu.SemaphoreType.DMA
    outs = pl.pallas_call(
        functools.partial(spread_kernel, count, more),
        out_shape=[jax.ShapeDtypeStruct(square + s.shape, s.dtype) for s in shards]
        + [jax.ShapeDtypeStruct((ring, 2) + t.shape, t.dtype) for t in tables],
        in_specs=[pl.BlockSpec(memory_space=pltpu.VMEM)] * (count + more),
        out_specs=[pl.BlockSpec(memory_space=pl.ANY)] * (count + more),
        scratch_shapes=[
            dma((count, 10)), dma((count + more, 2, ring)), dma((count + more, 2, ring)), dma((count, ring)), dma((count, ring)),
            dma((count, 10)), dma((count + more,)), dma((more, 2)),
        ],
        compiler_params=pltpu.CompilerParams(collective_id=0, has_side_effects=True),
        cost_estimate=pl.CostEstimate(flops=150_000_000_000, bytes_accessed=300_000_000, transcendentals=0),
        name="spread",
    )(*shards, *tables)
    return outs[:count], outs[count:]


def collect_kernel(count, *refs):
    ring = lax.axis_size("ring")
    parts, refs = refs[:count], refs[count:]
    grads, matrices, (x, gain, passed), refs = refs[:3], refs[3:6], refs[6:9], refs[9:]
    outs, (input_grad, gain_out), refs = refs[:count], refs[count : count + 2], refs[count + 2 :]
    scratch, refs = refs[: 9 * count], refs[9 * count :]
    send, got, ring_send, ring_got, load, chunks, dn1, sums, arrived, ring_arrived, fetch, gain_send, gain_got = refs
    a, b, r, c = (lax.axis_index(n) for n in ALL)
    na, nb, nc = turn("ca", 1), turn("cb", 1), turn("core", 1)
    to_a, to_b, to_core = {"ca": na}, {"cb": nb}, {"core": nc}
    bufs = [scratch[9 * w : 9 * w + 9] for w in range(count)]
    greet([to_a, to_b, to_core] + [{"ring": turn("ring", k)} for k in range(1, ring)])

    def chunk(i, slot, w):
        rows = chunks.shape[2]
        return pltpu.make_async_copy(
            matrices[w].at[pl.ds(pl.multiple_of(i * rows, rows), rows), :], chunks.at[slot, w], fetch.at[slot, w]
        )

    def input_side():
        steps, rows = matrices[0].shape[0] // chunks.shape[2], chunks.shape[2]

        def one(i, carry):
            slot = lax.rem(i, 2)

            @pl.when(i + 1 < steps)
            def _():
                for w in range(3):
                    chunk(i + 1, 1 - slot, w).start()

            value = jnp.zeros((x.shape[0], rows), jnp.float32)
            for w in range(3):
                chunk(i, slot, w).wait()
                value = value + times_transposed(grads[w][...], chunks[slot, w])
            dn1[:, pl.ds(pl.multiple_of(i * rows, rows), rows)] = value
            return carry

        lax.fori_loop(0, steps, one, 0)
        tile = 32
        sums[0] = jnp.zeros(sums.shape[1:], jnp.float32)

        def back(i, carry):
            at = pl.ds(pl.multiple_of(i * tile, tile), tile)
            v, grad = x[at, :].astype(jnp.float32), dn1[at, :]
            factor = lax.rsqrt(jnp.mean(v * v, axis=-1, keepdims=True) + EPSILON)
            weighted = grad * gain[...]
            inner = jnp.mean(weighted * v, axis=-1, keepdims=True)
            total = passed[at, :] + factor * weighted - v * (factor * factor * factor * inner)
            input_grad[at, :] = total.astype(input_grad.dtype)
            gained = grad * v * factor
            sums[0] += sum(gained[k : k + 8] for k in range(0, tile, 8))
            return carry

        lax.fori_loop(0, x.shape[0] // tile, back, 0)
        push(sums.at[0], arrived.at[0], gain_send.at[0], gain_got.at[0], to_a)

    def gain_stage(stage):
        if stage < 3:
            await_bytes(arrived.at[stage], gain_got.at[stage])
            sums[stage + 1] = sums[stage] + arrived[stage]
            if stage < 2:
                push(sums.at[stage + 1], arrived.at[stage + 1], gain_send.at[stage + 1], gain_got.at[stage + 1], (to_b, to_core)[stage])
            else:
                for k in range(1, ring):
                    push(sums.at[3], ring_arrived.at[k - 1], gain_send.at[2 + k], gain_got.at[2 + k], {"ring": turn("ring", k)})
        else:
            total = sums[3]
            for k in range(1, ring):
                await_bytes(ring_arrived.at[k - 1], gain_got.at[2 + k])
                total = total + ring_arrived[k - 1]
            gain_out[...] = total
            for k in range(3 + ring - 1):
                await_bytes(sums.at[0], gain_send.at[k])

    def half(ref, which):
        rows, cols = ref.shape[-2:]
        lead = (slice(None),) * (len(ref.shape) - 2)
        if cols > 128:
            return ref.at[(*lead, slice(None), pl.ds(which * (cols // 2), cols // 2))]
        return ref.at[(*lead, pl.ds(which * (rows // 2), rows // 2), slice(None))]

    def loads(w):
        own_a, own_b = bufs[w][0:2]
        return (
            pltpu.make_async_copy(half(parts[w].at[a], 0), own_a, load.at[w, 0]),
            pltpu.make_async_copy(half(parts[w].at[:, b], 1), own_b, load.at[w, 1]),
        )

    def first(w):
        for copy in loads(w):
            copy.start()
        in_a, in_b = bufs[w][2:4]
        push(half(parts[w].at[na], 0), in_a, send.at[w, 0], got.at[w, 0], to_a)
        push(half(parts[w].at[:, nb], 1), in_b, send.at[w, 1], got.at[w, 1], to_b)

    def add(into, other):
        def one(k, carry):
            into[:, k] = (into[:, k].astype(jnp.float32) + other[:, k].astype(jnp.float32)).astype(into.dtype)
            return carry

        lax.fori_loop(0, ring, one, 0)

    def second(w):
        own_a, own_b, in_a, in_b, in_a2, in_b2 = bufs[w][:6]
        for copy in loads(w):
            copy.wait()
        await_bytes(in_a, got.at[w, 0])
        add(own_a, in_a)
        push(own_a.at[nb], in_a2, send.at[w, 2], got.at[w, 2], to_b)
        await_bytes(in_b, got.at[w, 1])
        add(own_b, in_b)
        push(own_b.at[na], in_b2, send.at[w, 3], got.at[w, 3], to_a)

    def third(w):
        own_a, own_b, _, _, in_a2, in_b2, total, in_ring = bufs[w][:8]
        await_bytes(in_a2, got.at[w, 2])
        await_bytes(in_b2, got.at[w, 3])

        def one(k, carry):
            sums = [
                own[own_at, k].astype(jnp.float32) + more[k].astype(jnp.float32)
                for own, own_at, more in ((own_a, b, in_a2), (own_b, a, in_b2))
            ]
            for which in range(2):
                half(total.at[k], which)[...] = sums[which].astype(total.dtype)
            return carry

        lax.fori_loop(0, ring, one, 0)
        for k in range(1, ring):
            at = turn("ring", k)
            push(total.at[at], in_ring.at[k - 1], ring_send.at[w, k - 1], ring_got.at[w, k - 1], {"ring": at})

    def fourth(w):
        total, in_ring, final = bufs[w][6:9]
        for k in range(1, ring):
            await_bytes(in_ring.at[k - 1], ring_got.at[w, k - 1])
        if final.shape[0] == 2:
            rows = final.shape[1]
            for core in range(2):
                at = pl.ds(core * rows, rows)
                value = total[r, at, :].astype(jnp.float32)
                for k in range(ring - 1):
                    value = value + in_ring[k, at, :].astype(jnp.float32)
                final[core] = value
            cols = final.shape[2]
            there = outs[w].at[:, pl.ds(pl.multiple_of(c * cols, cols), cols)]
            push(final.at[nc], there, send.at[w, 4], got.at[w, 4], to_core)
            pltpu.make_async_copy(final.at[c], there, load.at[w, 2]).start()
        else:
            value = total[r].astype(jnp.float32)
            for k in range(ring - 1):
                value = value + in_ring[k].astype(jnp.float32)
            outs[w][...] = value

    def finish(w):
        own_a, own_b, in_a, in_b, in_a2, in_b2, total, in_ring, final = bufs[w]
        await_bytes(in_a, send.at[w, 0])
        await_bytes(in_b, send.at[w, 1])
        await_bytes(in_a2, send.at[w, 2])
        await_bytes(in_b2, send.at[w, 3])
        for k in range(1, ring):
            await_bytes(in_ring.at[k - 1], ring_send.at[w, k - 1])
        if final.shape[0] == 2:
            await_bytes(final.at[0], send.at[w, 4])
            await_bytes(final.at[0], got.at[w, 4])
            await_bytes(final.at[0], load.at[w, 2])

    for w in range(3):
        chunk(0, 0, w).start()
    first(0)
    first(1)
    first(2)
    input_side()
    for step in range(count + 3):
        if 0 < step and step + 2 < count:
            first(step + 2)
        if step < count:
            second(step)
        if 0 <= step - 1 < count:
            third(step - 1)
        if 0 <= step - 2 < count:
            fourth(step - 2)
        if 1 <= step < 5:
            gain_stage(step - 1)
    for w in range(count):
        finish(w)


def collect(parts, small, grads, matrices, x, gain, passed):
    count, ring = len(parts) + 1, lax.axis_size("ring")
    chips = lax.axis_size("ca") * lax.axis_size("cb") * ring
    square = (lax.axis_size("ca"), lax.axis_size("cb"), ring)
    views = [p.reshape(square + (p.shape[0] // chips, p.shape[1])) for p in parts]
    views = [small.reshape(square + small.shape[1:])] + views
    shapes, scratch = [], []
    for v in views:
        rows, cols = v.shape[3:]
        piece = (rows, cols // 2) if cols > 128 else (rows // 2, cols)
        big = cols > 128
        vm = lambda *shape: pltpu.VMEM(shape, v.dtype)
        scratch += [vm(2, ring, *piece)] * 4 + [vm(ring, *piece)] * 2
        scratch += [vm(ring, rows, cols), vm(ring - 1, rows, cols)]
        scratch += [pltpu.VMEM((2, rows // 2, cols) if big else (1, 8, 128), jnp.float32)]
        shapes.append(jax.ShapeDtypeStruct((rows // 2, 2 * cols) if big else (rows, cols), jnp.float32))
    dma = pltpu.SemaphoreType.DMA
    vm, anywhere = pl.BlockSpec(memory_space=pltpu.VMEM), pl.BlockSpec(memory_space=pl.ANY)
    wide = (8, gain.shape[1])
    f32 = lambda *shape: pltpu.VMEM(shape, jnp.float32)
    outs = pl.pallas_call(
        functools.partial(collect_kernel, count),
        out_shape=shapes + [jax.ShapeDtypeStruct(x.shape, x.dtype), jax.ShapeDtypeStruct(wide, jnp.float32)],
        in_specs=[anywhere] * count + [vm] * 3 + [anywhere] * 3 + [vm] * 3,
        out_specs=[vm] * (count + 2),
        scratch_shapes=scratch
        + [dma((count, 5)), dma((count, 5)), dma((count, ring - 1)), dma((count, ring - 1)), dma((count, 3))]
        + [pltpu.VMEM((2, 3, 256, x.shape[1]), x.dtype), f32(*x.shape), f32(4, *wide), f32(3, *wide), f32(ring - 1, *wide)]
        + [dma((2, 3)), dma((2 + ring,)), dma((2 + ring,))],
        compiler_params=pltpu.CompilerParams(collective_id=1, has_side_effects=True, vmem_limit_bytes=62 << 20),
        cost_estimate=pl.CostEstimate(flops=160_000_000_000, bytes_accessed=320_000_000, transcendentals=0),
        name="collect",
    )(*views, *grads, *matrices, x, gain, passed)
    return outs[1:count], outs[0], outs[count], outs[count + 1]


def dispatch_kernel(rows, out, send, got, place, core_send, core_got):
    ring, r, c, nc = lax.axis_size("ring"), lax.axis_index("ring"), lax.axis_index("core"), turn("core", 1)
    to_core = {"core": nc}
    greet([to_core] + [{"ring": turn("ring", k)} for k in range(1, ring)])
    block_of = lambda at: out.at[at, c]
    own = pltpu.make_async_copy(rows, block_of(r), place)
    own.start()
    send_along(0, rows, block_of, send, got)
    push(rows, block_of(r), core_send, core_got, to_core)

    def on(at):
        push(block_of(at), block_of(at), core_send, core_got, to_core)

    for step in range(ring - 1):
        if step + 1 < ring - 1:
            take_along(step, block_of, got, lambda at: None)
            send_along(step + 1, rows, block_of, send, got)
            for _, comes, _, block, _, _ in along(step):
                pl.when(comes)(functools.partial(on, block))
        else:
            take_along(step, block_of, got, on)
    own.wait()
    sent_along(rows, send)
    await_bytes(out.at[:, c], core_send)
    await_bytes(out.at[:, nc], core_got)


def dispatch(rows):
    ring, dma = lax.axis_size("ring"), pltpu.SemaphoreType.DMA
    return pl.pallas_call(
        dispatch_kernel,
        out_shape=jax.ShapeDtypeStruct((ring, 2) + rows.shape, rows.dtype),
        in_specs=[pl.BlockSpec(memory_space=pltpu.VMEM)],
        out_specs=pl.BlockSpec(memory_space=pl.ANY),
        scratch_shapes=[dma((2, ring)), dma((2, ring)), dma, dma, dma],
        compiler_params=pltpu.CompilerParams(collective_id=2, has_side_effects=True),
        cost_estimate=pl.CostEstimate(flops=1_000_000, bytes_accessed=10_000, transcendentals=0),
        name="dispatch",
    )(rows)


def give_back_kernel(part, out, own, core_in, ring_in, load, core_send, core_got, ring_send, ring_got):
    ring = lax.axis_size("ring")
    r, c, nc = lax.axis_index("ring"), lax.axis_index("core"), turn("core", 1)
    greet([{"core": nc}] + [{"ring": turn("ring", k)} for k in range(1, ring)])
    order = list(range(1, ring)) + [0]
    block_of = lambda k: lax.rem(r + k, ring)
    for k in order:
        push(part.at[block_of(k), nc], core_in.at[k], core_send.at[k], core_got.at[k], {"core": nc})
        pltpu.make_async_copy(part.at[block_of(k), c], own.at[k], load.at[k]).start()
    rows, cols = own.shape[1:]
    tile = 32
    for k in order:
        await_bytes(own.at[k], load.at[k])
        await_bytes(core_in.at[k], core_got.at[k])
        if k == 0:
            continue

        def add(i, carry):
            at = pl.ds(pl.multiple_of(i * tile, tile), tile)
            own[k, at] = (own[k, at].astype(jnp.float32) + core_in[k, at].astype(jnp.float32)).astype(own.dtype)
            return carry

        lax.fori_loop(0, rows // tile, add, 0)
        push(own.at[k], ring_in.at[k - 1], ring_send.at[k - 1], ring_got.at[k - 1], {"ring": block_of(k)})
    for k in range(1, ring):
        await_bytes(ring_in.at[k - 1], ring_got.at[k - 1])

    def total(i, carry):
        at = pl.ds(pl.multiple_of(i * tile, tile), tile)
        value = own[0, at].astype(jnp.float32) + core_in[0, at].astype(jnp.float32)
        for k in range(ring - 1):
            value = value + ring_in[k, at].astype(jnp.float32)
        out[at, :] = value
        return carry

    lax.fori_loop(0, rows // tile, total, 0)
    for k in order:
        await_bytes(core_in.at[k], core_send.at[k])
        if k:
            await_bytes(ring_in.at[k - 1], ring_send.at[k - 1])


def give_back(part):
    ring, dma = lax.axis_size("ring"), pltpu.SemaphoreType.DMA
    rows, cols = part.shape[1:]
    block = lambda n: pltpu.VMEM((n, rows, cols), part.dtype)
    return pl.pallas_call(
        give_back_kernel,
        out_shape=jax.ShapeDtypeStruct((rows, cols), jnp.float32),
        in_specs=[pl.BlockSpec(memory_space=pl.ANY)],
        out_specs=pl.BlockSpec(memory_space=pltpu.VMEM),
        scratch_shapes=[block(ring), block(ring), block(ring - 1), dma((ring,)), dma((ring,)), dma((ring,)), dma((ring,)), dma((ring,))],
        compiler_params=pltpu.CompilerParams(collective_id=3, has_side_effects=True, vmem_limit_bytes=60 << 20),
        cost_estimate=pl.CostEstimate(flops=100000000000, bytes_accessed=200000000, transcendentals=0),
        name="give_back",
    )(part.reshape(ring, 2, rows, cols))


def matmul(left, right):
    return jnp.dot(left, right, preferred_element_type=jnp.float32)


def times_transposed(left, right):
    return lax.dot_general(
        left, right, (((1,), (1,)), ((), ())), preferred_element_type=jnp.float32
    )


def transposed_times(left, right):
    return lax.dot_general(
        left, right, (((0,), (0,)), ((), ())), preferred_element_type=jnp.float32
    )


def corners():
    return ((0, 1), (1, 0), (1, 1))


def corner(da, db):
    pa, pb = turn("ca", da), turn("cb", db)
    return 2 * pa + pb, {"ca": pa, "cb": pb}


def rows_to_heads(src, dst, send, got, place):
    rows, width = src.shape[0], dst.shape[1]
    me, _ = corner(0, 0)
    there = dst.at[pl.ds(pl.multiple_of(me * rows, rows), rows), :]
    for i, (da, db) in enumerate(corners()):
        peer, to = corner(da, db)
        push(src.at[:, pl.ds(pl.multiple_of(peer * width, width), width)], there, send.at[i], got.at[i], to)
    pltpu.make_async_copy(src.at[:, pl.ds(pl.multiple_of(me * width, width), width)], there, place).start()


def wait_heads(src, dst, got, place):
    rows = src.shape[0]
    here = lambda at: dst.at[pl.ds(pl.multiple_of(at * rows, rows), rows), :]
    await_bytes(here(corner(0, 0)[0]), place)
    for i, (da, db) in enumerate(corners()):
        await_bytes(here(corner(da, db)[0]), got.at[i])


def swap_halves(v):
    return pltpu.roll(v, HD // 2, 1)


def norm_and_turn(raw, gain, cosine, sine, out):
    rows, width = raw.shape
    tile = 32

    def part(i, carry):
        at = pl.ds(pl.multiple_of(i * tile, tile), tile)
        value = raw[at, :]
        factor = lax.rsqrt(jnp.mean(value * value, axis=-1, keepdims=True) + EPSILON)
        for h in range(width // HD):
            lanes = pl.ds(h * HD, HD)
            v = raw[at, lanes] * factor * gain[:, lanes]
            out[at, lanes] = (v * cosine[at, :] + swap_halves(v) * sine[at, :]).astype(out.dtype)
        return carry

    lax.fori_loop(0, rows // tile, part, 0)


def norm_and_turn_back(grad, raw, gain, cosine, sine, out, gain_grad, turned):
    rows, width = raw.shape
    tile = 32
    gain_grad[...] = jnp.zeros_like(gain_grad)

    def part(i, carry):
        at = pl.ds(pl.multiple_of(i * tile, tile), tile)
        value = raw[at, :]
        factor = lax.rsqrt(jnp.mean(value * value, axis=-1, keepdims=True) + EPSILON)
        inner = jnp.zeros((tile, HD), jnp.float32)
        for h in range(width // HD):
            lanes = pl.ds(h * HD, HD)
            g = grad[at, lanes].astype(jnp.float32)
            g = g * cosine[at, :] - swap_halves(g) * sine[at, :]
            turned[:, lanes] = g
            inner = inner + g * gain[:, lanes] * raw[at, lanes]
        inner = jnp.sum(inner, axis=-1, keepdims=True) * (factor * factor * factor / width)
        for h in range(width // HD):
            lanes = pl.ds(h * HD, HD)
            g, v = turned[:, lanes], raw[at, lanes]
            out[at, lanes] = (factor * (g * gain[:, lanes]) - v * inner).astype(out.dtype)
            gained = g * v * factor
            gain_grad[:, lanes] += sum(gained[k : k + 8] for k in range(0, tile, 8))
        return carry

    lax.fori_loop(0, rows // tile, part, 0)


def attend_kernel(scale, q_raw, k_raw, v, q_gain, k_gain, cosine, sine, keep, o, qh, kh, vh, logs, q, k, oh, send, got, place, send_o, got_o, place_o):
    rows, width = v.shape[0], qh.shape[1]
    greet([corner(da, db)[1] for da, db in corners()])
    pairs = ((v, vh), (k, kh), (q, qh))
    rows_to_heads(v, vh, send.at[0], got.at[0], place.at[0])
    norm_and_turn(k_raw, k_gain, cosine, sine, k)
    rows_to_heads(k, kh, send.at[1], got.at[1], place.at[1])
    norm_and_turn(q_raw, q_gain, cosine, sine, q)
    rows_to_heads(q, qh, send.at[2], got.at[2], place.at[2])
    for i, (src, dst) in enumerate(pairs):
        wait_heads(src, dst, got.at[i], place.at[i])
    me, _ = corner(0, 0)
    tile = 128
    mine = pl.ds(pl.multiple_of(me * width, width), width)

    def block(at_block):
        def part(i, carry):
            at = pl.ds(pl.multiple_of(at_block * rows + i * tile, tile), tile)
            for h in range(width // HD):
                lanes = pl.ds(h * HD, HD)
                s = times_transposed(qh[at, lanes], kh[:, lanes]) * scale
                s = jnp.where(keep[...] > 0.0, s, NEG_FILL)
                peak = jnp.max(s, axis=-1, keepdims=True)
                p = jnp.exp(s - peak)
                total = jnp.sum(p, axis=-1, keepdims=True)
                logs[h, at, :] = peak + jnp.log(total)
                low = (p * (1.0 / total)).astype(jnp.bfloat16)
                oh[at, lanes] = matmul(low, vh[:, lanes]).astype(jnp.bfloat16)
            return carry

        lax.fori_loop(0, rows // tile, part, 0)

    for i, (da, db) in enumerate(corners()):
        peer, to = corner(da, db)
        block(peer)
        push(oh.at[pl.ds(pl.multiple_of(peer * rows, rows), rows), :], o.at[:, mine], send_o.at[i], got_o.at[i], to)
    block(me)
    pltpu.make_async_copy(oh.at[pl.ds(pl.multiple_of(me * rows, rows), rows), :], o.at[:, mine], place_o).start()
    pltpu.make_async_copy(oh.at[pl.ds(pl.multiple_of(me * rows, rows), rows), :], o.at[:, mine], place_o).wait()
    piece = o.at[:, mine]
    for i in range(3):
        await_bytes(piece, got_o.at[i])
        await_bytes(piece, send_o.at[i])
        for j in range(3):
            await_bytes(piece, send.at[j, i])


def attend(q_raw, k_raw, v, q_gain, k_gain, cosine, sine, keep, scale):
    rows, width = v.shape
    chips = lax.axis_size("ca") * lax.axis_size("cb")
    heads = jax.ShapeDtypeStruct((rows * chips, width // chips), v.dtype)
    vm, dma = pl.BlockSpec(memory_space=pltpu.VMEM), pltpu.SemaphoreType.DMA
    return pl.pallas_call(
        functools.partial(attend_kernel, scale),
        out_shape=[jax.ShapeDtypeStruct(v.shape, v.dtype), heads, heads, heads]
        + [jax.ShapeDtypeStruct((width // chips // HD, rows * chips, 1), jnp.float32)],
        in_specs=[vm] * 8,
        out_specs=[vm] * 5,
        scratch_shapes=[pltpu.VMEM(v.shape, v.dtype)] * 2 + [pltpu.VMEM(heads.shape, v.dtype)]
        + [dma((3, 3)), dma((3, 3)), dma((3,)), dma((3,)), dma((3,)), dma],
        compiler_params=pltpu.CompilerParams(collective_id=4, has_side_effects=True, vmem_limit_bytes=48 << 20),
        cost_estimate=pl.CostEstimate(flops=1_000_000, bytes_accessed=10_000, transcendentals=0),
        name="attend",
    )(q_raw, k_raw, v, q_gain, k_gain, cosine, sine, keep)


def attend_back_kernel(
    scale, do, qh, kh, vh, logs, keep, q_raw, k_raw, q_gain, k_gain, cosine, sine,
    dq_raw, dk_raw, dv, q_gain_grad, k_gain_grad,
    doh, dqh, dkh, dvh, dq, dk, turned, send, got, place, send_g, got_g, place_g,
):
    rows, width = do.shape[0], qh.shape[1]
    greet([corner(da, db)[1] for da, db in corners()])
    rows_to_heads(do, doh, send, got, place)
    wait_heads(do, doh, got, place)
    me, _ = corner(0, 0)
    tile, total_rows = 128, qh.shape[0]
    grads = ((dqh, dq), (dkh, dk), (dvh, dv))

    def one_head(h):
        lanes = pl.ds(h * HD, HD)

        def part(i, carry):
            dk_sum, dv_sum = carry
            at = pl.ds(pl.multiple_of(i * tile, tile), tile)
            qb, db, kb, vb = qh[at, lanes], doh[at, lanes], kh[:, lanes], vh[:, lanes]
            s = times_transposed(qb, kb) * scale
            s = jnp.where(keep[...] > 0.0, s, NEG_FILL)
            p = jnp.exp(s - logs[h, at, :])
            dp = times_transposed(db, vb)
            ds = (p * (dp - jnp.sum(dp * p, axis=-1, keepdims=True))).astype(jnp.bfloat16)
            dqh[at, lanes] = (matmul(ds, kb) * scale).astype(jnp.bfloat16)
            dk_sum = dk_sum + transposed_times(ds, qb)
            dv_sum = dv_sum + transposed_times(p.astype(jnp.bfloat16), db)
            return dk_sum, dv_sum

        zero = jnp.zeros((total_rows, HD), jnp.float32)
        dk_sum, dv_sum = lax.fori_loop(0, total_rows // tile, part, (zero, zero))
        dkh[:, lanes] = (dk_sum * scale).astype(jnp.bfloat16)
        dvh[:, lanes] = dv_sum.astype(jnp.bfloat16)

    for h in range(width // HD):
        one_head(h)
        lanes = pl.ds(h * HD, HD)
        here = pl.ds(pl.multiple_of(me * width + h * HD, HD), HD)
        for g, (src, dst) in enumerate(grads):
            for i, (da, db) in enumerate(corners()):
                peer, to = corner(da, db)
                push(src.at[pl.ds(pl.multiple_of(peer * rows, rows), rows), lanes], dst.at[:, here], send_g.at[g, i, h], got_g.at[g, i, h], to)
            own = src.at[pl.ds(pl.multiple_of(me * rows, rows), rows), lanes]
            pltpu.make_async_copy(own, dst.at[:, here], place_g.at[g, h]).start()
    piece = dq.at[:, pl.ds(0, HD)]
    for h in range(width // HD):
        for g in range(3):
            await_bytes(piece, place_g.at[g, h])
            for i in range(3):
                await_bytes(piece, send_g.at[g, i, h])
                await_bytes(piece, got_g.at[g, i, h])
    for i in range(3):
        await_bytes(do.at[:, pl.ds(0, width)], send.at[i])
    norm_and_turn_back(dk, k_raw, k_gain, cosine, sine, dk_raw, k_gain_grad, turned)
    norm_and_turn_back(dq, q_raw, q_gain, cosine, sine, dq_raw, q_gain_grad, turned)


def attend_back(do, qh, kh, vh, logs, keep, q_raw, k_raw, q_gain, k_gain, cosine, sine, scale):
    heads = qh.shape[1] // HD
    vm, dma = pl.BlockSpec(memory_space=pltpu.VMEM), pltpu.SemaphoreType.DMA
    return pl.pallas_call(
        functools.partial(attend_back_kernel, scale),
        out_shape=[jax.ShapeDtypeStruct(do.shape, do.dtype)] * 3 + [jax.ShapeDtypeStruct((8, do.shape[1]), jnp.float32)] * 2,
        in_specs=[vm] * 12,
        out_specs=[vm] * 5,
        scratch_shapes=[pltpu.VMEM(qh.shape, qh.dtype)] * 4
        + [pltpu.VMEM(do.shape, do.dtype)] * 2
        + [pltpu.VMEM((32, do.shape[1]), jnp.float32)]
        + [dma((3,)), dma((3,)), dma, dma((3, 3, heads)), dma((3, 3, heads)), dma((3, heads))],
        compiler_params=pltpu.CompilerParams(collective_id=5, has_side_effects=True, vmem_limit_bytes=56 << 20),
        cost_estimate=pl.CostEstimate(flops=50_000_000_000, bytes_accessed=10_000_000, transcendentals=0),
        name="attend_back",
    )(do, qh, kh, vh, logs, keep, q_raw, k_raw, q_gain, k_gain, cosine, sine)


def norm_rows(values, gain):
    factor = lax.rsqrt(jnp.mean(values * values, axis=-1, keepdims=True) + EPSILON)
    return (values * factor * gain, factor)


def norm_back(grad, values, factor, gain):
    weighted = grad * gain
    inner = jnp.mean(weighted * values, axis=-1, keepdims=True)
    return (factor * weighted - values * factor**3 * inner, jnp.sum(grad * values * factor, axis=0))


def rotary_tables(positions, head_dim):
    half_dim = head_dim // 2
    frequency = jnp.exp(-math.log(ROPE_THETA) * jnp.arange(half_dim, dtype=jnp.float32) / half_dim)
    angles = positions.astype(jnp.float32)[:, None] * frequency[None, :]
    return (jnp.cos(angles), jnp.sin(angles))


def local(
    tokens, cotangent, lengths, expert_ids, query_weight, key_weight, value_weight, out_weight,
    router_weight, first_gain, second_gain, query_gain, key_gain, gate_weight, up_weight, down_weight,
):
    token_count = tokens.shape[1]
    model_width = tokens.shape[2]
    head_dim = HD
    top_count = expert_ids.shape[2]
    experts = router_weight.shape[1]
    local_experts = gate_weight.shape[0]
    ctx_size = lax.axis_size(CTX)
    sources = lax.axis_size(EXP)
    capacity = max(2, -(-(token_count * top_count * 9) // (experts * 8)))
    score_scale = 1.0 / math.sqrt(head_dim)
    seq_len = token_count * ctx_size

    inputs = tokens[0].astype(jnp.float32)
    length = lengths[0]
    positions = lax.axis_index(CTX) * token_count + jnp.arange(token_count, dtype=jnp.int32)
    row_valid = positions < length
    row_valid = row_valid.astype(jnp.float32)[:, None]
    key_valid = jnp.arange(seq_len, dtype=jnp.int32) < length
    grad_total_low = (cotangent[0].astype(jnp.float32) * row_valid).astype(jnp.bfloat16)
    grad_total = grad_total_low.astype(jnp.float32)

    rows_each = query_weight.shape[0]
    packed = jnp.concatenate(
        [g.reshape(-1) for g in (first_gain, second_gain, query_gain, key_gain)] + [router_weight.reshape(-1)]
    )
    small = jnp.pad(packed, (0, -packed.size % 2048)).reshape(-1, 128)
    ids_low = expert_ids[0].astype(jnp.bfloat16).reshape(-1, 128)
    gathered, (ids_all, g_all) = spread([query_weight, key_weight, value_weight, out_weight, small], [ids_low, grad_total_low])
    g_all = g_all.reshape(sources, token_count, model_width)
    full_query, full_key, full_value, full_out = (w.reshape(model_width, -1) for w in gathered[:4])
    smalls = gathered[4].reshape(-1, small.size)
    gains = [smalls[:, i * rows_each : (i + 1) * rows_each].reshape(-1).astype(jnp.float32) for i in range(4)]
    gain_first, gain_second, gain_queries, gain_keys = gains
    full_router = smalls[:, 4 * rows_each : packed.size].reshape(model_width, experts)
    ids_all = ids_all.reshape(sources, token_count, top_count).astype(jnp.int32)
    full_value, gate_weight, up_weight, down_weight = lax.optimization_barrier((full_value, gate_weight, up_weight, down_weight))
    gate_all, up_all = (lax.all_gather(w, CTX, axis=2, tiled=True) for w in (gate_weight, up_weight))
    down_all = lax.all_gather(down_weight, CTX, axis=1, tiled=True)
    cosine, sine = rotary_tables(positions, head_dim)
    normed_one, factor_one = norm_rows(inputs, gain_first)
    normed_one_low = normed_one.astype(jnp.bfloat16)
    query_raw = matmul(normed_one_low, full_query)
    key_raw = matmul(normed_one_low, full_key)
    value_low = matmul(normed_one_low, full_value).astype(jnp.bfloat16)
    keep = key_valid.astype(jnp.float32)[None, :]
    turns = (jnp.concatenate([cosine, cosine], axis=1), jnp.concatenate([-sine, sine], axis=1))
    row = lambda g: g.reshape(1, model_width)
    shared = (row(gain_queries), row(gain_keys), *turns)
    attended_low, *saved = attend(query_raw, key_raw, value_low, *shared, keep, score_scale)
    hidden_state = inputs + matmul(attended_low, full_out)
    normed_two, factor_two = norm_rows(hidden_state, gain_second)
    normed_two_low = normed_two.astype(jnp.bfloat16)

    n2_all = dispatch(normed_two_low)
    n2_all, gate_all = lax.optimization_barrier((n2_all, gate_all))
    n2_all = n2_all.reshape(sources, token_count, model_width)
    first_expert = lax.axis_index(EXP) * local_experts
    own_experts = first_expert + jnp.arange(local_experts, dtype=jnp.int32)
    mask = jnp.any(ids_all[:, None, :, :] == own_experts[None, :, None, None], axis=-1)
    before = (jnp.arange(token_count)[:, None] < jnp.arange(token_count)[None, :]).astype(jnp.bfloat16)
    ranks = jnp.einsum("seu,ut->set", mask.astype(jnp.bfloat16), before, preferred_element_type=jnp.float32)
    slots = jnp.arange(capacity, dtype=jnp.float32)
    hot = (mask[:, :, None, :] & (ranks[:, :, None, :] == slots[None, None, :, None])).astype(jnp.bfloat16)
    logits = matmul(n2_all.reshape(-1, model_width), full_router)
    probs = jax.nn.softmax(logits, axis=-1)
    own_probs = lax.dynamic_slice_in_dim(probs, first_expert, local_experts, 1).reshape(sources, token_count, local_experts)
    hot32 = hot.astype(jnp.float32)
    row_gate = jnp.sum(hot32 * own_probs.transpose(0, 2, 1)[:, :, None, :], axis=-1)
    x = jnp.einsum("sect,std->escd", hot, n2_all, preferred_element_type=jnp.float32).astype(jnp.bfloat16)
    row_gate = row_gate.transpose(1, 0, 2)[..., None]
    ee = lambda eq, a, b: jnp.einsum(eq, a, b, preferred_element_type=jnp.float32)
    gp = ee("escd,edf->escf", x, gate_all)
    up = ee("escd,edf->escf", x, up_all)
    up, g_all = lax.optimization_barrier((up, g_all))
    g_rows = jnp.einsum("sect,std->escd", hot, g_all, preferred_element_type=jnp.float32)
    de = (g_rows * row_gate).astype(jnp.bfloat16)
    sig = jax.nn.sigmoid(gp)
    hid = (gp * sig * up).astype(jnp.bfloat16)
    down_part = ee("escf,escd->efd", hid, de).astype(jnp.bfloat16)
    down_all, down_part = lax.optimization_barrier((down_all, down_part))
    eo = ee("escf,efd->escd", hid, down_all).astype(jnp.bfloat16)
    dgate_rows = jnp.sum(g_rows * eo.astype(jnp.float32), axis=-1)
    mixed_rows = (row_gate * eo.astype(jnp.float32)).astype(jnp.bfloat16)
    mixed_part = jnp.einsum("sect,escd->std", hot, mixed_rows, preferred_element_type=jnp.float32)
    mixed_part = mixed_part.astype(jnp.bfloat16)

    dhid = ee("escd,efd->escf", de, down_all)
    dgp = (dhid * up * sig * (1.0 + gp * (1.0 - sig))).astype(jnp.bfloat16)
    dup = (dhid * gp * sig).astype(jnp.bfloat16)
    gate_part = ee("escd,escf->edf", x, dgp)
    up_part = ee("escd,escf->edf", x, dup)
    parts = [v.astype(jnp.bfloat16) for v in (down_part, gate_part, up_part)]
    dgp, dup, *_ = lax.optimization_barrier((dgp, dup, *parts))
    rs_ctx = lambda v, a: lax.psum_scatter(v, CTX, scatter_dimension=a, tiled=True)
    down_grad, gate_grad, up_grad = rs_ctx(parts[0], 1), rs_ctx(parts[1], 2), rs_ctx(parts[2], 2)
    dpair = (ee("escf,edf->escd", dgp, gate_all) + ee("escf,edf->escd", dup, up_all)).astype(jnp.bfloat16)

    dprobs_own = jnp.sum(hot32 * dgate_rows.transpose(1, 0, 2)[..., None], axis=2)
    dprobs_own = dprobs_own.transpose(0, 2, 1).reshape(-1, local_experts)
    onto = (jnp.arange(experts)[None, :] == own_experts[:, None]).astype(jnp.float32)
    dprobs = jnp.sum(dprobs_own[:, :, None] * onto[None], axis=1)
    dlogit_low = (probs * (dprobs - jnp.sum(dprobs * probs, axis=-1, keepdims=True))).astype(jnp.bfloat16)
    router_part = transposed_times(n2_all.reshape(-1, model_width), dlogit_low)
    dn2_part = jnp.einsum("sect,escd->std", hot, dpair, preferred_element_type=jnp.float32).reshape(-1, model_width)
    dn2_part = dn2_part + times_transposed(dlogit_low, full_router)
    dn2_part = dn2_part.astype(jnp.bfloat16).reshape(sources, token_count, model_width)
    dn2_part, down_grad = lax.optimization_barrier((dn2_part, down_grad))
    dn2 = give_back(dn2_part)
    dn2, gate_grad = lax.optimization_barrier((dn2, gate_grad))
    dn2, mixed_part = lax.optimization_barrier((dn2, mixed_part))
    mixed = lax.psum_scatter(mixed_part.reshape(-1, model_width), EXP, scatter_dimension=0, tiled=True)

    dh_norm, gain_second_part = norm_back(dn2, hidden_state, factor_two, gain_second)
    grad_hidden = grad_total + dh_norm
    dh_low = grad_hidden.astype(jnp.bfloat16)
    out_part = transposed_times(attended_low, dh_low)
    d_att = times_transposed(dh_low, full_out).astype(jnp.bfloat16)
    dq_low, dk_low, dv_low, *gain_parts = attend_back(d_att, *saved, keep, query_raw, key_raw, *shared, score_scale)
    dv_low, up_grad = lax.optimization_barrier((dv_low, up_grad))
    gain_queries_part, gain_keys_part = (jnp.sum(g, axis=0) for g in gain_parts)
    core = lax.axis_index("core")
    swap = lambda v: lax.ppermute(v, "core", [(0, 1), (1, 0)])

    def columns_of_core(v):
        width = model_width // 2
        mine = lax.dynamic_slice_in_dim(v, core * width, width, 1)
        other = lax.dynamic_slice_in_dim(v, (1 - core) * width, width, 1)
        return jnp.concatenate([mine, swap(other)], axis=0)

    both = lambda v: jnp.concatenate([v, swap(v)], axis=0)
    n1_both, att_both = both(normed_one_low), both(attended_low)
    parts = [
        transposed_times(l, columns_of_core(r)).astype(jnp.bfloat16)
        for l, r in ((att_both, dh_low), (n1_both, dq_low), (n1_both, dk_low), (n1_both, dv_low))
    ]
    split = lambda v: v.reshape(ctx_size * sources // 2, 2, -1)
    small_parts = jnp.concatenate(
        [split(v) for v in (gain_second_part, gain_queries_part, gain_keys_part, router_part)], axis=2
    )
    small_parts = jnp.pad(small_parts, ((0, 0), (0, 0), (0, -small_parts.shape[2] % 2048)))
    small_parts = lax.dynamic_index_in_dim(small_parts, core, 1, False) + swap(lax.dynamic_index_in_dim(small_parts, 1 - core, 1, False))
    weight_grads, small_grads, input_grad, gain_first_sums = collect(
        parts, small_parts.reshape(ctx_size * sources // 2, -1, 128), (dq_low, dk_low, dv_low),
        (full_query, full_key, full_value), tokens[0], row(gain_first), grad_hidden,
    )
    weight_grads, mixed, gate_grad, up_grad, down_grad = lax.optimization_barrier(
        (list(weight_grads), mixed, gate_grad, up_grad, down_grad)
    )
    layer_out = (row_valid * (hidden_state + mixed.astype(jnp.float32))).astype(jnp.bfloat16)
    gate_grad, up_grad, down_grad = (v.astype(jnp.float32) for v in (gate_grad, up_grad, down_grad))
    weight_grads = list(weight_grads[1:]) + [weight_grads[0]]
    small_grads = small_grads.reshape(-1)
    gain_grads = [lax.dynamic_slice_in_dim(jnp.sum(gain_first_sums, axis=0), lax.axis_index(ALL) * rows_each, rows_each)]
    gain_grads += [small_grads[i * rows_each : (i + 1) * rows_each] for i in range(3)]
    router_grad = small_grads[3 * rows_each : packed.size - rows_each].reshape(rows_each, experts)
    return (layer_out[None], input_grad[None], *weight_grads, router_grad, *gain_grads, gate_grad, up_grad, down_grad)


def solution(mesh):
    ctx, exp = mesh.devices.shape
    fine = Mesh(mesh.devices.reshape(2, ctx // 2, exp // 2, 2), ("ca", "cb", "ring", "core"))
    rows = P(EXP, CTX, None)
    flat2, flat1 = P(ALL, None), P(ALL)
    placed = (rows, rows, P(EXP), rows) + (flat2,) * 5 + (flat1,) * 4 + (P(EXP, None, CTX),) * 2 + (P(EXP, CTX, None),)
    outs = (rows, rows) + (flat2,) * 5 + (flat1,) * 4 + (P(EXP, None, CTX),) * 2 + (P(EXP, CTX, None),)
    return jax.shard_map(local, mesh=fine, in_specs=placed, out_specs=outs, check_vma=False)
```

```python
import functools
import math

import jax
import jax.numpy as jnp
from jax import lax
from jax.experimental import pallas as pl
from jax.experimental.pallas import tpu as pltpu
from jax.sharding import Mesh
from jax.sharding import PartitionSpec as P

HEADS = 16
HD = 128
EPSILON = 1e-06
ROPE_THETA = 10000.0
NEG_FILL = -1e30

CTX = ("ca", "cb")
EXP = ("ring", "core")
ALL = CTX + EXP


MESH = pl.DeviceIdType.MESH


def turn(name, by):
    size = lax.axis_size(name)
    return lax.rem(lax.axis_index(name) + by, size)


def await_bytes(ref, sem):
    pltpu.make_async_copy(ref, ref, sem).wait()


def greet(peers):
    barrier = pltpu.get_barrier_semaphore()
    for peer in peers:
        pl.semaphore_signal(barrier, inc=1, device_id=peer, device_id_type=MESH)
    pl.semaphore_wait(barrier, len(peers))


def push(src, dst, ssem, rsem, to):
    pltpu.make_async_remote_copy(
        src_ref=src, dst_ref=dst, send_sem=ssem, recv_sem=rsem, device_id=to, device_id_type=MESH
    ).start()


RING, SIDE_B, SIDE_A, FIRST, SECOND, CORE_OWN, CORE_B, CORE_A, CORE_FIRST, CORE_SECOND = range(10)


def along(step):
    ring, r = lax.axis_size("ring"), lax.axis_index("ring")
    to_next, to_last = {"ring": turn("ring", 1)}, {"ring": turn("ring", ring - 1)}
    return (
        ((r + 1 < ring) & (r >= step), r >= step + 1, lax.rem(r + ring - step, ring), lax.rem(r + ring - 1 - step, ring), to_next, 0),
        ((r >= 1) & (r + step < ring), r + 1 + step < ring, lax.rem(r + step, ring), lax.rem(r + 1 + step, ring), to_last, 1),
    )


def send_along(step, own, block_of, send, got):
    for sent, _, block, _, to, side in along(step):

        @pl.when(sent)
        def _(block=block, to=to, side=side):
            src = own if isinstance(step, int) and step == 0 else block_of(block)
            push(src, block_of(block), send.at[side, step], got.at[side, step], to)


def take_along(step, block_of, got, then):
    for _, comes, _, block, _, side in along(step):

        @pl.when(comes)
        def _(block=block, side=side):
            await_bytes(block_of(block), got.at[side, step])

    for _, comes, _, block, _, side in along(step):

        @pl.when(comes)
        def _(block=block):
            then(block)


def sent_along(own, send):
    ring = lax.axis_size("ring")
    for step in range(ring - 1):
        for sent, _, _, _, _, side in along(step):

            @pl.when(sent)
            def _(side=side):
                await_bytes(own, send.at[side, step])


def spread_kernel(count, tables, *refs):
    ring = lax.axis_size("ring")
    ins, refs = refs[: count + tables], refs[count + tables :]
    outs, sems = refs[: count + tables], refs[count + tables :]
    send, send_ring, got_ring, got_b, got_a, got, place, core_sem = sems
    a, b, r, c = (lax.axis_index(n) for n in ALL)
    na, nb, nc = turn("ca", 1), turn("cb", 1), turn("core", 1)
    to_a, to_b, to_core = {"ca": na}, {"cb": nb}, {"core": nc}
    greet([to_a, to_b, to_core] + [{"ring": turn("ring", k)} for k in range(1, ring)])

    def half(ref, which):
        rows, cols = ref.shape[-2:]
        if rows * 8 < cols:
            return ref.at[..., pl.ds(which * (cols // 2), cols // 2)]
        return ref.at[..., pl.ds(which * (rows // 2), rows // 2), :]

    def halves(ref, which):
        rows, cols = ref.shape[-2:]
        if rows * 8 < cols:
            return ref.at[:, :, pl.ds(which * (cols // 2), cols // 2)]
        return ref.at[:, pl.ds(which * (rows // 2), rows // 2), :]

    def place_of(w):
        return (lambda at: outs[w].at[a, b, at, c]) if w < count else (lambda at: outs[w].at[at, c])

    for w in range(count + tables):
        pltpu.make_async_copy(ins[w], place_of(w)(r), place.at[w]).start()
    for w in reversed(range(count)):
        send_along(0, ins[w], place_of(w), send_ring.at[w], got_ring.at[w])
        here = place_of(w)(r)
        push(ins[w], here, send.at[w, SIDE_B], got_b.at[w, r], to_b)
        push(ins[w], here, send.at[w, SIDE_A], got_a.at[w, r], to_a)
        push(ins[w], here, send.at[w, CORE_OWN], got.at[w, CORE_OWN], to_core)
    for t in range(tables):
        push(ins[count + t], place_of(count + t)(r), core_sem.at[t, 0], core_sem.at[t, 1], to_core)

    def sides(w):
        for step in range(ring - 1):

            def on(at):
                block = place_of(w)(at)
                push(block, block, send.at[w, SIDE_B], got_b.at[w, at], to_b)
                push(block, block, send.at[w, SIDE_A], got_a.at[w, at], to_a)
                push(block, block, send.at[w, CORE_OWN], got.at[w, CORE_OWN], to_core)

            take_along(step, place_of(w), got_ring.at[w], on)
            if step + 1 < ring - 1:
                send_along(step + 1, ins[w], place_of(w), send_ring.at[w], got_ring.at[w])

    def diagonal(w):
        out = outs[w]

        def one(k, carry):
            at = lax.rem(r + ring - k, ring)
            block = out.at[a, nb, at, c]
            await_bytes(block, got_b.at[w, at])
            push(half(block, 0), half(block, 0), send.at[w, FIRST], got.at[w, FIRST], to_a)
            push(block, block, send.at[w, CORE_B], got.at[w, CORE_B], to_core)
            block = out.at[na, b, at, c]
            await_bytes(block, got_a.at[w, at])
            push(half(block, 1), half(block, 1), send.at[w, SECOND], got.at[w, SECOND], to_b)
            push(block, block, send.at[w, CORE_A], got.at[w, CORE_A], to_core)
            return carry

        lax.fori_loop(0, ring, one, 0)

    def last(w):
        block = outs[w].at[na, nb, :, c]
        for which, kind, core_kind in ((0, FIRST, CORE_FIRST), (1, SECOND, CORE_SECOND)):
            part = halves(block, which)
            await_bytes(part, got.at[w, kind])
            push(part, part, send.at[w, core_kind], got.at[w, core_kind], to_core)

    def table_step(t, step):
        w = count + t

        def on(at):
            push(place_of(w)(at), place_of(w)(at), core_sem.at[t, 0], core_sem.at[t, 1], to_core)

        if step >= 0:
            take_along(step, place_of(w), got_ring.at[w], on)
        if step + 1 < ring - 1:
            send_along(step + 1, ins[w], place_of(w), send_ring.at[w], got_ring.at[w])

    order = list(reversed(range(count)))
    for step in range(count + 2):
        if step < count:
            sides(order[step])
        if step >= count - 1:
            for t in range(tables):
                table_step(t, step - count)
        if 0 <= step - 1 < count:
            diagonal(order[step - 1])
        if 0 <= step - 2 < count:
            last(order[step - 2])
    for step in range(2, ring - 1):
        for t in range(tables):
            table_step(t, step)

    for w in range(count):
        out = outs[w]
        mine = lambda p, q: out.at[p, q, :, c]
        await_bytes(ins[w], place.at[w])
        sent_along(ins[w], send_ring.at[w])
        for kind in (SIDE_B, SIDE_A, CORE_OWN, CORE_B, CORE_A):
            await_bytes(mine(a, b), send.at[w, kind])
        for which, kind in ((0, FIRST), (1, SECOND), (0, CORE_FIRST), (1, CORE_SECOND)):
            await_bytes(halves(mine(a, b), which), send.at[w, kind])
        for kind, p, q in ((CORE_OWN, a, b), (CORE_B, a, nb), (CORE_A, na, b)):
            await_bytes(out.at[p, q, :, nc], got.at[w, kind])
        for which, kind in ((0, CORE_FIRST), (1, CORE_SECOND)):
            await_bytes(halves(out.at[na, nb, :, nc], which), got.at[w, kind])
    for t in range(tables):
        w = count + t
        await_bytes(ins[w], place.at[w])
        sent_along(ins[w], send_ring.at[w])
        await_bytes(outs[w].at[:, c], core_sem.at[t, 0])
        await_bytes(outs[w].at[:, nc], core_sem.at[t, 1])


def spread(shards, tables):
    count, more, ring = len(shards), len(tables), lax.axis_size("ring")
    square = (lax.axis_size("ca"), lax.axis_size("cb"), ring, 2)
    dma = pltpu.SemaphoreType.DMA
    outs = pl.pallas_call(
        functools.partial(spread_kernel, count, more),
        out_shape=[jax.ShapeDtypeStruct(square + s.shape, s.dtype) for s in shards]
        + [jax.ShapeDtypeStruct((ring, 2) + t.shape, t.dtype) for t in tables],
        in_specs=[pl.BlockSpec(memory_space=pltpu.VMEM)] * (count + more),
        out_specs=[pl.BlockSpec(memory_space=pl.ANY)] * (count + more),
        scratch_shapes=[
            dma((count, 10)), dma((count + more, 2, ring)), dma((count + more, 2, ring)), dma((count, ring)), dma((count, ring)),
            dma((count, 10)), dma((count + more,)), dma((more, 2)),
        ],
        compiler_params=pltpu.CompilerParams(collective_id=0, has_side_effects=True),
        cost_estimate=pl.CostEstimate(flops=150_000_000_000, bytes_accessed=300_000_000, transcendentals=0),
        name="spread",
    )(*shards, *tables)
    return outs[:count], outs[count:]


def collect_kernel(count, *refs):
    ring = lax.axis_size("ring")
    parts, refs = refs[:count], refs[count:]
    grads, matrices, (x, gain, passed), refs = refs[:3], refs[3:6], refs[6:9], refs[9:]
    outs, (input_grad, gain_out), refs = refs[:count], refs[count : count + 2], refs[count + 2 :]
    scratch, refs = refs[: 9 * count], refs[9 * count :]
    send, got, ring_send, ring_got, load, chunks, dn1, sums, arrived, ring_arrived, fetch, gain_send, gain_got = refs
    a, b, r, c = (lax.axis_index(n) for n in ALL)
    na, nb, nc = turn("ca", 1), turn("cb", 1), turn("core", 1)
    to_a, to_b, to_core = {"ca": na}, {"cb": nb}, {"core": nc}
    bufs = [scratch[9 * w : 9 * w + 9] for w in range(count)]
    greet([to_a, to_b, to_core] + [{"ring": turn("ring", k)} for k in range(1, ring)])

    def chunk(i, slot, w):
        rows = chunks.shape[2]
        return pltpu.make_async_copy(
            matrices[w].at[pl.ds(pl.multiple_of(i * rows, rows), rows), :], chunks.at[slot, w], fetch.at[slot, w]
        )

    steps, chunk_rows = matrices[0].shape[0] // chunks.shape[2], chunks.shape[2]

    def input_part(begin, end):
        rows = chunk_rows

        def one(i, carry):
            slot = lax.rem(i, 2)

            @pl.when(i + 1 < steps)
            def _():
                for w in range(3):
                    chunk(i + 1, 1 - slot, w).start()

            value = jnp.zeros((x.shape[0], rows), jnp.float32)
            for w in range(3):
                chunk(i, slot, w).wait()
                value = value + times_transposed(grads[w][...], chunks[slot, w])
            dn1[:, pl.ds(pl.multiple_of(i * rows, rows), rows)] = value
            return carry

        lax.fori_loop(begin, end, one, 0)

    def input_end():
        tile = 32
        sums[0] = jnp.zeros(sums.shape[1:], jnp.float32)

        def back(i, carry):
            at = pl.ds(pl.multiple_of(i * tile, tile), tile)
            v, grad = x[at, :].astype(jnp.float32), dn1[at, :]
            factor = lax.rsqrt(jnp.mean(v * v, axis=-1, keepdims=True) + EPSILON)
            weighted = grad * gain[...]
            inner = jnp.mean(weighted * v, axis=-1, keepdims=True)
            total = passed[at, :] + factor * weighted - v * (factor * factor * factor * inner)
            input_grad[at, :] = total.astype(input_grad.dtype)
            gained = grad * v * factor
            sums[0] += sum(gained[k : k + 8] for k in range(0, tile, 8))
            return carry

        lax.fori_loop(0, x.shape[0] // tile, back, 0)
        push(sums.at[0], arrived.at[0], gain_send.at[0], gain_got.at[0], to_a)

    def gain_stage(stage):
        if stage < 3:
            await_bytes(arrived.at[stage], gain_got.at[stage])
            sums[stage + 1] = sums[stage] + arrived[stage]
            if stage < 2:
                push(sums.at[stage + 1], arrived.at[stage + 1], gain_send.at[stage + 1], gain_got.at[stage + 1], (to_b, to_core)[stage])
            else:
                for k in range(1, ring):
                    push(sums.at[3], ring_arrived.at[k - 1], gain_send.at[2 + k], gain_got.at[2 + k], {"ring": turn("ring", k)})
        else:
            total = sums[3]
            for k in range(1, ring):
                await_bytes(ring_arrived.at[k - 1], gain_got.at[2 + k])
                total = total + ring_arrived[k - 1]
            gain_out[...] = total
            for k in range(3 + ring - 1):
                await_bytes(sums.at[0], gain_send.at[k])

    def half(ref, which):
        rows, cols = ref.shape[-2:]
        lead = (slice(None),) * (len(ref.shape) - 2)
        if cols > 128:
            return ref.at[(*lead, slice(None), pl.ds(which * (cols // 2), cols // 2))]
        return ref.at[(*lead, pl.ds(which * (rows // 2), rows // 2), slice(None))]

    def loads(w):
        own_a, own_b = bufs[w][0:2]
        return (
            pltpu.make_async_copy(half(parts[w].at[a], 0), own_a, load.at[w, 0]),
            pltpu.make_async_copy(half(parts[w].at[:, b], 1), own_b, load.at[w, 1]),
        )

    def first(w):
        for copy in loads(w):
            copy.start()
        in_a, in_b = bufs[w][2:4]
        push(half(parts[w].at[na], 0), in_a, send.at[w, 0], got.at[w, 0], to_a)
        push(half(parts[w].at[:, nb], 1), in_b, send.at[w, 1], got.at[w, 1], to_b)

    def add(into, other):
        def one(k, carry):
            into[:, k] = (into[:, k].astype(jnp.float32) + other[:, k].astype(jnp.float32)).astype(into.dtype)
            return carry

        lax.fori_loop(0, ring, one, 0)

    def second(w):
        own_a, own_b, in_a, in_b, in_a2, in_b2 = bufs[w][:6]
        for copy in loads(w):
            copy.wait()
        await_bytes(in_a, got.at[w, 0])
        add(own_a, in_a)
        push(own_a.at[nb], in_a2, send.at[w, 2], got.at[w, 2], to_b)
        await_bytes(in_b, got.at[w, 1])
        add(own_b, in_b)
        push(own_b.at[na], in_b2, send.at[w, 3], got.at[w, 3], to_a)

    def third(w):
        own_a, own_b, _, _, in_a2, in_b2, total, in_ring = bufs[w][:8]
        await_bytes(in_a2, got.at[w, 2])
        await_bytes(in_b2, got.at[w, 3])

        def one(k, carry):
            sums = [
                own[own_at, k].astype(jnp.float32) + more[k].astype(jnp.float32)
                for own, own_at, more in ((own_a, b, in_a2), (own_b, a, in_b2))
            ]
            for which in range(2):
                half(total.at[k], which)[...] = sums[which].astype(total.dtype)
            return carry

        lax.fori_loop(0, ring, one, 0)
        for k in range(1, ring):
            at = turn("ring", k)
            push(total.at[at], in_ring.at[k - 1], ring_send.at[w, k - 1], ring_got.at[w, k - 1], {"ring": at})

    def fourth(w):
        total, in_ring, final = bufs[w][6:9]
        for k in range(1, ring):
            await_bytes(in_ring.at[k - 1], ring_got.at[w, k - 1])
        if final.shape[0] == 2:
            rows = final.shape[1]
            for core in range(2):
                at = pl.ds(core * rows, rows)
                value = total[r, at, :].astype(jnp.float32)
                for k in range(ring - 1):
                    value = value + in_ring[k, at, :].astype(jnp.float32)
                final[core] = value
            cols = final.shape[2]
            there = outs[w].at[:, pl.ds(pl.multiple_of(c * cols, cols), cols)]
            push(final.at[nc], there, send.at[w, 4], got.at[w, 4], to_core)
            pltpu.make_async_copy(final.at[c], there, load.at[w, 2]).start()
        else:
            value = total[r].astype(jnp.float32)
            for k in range(ring - 1):
                value = value + in_ring[k].astype(jnp.float32)
            outs[w][...] = value

    def finish(w):
        own_a, own_b, in_a, in_b, in_a2, in_b2, total, in_ring, final = bufs[w]
        await_bytes(in_a, send.at[w, 0])
        await_bytes(in_b, send.at[w, 1])
        await_bytes(in_a2, send.at[w, 2])
        await_bytes(in_b2, send.at[w, 3])
        for k in range(1, ring):
            await_bytes(in_ring.at[k - 1], ring_send.at[w, k - 1])
        if final.shape[0] == 2:
            await_bytes(final.at[0], send.at[w, 4])
            await_bytes(final.at[0], got.at[w, 4])
            await_bytes(final.at[0], load.at[w, 2])

    for w in range(3):
        chunk(0, 0, w).start()
    first(0)
    for step in range(max(count + 3, 9)):
        if step + 1 < count:
            first(step + 1)
        if step < count:
            second(step)
        if 0 <= step - 1 < count:
            third(step - 1)
        if 0 <= step - 2 < count:
            fourth(step - 2)
        if 1 <= step < 5:
            input_part((step - 1) * steps // 4, step * steps // 4)
        if step == 4:
            input_end()
        if step > 4:
            gain_stage(step - 5)
    for w in range(count):
        finish(w)


def collect(parts, small, grads, matrices, x, gain, passed):
    count, ring = len(parts) + 1, lax.axis_size("ring")
    chips = lax.axis_size("ca") * lax.axis_size("cb") * ring
    square = (lax.axis_size("ca"), lax.axis_size("cb"), ring)
    views = [p.reshape(square + (p.shape[0] // chips, p.shape[1])) for p in parts]
    views = [small.reshape(square + small.shape[1:])] + views
    shapes, scratch = [], []
    for v in views:
        rows, cols = v.shape[3:]
        piece = (rows, cols // 2) if cols > 128 else (rows // 2, cols)
        big = cols > 128
        vm = lambda *shape: pltpu.VMEM(shape, v.dtype)
        scratch += [vm(2, ring, *piece)] * 4 + [vm(ring, *piece)] * 2
        scratch += [vm(ring, rows, cols), vm(ring - 1, rows, cols)]
        scratch += [pltpu.VMEM((2, rows // 2, cols) if big else (1, 8, 128), jnp.float32)]
        shapes.append(jax.ShapeDtypeStruct((rows // 2, 2 * cols) if big else (rows, cols), jnp.float32))
    dma = pltpu.SemaphoreType.DMA
    vm, anywhere = pl.BlockSpec(memory_space=pltpu.VMEM), pl.BlockSpec(memory_space=pl.ANY)
    wide = (8, gain.shape[1])
    f32 = lambda *shape: pltpu.VMEM(shape, jnp.float32)
    outs = pl.pallas_call(
        functools.partial(collect_kernel, count),
        out_shape=shapes + [jax.ShapeDtypeStruct(x.shape, x.dtype), jax.ShapeDtypeStruct(wide, jnp.float32)],
        in_specs=[anywhere] * count + [vm] * 3 + [anywhere] * 3 + [vm] * 3,
        out_specs=[vm] * (count + 2),
        scratch_shapes=scratch
        + [dma((count, 5)), dma((count, 5)), dma((count, ring - 1)), dma((count, ring - 1)), dma((count, 3))]
        + [pltpu.VMEM((2, 3, 256, x.shape[1]), x.dtype), f32(*x.shape), f32(4, *wide), f32(3, *wide), f32(ring - 1, *wide)]
        + [dma((2, 3)), dma((2 + ring,)), dma((2 + ring,))],
        compiler_params=pltpu.CompilerParams(collective_id=1, has_side_effects=True, vmem_limit_bytes=62 << 20),
        cost_estimate=pl.CostEstimate(flops=160_000_000_000, bytes_accessed=320_000_000, transcendentals=0),
        name="collect",
    )(*views, *grads, *matrices, x, gain, passed)
    return outs[1:count], outs[0], outs[count], outs[count + 1]


def dispatch_kernel(
    rows, router, hot, g_all, out, picked, grads, gates, probs,
    rows_in, g_in, picked_low, grads_low, load, store, ring_send, ring_got, place, core_send, core_got,
):
    ring = lax.axis_size("ring")
    r, c, nc = lax.axis_index("ring"), lax.axis_index("core"), turn("core", 1)
    to_core, experts = {"core": nc}, hot.shape[1]
    greet([to_core] + [{"ring": turn("ring", k)} for k in range(1, ring)])
    block_of = lambda at: out.at[at, c]

    own = pltpu.make_async_copy(rows, block_of(r), place)
    own.start()
    push(rows, block_of(r), core_send, core_got.at[r], to_core)
    own.wait()
    send_along(0, block_of(r), block_of, ring_send, ring_got)
    first = (r * 2 + c) * experts
    width = rows.shape[1]
    cols = min(512, width)

    def pick(at, core):
        source = at * 2 + core
        copies = (
            pltpu.make_async_copy(out.at[at, core], rows_in, load.at[0]),
            pltpu.make_async_copy(g_all.at[at, core], g_in, load.at[1]),
        )
        for copy in copies:
            copy.start()
        copies[0].wait()
        logits = times_transposed(router[...], rows_in[...])
        likely = jnp.exp(logits - jnp.max(logits, axis=0, keepdims=True))
        probs[source] = likely / jnp.sum(likely, axis=0, keepdims=True)
        copies[1].wait()
        for e in range(experts):
            own_probs = probs[source, pl.ds(first + e, 1), :]
            gate = jnp.sum(hot[source, e].astype(jnp.float32) * own_probs, axis=-1, keepdims=True)
            gates[e, source] = gate

            def part(i, carry):
                lanes = pl.ds(pl.multiple_of(i * cols, cols), cols)
                chosen = hot[source, e]
                picked_low[e, :, lanes] = matmul(chosen, rows_in[:, lanes]).astype(picked_low.dtype)
                grads_low[e, :, lanes] = (matmul(chosen, g_in[:, lanes]) * gate).astype(grads_low.dtype)
                return carry

            lax.fori_loop(0, width // cols, part, 0)
        stores = (
            pltpu.make_async_copy(picked_low, picked.at[:, source], store.at[0]),
            pltpu.make_async_copy(grads_low, grads.at[:, source], store.at[1]),
        )
        for copy in stores:
            copy.start()
        for copy in stores:
            copy.wait()

    pick(r, c)
    await_bytes(out.at[r, nc], core_got.at[r])
    pick(r, nc)

    def step_on(step, carry):
        take_along(step, block_of, ring_got, lambda at: None)

        @pl.when(step + 1 < ring - 1)
        def _():
            send_along(step + 1, None, block_of, ring_send, ring_got)

        for _, comes, _, block, _, _ in along(step):

            @pl.when(comes)
            def _(block=block):
                push(block_of(block), block_of(block), core_send, core_got.at[block], to_core)

        def four(k, carry):
            side, other = k // 2, lax.rem(k, 2)
            (_, comes0, _, block0, _, _), (_, comes1, _, block1, _, _) = along(step)
            block = jnp.where(side == 0, block0, block1)
            comes = ((side == 0) & comes0) | ((side == 1) & comes1)
            core = lax.rem(c + other, 2)

            @pl.when(comes & (other == 1))
            def _():
                await_bytes(out.at[block, nc], core_got.at[block])

            @pl.when(comes)
            def _():
                pick(block, core)

            return carry

        lax.fori_loop(0, 4, four, 0)
        return carry

    lax.fori_loop(0, ring - 1, step_on, 0)
    sent_along(rows, ring_send)
    await_bytes(out.at[:, c], core_send)


def dispatch(rows, router, hot, g_all):
    ring, dma = lax.axis_size("ring"), pltpu.SemaphoreType.DMA
    sources, experts, slots, count = hot.shape
    width = rows.shape[1]
    low = lambda *shape: jax.ShapeDtypeStruct(shape, rows.dtype)
    f32 = lambda *shape: jax.ShapeDtypeStruct(shape, jnp.float32)
    vm, anywhere = pl.BlockSpec(memory_space=pltpu.VMEM), pl.BlockSpec(memory_space=pl.ANY)
    block = pltpu.VMEM((experts, slots, width), rows.dtype)
    chosen = (experts, sources, slots, width)
    return pl.pallas_call(
        dispatch_kernel,
        out_shape=[
            low(ring, 2, count, width), low(*chosen), low(*chosen), f32(experts, sources, slots, 1),
            f32(sources, router.shape[0], count),
        ],
        in_specs=[vm, vm, vm, anywhere],
        out_specs=[anywhere, anywhere, anywhere, vm, vm],
        scratch_shapes=[pltpu.VMEM(rows.shape, rows.dtype)] * 2
        + [block, block]
        + [dma((2,)), dma((2,)), dma((2, ring)), dma((2, ring)), dma, dma, dma((ring,))],
        compiler_params=pltpu.CompilerParams(collective_id=2, has_side_effects=True, vmem_limit_bytes=56 << 20),
        cost_estimate=pl.CostEstimate(flops=1_000_000, bytes_accessed=10_000, transcendentals=0),
        name="dispatch",
    )(rows, router, hot, g_all)


def give_back_kernel(part, out, own, core_in, chain_in, load, core_send, core_got, chain_send, chain_got):
    ring, pieces, rows, cols = own.shape
    r, c, nc = lax.axis_index("ring"), lax.axis_index("core"), turn("core", 1)
    to_next, to_last = {"ring": turn("ring", 1)}, {"ring": turn("ring", ring - 1)}
    greet([{"core": nc}] + [{"ring": turn("ring", k)} for k in range(1, ring)])
    order = [d for pair in zip(reversed(range(ring)), range(ring)) for d in pair][:ring]
    for d in order:
        push(part.at[d, nc], core_in.at[d], core_send.at[d], core_got.at[d], {"core": nc})
        pltpu.make_async_copy(part.at[d, c], own.at[d], load.at[d]).start()
    tile = 32

    def add(d, piece, other):
        def one(i, carry):
            at = pl.ds(pl.multiple_of(i * tile, tile), tile)
            own[d, piece, at] = (own[d, piece, at].astype(jnp.float32) + other[at].astype(jnp.float32)).astype(own.dtype)
            return carry

        lax.fori_loop(0, rows // tile, one, 0)

    def slot(side, d, whose):
        return d if side == 0 else jnp.where(d == whose, ring, d)

    def pass_on(side, step, d, piece, to):
        there = chain_in.at[slot(side, d, r - 1), piece]
        push(own.at[d, piece], there, chain_send.at[side, step, piece], chain_got.at[side, step, piece], to)

    for d in order:
        await_bytes(own.at[d], load.at[d])
        await_bytes(core_in.at[d], core_got.at[d])
        for piece in range(pieces):
            add(d, piece, core_in.at[d, piece])

            @pl.when((r == 0) & (d != r))
            def _():
                pass_on(0, ring - 1 - d, d, piece, to_next)

            @pl.when((r == ring - 1) & (d != r))
            def _():
                pass_on(1, d, d, piece, to_last)

    def sides(time):
        up, down = time - r, time - (ring - 1 - r)
        return (
            ((r >= 1) & (up >= 0), jnp.maximum(up, 0), ring - 1 - jnp.maximum(up, 0), to_next, 0),
            ((r + 1 < ring) & (down >= 0), jnp.maximum(down, 0), jnp.maximum(down, 0), to_last, 1),
        )

    def on(time, carry):
        for piece in range(pieces):
            for comes, step, d, to, side in sides(time):

                @pl.when(comes)
                def _(step=step, d=d, to=to, side=side):
                    arrived = chain_in.at[slot(side, d, r), piece]
                    await_bytes(arrived, chain_got.at[side, step, piece])
                    add(d, piece, arrived)

                    @pl.when(time < ring - 1)
                    def _():
                        pass_on(side, step, d, piece, to)

        return carry

    lax.fori_loop(1, ring, on, 0)

    def total(i, carry):
        at = pl.ds(pl.multiple_of(i * tile, tile), tile)
        for piece in range(pieces):
            out[pl.ds(pl.multiple_of(piece * rows + i * tile, tile), tile), :] = own[r, piece, at].astype(jnp.float32)
        return carry

    lax.fori_loop(0, rows // tile, total, 0)
    for d in order:
        await_bytes(core_in.at[d], core_send.at[d])
    for step in range(ring - 1):
        for piece in range(pieces):
            for sent, side in ((r + step < ring - 1, 0), (step < r, 1)):

                @pl.when(sent)
                def _(side=side):
                    await_bytes(own.at[0, 0], chain_send.at[side, step, piece])


def give_back(part):
    ring, dma, pieces = lax.axis_size("ring"), pltpu.SemaphoreType.DMA, 2
    rows, cols = part.shape[1:]
    block = lambda *lead: pltpu.VMEM((*lead, pieces, rows // pieces, cols), part.dtype)
    chain = dma((2, ring, pieces))
    return pl.pallas_call(
        give_back_kernel,
        out_shape=jax.ShapeDtypeStruct((rows, cols), jnp.float32),
        in_specs=[pl.BlockSpec(memory_space=pl.ANY)],
        out_specs=pl.BlockSpec(memory_space=pltpu.VMEM),
        scratch_shapes=[block(ring), block(ring), block(ring + 1), dma((ring,)), dma((ring,)), dma((ring,)), chain, chain],
        compiler_params=pltpu.CompilerParams(collective_id=3, has_side_effects=True, vmem_limit_bytes=60 << 20),
        cost_estimate=pl.CostEstimate(flops=100_000_000_000, bytes_accessed=200_000_000, transcendentals=0),
        name="give_back",
    )(part.reshape(ring, 2, pieces, rows // pieces, cols))


def matmul(left, right):
    return jnp.dot(left, right, preferred_element_type=jnp.float32)


def times_transposed(left, right):
    return lax.dot_general(
        left, right, (((1,), (1,)), ((), ())), preferred_element_type=jnp.float32
    )


def transposed_times(left, right):
    return lax.dot_general(
        left, right, (((0,), (0,)), ((), ())), preferred_element_type=jnp.float32
    )


def corners():
    return ((0, 1), (1, 0), (1, 1))


def corner(da, db):
    pa, pb = turn("ca", da), turn("cb", db)
    return 2 * pa + pb, {"ca": pa, "cb": pb}


def rows_to_heads(src, dst, send, got, place):
    rows, width = src.shape[0], dst.shape[1]
    me, _ = corner(0, 0)
    there = dst.at[pl.ds(pl.multiple_of(me * rows, rows), rows), :]
    for i, (da, db) in enumerate(corners()):
        peer, to = corner(da, db)
        push(src.at[:, pl.ds(pl.multiple_of(peer * width, width), width)], there, send.at[i], got.at[i], to)
    pltpu.make_async_copy(src.at[:, pl.ds(pl.multiple_of(me * width, width), width)], there, place).start()


def wait_heads(src, dst, got, place):
    rows = src.shape[0]
    here = lambda at: dst.at[pl.ds(pl.multiple_of(at * rows, rows), rows), :]
    await_bytes(here(corner(0, 0)[0]), place)
    for i, (da, db) in enumerate(corners()):
        await_bytes(here(corner(da, db)[0]), got.at[i])


def swap_halves(v):
    return pltpu.roll(v, HD // 2, 1)


def norm_and_turn(raw, gain, cosine, sine, out):
    rows, width = raw.shape
    tile = 32

    def part(i, carry):
        at = pl.ds(pl.multiple_of(i * tile, tile), tile)
        value = raw[at, :]
        factor = lax.rsqrt(jnp.mean(value * value, axis=-1, keepdims=True) + EPSILON)
        for h in range(width // HD):
            lanes = pl.ds(h * HD, HD)
            v = raw[at, lanes] * factor * gain[:, lanes]
            out[at, lanes] = (v * cosine[at, :] + swap_halves(v) * sine[at, :]).astype(out.dtype)
        return carry

    lax.fori_loop(0, rows // tile, part, 0)


def norm_and_turn_back(grad, raw, gain, cosine, sine, out, gain_grad, turned):
    rows, width = raw.shape
    tile = 32
    gain_grad[...] = jnp.zeros_like(gain_grad)

    def part(i, carry):
        at = pl.ds(pl.multiple_of(i * tile, tile), tile)
        value = raw[at, :]
        factor = lax.rsqrt(jnp.mean(value * value, axis=-1, keepdims=True) + EPSILON)
        inner = jnp.zeros((tile, HD), jnp.float32)
        for h in range(width // HD):
            lanes = pl.ds(h * HD, HD)
            g = grad[at, lanes].astype(jnp.float32)
            g = g * cosine[at, :] - swap_halves(g) * sine[at, :]
            turned[:, lanes] = g
            inner = inner + g * gain[:, lanes] * raw[at, lanes]
        inner = jnp.sum(inner, axis=-1, keepdims=True) * (factor * factor * factor / width)
        for h in range(width // HD):
            lanes = pl.ds(h * HD, HD)
            g, v = turned[:, lanes], raw[at, lanes]
            out[at, lanes] = (factor * (g * gain[:, lanes]) - v * inner).astype(out.dtype)
            gained = g * v * factor
            gain_grad[:, lanes] += sum(gained[k : k + 8] for k in range(0, tile, 8))
        return carry

    lax.fori_loop(0, rows // tile, part, 0)


def attend_kernel(scale, q_raw, k_raw, v, q_gain, k_gain, cosine, sine, keep, o, qh, kh, vh, logs, q, k, oh, send, got, place, send_o, got_o, place_o):
    rows, width = v.shape[0], qh.shape[1]
    greet([corner(da, db)[1] for da, db in corners()])
    pairs = ((v, vh), (k, kh), (q, qh))
    rows_to_heads(v, vh, send.at[0], got.at[0], place.at[0])
    norm_and_turn(k_raw, k_gain, cosine, sine, k)
    rows_to_heads(k, kh, send.at[1], got.at[1], place.at[1])
    norm_and_turn(q_raw, q_gain, cosine, sine, q)
    rows_to_heads(q, qh, send.at[2], got.at[2], place.at[2])
    for i, (src, dst) in enumerate(pairs):
        wait_heads(src, dst, got.at[i], place.at[i])
    me, _ = corner(0, 0)
    tile = 128
    mine = pl.ds(pl.multiple_of(me * width, width), width)

    def block(at_block):
        def part(i, carry):
            at = pl.ds(pl.multiple_of(at_block * rows + i * tile, tile), tile)
            for h in range(width // HD):
                lanes = pl.ds(h * HD, HD)
                s = times_transposed(qh[at, lanes], kh[:, lanes]) * scale
                s = jnp.where(keep[...] > 0.0, s, NEG_FILL)
                peak = jnp.max(s, axis=-1, keepdims=True)
                p = jnp.exp(s - peak)
                total = jnp.sum(p, axis=-1, keepdims=True)
                logs[h, at, :] = peak + jnp.log(total)
                low = (p * (1.0 / total)).astype(jnp.bfloat16)
                oh[at, lanes] = matmul(low, vh[:, lanes]).astype(jnp.bfloat16)
            return carry

        lax.fori_loop(0, rows // tile, part, 0)

    for i, (da, db) in enumerate(corners()):
        peer, to = corner(da, db)
        block(peer)
        push(oh.at[pl.ds(pl.multiple_of(peer * rows, rows), rows), :], o.at[:, mine], send_o.at[i], got_o.at[i], to)
    block(me)
    pltpu.make_async_copy(oh.at[pl.ds(pl.multiple_of(me * rows, rows), rows), :], o.at[:, mine], place_o).start()
    pltpu.make_async_copy(oh.at[pl.ds(pl.multiple_of(me * rows, rows), rows), :], o.at[:, mine], place_o).wait()
    piece = o.at[:, mine]
    for i in range(3):
        await_bytes(piece, got_o.at[i])
        await_bytes(piece, send_o.at[i])
        for j in range(3):
            await_bytes(piece, send.at[j, i])


def attend(q_raw, k_raw, v, q_gain, k_gain, cosine, sine, keep, scale):
    rows, width = v.shape
    chips = lax.axis_size("ca") * lax.axis_size("cb")
    heads = jax.ShapeDtypeStruct((rows * chips, width // chips), v.dtype)
    vm, dma = pl.BlockSpec(memory_space=pltpu.VMEM), pltpu.SemaphoreType.DMA
    return pl.pallas_call(
        functools.partial(attend_kernel, scale),
        out_shape=[jax.ShapeDtypeStruct(v.shape, v.dtype), heads, heads, heads]
        + [jax.ShapeDtypeStruct((width // chips // HD, rows * chips, 1), jnp.float32)],
        in_specs=[vm] * 8,
        out_specs=[vm] * 5,
        scratch_shapes=[pltpu.VMEM(v.shape, v.dtype)] * 2 + [pltpu.VMEM(heads.shape, v.dtype)]
        + [dma((3, 3)), dma((3, 3)), dma((3,)), dma((3,)), dma((3,)), dma],
        compiler_params=pltpu.CompilerParams(collective_id=4, has_side_effects=True, vmem_limit_bytes=48 << 20),
        cost_estimate=pl.CostEstimate(flops=1_000_000, bytes_accessed=10_000, transcendentals=0),
        name="attend",
    )(q_raw, k_raw, v, q_gain, k_gain, cosine, sine, keep)


def attend_back_kernel(
    scale, do, qh, kh, vh, logs, keep, q_raw, k_raw, q_gain, k_gain, cosine, sine,
    dq_raw, dk_raw, dv, q_gain_grad, k_gain_grad,
    doh, dqh, dkh, dvh, dq, dk, turned, send, got, place, send_g, got_g, place_g,
):
    rows, width = do.shape[0], qh.shape[1]
    greet([corner(da, db)[1] for da, db in corners()])
    rows_to_heads(do, doh, send, got, place)
    wait_heads(do, doh, got, place)
    me, _ = corner(0, 0)
    tile, total_rows = 128, qh.shape[0]
    grads = ((dqh, dq), (dkh, dk), (dvh, dv))

    def one_head(h):
        lanes = pl.ds(h * HD, HD)

        def part(i, carry):
            dk_sum, dv_sum = carry
            at = pl.ds(pl.multiple_of(i * tile, tile), tile)
            qb, db, kb, vb = qh[at, lanes], doh[at, lanes], kh[:, lanes], vh[:, lanes]
            s = times_transposed(qb, kb) * scale
            s = jnp.where(keep[...] > 0.0, s, NEG_FILL)
            p = jnp.exp(s - logs[h, at, :])
            dp = times_transposed(db, vb)
            ds = (p * (dp - jnp.sum(dp * p, axis=-1, keepdims=True))).astype(jnp.bfloat16)
            dqh[at, lanes] = (matmul(ds, kb) * scale).astype(jnp.bfloat16)
            dk_sum = dk_sum + transposed_times(ds, qb)
            dv_sum = dv_sum + transposed_times(p.astype(jnp.bfloat16), db)
            return dk_sum, dv_sum

        zero = jnp.zeros((total_rows, HD), jnp.float32)
        dk_sum, dv_sum = lax.fori_loop(0, total_rows // tile, part, (zero, zero))
        dkh[:, lanes] = (dk_sum * scale).astype(jnp.bfloat16)
        dvh[:, lanes] = dv_sum.astype(jnp.bfloat16)

    for h in range(width // HD):
        one_head(h)
        lanes = pl.ds(h * HD, HD)
        here = pl.ds(pl.multiple_of(me * width + h * HD, HD), HD)
        for g, (src, dst) in enumerate(grads):
            for i, (da, db) in enumerate(corners()):
                peer, to = corner(da, db)
                push(src.at[pl.ds(pl.multiple_of(peer * rows, rows), rows), lanes], dst.at[:, here], send_g.at[g, i, h], got_g.at[g, i, h], to)
            own = src.at[pl.ds(pl.multiple_of(me * rows, rows), rows), lanes]
            pltpu.make_async_copy(own, dst.at[:, here], place_g.at[g, h]).start()
    piece = dq.at[:, pl.ds(0, HD)]
    for h in range(width // HD):
        for g in range(3):
            await_bytes(piece, place_g.at[g, h])
            for i in range(3):
                await_bytes(piece, send_g.at[g, i, h])
                await_bytes(piece, got_g.at[g, i, h])
    for i in range(3):
        await_bytes(do.at[:, pl.ds(0, width)], send.at[i])
    norm_and_turn_back(dk, k_raw, k_gain, cosine, sine, dk_raw, k_gain_grad, turned)
    norm_and_turn_back(dq, q_raw, q_gain, cosine, sine, dq_raw, q_gain_grad, turned)


def attend_back(do, qh, kh, vh, logs, keep, q_raw, k_raw, q_gain, k_gain, cosine, sine, scale):
    heads = qh.shape[1] // HD
    vm, dma = pl.BlockSpec(memory_space=pltpu.VMEM), pltpu.SemaphoreType.DMA
    return pl.pallas_call(
        functools.partial(attend_back_kernel, scale),
        out_shape=[jax.ShapeDtypeStruct(do.shape, do.dtype)] * 3 + [jax.ShapeDtypeStruct((8, do.shape[1]), jnp.float32)] * 2,
        in_specs=[vm] * 12,
        out_specs=[vm] * 5,
        scratch_shapes=[pltpu.VMEM(qh.shape, qh.dtype)] * 4
        + [pltpu.VMEM(do.shape, do.dtype)] * 2
        + [pltpu.VMEM((32, do.shape[1]), jnp.float32)]
        + [dma((3,)), dma((3,)), dma, dma((3, 3, heads)), dma((3, 3, heads)), dma((3, heads))],
        compiler_params=pltpu.CompilerParams(collective_id=5, has_side_effects=True, vmem_limit_bytes=56 << 20),
        cost_estimate=pl.CostEstimate(flops=50_000_000_000, bytes_accessed=10_000_000, transcendentals=0),
        name="attend_back",
    )(do, qh, kh, vh, logs, keep, q_raw, k_raw, q_gain, k_gain, cosine, sine)


def norm_rows(values, gain):
    factor = lax.rsqrt(jnp.mean(values * values, axis=-1, keepdims=True) + EPSILON)
    return (values * factor * gain, factor)


def norm_back(grad, values, factor, gain):
    weighted = grad * gain
    inner = jnp.mean(weighted * values, axis=-1, keepdims=True)
    return (factor * weighted - values * factor**3 * inner, jnp.sum(grad * values * factor, axis=0))


def rotary_tables(positions, head_dim):
    half_dim = head_dim // 2
    frequency = jnp.exp(-math.log(ROPE_THETA) * jnp.arange(half_dim, dtype=jnp.float32) / half_dim)
    angles = positions.astype(jnp.float32)[:, None] * frequency[None, :]
    return (jnp.cos(angles), jnp.sin(angles))


def local(
    tokens, cotangent, lengths, expert_ids, query_weight, key_weight, value_weight, out_weight,
    router_weight, first_gain, second_gain, query_gain, key_gain, gate_weight, up_weight, down_weight,
):
    token_count = tokens.shape[1]
    model_width = tokens.shape[2]
    head_dim = HD
    top_count = expert_ids.shape[2]
    experts = router_weight.shape[1]
    local_experts = gate_weight.shape[0]
    ctx_size = lax.axis_size(CTX)
    sources = lax.axis_size(EXP)
    capacity = max(2, -(-(token_count * top_count * 9) // (experts * 8)))
    score_scale = 1.0 / math.sqrt(head_dim)
    seq_len = token_count * ctx_size

    inputs = tokens[0].astype(jnp.float32)
    length = lengths[0]
    positions = lax.axis_index(CTX) * token_count + jnp.arange(token_count, dtype=jnp.int32)
    row_valid = positions < length
    row_valid = row_valid.astype(jnp.float32)[:, None]
    key_valid = jnp.arange(seq_len, dtype=jnp.int32) < length
    grad_total_low = (cotangent[0].astype(jnp.float32) * row_valid).astype(jnp.bfloat16)
    grad_total = grad_total_low.astype(jnp.float32)

    rows_each = query_weight.shape[0]
    packed = jnp.concatenate(
        [g.reshape(-1) for g in (first_gain, second_gain, query_gain, key_gain)] + [router_weight.reshape(-1)]
    )
    small = jnp.pad(packed, (0, -packed.size % 2048)).reshape(-1, 128)
    ids_low = expert_ids[0].astype(jnp.bfloat16).reshape(-1, 128)
    gathered, (ids_all, g_all) = spread([query_weight, key_weight, value_weight, out_weight, small], [ids_low, grad_total_low])
    full_query, full_key, full_value, full_out = (w.reshape(model_width, -1) for w in gathered[:4])
    smalls = gathered[4].reshape(-1, small.size)
    gains = [smalls[:, i * rows_each : (i + 1) * rows_each].reshape(-1).astype(jnp.float32) for i in range(4)]
    gain_first, gain_second, gain_queries, gain_keys = gains
    full_router = smalls[:, 4 * rows_each : packed.size].reshape(model_width, experts)
    ids_all = ids_all.reshape(sources, token_count, top_count).astype(jnp.int32)
    full_value, gate_weight, up_weight = lax.optimization_barrier((full_value, gate_weight, up_weight))
    gate_all, up_all = (lax.all_gather(w, CTX, axis=2, tiled=True) for w in (gate_weight, up_weight))
    cosine, sine = rotary_tables(positions, head_dim)
    normed_one, factor_one = norm_rows(inputs, gain_first)
    normed_one_low = normed_one.astype(jnp.bfloat16)
    query_raw = matmul(normed_one_low, full_query)
    key_raw = matmul(normed_one_low, full_key)
    value_low = matmul(normed_one_low, full_value).astype(jnp.bfloat16)
    keep = key_valid.astype(jnp.float32)[None, :]
    turns = (jnp.concatenate([cosine, cosine], axis=1), jnp.concatenate([-sine, sine], axis=1))
    row = lambda g: g.reshape(1, model_width)
    shared = (row(gain_queries), row(gain_keys), *turns)
    attended_low, *saved = attend(query_raw, key_raw, value_low, *shared, keep, score_scale)
    flip = lambda v, axis: lax.ppermute(v, axis, [(0, 1), (1, 0)])
    hidden_state = inputs + matmul(attended_low, full_out)
    normed_two, factor_two = norm_rows(hidden_state, gain_second)
    normed_two_low = normed_two.astype(jnp.bfloat16)

    first_expert = lax.axis_index(EXP) * local_experts
    own_experts = first_expert + jnp.arange(local_experts, dtype=jnp.int32)
    mask = jnp.any(ids_all[:, None, :, :] == own_experts[None, :, None, None], axis=-1)
    before = (jnp.arange(token_count)[:, None] < jnp.arange(token_count)[None, :]).astype(jnp.bfloat16)
    ranks = jnp.einsum("seu,ut->set", mask.astype(jnp.bfloat16), before, preferred_element_type=jnp.float32)
    slots = jnp.arange(capacity, dtype=jnp.float32)
    hot = (mask[:, :, None, :] & (ranks[:, :, None, :] == slots[None, None, :, None])).astype(jnp.bfloat16)
    n2_all, x, de, row_gate, probs = dispatch(normed_two_low, full_router.T, hot, g_all)
    n2_all = n2_all.reshape(sources, token_count, model_width)
    probs = probs.transpose(0, 2, 1).reshape(-1, experts)
    hot32 = hot.astype(jnp.float32)
    x, gate_all, down_weight = lax.optimization_barrier((x, gate_all, down_weight))
    down_b, down_a = flip(down_weight, "cb"), flip(down_weight, "ca")
    first_half = local_experts // 2
    down_corner = [flip(down_b[:first_half], "ca"), flip(down_a[first_half:], "cb")]
    ee = lambda eq, a, b: jnp.einsum(eq, a, b, preferred_element_type=jnp.float32)
    gp = ee("escd,edf->escf", x, gate_all)
    up = ee("escd,edf->escf", x, up_all)
    sig = jax.nn.sigmoid(gp)
    hid = (gp * sig * up).astype(jnp.bfloat16)
    down_part = ee("escf,escd->efd", hid, de).astype(jnp.bfloat16)
    *down_corner, down_part = lax.optimization_barrier((*down_corner, down_part))
    at_a, at_b = lax.axis_index("ca"), lax.axis_index("cb")
    units = down_weight.shape[1]
    down_all = jnp.zeros((local_experts, ctx_size * units, model_width), jnp.bfloat16)
    for piece, p, q in (
        (down_weight, at_a, at_b), (down_b, at_a, 1 - at_b), (down_a, 1 - at_a, at_b), (jnp.concatenate(down_corner), 1 - at_a, 1 - at_b)
    ):
        down_all = lax.dynamic_update_slice_in_dim(down_all, piece, (2 * p + q) * units, 1)
    eo = ee("escf,efd->escd", hid, down_all).astype(jnp.bfloat16)
    gained = jnp.sum(de.astype(jnp.float32) * eo.astype(jnp.float32), axis=-1)
    mixed_rows = (row_gate * eo.astype(jnp.float32)).astype(jnp.bfloat16)
    mixed_part = jnp.einsum("sect,escd->std", hot, mixed_rows, preferred_element_type=jnp.float32)
    mixed_part = mixed_part.astype(jnp.bfloat16)

    dhid = ee("escd,efd->escf", de, down_all)
    dgp = (dhid * up * sig * (1.0 + gp * (1.0 - sig))).astype(jnp.bfloat16)
    dup = (dhid * gp * sig).astype(jnp.bfloat16)
    gate_part = ee("escd,escf->edf", x, dgp)
    up_part = ee("escd,escf->edf", x, dup)
    parts = [v.astype(jnp.bfloat16) for v in (down_part, gate_part, up_part)]
    dgp, dup, *_ = lax.optimization_barrier((dgp, dup, *parts))
    rs_ctx = lambda v, a: lax.psum_scatter(v, CTX, scatter_dimension=a, tiled=True)
    down_grad, gate_grad, up_grad = rs_ctx(parts[0], 1), rs_ctx(parts[1], 2), rs_ctx(parts[2], 2)
    dpair = (ee("escf,edf->escd", dgp, gate_all) + ee("escf,edf->escd", dup, up_all)).astype(jnp.bfloat16)

    gained = jnp.sum(hot32 * gained.transpose(1, 0, 2)[..., None], axis=2)
    gained = gained.transpose(0, 2, 1).reshape(-1, local_experts)
    onto = (jnp.arange(experts)[None, :] == own_experts[:, None]).astype(jnp.float32)
    weighed = jnp.sum(gained[:, :, None] * onto[None], axis=1)
    dlogit_low = (weighed - probs * jnp.sum(gained, axis=-1, keepdims=True)).astype(jnp.bfloat16)
    router_part = transposed_times(n2_all.reshape(-1, model_width), dlogit_low)
    dn2_part = jnp.einsum("sect,escd->std", hot, dpair, preferred_element_type=jnp.float32).reshape(-1, model_width)
    dn2_part = dn2_part + times_transposed(dlogit_low, full_router)
    dn2_part = dn2_part.astype(jnp.bfloat16).reshape(sources, token_count, model_width)
    dn2_part, down_grad = lax.optimization_barrier((dn2_part, down_grad))
    dn2 = give_back(dn2_part)
    dn2, gate_grad = lax.optimization_barrier((dn2, gate_grad))
    dn2, mixed_part = lax.optimization_barrier((dn2, mixed_part))
    mixed = lax.psum_scatter(mixed_part.reshape(-1, model_width), EXP, scatter_dimension=0, tiled=True)

    dh_norm, gain_second_part = norm_back(dn2, hidden_state, factor_two, gain_second)
    grad_hidden = grad_total + dh_norm
    dh_low = grad_hidden.astype(jnp.bfloat16)
    out_part = transposed_times(attended_low, dh_low)
    d_att = times_transposed(dh_low, full_out).astype(jnp.bfloat16)
    dq_low, dk_low, dv_low, *gain_parts = attend_back(d_att, *saved, keep, query_raw, key_raw, *shared, score_scale)
    dv_low, up_grad = lax.optimization_barrier((dv_low, up_grad))
    gain_queries_part, gain_keys_part = (jnp.sum(g, axis=0) for g in gain_parts)
    core = lax.axis_index("core")
    swap = lambda v: lax.ppermute(v, "core", [(0, 1), (1, 0)])

    def columns_of_core(v):
        width = model_width // 2
        mine = lax.dynamic_slice_in_dim(v, core * width, width, 1)
        other = lax.dynamic_slice_in_dim(v, (1 - core) * width, width, 1)
        return jnp.concatenate([mine, swap(other)], axis=0)

    both = lambda v: jnp.concatenate([v, swap(v)], axis=0)
    n1_both, att_both = both(normed_one_low), both(attended_low)
    parts = [
        transposed_times(l, columns_of_core(r)).astype(jnp.bfloat16)
        for l, r in ((att_both, dh_low), (n1_both, dq_low), (n1_both, dk_low), (n1_both, dv_low))
    ]
    split = lambda v: v.reshape(ctx_size * sources // 2, 2, -1)
    small_parts = jnp.concatenate(
        [split(v) for v in (gain_second_part, gain_queries_part, gain_keys_part, router_part)], axis=2
    )
    small_parts = jnp.pad(small_parts, ((0, 0), (0, 0), (0, -small_parts.shape[2] % 2048)))
    small_parts = lax.dynamic_index_in_dim(small_parts, core, 1, False) + swap(lax.dynamic_index_in_dim(small_parts, 1 - core, 1, False))
    small_parts, mixed = lax.optimization_barrier((small_parts, mixed))
    weight_grads, small_grads, input_grad, gain_first_sums = collect(
        parts, small_parts.reshape(ctx_size * sources // 2, -1, 128), (dq_low, dk_low, dv_low),
        (full_query, full_key, full_value), tokens[0], row(gain_first), grad_hidden,
    )
    weight_grads, mixed, gate_grad, up_grad, down_grad = lax.optimization_barrier(
        (list(weight_grads), mixed, gate_grad, up_grad, down_grad)
    )
    layer_out = (row_valid * (hidden_state + mixed.astype(jnp.float32))).astype(jnp.bfloat16)
    gate_grad, up_grad, down_grad = (v.astype(jnp.float32) for v in (gate_grad, up_grad, down_grad))
    weight_grads = list(weight_grads[1:]) + [weight_grads[0]]
    small_grads = small_grads.reshape(-1)
    gain_grads = [lax.dynamic_slice_in_dim(jnp.sum(gain_first_sums, axis=0), lax.axis_index(ALL) * rows_each, rows_each)]
    gain_grads += [small_grads[i * rows_each : (i + 1) * rows_each] for i in range(3)]
    router_grad = small_grads[3 * rows_each : packed.size - rows_each].reshape(rows_each, experts)
    return (layer_out[None], input_grad[None], *weight_grads, router_grad, *gain_grads, gate_grad, up_grad, down_grad)


def solution(mesh):
    ctx, exp = mesh.devices.shape
    fine = Mesh(mesh.devices.reshape(2, ctx // 2, exp // 2, 2), ("ca", "cb", "ring", "core"))
    rows = P(EXP, CTX, None)
    flat2, flat1 = P(ALL, None), P(ALL)
    placed = (rows, rows, P(EXP), rows) + (flat2,) * 5 + (flat1,) * 4 + (P(EXP, None, CTX),) * 2 + (P(EXP, CTX, None),)
    outs = (rows, rows) + (flat2,) * 5 + (flat1,) * 4 + (P(EXP, None, CTX),) * 2 + (P(EXP, CTX, None),)
    return jax.shard_map(local, mesh=fine, in_specs=placed, out_specs=outs, check_vma=False)
```

```python
import functools
import math

import jax
import jax.numpy as jnp
from jax import lax
from jax.experimental import pallas as pl
from jax.experimental.pallas import tpu as pltpu
from jax.sharding import Mesh
from jax.sharding import PartitionSpec as P

HEADS = 16
HD = 128
EPSILON = 1e-06
ROPE_THETA = 10000.0
NEG_FILL = -1e30

CTX = ("ca", "cb")
EXP = ("ring", "core")
ALL = CTX + EXP


MESH = pl.DeviceIdType.MESH


def turn(name, by):
    size = lax.axis_size(name)
    return lax.rem(lax.axis_index(name) + by, size)


def await_bytes(ref, sem):
    pltpu.make_async_copy(ref, ref, sem).wait()


def greet(peers):
    barrier = pltpu.get_barrier_semaphore()
    for peer in peers:
        pl.semaphore_signal(barrier, inc=1, device_id=peer, device_id_type=MESH)
    pl.semaphore_wait(barrier, len(peers))


def push(src, dst, ssem, rsem, to):
    pltpu.make_async_remote_copy(
        src_ref=src, dst_ref=dst, send_sem=ssem, recv_sem=rsem, device_id=to, device_id_type=MESH
    ).start()


RING, SIDE_B, SIDE_A, FIRST, SECOND, CORE_OWN, CORE_B, CORE_A, CORE_FIRST, CORE_SECOND = range(10)


def along(step):
    ring, r = lax.axis_size("ring"), lax.axis_index("ring")
    to_next, to_last = {"ring": turn("ring", 1)}, {"ring": turn("ring", ring - 1)}
    return (
        ((r + 1 < ring) & (r >= step), r >= step + 1, lax.rem(r + ring - step, ring), lax.rem(r + ring - 1 - step, ring), to_next, 0),
        ((r >= 1) & (r + step < ring), r + 1 + step < ring, lax.rem(r + step, ring), lax.rem(r + 1 + step, ring), to_last, 1),
    )


def send_along(step, own, block_of, send, got):
    for sent, _, block, _, to, side in along(step):

        @pl.when(sent)
        def _(block=block, to=to, side=side):
            src = own if isinstance(step, int) and step == 0 else block_of(block)
            push(src, block_of(block), send.at[side, step], got.at[side, step], to)


def take_along(step, block_of, got, then):
    for _, comes, _, block, _, side in along(step):

        @pl.when(comes)
        def _(block=block, side=side):
            await_bytes(block_of(block), got.at[side, step])

    for _, comes, _, block, _, side in along(step):

        @pl.when(comes)
        def _(block=block):
            then(block)


def sent_along(own, send):
    ring = lax.axis_size("ring")
    for step in range(ring - 1):
        for sent, _, _, _, _, side in along(step):

            @pl.when(sent)
            def _(side=side):
                await_bytes(own, send.at[side, step])


def spread_kernel(count, tables, *refs):
    ring = lax.axis_size("ring")
    ins, refs = refs[: count + tables], refs[count + tables :]
    outs, sems = refs[: count + tables], refs[count + tables :]
    send, send_ring, got_ring, got_b, got_a, got, place, core_sem = sems
    a, b, r, c = (lax.axis_index(n) for n in ALL)
    na, nb, nc = turn("ca", 1), turn("cb", 1), turn("core", 1)
    to_a, to_b, to_core = {"ca": na}, {"cb": nb}, {"core": nc}
    greet([to_a, to_b, to_core] + [{"ring": turn("ring", k)} for k in range(1, ring)])

    def half(ref, which):
        rows, cols = ref.shape[-2:]
        if rows * 8 < cols:
            return ref.at[..., pl.ds(which * (cols // 2), cols // 2)]
        return ref.at[..., pl.ds(which * (rows // 2), rows // 2), :]

    def halves(ref, which):
        rows, cols = ref.shape[-2:]
        if rows * 8 < cols:
            return ref.at[:, :, pl.ds(which * (cols // 2), cols // 2)]
        return ref.at[:, pl.ds(which * (rows // 2), rows // 2), :]

    def place_of(w):
        return (lambda at: outs[w].at[a, b, at, c]) if w < count else (lambda at: outs[w].at[at, c])

    for w in range(count + tables):
        pltpu.make_async_copy(ins[w], place_of(w)(r), place.at[w]).start()
    for w in reversed(range(count)):
        send_along(0, ins[w], place_of(w), send_ring.at[w], got_ring.at[w])
        here = place_of(w)(r)
        push(ins[w], here, send.at[w, SIDE_B], got_b.at[w, r], to_b)
        push(ins[w], here, send.at[w, SIDE_A], got_a.at[w, r], to_a)
        push(ins[w], here, send.at[w, CORE_OWN], got.at[w, CORE_OWN], to_core)
    for t in range(tables):
        push(ins[count + t], place_of(count + t)(r), core_sem.at[t, 0], core_sem.at[t, 1], to_core)

    def sides(w):
        for step in range(ring - 1):

            def on(at):
                block = place_of(w)(at)
                push(block, block, send.at[w, SIDE_B], got_b.at[w, at], to_b)
                push(block, block, send.at[w, SIDE_A], got_a.at[w, at], to_a)
                push(block, block, send.at[w, CORE_OWN], got.at[w, CORE_OWN], to_core)

            take_along(step, place_of(w), got_ring.at[w], on)
            if step + 1 < ring - 1:
                send_along(step + 1, ins[w], place_of(w), send_ring.at[w], got_ring.at[w])

    def diagonal(w):
        out = outs[w]

        def one(k, carry):
            at = lax.rem(r + ring - k, ring)
            block = out.at[a, nb, at, c]
            await_bytes(block, got_b.at[w, at])
            push(half(block, 0), half(block, 0), send.at[w, FIRST], got.at[w, FIRST], to_a)
            push(block, block, send.at[w, CORE_B], got.at[w, CORE_B], to_core)
            block = out.at[na, b, at, c]
            await_bytes(block, got_a.at[w, at])
            push(half(block, 1), half(block, 1), send.at[w, SECOND], got.at[w, SECOND], to_b)
            push(block, block, send.at[w, CORE_A], got.at[w, CORE_A], to_core)
            return carry

        lax.fori_loop(0, ring, one, 0)

    def last(w):
        block = outs[w].at[na, nb, :, c]
        for which, kind, core_kind in ((0, FIRST, CORE_FIRST), (1, SECOND, CORE_SECOND)):
            part = halves(block, which)
            await_bytes(part, got.at[w, kind])
            push(part, part, send.at[w, core_kind], got.at[w, core_kind], to_core)

    def table_step(t, step):
        w = count + t

        def on(at):
            push(place_of(w)(at), place_of(w)(at), core_sem.at[t, 0], core_sem.at[t, 1], to_core)

        if step >= 0:
            take_along(step, place_of(w), got_ring.at[w], on)
        if step + 1 < ring - 1:
            send_along(step + 1, ins[w], place_of(w), send_ring.at[w], got_ring.at[w])

    order = list(reversed(range(count)))
    for step in range(count + 2):
        if step < count:
            sides(order[step])
        if step >= count - 1:
            for t in range(tables):
                table_step(t, step - count)
        if 0 <= step - 1 < count:
            diagonal(order[step - 1])
        if 0 <= step - 2 < count:
            last(order[step - 2])
    for step in range(2, ring - 1):
        for t in range(tables):
            table_step(t, step)

    for w in range(count):
        out = outs[w]
        mine = lambda p, q: out.at[p, q, :, c]
        await_bytes(ins[w], place.at[w])
        sent_along(ins[w], send_ring.at[w])
        for kind in (SIDE_B, SIDE_A, CORE_OWN, CORE_B, CORE_A):
            await_bytes(mine(a, b), send.at[w, kind])
        for which, kind in ((0, FIRST), (1, SECOND), (0, CORE_FIRST), (1, CORE_SECOND)):
            await_bytes(halves(mine(a, b), which), send.at[w, kind])
        for kind, p, q in ((CORE_OWN, a, b), (CORE_B, a, nb), (CORE_A, na, b)):
            await_bytes(out.at[p, q, :, nc], got.at[w, kind])
        for which, kind in ((0, CORE_FIRST), (1, CORE_SECOND)):
            await_bytes(halves(out.at[na, nb, :, nc], which), got.at[w, kind])
    for t in range(tables):
        w = count + t
        await_bytes(ins[w], place.at[w])
        sent_along(ins[w], send_ring.at[w])
        await_bytes(outs[w].at[:, c], core_sem.at[t, 0])
        await_bytes(outs[w].at[:, nc], core_sem.at[t, 1])


def spread(shards, tables):
    count, more, ring = len(shards), len(tables), lax.axis_size("ring")
    square = (lax.axis_size("ca"), lax.axis_size("cb"), ring, 2)
    dma = pltpu.SemaphoreType.DMA
    outs = pl.pallas_call(
        functools.partial(spread_kernel, count, more),
        out_shape=[jax.ShapeDtypeStruct(square + s.shape, s.dtype) for s in shards]
        + [jax.ShapeDtypeStruct((ring, 2) + t.shape, t.dtype) for t in tables],
        in_specs=[pl.BlockSpec(memory_space=pltpu.VMEM)] * (count + more),
        out_specs=[pl.BlockSpec(memory_space=pl.ANY)] * (count + more),
        scratch_shapes=[
            dma((count, 10)), dma((count + more, 2, ring)), dma((count + more, 2, ring)), dma((count, ring)), dma((count, ring)),
            dma((count, 10)), dma((count + more,)), dma((more, 2)),
        ],
        compiler_params=pltpu.CompilerParams(collective_id=0, has_side_effects=True),
        cost_estimate=pl.CostEstimate(flops=150_000_000_000, bytes_accessed=300_000_000, transcendentals=0),
        name="spread",
    )(*shards, *tables)
    return outs[:count], outs[count:]


def collect_kernel(count, *refs):
    ring = lax.axis_size("ring")
    parts, refs = refs[:count], refs[count:]
    grads, matrices, (x, gain, passed), refs = refs[:3], refs[3:6], refs[6:9], refs[9:]
    outs, (input_grad, gain_out), refs = refs[:count], refs[count : count + 2], refs[count + 2 :]
    scratch, refs = refs[: 9 * count], refs[9 * count :]
    send, got, ring_send, ring_got, load, chunks, dn1, sums, arrived, ring_arrived, fetch, gain_send, gain_got = refs
    a, b, r, c = (lax.axis_index(n) for n in ALL)
    na, nb, nc = turn("ca", 1), turn("cb", 1), turn("core", 1)
    to_a, to_b, to_core = {"ca": na}, {"cb": nb}, {"core": nc}
    bufs = [scratch[9 * w : 9 * w + 9] for w in range(count)]
    greet([to_a, to_b, to_core] + [{"ring": turn("ring", k)} for k in range(1, ring)])

    def chunk(i, slot, w):
        rows = chunks.shape[2]
        return pltpu.make_async_copy(
            matrices[w].at[pl.ds(pl.multiple_of(i * rows, rows), rows), :], chunks.at[slot, w], fetch.at[slot, w]
        )

    steps, chunk_rows = matrices[0].shape[0] // chunks.shape[2], chunks.shape[2]

    def input_part(begin, end):
        rows = chunk_rows

        def one(i, carry):
            slot = lax.rem(i, 2)

            @pl.when(i + 1 < steps)
            def _():
                for w in range(3):
                    chunk(i + 1, 1 - slot, w).start()

            value = jnp.zeros((x.shape[0], rows), jnp.float32)
            for w in range(3):
                chunk(i, slot, w).wait()
                value = value + times_transposed(grads[w][...], chunks[slot, w])
            dn1[:, pl.ds(pl.multiple_of(i * rows, rows), rows)] = value
            return carry

        lax.fori_loop(begin, end, one, 0)

    def input_end():
        tile = 32
        sums[0] = jnp.zeros(sums.shape[1:], jnp.float32)

        def back(i, carry):
            at = pl.ds(pl.multiple_of(i * tile, tile), tile)
            v, grad = x[at, :].astype(jnp.float32), dn1[at, :]
            factor = lax.rsqrt(jnp.mean(v * v, axis=-1, keepdims=True) + EPSILON)
            weighted = grad * gain[...]
            inner = jnp.mean(weighted * v, axis=-1, keepdims=True)
            total = passed[at, :] + factor * weighted - v * (factor * factor * factor * inner)
            input_grad[at, :] = total.astype(input_grad.dtype)
            gained = grad * v * factor
            sums[0] += sum(gained[k : k + 8] for k in range(0, tile, 8))
            return carry

        lax.fori_loop(0, x.shape[0] // tile, back, 0)
        push(sums.at[0], arrived.at[0], gain_send.at[0], gain_got.at[0], to_a)

    def gain_stage(stage):
        if stage < 3:
            await_bytes(arrived.at[stage], gain_got.at[stage])
            sums[stage + 1] = sums[stage] + arrived[stage]
            if stage < 2:
                push(sums.at[stage + 1], arrived.at[stage + 1], gain_send.at[stage + 1], gain_got.at[stage + 1], (to_b, to_core)[stage])
            else:
                for k in range(1, ring):
                    push(sums.at[3], ring_arrived.at[k - 1], gain_send.at[2 + k], gain_got.at[2 + k], {"ring": turn("ring", k)})
        else:
            total = sums[3]
            for k in range(1, ring):
                await_bytes(ring_arrived.at[k - 1], gain_got.at[2 + k])
                total = total + ring_arrived[k - 1]
            gain_out[...] = total
            for k in range(3 + ring - 1):
                await_bytes(sums.at[0], gain_send.at[k])

    def half(ref, which):
        rows, cols = ref.shape[-2:]
        lead = (slice(None),) * (len(ref.shape) - 2)
        if cols > 128:
            return ref.at[(*lead, slice(None), pl.ds(which * (cols // 2), cols // 2))]
        return ref.at[(*lead, pl.ds(which * (rows // 2), rows // 2), slice(None))]

    def loads(w):
        own_a, own_b = bufs[w][0:2]
        return (
            pltpu.make_async_copy(half(parts[w].at[a], 0), own_a, load.at[w, 0]),
            pltpu.make_async_copy(half(parts[w].at[:, b], 1), own_b, load.at[w, 1]),
        )

    def first(w):
        for copy in loads(w):
            copy.start()
        in_a, in_b = bufs[w][2:4]
        push(half(parts[w].at[na], 0), in_a, send.at[w, 0], got.at[w, 0], to_a)
        push(half(parts[w].at[:, nb], 1), in_b, send.at[w, 1], got.at[w, 1], to_b)

    def add(into, other):
        def one(k, carry):
            into[:, k] = (into[:, k].astype(jnp.float32) + other[:, k].astype(jnp.float32)).astype(into.dtype)
            return carry

        lax.fori_loop(0, ring, one, 0)

    def second(w):
        own_a, own_b, in_a, in_b, in_a2, in_b2 = bufs[w][:6]
        for copy in loads(w):
            copy.wait()
        await_bytes(in_a, got.at[w, 0])
        add(own_a, in_a)
        push(own_a.at[nb], in_a2, send.at[w, 2], got.at[w, 2], to_b)
        await_bytes(in_b, got.at[w, 1])
        add(own_b, in_b)
        push(own_b.at[na], in_b2, send.at[w, 3], got.at[w, 3], to_a)

    def third(w):
        own_a, own_b, _, _, in_a2, in_b2, total, in_ring = bufs[w][:8]
        await_bytes(in_a2, got.at[w, 2])
        await_bytes(in_b2, got.at[w, 3])

        def one(k, carry):
            sums = [
                own[own_at, k].astype(jnp.float32) + more[k].astype(jnp.float32)
                for own, own_at, more in ((own_a, b, in_a2), (own_b, a, in_b2))
            ]
            for which in range(2):
                half(total.at[k], which)[...] = sums[which].astype(total.dtype)
            return carry

        lax.fori_loop(0, ring, one, 0)
        for k in range(1, ring):
            at = turn("ring", k)
            push(total.at[at], in_ring.at[k - 1], ring_send.at[w, k - 1], ring_got.at[w, k - 1], {"ring": at})

    def fourth(w):
        total, in_ring, final = bufs[w][6:9]
        for k in range(1, ring):
            await_bytes(in_ring.at[k - 1], ring_got.at[w, k - 1])
        if final.shape[0] == 2:
            rows = final.shape[1]
            for core in range(2):
                at = pl.ds(core * rows, rows)
                value = total[r, at, :].astype(jnp.float32)
                for k in range(ring - 1):
                    value = value + in_ring[k, at, :].astype(jnp.float32)
                final[core] = value
            cols = final.shape[2]
            there = outs[w].at[:, pl.ds(pl.multiple_of(c * cols, cols), cols)]
            push(final.at[nc], there, send.at[w, 4], got.at[w, 4], to_core)
            pltpu.make_async_copy(final.at[c], there, load.at[w, 2]).start()
        else:
            value = total[r].astype(jnp.float32)
            for k in range(ring - 1):
                value = value + in_ring[k].astype(jnp.float32)
            outs[w][...] = value

    def finish(w):
        own_a, own_b, in_a, in_b, in_a2, in_b2, total, in_ring, final = bufs[w]
        await_bytes(in_a, send.at[w, 0])
        await_bytes(in_b, send.at[w, 1])
        await_bytes(in_a2, send.at[w, 2])
        await_bytes(in_b2, send.at[w, 3])
        for k in range(1, ring):
            await_bytes(in_ring.at[k - 1], ring_send.at[w, k - 1])
        if final.shape[0] == 2:
            await_bytes(final.at[0], send.at[w, 4])
            await_bytes(final.at[0], got.at[w, 4])
            await_bytes(final.at[0], load.at[w, 2])

    for w in range(3):
        chunk(0, 0, w).start()
    first(0)
    for step in range(max(count + 3, 9)):
        if step + 1 < count:
            first(step + 1)
        if step < count:
            second(step)
        if 0 <= step - 1 < count:
            third(step - 1)
        if 0 <= step - 2 < count:
            fourth(step - 2)
        if 1 <= step < 5:
            input_part((step - 1) * steps // 4, step * steps // 4)
        if step == 4:
            input_end()
        if step > 4:
            gain_stage(step - 5)
    for w in range(count):
        finish(w)


def collect(parts, small, grads, matrices, x, gain, passed):
    count, ring = len(parts) + 1, lax.axis_size("ring")
    chips = lax.axis_size("ca") * lax.axis_size("cb") * ring
    square = (lax.axis_size("ca"), lax.axis_size("cb"), ring)
    views = [p.reshape(square + (p.shape[0] // chips, p.shape[1])) for p in parts]
    views = [small.reshape(square + small.shape[1:])] + views
    shapes, scratch = [], []
    for v in views:
        rows, cols = v.shape[3:]
        piece = (rows, cols // 2) if cols > 128 else (rows // 2, cols)
        big = cols > 128
        vm = lambda *shape: pltpu.VMEM(shape, v.dtype)
        scratch += [vm(2, ring, *piece)] * 4 + [vm(ring, *piece)] * 2
        scratch += [vm(ring, rows, cols), vm(ring - 1, rows, cols)]
        scratch += [pltpu.VMEM((2, rows // 2, cols) if big else (1, 8, 128), jnp.float32)]
        shapes.append(jax.ShapeDtypeStruct((rows // 2, 2 * cols) if big else (rows, cols), jnp.float32))
    dma = pltpu.SemaphoreType.DMA
    vm, anywhere = pl.BlockSpec(memory_space=pltpu.VMEM), pl.BlockSpec(memory_space=pl.ANY)
    wide = (8, gain.shape[1])
    f32 = lambda *shape: pltpu.VMEM(shape, jnp.float32)
    outs = pl.pallas_call(
        functools.partial(collect_kernel, count),
        out_shape=shapes + [jax.ShapeDtypeStruct(x.shape, x.dtype), jax.ShapeDtypeStruct(wide, jnp.float32)],
        in_specs=[anywhere] * count + [vm] * 3 + [anywhere] * 3 + [vm] * 3,
        out_specs=[vm] * (count + 2),
        scratch_shapes=scratch
        + [dma((count, 5)), dma((count, 5)), dma((count, ring - 1)), dma((count, ring - 1)), dma((count, 3))]
        + [pltpu.VMEM((2, 3, 256, x.shape[1]), x.dtype), f32(*x.shape), f32(4, *wide), f32(3, *wide), f32(ring - 1, *wide)]
        + [dma((2, 3)), dma((2 + ring,)), dma((2 + ring,))],
        compiler_params=pltpu.CompilerParams(collective_id=1, has_side_effects=True, vmem_limit_bytes=62 << 20),
        cost_estimate=pl.CostEstimate(flops=160_000_000_000, bytes_accessed=320_000_000, transcendentals=0),
        name="collect",
    )(*views, *grads, *matrices, x, gain, passed)
    return outs[1:count], outs[0], outs[count], outs[count + 1]


def dispatch_kernel(
    rows, router, hot, g_all, out, picked, grads, gates, probs,
    rows_in, g_in, picked_low, grads_low, load, store, ring_send, ring_got, place, core_send, core_got,
):
    ring = lax.axis_size("ring")
    r, c, nc = lax.axis_index("ring"), lax.axis_index("core"), turn("core", 1)
    to_core, experts = {"core": nc}, hot.shape[1]
    greet([to_core] + [{"ring": turn("ring", k)} for k in range(1, ring)])
    block_of = lambda at: out.at[at, c]

    own = pltpu.make_async_copy(rows, block_of(r), place)
    own.start()
    push(rows, block_of(r), core_send, core_got.at[r], to_core)
    own.wait()
    send_along(0, block_of(r), block_of, ring_send, ring_got)
    first = (r * 2 + c) * experts
    width = rows.shape[1]
    cols = min(512, width)

    def pick(at, core):
        source = at * 2 + core
        copies = (
            pltpu.make_async_copy(out.at[at, core], rows_in, load.at[0]),
            pltpu.make_async_copy(g_all.at[at, core], g_in, load.at[1]),
        )
        for copy in copies:
            copy.start()
        copies[0].wait()
        logits = times_transposed(router[...], rows_in[...])
        likely = jnp.exp(logits - jnp.max(logits, axis=0, keepdims=True))
        probs[source] = likely / jnp.sum(likely, axis=0, keepdims=True)
        copies[1].wait()
        for e in range(experts):
            own_probs = probs[source, pl.ds(first + e, 1), :]
            gate = jnp.sum(hot[source, e].astype(jnp.float32) * own_probs, axis=-1, keepdims=True)
            gates[e, source] = gate

            def part(i, carry):
                lanes = pl.ds(pl.multiple_of(i * cols, cols), cols)
                chosen = hot[source, e]
                picked_low[e, :, lanes] = matmul(chosen, rows_in[:, lanes]).astype(picked_low.dtype)
                grads_low[e, :, lanes] = (matmul(chosen, g_in[:, lanes]) * gate).astype(grads_low.dtype)
                return carry

            lax.fori_loop(0, width // cols, part, 0)
        stores = (
            pltpu.make_async_copy(picked_low, picked.at[:, source], store.at[0]),
            pltpu.make_async_copy(grads_low, grads.at[:, source], store.at[1]),
        )
        for copy in stores:
            copy.start()
        for copy in stores:
            copy.wait()

    pick(r, c)
    await_bytes(out.at[r, nc], core_got.at[r])
    pick(r, nc)

    def step_on(step, carry):
        take_along(step, block_of, ring_got, lambda at: None)

        @pl.when(step + 1 < ring - 1)
        def _():
            send_along(step + 1, None, block_of, ring_send, ring_got)

        for _, comes, _, block, _, _ in along(step):

            @pl.when(comes)
            def _(block=block):
                push(block_of(block), block_of(block), core_send, core_got.at[block], to_core)

        def four(k, carry):
            side, other = k // 2, lax.rem(k, 2)
            (_, comes0, _, block0, _, _), (_, comes1, _, block1, _, _) = along(step)
            block = jnp.where(side == 0, block0, block1)
            comes = ((side == 0) & comes0) | ((side == 1) & comes1)
            core = lax.rem(c + other, 2)

            @pl.when(comes & (other == 1))
            def _():
                await_bytes(out.at[block, nc], core_got.at[block])

            @pl.when(comes)
            def _():
                pick(block, core)

            return carry

        lax.fori_loop(0, 4, four, 0)
        return carry

    lax.fori_loop(0, ring - 1, step_on, 0)
    sent_along(rows, ring_send)
    await_bytes(out.at[:, c], core_send)


def dispatch(rows, router, hot, g_all):
    ring, dma = lax.axis_size("ring"), pltpu.SemaphoreType.DMA
    sources, experts, slots, count = hot.shape
    width = rows.shape[1]
    low = lambda *shape: jax.ShapeDtypeStruct(shape, rows.dtype)
    f32 = lambda *shape: jax.ShapeDtypeStruct(shape, jnp.float32)
    vm, anywhere = pl.BlockSpec(memory_space=pltpu.VMEM), pl.BlockSpec(memory_space=pl.ANY)
    block = pltpu.VMEM((experts, slots, width), rows.dtype)
    chosen = (experts, sources, slots, width)
    return pl.pallas_call(
        dispatch_kernel,
        out_shape=[
            low(ring, 2, count, width), low(*chosen), low(*chosen), f32(experts, sources, slots, 1),
            f32(sources, router.shape[0], count),
        ],
        in_specs=[vm, vm, vm, anywhere],
        out_specs=[anywhere, anywhere, anywhere, vm, vm],
        scratch_shapes=[pltpu.VMEM(rows.shape, rows.dtype)] * 2
        + [block, block]
        + [dma((2,)), dma((2,)), dma((2, ring)), dma((2, ring)), dma, dma, dma((ring,))],
        compiler_params=pltpu.CompilerParams(collective_id=2, has_side_effects=True, vmem_limit_bytes=56 << 20),
        cost_estimate=pl.CostEstimate(flops=1_000_000, bytes_accessed=10_000, transcendentals=0),
        name="dispatch",
    )(rows, router, hot, g_all)


def give_back_kernel(
    hot, logit, logit_turned, router, pairs, mixed, n2, out, mixed_out, router_part,
    sums, chain_in, to_core, pair_in, mixed_in, mixed_low, n2_in,
    load, core_send, core_got, chain_send, chain_got, load_more, store,
):
    ring, pieces, rows, width = sums.shape
    sources, experts = hot.shape[:2]
    r, c, nc = lax.axis_index("ring"), lax.axis_index("core"), turn("core", 1)
    to_next, to_last = {"ring": turn("ring", 1)}, {"ring": turn("ring", ring - 1)}
    greet([{"core": nc}] + [{"ring": turn("ring", k)} for k in range(1, ring)])
    cols, tile = min(512, width), 32

    def whose(i):
        return (1 - i % 2) * (ring - 1 - i // 2) + (i % 2) * (i // 2)

    def fetch(i, j):
        return pltpu.make_async_copy(pairs.at[:, whose(i) * 2 + (nc, c)[j]], pair_in.at[j], load.at[j])

    def put_back(source, ref, lanes):
        return sum(matmul(hot[source, e], ref[e, :, lanes]) for e in range(experts))

    def block(source, j, into, more):
        def part(k, carry):
            lanes = pl.ds(pl.multiple_of(k * cols, cols), cols)
            value = put_back(source, pair_in.at[j], lanes) + matmul(logit[source], router[:, lanes])
            for piece in range(pieces):
                got = value[piece * rows : (piece + 1) * rows]
                if more is not None:
                    got = got + more[piece, :, lanes].astype(jnp.float32)
                into[piece, :, lanes] = got.astype(into.dtype)
            return carry

        lax.fori_loop(0, width // cols, part, 0)

    def fetch_beside(source):
        at = lax.rem(source, 2)
        return (
            pltpu.make_async_copy(mixed.at[:, source], mixed_in.at[at], load_more.at[at, 0]),
            pltpu.make_async_copy(n2.at[source], n2_in.at[at], load_more.at[at, 1]),
        )

    def beside(source):
        at = lax.rem(source, 2)

        @pl.when(source + 1 < sources)
        def _():
            for copy in fetch_beside(source + 1):
                copy.start()

        for copy in fetch_beside(source):
            copy.wait()

        @pl.when(source > 0)
        def _():
            await_bytes(mixed_low, store)

        def part(k, carry):
            lanes = pl.ds(pl.multiple_of(k * cols, cols), cols)
            mixed_low[:, lanes] = put_back(source, mixed_in.at[at], lanes).astype(mixed_low.dtype)
            router_part[:, lanes] += matmul(logit_turned[source], n2_in[at, :, lanes])
            return carry

        lax.fori_loop(0, width // cols, part, 0)
        pltpu.make_async_copy(mixed_low, mixed_out.at[source], store).start()

    def slot(side, d, at):
        return d if side == 0 else jnp.where(d == at, ring, d)

    def pass_on(side, step, d, piece, to):
        there = chain_in.at[slot(side, d, r - 1), piece]
        push(sums.at[d, piece], there, chain_send.at[side, step, piece], chain_got.at[side, step, piece], to)

    router_part[...] = jnp.zeros_like(router_part)
    fetch(0, 0).start()
    fetch(0, 1).start()
    for copy in fetch_beside(0):
        copy.start()

    def start(i, carry):
        d = whose(i)
        outgoing = to_core.at[lax.rem(i, 2)]
        fetch(i, 0).wait()

        @pl.when(i >= 2)
        def _():
            await_bytes(outgoing, core_send.at[lax.rem(i, 2)])

        block(d * 2 + nc, 0, outgoing, None)
        push(outgoing, sums.at[d], core_send.at[lax.rem(i, 2)], core_got.at[d], {"core": nc})
        fetch(i, 1).wait()
        await_bytes(sums.at[d], core_got.at[d])
        block(d * 2 + c, 1, sums.at[d], sums.at[d])
        for piece in range(pieces):

            @pl.when((r == 0) & (d != r))
            def _():
                pass_on(0, ring - 1 - d, d, piece, to_next)

            @pl.when((r == ring - 1) & (d != r))
            def _():
                pass_on(1, d, d, piece, to_last)

        @pl.when(i + 1 < ring)
        def _():
            fetch(i + 1, 0).start()
            fetch(i + 1, 1).start()

        beside(i)
        return carry

    lax.fori_loop(0, ring, start, 0)

    def sides(time):
        up, down = time - r, time - (ring - 1 - r)
        return (
            ((r >= 1) & (up >= 0), jnp.maximum(up, 0), ring - 1 - jnp.maximum(up, 0), to_next, 0),
            ((r + 1 < ring) & (down >= 0), jnp.maximum(down, 0), jnp.maximum(down, 0), to_last, 1),
        )

    def on(time, carry):
        for piece in range(pieces):
            for comes, step, d, to, side in sides(time):

                @pl.when(comes)
                def _(step=step, d=d, to=to, side=side):
                    arrived = chain_in.at[slot(side, d, r), piece]
                    await_bytes(arrived, chain_got.at[side, step, piece])

                    def one(k, carry):
                        at = pl.ds(pl.multiple_of(k * tile, tile), tile)
                        total = sums[d, piece, at].astype(jnp.float32) + arrived[at].astype(jnp.float32)
                        sums[d, piece, at] = total.astype(sums.dtype)
                        return carry

                    lax.fori_loop(0, rows // tile, one, 0)

                    @pl.when(time < ring - 1)
                    def _():
                        pass_on(side, step, d, piece, to)

        @pl.when(time < ring - 1)
        def _():
            beside(ring + time - 1)

        return carry

    def rest(source, carry):
        beside(source)
        return carry

    lax.fori_loop(1, ring - 1, on, 0)
    lax.fori_loop(2 * ring - 2, sources, rest, 0)
    on(ring - 1, 0)
    await_bytes(mixed_low, store)

    def total(k, carry):
        at = pl.ds(pl.multiple_of(k * tile, tile), tile)
        for piece in range(pieces):
            out[pl.ds(pl.multiple_of(piece * rows + k * tile, tile), tile), :] = sums[r, piece, at].astype(jnp.float32)
        return carry

    lax.fori_loop(0, rows // tile, total, 0)
    for k in range(2):
        await_bytes(to_core.at[k], core_send.at[k])
    for step in range(ring - 1):
        for piece in range(pieces):
            for sent, side in ((r + step < ring - 1, 0), (step < r, 1)):

                @pl.when(sent)
                def _(side=side):
                    await_bytes(sums.at[0, 0], chain_send.at[side, step, piece])


def give_back(hot, logit, router, pairs, mixed, n2):
    ring, dma, pieces = lax.axis_size("ring"), pltpu.SemaphoreType.DMA, 2
    experts, sources, slots, width = pairs.shape
    rows, all_experts = hot.shape[2], router.shape[0]
    vm, anywhere = pl.BlockSpec(memory_space=pltpu.VMEM), pl.BlockSpec(memory_space=pl.ANY)
    low = lambda *shape: pltpu.VMEM(shape, pairs.dtype)
    block = lambda n: low(n, pieces, rows // pieces, width)
    chain = dma((2, ring, pieces))
    return pl.pallas_call(
        give_back_kernel,
        out_shape=[
            jax.ShapeDtypeStruct((rows, width), jnp.float32),
            jax.ShapeDtypeStruct((sources, rows, width), pairs.dtype),
            jax.ShapeDtypeStruct((all_experts, width), jnp.float32),
        ],
        in_specs=[vm] * 4 + [anywhere] * 3,
        out_specs=[vm, anywhere, vm],
        scratch_shapes=[block(ring), block(ring + 1), block(2), low(2, experts, slots, width), low(2, experts, slots, width)]
        + [low(rows, width), low(2, rows, width)]
        + [dma((2,)), dma((2,)), dma((ring,)), chain, chain, dma((2, 2)), dma],
        compiler_params=pltpu.CompilerParams(collective_id=3, has_side_effects=True, vmem_limit_bytes=60 << 20),
        cost_estimate=pl.CostEstimate(flops=100_000_000_000, bytes_accessed=200_000_000, transcendentals=0),
        name="give_back",
    )(hot, logit, logit.transpose(0, 2, 1), router, pairs, mixed, n2)


def matmul(left, right):
    return jnp.dot(left, right, preferred_element_type=jnp.float32)


def times_transposed(left, right):
    return lax.dot_general(
        left, right, (((1,), (1,)), ((), ())), preferred_element_type=jnp.float32
    )


def transposed_times(left, right):
    return lax.dot_general(
        left, right, (((0,), (0,)), ((), ())), preferred_element_type=jnp.float32
    )


def corners():
    return ((0, 1), (1, 0), (1, 1))


def corner(da, db):
    pa, pb = turn("ca", da), turn("cb", db)
    return 2 * pa + pb, {"ca": pa, "cb": pb}


def rows_to_heads(src, dst, send, got, place):
    rows, width = src.shape[0], dst.shape[1]
    me, _ = corner(0, 0)
    there = dst.at[pl.ds(pl.multiple_of(me * rows, rows), rows), :]
    for i, (da, db) in enumerate(corners()):
        peer, to = corner(da, db)
        push(src.at[:, pl.ds(pl.multiple_of(peer * width, width), width)], there, send.at[i], got.at[i], to)
    pltpu.make_async_copy(src.at[:, pl.ds(pl.multiple_of(me * width, width), width)], there, place).start()


def wait_heads(src, dst, got, place):
    rows = src.shape[0]
    here = lambda at: dst.at[pl.ds(pl.multiple_of(at * rows, rows), rows), :]
    await_bytes(here(corner(0, 0)[0]), place)
    for i, (da, db) in enumerate(corners()):
        await_bytes(here(corner(da, db)[0]), got.at[i])


def swap_halves(v):
    return pltpu.roll(v, HD // 2, 1)


def norm_and_turn(raw, gain, cosine, sine, out):
    rows, width = raw.shape
    tile = 32

    def part(i, carry):
        at = pl.ds(pl.multiple_of(i * tile, tile), tile)
        value = raw[at, :]
        factor = lax.rsqrt(jnp.mean(value * value, axis=-1, keepdims=True) + EPSILON)
        for h in range(width // HD):
            lanes = pl.ds(h * HD, HD)
            v = raw[at, lanes] * factor * gain[:, lanes]
            out[at, lanes] = (v * cosine[at, :] + swap_halves(v) * sine[at, :]).astype(out.dtype)
        return carry

    lax.fori_loop(0, rows // tile, part, 0)


def norm_and_turn_back(grad, raw, gain, cosine, sine, out, gain_grad, turned):
    rows, width = raw.shape
    tile = 32
    gain_grad[...] = jnp.zeros_like(gain_grad)

    def part(i, carry):
        at = pl.ds(pl.multiple_of(i * tile, tile), tile)
        value = raw[at, :]
        factor = lax.rsqrt(jnp.mean(value * value, axis=-1, keepdims=True) + EPSILON)
        inner = jnp.zeros((tile, HD), jnp.float32)
        for h in range(width // HD):
            lanes = pl.ds(h * HD, HD)
            g = grad[at, lanes].astype(jnp.float32)
            g = g * cosine[at, :] - swap_halves(g) * sine[at, :]
            turned[:, lanes] = g
            inner = inner + g * gain[:, lanes] * raw[at, lanes]
        inner = jnp.sum(inner, axis=-1, keepdims=True) * (factor * factor * factor / width)
        for h in range(width // HD):
            lanes = pl.ds(h * HD, HD)
            g, v = turned[:, lanes], raw[at, lanes]
            out[at, lanes] = (factor * (g * gain[:, lanes]) - v * inner).astype(out.dtype)
            gained = g * v * factor
            gain_grad[:, lanes] += sum(gained[k : k + 8] for k in range(0, tile, 8))
        return carry

    lax.fori_loop(0, rows // tile, part, 0)


def attend_kernel(scale, q_raw, k_raw, v, q_gain, k_gain, cosine, sine, keep, o, qh, kh, vh, logs, q, k, oh, send, got, place, send_o, got_o, place_o):
    rows, width = v.shape[0], qh.shape[1]
    greet([corner(da, db)[1] for da, db in corners()])
    pairs = ((v, vh), (k, kh), (q, qh))
    rows_to_heads(v, vh, send.at[0], got.at[0], place.at[0])
    norm_and_turn(k_raw, k_gain, cosine, sine, k)
    rows_to_heads(k, kh, send.at[1], got.at[1], place.at[1])
    norm_and_turn(q_raw, q_gain, cosine, sine, q)
    rows_to_heads(q, qh, send.at[2], got.at[2], place.at[2])
    for i, (src, dst) in enumerate(pairs):
        wait_heads(src, dst, got.at[i], place.at[i])
    me, _ = corner(0, 0)
    tile = 128
    mine = pl.ds(pl.multiple_of(me * width, width), width)

    def block(at_block):
        def part(i, carry):
            at = pl.ds(pl.multiple_of(at_block * rows + i * tile, tile), tile)
            for h in range(width // HD):
                lanes = pl.ds(h * HD, HD)
                s = times_transposed(qh[at, lanes], kh[:, lanes]) * scale
                s = jnp.where(keep[...] > 0.0, s, NEG_FILL)
                peak = jnp.max(s, axis=-1, keepdims=True)
                p = jnp.exp(s - peak)
                total = jnp.sum(p, axis=-1, keepdims=True)
                logs[h, at, :] = peak + jnp.log(total)
                low = (p * (1.0 / total)).astype(jnp.bfloat16)
                oh[at, lanes] = matmul(low, vh[:, lanes]).astype(jnp.bfloat16)
            return carry

        lax.fori_loop(0, rows // tile, part, 0)

    for i, (da, db) in enumerate(corners()):
        peer, to = corner(da, db)
        block(peer)
        push(oh.at[pl.ds(pl.multiple_of(peer * rows, rows), rows), :], o.at[:, mine], send_o.at[i], got_o.at[i], to)
    block(me)
    pltpu.make_async_copy(oh.at[pl.ds(pl.multiple_of(me * rows, rows), rows), :], o.at[:, mine], place_o).start()
    pltpu.make_async_copy(oh.at[pl.ds(pl.multiple_of(me * rows, rows), rows), :], o.at[:, mine], place_o).wait()
    piece = o.at[:, mine]
    for i in range(3):
        await_bytes(piece, got_o.at[i])
        await_bytes(piece, send_o.at[i])
        for j in range(3):
            await_bytes(piece, send.at[j, i])


def attend(q_raw, k_raw, v, q_gain, k_gain, cosine, sine, keep, scale):
    rows, width = v.shape
    chips = lax.axis_size("ca") * lax.axis_size("cb")
    heads = jax.ShapeDtypeStruct((rows * chips, width // chips), v.dtype)
    vm, dma = pl.BlockSpec(memory_space=pltpu.VMEM), pltpu.SemaphoreType.DMA
    return pl.pallas_call(
        functools.partial(attend_kernel, scale),
        out_shape=[jax.ShapeDtypeStruct(v.shape, v.dtype), heads, heads, heads]
        + [jax.ShapeDtypeStruct((width // chips // HD, rows * chips, 1), jnp.float32)],
        in_specs=[vm] * 8,
        out_specs=[vm] * 5,
        scratch_shapes=[pltpu.VMEM(v.shape, v.dtype)] * 2 + [pltpu.VMEM(heads.shape, v.dtype)]
        + [dma((3, 3)), dma((3, 3)), dma((3,)), dma((3,)), dma((3,)), dma],
        compiler_params=pltpu.CompilerParams(collective_id=4, has_side_effects=True, vmem_limit_bytes=48 << 20),
        cost_estimate=pl.CostEstimate(flops=1_000_000, bytes_accessed=10_000, transcendentals=0),
        name="attend",
    )(q_raw, k_raw, v, q_gain, k_gain, cosine, sine, keep)


def attend_back_kernel(
    scale, do, qh, kh, vh, logs, keep, q_raw, k_raw, q_gain, k_gain, cosine, sine,
    dq_raw, dk_raw, dv, q_gain_grad, k_gain_grad,
    doh, dqh, dkh, dvh, dq, dk, turned, send, got, place, send_g, got_g, place_g,
):
    rows, width = do.shape[0], qh.shape[1]
    greet([corner(da, db)[1] for da, db in corners()])
    rows_to_heads(do, doh, send, got, place)
    wait_heads(do, doh, got, place)
    me, _ = corner(0, 0)
    tile, total_rows = 128, qh.shape[0]
    grads = ((dqh, dq), (dkh, dk), (dvh, dv))

    def one_head(h):
        lanes = pl.ds(h * HD, HD)

        def part(i, carry):
            dk_sum, dv_sum = carry
            at = pl.ds(pl.multiple_of(i * tile, tile), tile)
            qb, db, kb, vb = qh[at, lanes], doh[at, lanes], kh[:, lanes], vh[:, lanes]
            s = times_transposed(qb, kb) * scale
            s = jnp.where(keep[...] > 0.0, s, NEG_FILL)
            p = jnp.exp(s - logs[h, at, :])
            dp = times_transposed(db, vb)
            ds = (p * (dp - jnp.sum(dp * p, axis=-1, keepdims=True))).astype(jnp.bfloat16)
            dqh[at, lanes] = (matmul(ds, kb) * scale).astype(jnp.bfloat16)
            dk_sum = dk_sum + transposed_times(ds, qb)
            dv_sum = dv_sum + transposed_times(p.astype(jnp.bfloat16), db)
            return dk_sum, dv_sum

        zero = jnp.zeros((total_rows, HD), jnp.float32)
        dk_sum, dv_sum = lax.fori_loop(0, total_rows // tile, part, (zero, zero))
        dkh[:, lanes] = (dk_sum * scale).astype(jnp.bfloat16)
        dvh[:, lanes] = dv_sum.astype(jnp.bfloat16)

    for h in range(width // HD):
        one_head(h)
        lanes = pl.ds(h * HD, HD)
        here = pl.ds(pl.multiple_of(me * width + h * HD, HD), HD)
        for g, (src, dst) in enumerate(grads):
            for i, (da, db) in enumerate(corners()):
                peer, to = corner(da, db)
                push(src.at[pl.ds(pl.multiple_of(peer * rows, rows), rows), lanes], dst.at[:, here], send_g.at[g, i, h], got_g.at[g, i, h], to)
            own = src.at[pl.ds(pl.multiple_of(me * rows, rows), rows), lanes]
            pltpu.make_async_copy(own, dst.at[:, here], place_g.at[g, h]).start()
    piece = dq.at[:, pl.ds(0, HD)]
    for h in range(width // HD):
        for g in range(3):
            await_bytes(piece, place_g.at[g, h])
            for i in range(3):
                await_bytes(piece, send_g.at[g, i, h])
                await_bytes(piece, got_g.at[g, i, h])
    for i in range(3):
        await_bytes(do.at[:, pl.ds(0, width)], send.at[i])
    norm_and_turn_back(dk, k_raw, k_gain, cosine, sine, dk_raw, k_gain_grad, turned)
    norm_and_turn_back(dq, q_raw, q_gain, cosine, sine, dq_raw, q_gain_grad, turned)


def attend_back(do, qh, kh, vh, logs, keep, q_raw, k_raw, q_gain, k_gain, cosine, sine, scale):
    heads = qh.shape[1] // HD
    vm, dma = pl.BlockSpec(memory_space=pltpu.VMEM), pltpu.SemaphoreType.DMA
    return pl.pallas_call(
        functools.partial(attend_back_kernel, scale),
        out_shape=[jax.ShapeDtypeStruct(do.shape, do.dtype)] * 3 + [jax.ShapeDtypeStruct((8, do.shape[1]), jnp.float32)] * 2,
        in_specs=[vm] * 12,
        out_specs=[vm] * 5,
        scratch_shapes=[pltpu.VMEM(qh.shape, qh.dtype)] * 4
        + [pltpu.VMEM(do.shape, do.dtype)] * 2
        + [pltpu.VMEM((32, do.shape[1]), jnp.float32)]
        + [dma((3,)), dma((3,)), dma, dma((3, 3, heads)), dma((3, 3, heads)), dma((3, heads))],
        compiler_params=pltpu.CompilerParams(collective_id=5, has_side_effects=True, vmem_limit_bytes=56 << 20),
        cost_estimate=pl.CostEstimate(flops=50_000_000_000, bytes_accessed=10_000_000, transcendentals=0),
        name="attend_back",
    )(do, qh, kh, vh, logs, keep, q_raw, k_raw, q_gain, k_gain, cosine, sine)


def join_kernel(own, from_b, from_a, first, second, out, held, load, store):
    experts, units = own.shape[:2]
    a, b = lax.axis_index("ca"), lax.axis_index("cb")
    na, nb = turn("ca", 1), turn("cb", 1)
    loads, stores = [], []
    for piece, (p, q) in enumerate(((a, b), (a, nb), (na, b), (na, nb))):
        for e in range(experts):
            if piece < 3:
                src = (own, from_b, from_a)[piece].at[e]
            else:
                src = first.at[e] if e < experts // 2 else second.at[e - experts // 2]
            here = held.at[piece, e]
            loads.append(pltpu.make_async_copy(src, here, load.at[piece, e]))
            at = pl.ds(pl.multiple_of((2 * p + q) * units, units), units)
            stores.append(pltpu.make_async_copy(here, out.at[e, at, :], store.at[piece, e]))
    for copy in loads:
        copy.start()
    for fetch, copy in zip(loads, stores):
        fetch.wait()
        copy.start()
    for copy in stores:
        copy.wait()


def join(own, from_b, from_a, first, second):
    experts, units, width = own.shape
    anywhere, dma = pl.BlockSpec(memory_space=pl.ANY), pltpu.SemaphoreType.DMA((4, experts))
    return pl.pallas_call(
        join_kernel,
        out_shape=jax.ShapeDtypeStruct((experts, 4 * units, width), own.dtype),
        in_specs=[anywhere] * 5,
        out_specs=anywhere,
        scratch_shapes=[pltpu.VMEM((4, experts, units, width), own.dtype), dma, dma],
        cost_estimate=pl.CostEstimate(flops=0, bytes_accessed=8 * experts * units * width * 2, transcendentals=0),
        name="join",
    )(own, from_b, from_a, first, second)


def norm_rows(values, gain):
    factor = lax.rsqrt(jnp.mean(values * values, axis=-1, keepdims=True) + EPSILON)
    return (values * factor * gain, factor)


def norm_back(grad, values, factor, gain):
    weighted = grad * gain
    inner = jnp.mean(weighted * values, axis=-1, keepdims=True)
    return (factor * weighted - values * factor**3 * inner, jnp.sum(grad * values * factor, axis=0))


def rotary_tables(positions, head_dim):
    half_dim = head_dim // 2
    frequency = jnp.exp(-math.log(ROPE_THETA) * jnp.arange(half_dim, dtype=jnp.float32) / half_dim)
    angles = positions.astype(jnp.float32)[:, None] * frequency[None, :]
    return (jnp.cos(angles), jnp.sin(angles))


def local(
    tokens, cotangent, lengths, expert_ids, query_weight, key_weight, value_weight, out_weight,
    router_weight, first_gain, second_gain, query_gain, key_gain, gate_weight, up_weight, down_weight,
):
    token_count = tokens.shape[1]
    model_width = tokens.shape[2]
    head_dim = HD
    top_count = expert_ids.shape[2]
    experts = router_weight.shape[1]
    local_experts = gate_weight.shape[0]
    ctx_size = lax.axis_size(CTX)
    sources = lax.axis_size(EXP)
    capacity = max(2, -(-(token_count * top_count * 9) // (experts * 8)))
    score_scale = 1.0 / math.sqrt(head_dim)
    seq_len = token_count * ctx_size

    inputs = tokens[0].astype(jnp.float32)
    length = lengths[0]
    positions = lax.axis_index(CTX) * token_count + jnp.arange(token_count, dtype=jnp.int32)
    row_valid = positions < length
    row_valid = row_valid.astype(jnp.float32)[:, None]
    key_valid = jnp.arange(seq_len, dtype=jnp.int32) < length
    grad_total_low = (cotangent[0].astype(jnp.float32) * row_valid).astype(jnp.bfloat16)
    grad_total = grad_total_low.astype(jnp.float32)

    rows_each = query_weight.shape[0]
    packed = jnp.concatenate(
        [g.reshape(-1) for g in (first_gain, second_gain, query_gain, key_gain)] + [router_weight.reshape(-1)]
    )
    small = jnp.pad(packed, (0, -packed.size % 2048)).reshape(-1, 128)
    ids_low = expert_ids[0].astype(jnp.bfloat16).reshape(-1, 128)
    gathered, (ids_all, g_all) = spread([query_weight, key_weight, value_weight, out_weight, small], [ids_low, grad_total_low])
    full_query, full_key, full_value, full_out = (w.reshape(model_width, -1) for w in gathered[:4])
    smalls = gathered[4].reshape(-1, small.size)
    gains = [smalls[:, i * rows_each : (i + 1) * rows_each].reshape(-1).astype(jnp.float32) for i in range(4)]
    gain_first, gain_second, gain_queries, gain_keys = gains
    full_router = smalls[:, 4 * rows_each : packed.size].reshape(model_width, experts)
    ids_all = ids_all.reshape(sources, token_count, top_count).astype(jnp.int32)
    full_value, gate_weight, up_weight = lax.optimization_barrier((full_value, gate_weight, up_weight))
    gate_all, up_all = (lax.all_gather(w, CTX, axis=2, tiled=True) for w in (gate_weight, up_weight))
    cosine, sine = rotary_tables(positions, head_dim)
    normed_one, factor_one = norm_rows(inputs, gain_first)
    normed_one_low = normed_one.astype(jnp.bfloat16)
    query_raw = matmul(normed_one_low, full_query)
    key_raw = matmul(normed_one_low, full_key)
    value_low = matmul(normed_one_low, full_value).astype(jnp.bfloat16)
    keep = key_valid.astype(jnp.float32)[None, :]
    turns = (jnp.concatenate([cosine, cosine], axis=1), jnp.concatenate([-sine, sine], axis=1))
    row = lambda g: g.reshape(1, model_width)
    shared = (row(gain_queries), row(gain_keys), *turns)
    attended_low, *saved = attend(query_raw, key_raw, value_low, *shared, keep, score_scale)
    flip = lambda v, axis: lax.ppermute(v, axis, [(0, 1), (1, 0)])
    hidden_state = inputs + matmul(attended_low, full_out)
    normed_two, factor_two = norm_rows(hidden_state, gain_second)
    normed_two_low = normed_two.astype(jnp.bfloat16)

    first_expert = lax.axis_index(EXP) * local_experts
    own_experts = first_expert + jnp.arange(local_experts, dtype=jnp.int32)
    mask = jnp.any(ids_all[:, None, :, :] == own_experts[None, :, None, None], axis=-1)
    before = (jnp.arange(token_count)[:, None] < jnp.arange(token_count)[None, :]).astype(jnp.bfloat16)
    ranks = jnp.einsum("seu,ut->set", mask.astype(jnp.bfloat16), before, preferred_element_type=jnp.float32)
    slots = jnp.arange(capacity, dtype=jnp.float32)
    hot = (mask[:, :, None, :] & (ranks[:, :, None, :] == slots[None, None, :, None])).astype(jnp.bfloat16)
    router_turned = full_router.T
    n2_all, x, de, row_gate, probs = dispatch(normed_two_low, router_turned, hot, g_all)
    n2_all = n2_all.reshape(sources, token_count, model_width)
    probs = probs.transpose(0, 2, 1).reshape(-1, experts)
    hot32 = hot.astype(jnp.float32)
    x, gate_all, down_weight = lax.optimization_barrier((x, gate_all, down_weight))
    down_b, down_a = flip(down_weight, "cb"), flip(down_weight, "ca")
    first_half = local_experts // 2
    down_corner = [flip(down_b[:first_half], "ca"), flip(down_a[first_half:], "cb")]
    ee = lambda eq, a, b: jnp.einsum(eq, a, b, preferred_element_type=jnp.float32)
    gp = ee("escd,edf->escf", x, gate_all)
    up = ee("escd,edf->escf", x, up_all)
    sig = jax.nn.sigmoid(gp)
    hid = (gp * sig * up).astype(jnp.bfloat16)
    down_part = ee("escf,escd->efd", hid, de).astype(jnp.bfloat16)
    *down_corner, down_part = lax.optimization_barrier((*down_corner, down_part))
    down_all = join(down_weight, down_b, down_a, *down_corner)
    eo = ee("escf,efd->escd", hid, down_all).astype(jnp.bfloat16)
    gained = jnp.sum(de.astype(jnp.float32) * eo.astype(jnp.float32), axis=-1)
    mixed_rows = (row_gate * eo.astype(jnp.float32)).astype(jnp.bfloat16)
    dhid = ee("escd,efd->escf", de, down_all)
    dgp = (dhid * up * sig * (1.0 + gp * (1.0 - sig))).astype(jnp.bfloat16)
    dup = (dhid * gp * sig).astype(jnp.bfloat16)
    gate_part = ee("escd,escf->edf", x, dgp)
    up_part = ee("escd,escf->edf", x, dup)
    parts = [v.astype(jnp.bfloat16) for v in (down_part, gate_part, up_part)]
    dgp, dup, *_ = lax.optimization_barrier((dgp, dup, *parts))
    rs_ctx = lambda v, a: lax.psum_scatter(v, CTX, scatter_dimension=a, tiled=True)
    down_grad, gate_grad, up_grad = rs_ctx(parts[0], 1), rs_ctx(parts[1], 2), rs_ctx(parts[2], 2)
    dpair = (ee("escf,edf->escd", dgp, gate_all) + ee("escf,edf->escd", dup, up_all)).astype(jnp.bfloat16)

    gained = jnp.sum(hot32 * gained.transpose(1, 0, 2)[..., None], axis=2)
    gained = gained.transpose(0, 2, 1).reshape(-1, local_experts)
    onto = (jnp.arange(experts)[None, :] == own_experts[:, None]).astype(jnp.float32)
    weighed = jnp.sum(gained[:, :, None] * onto[None], axis=1)
    dlogit_low = (weighed - probs * jnp.sum(gained, axis=-1, keepdims=True)).astype(jnp.bfloat16)
    dpair, down_grad = lax.optimization_barrier((dpair, down_grad))
    dn2, mixed_part, router_part = give_back(
        hot.transpose(0, 1, 3, 2), dlogit_low.reshape(sources, token_count, experts), router_turned, dpair, mixed_rows, n2_all
    )
    router_part = router_part.T
    dn2, gate_grad = lax.optimization_barrier((dn2, gate_grad))
    mixed = lax.psum_scatter(mixed_part.reshape(-1, model_width), EXP, scatter_dimension=0, tiled=True)

    dh_norm, gain_second_part = norm_back(dn2, hidden_state, factor_two, gain_second)
    grad_hidden = grad_total + dh_norm
    dh_low = grad_hidden.astype(jnp.bfloat16)
    out_part = transposed_times(attended_low, dh_low)
    d_att = times_transposed(dh_low, full_out).astype(jnp.bfloat16)
    dq_low, dk_low, dv_low, *gain_parts = attend_back(d_att, *saved, keep, query_raw, key_raw, *shared, score_scale)
    dv_low, up_grad = lax.optimization_barrier((dv_low, up_grad))
    gain_queries_part, gain_keys_part = (jnp.sum(g, axis=0) for g in gain_parts)
    core = lax.axis_index("core")
    swap = lambda v: lax.ppermute(v, "core", [(0, 1), (1, 0)])

    def columns_of_core(v):
        width = model_width // 2
        mine = lax.dynamic_slice_in_dim(v, core * width, width, 1)
        other = lax.dynamic_slice_in_dim(v, (1 - core) * width, width, 1)
        return jnp.concatenate([mine, swap(other)], axis=0)

    both = lambda v: jnp.concatenate([v, swap(v)], axis=0)
    n1_both, att_both = both(normed_one_low), both(attended_low)
    parts = [
        transposed_times(l, columns_of_core(r)).astype(jnp.bfloat16)
        for l, r in ((att_both, dh_low), (n1_both, dq_low), (n1_both, dk_low), (n1_both, dv_low))
    ]
    split = lambda v: v.reshape(ctx_size * sources // 2, 2, -1)
    small_parts = jnp.concatenate(
        [split(v) for v in (gain_second_part, gain_queries_part, gain_keys_part, router_part)], axis=2
    )
    small_parts = jnp.pad(small_parts, ((0, 0), (0, 0), (0, -small_parts.shape[2] % 2048)))
    small_parts = lax.dynamic_index_in_dim(small_parts, core, 1, False) + swap(lax.dynamic_index_in_dim(small_parts, 1 - core, 1, False))
    weight_grads, small_grads, input_grad, gain_first_sums = collect(
        parts, small_parts.reshape(ctx_size * sources // 2, -1, 128), (dq_low, dk_low, dv_low),
        (full_query, full_key, full_value), tokens[0], row(gain_first), grad_hidden,
    )
    weight_grads, mixed, gate_grad, up_grad, down_grad = lax.optimization_barrier(
        (list(weight_grads), mixed, gate_grad, up_grad, down_grad)
    )
    layer_out = (row_valid * (hidden_state + mixed.astype(jnp.float32))).astype(jnp.bfloat16)
    gate_grad, up_grad, down_grad = (v.astype(jnp.float32) for v in (gate_grad, up_grad, down_grad))
    weight_grads = list(weight_grads[1:]) + [weight_grads[0]]
    small_grads = small_grads.reshape(-1)
    gain_grads = [lax.dynamic_slice_in_dim(jnp.sum(gain_first_sums, axis=0), lax.axis_index(ALL) * rows_each, rows_each)]
    gain_grads += [small_grads[i * rows_each : (i + 1) * rows_each] for i in range(3)]
    router_grad = small_grads[3 * rows_each : packed.size - rows_each].reshape(rows_each, experts)
    return (layer_out[None], input_grad[None], *weight_grads, router_grad, *gain_grads, gate_grad, up_grad, down_grad)


def solution(mesh):
    ctx, exp = mesh.devices.shape
    fine = Mesh(mesh.devices.reshape(2, ctx // 2, exp // 2, 2), ("ca", "cb", "ring", "core"))
    rows = P(EXP, CTX, None)
    flat2, flat1 = P(ALL, None), P(ALL)
    placed = (rows, rows, P(EXP), rows) + (flat2,) * 5 + (flat1,) * 4 + (P(EXP, None, CTX),) * 2 + (P(EXP, CTX, None),)
    outs = (rows, rows) + (flat2,) * 5 + (flat1,) * 4 + (P(EXP, None, CTX),) * 2 + (P(EXP, CTX, None),)
    return jax.shard_map(local, mesh=fine, in_specs=placed, out_specs=outs, check_vma=False)
```

```python
import functools
import math

import jax
import jax.numpy as jnp
from jax import lax
from jax.experimental import pallas as pl
from jax.experimental.pallas import tpu as pltpu
from jax.sharding import Mesh
from jax.sharding import PartitionSpec as P

HEADS = 16
HD = 128
EPSILON = 1e-06
ROPE_THETA = 10000.0
NEG_FILL = -1e30

CTX = ("ca", "cb")
EXP = ("ring", "core")
ALL = CTX + EXP


MESH = pl.DeviceIdType.MESH


def turn(name, by):
    size = lax.axis_size(name)
    return lax.rem(lax.axis_index(name) + by, size)


def await_bytes(ref, sem):
    pltpu.make_async_copy(ref, ref, sem).wait()


def greet(peers):
    barrier = pltpu.get_barrier_semaphore()
    for peer in peers:
        pl.semaphore_signal(barrier, inc=1, device_id=peer, device_id_type=MESH)
    pl.semaphore_wait(barrier, len(peers))


def push(src, dst, ssem, rsem, to):
    pltpu.make_async_remote_copy(
        src_ref=src, dst_ref=dst, send_sem=ssem, recv_sem=rsem, device_id=to, device_id_type=MESH
    ).start()


RING, SIDE_B, SIDE_A, FIRST, SECOND, CORE_OWN, CORE_B, CORE_A, CORE_FIRST, CORE_SECOND = range(10)


def along(step):
    ring, r = lax.axis_size("ring"), lax.axis_index("ring")
    to_next, to_last = {"ring": turn("ring", 1)}, {"ring": turn("ring", ring - 1)}
    return (
        ((r + 1 < ring) & (r >= step), r >= step + 1, lax.rem(r + ring - step, ring), lax.rem(r + ring - 1 - step, ring), to_next, 0),
        ((r >= 1) & (r + step < ring), r + 1 + step < ring, lax.rem(r + step, ring), lax.rem(r + 1 + step, ring), to_last, 1),
    )


def send_along(step, own, block_of, send, got):
    for sent, _, block, _, to, side in along(step):

        @pl.when(sent)
        def _(block=block, to=to, side=side):
            src = own if isinstance(step, int) and step == 0 else block_of(block)
            push(src, block_of(block), send.at[side, step], got.at[side, step], to)


def take_along(step, block_of, got, then):
    for _, comes, _, block, _, side in along(step):

        @pl.when(comes)
        def _(block=block, side=side):
            await_bytes(block_of(block), got.at[side, step])

    for _, comes, _, block, _, side in along(step):

        @pl.when(comes)
        def _(block=block):
            then(block)


def sent_along(own, send):
    ring = lax.axis_size("ring")
    for step in range(ring - 1):
        for sent, _, _, _, _, side in along(step):

            @pl.when(sent)
            def _(side=side):
                await_bytes(own, send.at[side, step])


def spread_kernel(count, tables, *refs):
    ring = lax.axis_size("ring")
    ins, refs = refs[: count + tables], refs[count + tables :]
    outs, sems = refs[: count + tables], refs[count + tables :]
    send, send_ring, got_ring, got_b, got_a, got, place, core_sem = sems
    a, b, r, c = (lax.axis_index(n) for n in ALL)
    na, nb, nc = turn("ca", 1), turn("cb", 1), turn("core", 1)
    to_a, to_b, to_core = {"ca": na}, {"cb": nb}, {"core": nc}
    greet([to_a, to_b, to_core] + [{"ring": turn("ring", k)} for k in range(1, ring)])

    def half(ref, which):
        rows, cols = ref.shape[-2:]
        if rows * 8 < cols:
            return ref.at[..., pl.ds(which * (cols // 2), cols // 2)]
        return ref.at[..., pl.ds(which * (rows // 2), rows // 2), :]

    def halves(ref, which):
        rows, cols = ref.shape[-2:]
        if rows * 8 < cols:
            return ref.at[:, :, pl.ds(which * (cols // 2), cols // 2)]
        return ref.at[:, pl.ds(which * (rows // 2), rows // 2), :]

    def place_of(w):
        return (lambda at: outs[w].at[a, b, at, c]) if w < count else (lambda at: outs[w].at[at, c])

    for w in range(count + tables):
        pltpu.make_async_copy(ins[w], place_of(w)(r), place.at[w]).start()
    for w in reversed(range(count)):
        send_along(0, ins[w], place_of(w), send_ring.at[w], got_ring.at[w])
        here = place_of(w)(r)
        push(ins[w], here, send.at[w, SIDE_B], got_b.at[w, r], to_b)
        push(ins[w], here, send.at[w, SIDE_A], got_a.at[w, r], to_a)
        push(ins[w], here, send.at[w, CORE_OWN], got.at[w, CORE_OWN], to_core)
    for t in range(tables):
        push(ins[count + t], place_of(count + t)(r), core_sem.at[t, 0], core_sem.at[t, 1], to_core)

    def sides(w):
        for step in range(ring - 1):

            def on(at):
                block = place_of(w)(at)
                push(block, block, send.at[w, SIDE_B], got_b.at[w, at], to_b)
                push(block, block, send.at[w, SIDE_A], got_a.at[w, at], to_a)
                push(block, block, send.at[w, CORE_OWN], got.at[w, CORE_OWN], to_core)

            take_along(step, place_of(w), got_ring.at[w], on)
            if step + 1 < ring - 1:
                send_along(step + 1, ins[w], place_of(w), send_ring.at[w], got_ring.at[w])

    def diagonal(w):
        out = outs[w]

        def one(k, carry):
            at = lax.rem(r + ring - k, ring)
            block = out.at[a, nb, at, c]
            await_bytes(block, got_b.at[w, at])
            push(half(block, 0), half(block, 0), send.at[w, FIRST], got.at[w, FIRST], to_a)
            push(block, block, send.at[w, CORE_B], got.at[w, CORE_B], to_core)
            block = out.at[na, b, at, c]
            await_bytes(block, got_a.at[w, at])
            push(half(block, 1), half(block, 1), send.at[w, SECOND], got.at[w, SECOND], to_b)
            push(block, block, send.at[w, CORE_A], got.at[w, CORE_A], to_core)
            return carry

        lax.fori_loop(0, ring, one, 0)

    def last(w):
        block = outs[w].at[na, nb, :, c]
        for which, kind, core_kind in ((0, FIRST, CORE_FIRST), (1, SECOND, CORE_SECOND)):
            part = halves(block, which)
            await_bytes(part, got.at[w, kind])
            push(part, part, send.at[w, core_kind], got.at[w, core_kind], to_core)

    def table_step(t, step):
        w = count + t

        def on(at):
            push(place_of(w)(at), place_of(w)(at), core_sem.at[t, 0], core_sem.at[t, 1], to_core)

        if step >= 0:
            take_along(step, place_of(w), got_ring.at[w], on)
        if step + 1 < ring - 1:
            send_along(step + 1, ins[w], place_of(w), send_ring.at[w], got_ring.at[w])

    order = list(reversed(range(count)))
    for step in range(count + 2):
        if step < count:
            sides(order[step])
        if step >= count - 1:
            for t in range(tables):
                table_step(t, step - count)
        if 0 <= step - 1 < count:
            diagonal(order[step - 1])
        if 0 <= step - 2 < count:
            last(order[step - 2])
    for step in range(2, ring - 1):
        for t in range(tables):
            table_step(t, step)

    for w in range(count):
        out = outs[w]
        mine = lambda p, q: out.at[p, q, :, c]
        await_bytes(ins[w], place.at[w])
        sent_along(ins[w], send_ring.at[w])
        for kind in (SIDE_B, SIDE_A, CORE_OWN, CORE_B, CORE_A):
            await_bytes(mine(a, b), send.at[w, kind])
        for which, kind in ((0, FIRST), (1, SECOND), (0, CORE_FIRST), (1, CORE_SECOND)):
            await_bytes(halves(mine(a, b), which), send.at[w, kind])
        for kind, p, q in ((CORE_OWN, a, b), (CORE_B, a, nb), (CORE_A, na, b)):
            await_bytes(out.at[p, q, :, nc], got.at[w, kind])
        for which, kind in ((0, CORE_FIRST), (1, CORE_SECOND)):
            await_bytes(halves(out.at[na, nb, :, nc], which), got.at[w, kind])
    for t in range(tables):
        w = count + t
        await_bytes(ins[w], place.at[w])
        sent_along(ins[w], send_ring.at[w])
        await_bytes(outs[w].at[:, c], core_sem.at[t, 0])
        await_bytes(outs[w].at[:, nc], core_sem.at[t, 1])


def spread(shards, tables):
    count, more, ring = len(shards), len(tables), lax.axis_size("ring")
    square = (lax.axis_size("ca"), lax.axis_size("cb"), ring, 2)
    dma = pltpu.SemaphoreType.DMA
    outs = pl.pallas_call(
        functools.partial(spread_kernel, count, more),
        out_shape=[jax.ShapeDtypeStruct(square + s.shape, s.dtype) for s in shards]
        + [jax.ShapeDtypeStruct((ring, 2) + t.shape, t.dtype) for t in tables],
        in_specs=[pl.BlockSpec(memory_space=pltpu.VMEM)] * (count + more),
        out_specs=[pl.BlockSpec(memory_space=pl.ANY)] * (count + more),
        scratch_shapes=[
            dma((count, 10)), dma((count + more, 2, ring)), dma((count + more, 2, ring)), dma((count, ring)), dma((count, ring)),
            dma((count, 10)), dma((count + more,)), dma((more, 2)),
        ],
        compiler_params=pltpu.CompilerParams(collective_id=0, has_side_effects=True),
        cost_estimate=pl.CostEstimate(flops=150_000_000_000, bytes_accessed=300_000_000, transcendentals=0),
        name="spread",
    )(*shards, *tables)
    return outs[:count], outs[count:]


def collect_kernel(count, *refs):
    ring = lax.axis_size("ring")
    small, lefts, rights, refs = refs[0], (refs[1],) + (refs[2],) * (count - 2), refs[3 : count + 2], refs[count + 2 :]
    grads, matrices, (x, gain, passed), refs = refs[:3], refs[3:6], refs[6:9], refs[9:]
    outs, (input_grad, gain_out), refs = refs[:count], refs[count : count + 2], refs[count + 2 :]
    scratch, (out_a, out_b), refs = refs[: 9 * count], refs[9 * count : 9 * count + 2], refs[9 * count + 2 :]
    send, got, ring_send, ring_got, load, chunks, dn1, sums, arrived, ring_arrived, fetch, gain_send, gain_got = refs
    a, b, r, c = (lax.axis_index(n) for n in ALL)
    na, nb, nc = turn("ca", 1), turn("cb", 1), turn("core", 1)
    to_a, to_b, to_core = {"ca": na}, {"cb": nb}, {"core": nc}
    bufs = [scratch[9 * w : 9 * w + 9] for w in range(count)]
    greet([to_a, to_b, to_core] + [{"ring": turn("ring", k)} for k in range(1, ring)])

    def chunk(i, slot, w):
        rows = chunks.shape[2]
        return pltpu.make_async_copy(
            matrices[w].at[pl.ds(pl.multiple_of(i * rows, rows), rows), :], chunks.at[slot, w], fetch.at[slot, w]
        )

    steps, chunk_rows = matrices[0].shape[0] // chunks.shape[2], chunks.shape[2]

    def input_part(begin, end):
        rows = chunk_rows

        def one(i, carry):
            slot = lax.rem(i, 2)

            @pl.when(i + 1 < steps)
            def _():
                for w in range(3):
                    chunk(i + 1, 1 - slot, w).start()

            value = jnp.zeros((x.shape[0], rows), jnp.float32)
            for w in range(3):
                chunk(i, slot, w).wait()
                value = value + times_transposed(grads[w][...], chunks[slot, w])
            dn1[:, pl.ds(pl.multiple_of(i * rows, rows), rows)] = value
            return carry

        lax.fori_loop(begin, end, one, 0)

    def input_end():
        tile = 32
        sums[0] = jnp.zeros(sums.shape[1:], jnp.float32)

        def back(i, carry):
            at = pl.ds(pl.multiple_of(i * tile, tile), tile)
            v, grad = x[at, :].astype(jnp.float32), dn1[at, :]
            factor = lax.rsqrt(jnp.mean(v * v, axis=-1, keepdims=True) + EPSILON)
            weighted = grad * gain[...]
            inner = jnp.mean(weighted * v, axis=-1, keepdims=True)
            total = passed[at, :] + factor * weighted - v * (factor * factor * factor * inner)
            input_grad[at, :] = total.astype(input_grad.dtype)
            gained = grad * v * factor
            sums[0] += sum(gained[k : k + 8] for k in range(0, tile, 8))
            return carry

        lax.fori_loop(0, x.shape[0] // tile, back, 0)
        push(sums.at[0], arrived.at[0], gain_send.at[0], gain_got.at[0], to_a)

    def gain_stage(stage):
        if stage < 3:
            await_bytes(arrived.at[stage], gain_got.at[stage])
            sums[stage + 1] = sums[stage] + arrived[stage]
            if stage < 2:
                push(sums.at[stage + 1], arrived.at[stage + 1], gain_send.at[stage + 1], gain_got.at[stage + 1], (to_b, to_core)[stage])
            else:
                for k in range(1, ring):
                    push(sums.at[3], ring_arrived.at[k - 1], gain_send.at[2 + k], gain_got.at[2 + k], {"ring": turn("ring", k)})
        else:
            total = sums[3]
            for k in range(1, ring):
                await_bytes(ring_arrived.at[k - 1], gain_got.at[2 + k])
                total = total + ring_arrived[k - 1]
            gain_out[...] = total
            for k in range(3 + ring - 1):
                await_bytes(sums.at[0], gain_send.at[k])

    def half(ref, which):
        rows, cols = ref.shape[-2:]
        lead = (slice(None),) * (len(ref.shape) - 2)
        if cols > 128:
            return ref.at[(*lead, slice(None), pl.ds(which * (cols // 2), cols // 2))]
        return ref.at[(*lead, pl.ds(which * (rows // 2), rows // 2), slice(None))]

    own_a, own_b = bufs[0][:2]
    loads = (
        pltpu.make_async_copy(half(small.at[a], 0), own_a, load.at[0, 0]),
        pltpu.make_async_copy(half(small.at[:, b], 1), own_b, load.at[0, 1]),
    )

    def product(w, block, which):
        own = bufs[w][0]
        rows, cols = own.shape[1] * own.shape[2], own.shape[3]
        left = lefts[w - 1][:, pl.ds(pl.multiple_of(block * rows, rows), rows)]
        value = transposed_times(left, rights[w - 1][:, pl.ds(which * cols, cols)])
        return value.reshape(own.shape[1:])

    def sent_first(w):
        await_bytes(bufs[w][2], send.at[w, 0])
        await_bytes(bufs[w][3], send.at[w, 1])

    def first(w):
        in_a, in_b = bufs[w][2:4]
        if w == 0:
            for copy in loads:
                copy.start()
            push(half(small.at[na], 0), in_a, send.at[w, 0], got.at[w, 0], to_a)
            push(half(small.at[:, nb], 1), in_b, send.at[w, 1], got.at[w, 1], to_b)
            return
        if w > 2:
            sent_first(w - 2)

        def one_a(i, carry):
            out_a[w % 2, i] = product(w, 2 * na + i, 0).astype(out_a.dtype)
            return carry

        def one_b(i, carry):
            out_b[w % 2, i] = product(w, 2 * i + nb, 1).astype(out_b.dtype)
            return carry

        lax.fori_loop(0, 2, one_a, 0)
        push(out_a.at[w % 2], in_a, send.at[w, 0], got.at[w, 0], to_a)
        lax.fori_loop(0, 2, one_b, 0)
        push(out_b.at[w % 2], in_b, send.at[w, 1], got.at[w, 1], to_b)

    def second(w):
        own_a, own_b, in_a, in_b, in_a2, in_b2 = bufs[w][:6]
        if w == 0:
            for copy in loads:
                copy.wait()

        def one_a(i, carry):
            mine = own_a[i] if w == 0 else product(w, 2 * a + i, 0)
            own_a[i] = (mine + in_a[i].astype(jnp.float32)).astype(own_a.dtype)
            return carry

        def one_b(i, carry):
            mine = own_b[i] if w == 0 else product(w, 2 * i + b, 1)
            own_b[i] = (mine + in_b[i].astype(jnp.float32)).astype(own_b.dtype)
            return carry

        await_bytes(in_a, got.at[w, 0])
        lax.fori_loop(0, 2, one_a, 0)
        push(own_a.at[nb], in_a2, send.at[w, 2], got.at[w, 2], to_b)
        await_bytes(in_b, got.at[w, 1])
        lax.fori_loop(0, 2, one_b, 0)
        push(own_b.at[na], in_b2, send.at[w, 3], got.at[w, 3], to_a)

    def third(w):
        own_a, own_b, _, _, in_a2, in_b2, total, in_ring = bufs[w][:8]
        await_bytes(in_a2, got.at[w, 2])
        await_bytes(in_b2, got.at[w, 3])

        def one(k, carry):
            sums = [
                own[own_at, k].astype(jnp.float32) + more[k].astype(jnp.float32)
                for own, own_at, more in ((own_a, b, in_a2), (own_b, a, in_b2))
            ]
            for which in range(2):
                half(total.at[k], which)[...] = sums[which].astype(total.dtype)
            return carry

        lax.fori_loop(0, ring, one, 0)
        for k in range(1, ring):
            at = turn("ring", k)
            push(total.at[at], in_ring.at[k - 1], ring_send.at[w, k - 1], ring_got.at[w, k - 1], {"ring": at})

    def fourth(w):
        total, in_ring, final = bufs[w][6:9]
        for k in range(1, ring):
            await_bytes(in_ring.at[k - 1], ring_got.at[w, k - 1])
        if final.shape[0] == 2:
            rows = final.shape[1]
            for core in range(2):
                at = pl.ds(core * rows, rows)
                value = total[r, at, :].astype(jnp.float32)
                for k in range(ring - 1):
                    value = value + in_ring[k, at, :].astype(jnp.float32)
                final[core] = value
            cols = final.shape[2]
            there = outs[w].at[:, pl.ds(pl.multiple_of(c * cols, cols), cols)]
            push(final.at[nc], there, send.at[w, 4], got.at[w, 4], to_core)
            pltpu.make_async_copy(final.at[c], there, load.at[w, 2]).start()
        else:
            value = total[r].astype(jnp.float32)
            for k in range(ring - 1):
                value = value + in_ring[k].astype(jnp.float32)
            outs[w][...] = value

    def finish(w):
        own_a, own_b, in_a, in_b, in_a2, in_b2, total, in_ring, final = bufs[w]
        if w == 0 or w + 2 >= count:
            sent_first(w)
        await_bytes(in_a2, send.at[w, 2])
        await_bytes(in_b2, send.at[w, 3])
        for k in range(1, ring):
            await_bytes(in_ring.at[k - 1], ring_send.at[w, k - 1])
        if final.shape[0] == 2:
            await_bytes(final.at[0], send.at[w, 4])
            await_bytes(final.at[0], got.at[w, 4])
            await_bytes(final.at[0], load.at[w, 2])

    for w in range(3):
        chunk(0, 0, w).start()
    first(0)
    for step in range(max(count + 3, 9)):
        if step + 1 < count:
            first(step + 1)
        if step < count:
            second(step)
        if 0 <= step - 1 < count:
            third(step - 1)
        if 0 <= step - 2 < count:
            fourth(step - 2)
        if 1 <= step < 5:
            input_part((step - 1) * steps // 4, step * steps // 4)
        if step == 4:
            input_end()
        if step > 4:
            gain_stage(step - 5)
    for w in range(count):
        finish(w)


def collect(small, lefts, rights, grads, matrices, x, gain, passed):
    count, ring = len(rights) + 1, lax.axis_size("ring")
    chips = lax.axis_size("ca") * lax.axis_size("cb") * ring
    square = (lax.axis_size("ca"), lax.axis_size("cb"), ring)
    view = small.reshape(square + small.shape[1:])
    forms = [(*view.shape[3:], view.dtype)] + [(lefts[0].shape[1] // chips, r.shape[1], r.dtype) for r in rights]
    shapes, scratch = [], []
    for rows, cols, dtype in forms:
        piece = (rows, cols // 2) if cols > 128 else (rows // 2, cols)
        big = cols > 128
        vmem = lambda *shape: pltpu.VMEM(shape, dtype)
        scratch += [vmem(2, ring, *piece)] * 4 + [vmem(ring, *piece)] * 2
        scratch += [vmem(ring, rows, cols), vmem(ring - 1, rows, cols)]
        scratch += [pltpu.VMEM((2, rows // 2, cols) if big else (1, 8, 128), jnp.float32)]
        shapes.append(jax.ShapeDtypeStruct((rows // 2, 2 * cols) if big else (rows, cols), jnp.float32))
    scratch += [vmem(2, 2, ring, *piece)] * 2
    dma = pltpu.SemaphoreType.DMA
    vm, anywhere = pl.BlockSpec(memory_space=pltpu.VMEM), pl.BlockSpec(memory_space=pl.ANY)
    wide = (8, gain.shape[1])
    f32 = lambda *shape: pltpu.VMEM(shape, jnp.float32)
    outs = pl.pallas_call(
        functools.partial(collect_kernel, count),
        out_shape=shapes + [jax.ShapeDtypeStruct(x.shape, x.dtype), jax.ShapeDtypeStruct(wide, jnp.float32)],
        in_specs=[anywhere] + [vm] * (count + 4) + [anywhere] * 3 + [vm] * 3,
        out_specs=[vm] * (count + 2),
        scratch_shapes=scratch
        + [dma((count, 5)), dma((count, 5)), dma((count, ring - 1)), dma((count, ring - 1)), dma((count, 3))]
        + [pltpu.VMEM((2, 3, 128, x.shape[1]), x.dtype), f32(*x.shape), f32(4, *wide), f32(3, *wide), f32(ring - 1, *wide)]
        + [dma((2, 3)), dma((2 + ring,)), dma((2 + ring,))],
        compiler_params=pltpu.CompilerParams(collective_id=1, has_side_effects=True, vmem_limit_bytes=62 << 20),
        cost_estimate=pl.CostEstimate(flops=160_000_000_000, bytes_accessed=320_000_000, transcendentals=0),
        name="collect",
    )(view, *lefts, *rights, *grads, *matrices, x, gain, passed)
    return outs[1:count], outs[0], outs[count], outs[count + 1]


def dispatch_kernel(
    rows, router, hot, g_all, out, picked, grads, gates, probs,
    rows_in, g_in, picked_low, grads_low, load, store, ring_send, ring_got, place, core_send, core_got,
):
    ring = lax.axis_size("ring")
    r, c, nc = lax.axis_index("ring"), lax.axis_index("core"), turn("core", 1)
    to_core, experts = {"core": nc}, hot.shape[1]
    greet([to_core] + [{"ring": turn("ring", k)} for k in range(1, ring)])
    block_of = lambda at: out.at[at, c]

    own = pltpu.make_async_copy(rows, block_of(r), place)
    own.start()
    push(rows, block_of(r), core_send, core_got.at[r], to_core)
    own.wait()
    send_along(0, block_of(r), block_of, ring_send, ring_got)
    first = (r * 2 + c) * experts
    width = rows.shape[1]
    cols = min(512, width)

    def pick(at, core):
        source = at * 2 + core
        copies = (
            pltpu.make_async_copy(out.at[at, core], rows_in, load.at[0]),
            pltpu.make_async_copy(g_all.at[at, core], g_in, load.at[1]),
        )
        for copy in copies:
            copy.start()
        copies[0].wait()
        logits = times_transposed(router[...], rows_in[...])
        likely = jnp.exp(logits - jnp.max(logits, axis=0, keepdims=True))
        probs[source] = likely / jnp.sum(likely, axis=0, keepdims=True)
        copies[1].wait()
        for e in range(experts):
            own_probs = probs[source, pl.ds(first + e, 1), :]
            gate = jnp.sum(hot[source, e].astype(jnp.float32) * own_probs, axis=-1, keepdims=True)
            gates[e, source] = gate

            def part(i, carry):
                lanes = pl.ds(pl.multiple_of(i * cols, cols), cols)
                chosen = hot[source, e]
                picked_low[e, :, lanes] = matmul(chosen, rows_in[:, lanes]).astype(picked_low.dtype)
                grads_low[e, :, lanes] = (matmul(chosen, g_in[:, lanes]) * gate).astype(grads_low.dtype)
                return carry

            lax.fori_loop(0, width // cols, part, 0)
        stores = (
            pltpu.make_async_copy(picked_low, picked.at[:, source], store.at[0]),
            pltpu.make_async_copy(grads_low, grads.at[:, source], store.at[1]),
        )
        for copy in stores:
            copy.start()
        for copy in stores:
            copy.wait()

    pick(r, c)
    await_bytes(out.at[r, nc], core_got.at[r])
    pick(r, nc)

    def step_on(step, carry):
        take_along(step, block_of, ring_got, lambda at: None)

        @pl.when(step + 1 < ring - 1)
        def _():
            send_along(step + 1, None, block_of, ring_send, ring_got)

        for _, comes, _, block, _, _ in along(step):

            @pl.when(comes)
            def _(block=block):
                push(block_of(block), block_of(block), core_send, core_got.at[block], to_core)

        def four(k, carry):
            side, other = k // 2, lax.rem(k, 2)
            (_, comes0, _, block0, _, _), (_, comes1, _, block1, _, _) = along(step)
            block = jnp.where(side == 0, block0, block1)
            comes = ((side == 0) & comes0) | ((side == 1) & comes1)
            core = lax.rem(c + other, 2)

            @pl.when(comes & (other == 1))
            def _():
                await_bytes(out.at[block, nc], core_got.at[block])

            @pl.when(comes)
            def _():
                pick(block, core)

            return carry

        lax.fori_loop(0, 4, four, 0)
        return carry

    lax.fori_loop(0, ring - 1, step_on, 0)
    sent_along(rows, ring_send)
    await_bytes(out.at[:, c], core_send)


def dispatch(rows, router, hot, g_all):
    ring, dma = lax.axis_size("ring"), pltpu.SemaphoreType.DMA
    sources, experts, slots, count = hot.shape
    width = rows.shape[1]
    low = lambda *shape: jax.ShapeDtypeStruct(shape, rows.dtype)
    f32 = lambda *shape: jax.ShapeDtypeStruct(shape, jnp.float32)
    vm, anywhere = pl.BlockSpec(memory_space=pltpu.VMEM), pl.BlockSpec(memory_space=pl.ANY)
    block = pltpu.VMEM((experts, slots, width), rows.dtype)
    chosen = (experts, sources, slots, width)
    return pl.pallas_call(
        dispatch_kernel,
        out_shape=[
            low(ring, 2, count, width), low(*chosen), low(*chosen), f32(experts, sources, slots, 1),
            f32(sources, router.shape[0], count),
        ],
        in_specs=[vm, vm, vm, anywhere],
        out_specs=[anywhere, anywhere, anywhere, vm, vm],
        scratch_shapes=[pltpu.VMEM(rows.shape, rows.dtype)] * 2
        + [block, block]
        + [dma((2,)), dma((2,)), dma((2, ring)), dma((2, ring)), dma, dma, dma((ring,))],
        compiler_params=pltpu.CompilerParams(collective_id=2, has_side_effects=True, vmem_limit_bytes=56 << 20),
        cost_estimate=pl.CostEstimate(flops=1_000_000, bytes_accessed=10_000, transcendentals=0),
        name="dispatch",
    )(rows, router, hot, g_all)


def give_back_kernel(
    hot, logit, logit_turned, router, pairs, mixed, n2, out, mixed_out, router_part,
    sums, chain_in, to_core, pair_in, mixed_in, mixed_low, n2_in,
    load, core_send, core_got, chain_send, chain_got, load_more, store,
):
    ring, pieces, rows, width = sums.shape
    sources, experts = hot.shape[:2]
    r, c, nc = lax.axis_index("ring"), lax.axis_index("core"), turn("core", 1)
    to_next, to_last = {"ring": turn("ring", 1)}, {"ring": turn("ring", ring - 1)}
    greet([{"core": nc}] + [{"ring": turn("ring", k)} for k in range(1, ring)])
    cols, tile = min(512, width), 32

    def whose(i):
        return (1 - i % 2) * (ring - 1 - i // 2) + (i % 2) * (i // 2)

    def fetch(i, j):
        return pltpu.make_async_copy(pairs.at[:, whose(i) * 2 + (nc, c)[j]], pair_in.at[j], load.at[j])

    def put_back(source, ref, lanes):
        return sum(matmul(hot[source, e], ref[e, :, lanes]) for e in range(experts))

    def block(source, j, into, more):
        def part(k, carry):
            lanes = pl.ds(pl.multiple_of(k * cols, cols), cols)
            value = put_back(source, pair_in.at[j], lanes) + matmul(logit[source], router[:, lanes])
            for piece in range(pieces):
                got = value[piece * rows : (piece + 1) * rows]
                if more is not None:
                    got = got + more[piece, :, lanes].astype(jnp.float32)
                into[piece, :, lanes] = got.astype(into.dtype)
            return carry

        lax.fori_loop(0, width // cols, part, 0)

    def fetch_beside(source):
        at = lax.rem(source, 2)
        return (
            pltpu.make_async_copy(mixed.at[:, source], mixed_in.at[at], load_more.at[at, 0]),
            pltpu.make_async_copy(n2.at[source], n2_in.at[at], load_more.at[at, 1]),
        )

    def beside(source):
        at = lax.rem(source, 2)

        @pl.when(source + 1 < sources)
        def _():
            for copy in fetch_beside(source + 1):
                copy.start()

        for copy in fetch_beside(source):
            copy.wait()

        @pl.when(source > 0)
        def _():
            await_bytes(mixed_low, store)

        def part(k, carry):
            lanes = pl.ds(pl.multiple_of(k * cols, cols), cols)
            mixed_low[:, lanes] = put_back(source, mixed_in.at[at], lanes).astype(mixed_low.dtype)
            router_part[:, lanes] += matmul(logit_turned[source], n2_in[at, :, lanes])
            return carry

        lax.fori_loop(0, width // cols, part, 0)
        pltpu.make_async_copy(mixed_low, mixed_out.at[source], store).start()

    def slot(side, d, at):
        return d if side == 0 else jnp.where(d == at, ring, d)

    def pass_on(side, step, d, piece, to):
        there = chain_in.at[slot(side, d, r - 1), piece]
        push(sums.at[d, piece], there, chain_send.at[side, step, piece], chain_got.at[side, step, piece], to)

    router_part[...] = jnp.zeros_like(router_part)
    fetch(0, 0).start()
    fetch(0, 1).start()
    for copy in fetch_beside(0):
        copy.start()

    def start(i, carry):
        d = whose(i)
        outgoing = to_core.at[lax.rem(i, 2)]
        fetch(i, 0).wait()

        @pl.when(i >= 2)
        def _():
            await_bytes(outgoing, core_send.at[lax.rem(i, 2)])

        block(d * 2 + nc, 0, outgoing, None)
        push(outgoing, sums.at[d], core_send.at[lax.rem(i, 2)], core_got.at[d], {"core": nc})
        fetch(i, 1).wait()
        await_bytes(sums.at[d], core_got.at[d])
        block(d * 2 + c, 1, sums.at[d], sums.at[d])
        for piece in range(pieces):

            @pl.when((r == 0) & (d != r))
            def _():
                pass_on(0, ring - 1 - d, d, piece, to_next)

            @pl.when((r == ring - 1) & (d != r))
            def _():
                pass_on(1, d, d, piece, to_last)

        @pl.when(i + 1 < ring)
        def _():
            fetch(i + 1, 0).start()
            fetch(i + 1, 1).start()

        beside(i)
        return carry

    lax.fori_loop(0, ring, start, 0)

    def sides(time):
        up, down = time - r, time - (ring - 1 - r)
        return (
            ((r >= 1) & (up >= 0), jnp.maximum(up, 0), ring - 1 - jnp.maximum(up, 0), to_next, 0),
            ((r + 1 < ring) & (down >= 0), jnp.maximum(down, 0), jnp.maximum(down, 0), to_last, 1),
        )

    def on(time, carry):
        for piece in range(pieces):
            for comes, step, d, to, side in sides(time):

                @pl.when(comes)
                def _(step=step, d=d, to=to, side=side):
                    arrived = chain_in.at[slot(side, d, r), piece]
                    await_bytes(arrived, chain_got.at[side, step, piece])

                    def one(k, carry):
                        at = pl.ds(pl.multiple_of(k * tile, tile), tile)
                        total = sums[d, piece, at].astype(jnp.float32) + arrived[at].astype(jnp.float32)
                        sums[d, piece, at] = total.astype(sums.dtype)
                        return carry

                    lax.fori_loop(0, rows // tile, one, 0)

                    @pl.when(time < ring - 1)
                    def _():
                        pass_on(side, step, d, piece, to)

        @pl.when(time < ring - 1)
        def _():
            beside(ring + time - 1)

        return carry

    def rest(source, carry):
        beside(source)
        return carry

    lax.fori_loop(1, ring - 1, on, 0)
    lax.fori_loop(2 * ring - 2, sources, rest, 0)
    on(ring - 1, 0)
    await_bytes(mixed_low, store)

    def total(k, carry):
        at = pl.ds(pl.multiple_of(k * tile, tile), tile)
        for piece in range(pieces):
            out[pl.ds(pl.multiple_of(piece * rows + k * tile, tile), tile), :] = sums[r, piece, at].astype(jnp.float32)
        return carry

    lax.fori_loop(0, rows // tile, total, 0)
    for k in range(2):
        await_bytes(to_core.at[k], core_send.at[k])
    for step in range(ring - 1):
        for piece in range(pieces):
            for sent, side in ((r + step < ring - 1, 0), (step < r, 1)):

                @pl.when(sent)
                def _(side=side):
                    await_bytes(sums.at[0, 0], chain_send.at[side, step, piece])


def give_back(hot, logit, router, pairs, mixed, n2):
    ring, dma, pieces = lax.axis_size("ring"), pltpu.SemaphoreType.DMA, 2
    experts, sources, slots, width = pairs.shape
    rows, all_experts = hot.shape[2], router.shape[0]
    vm, anywhere = pl.BlockSpec(memory_space=pltpu.VMEM), pl.BlockSpec(memory_space=pl.ANY)
    low = lambda *shape: pltpu.VMEM(shape, pairs.dtype)
    block = lambda n: low(n, pieces, rows // pieces, width)
    chain = dma((2, ring, pieces))
    return pl.pallas_call(
        give_back_kernel,
        out_shape=[
            jax.ShapeDtypeStruct((rows, width), jnp.float32),
            jax.ShapeDtypeStruct((sources, rows, width), pairs.dtype),
            jax.ShapeDtypeStruct((all_experts, width), jnp.float32),
        ],
        in_specs=[vm] * 4 + [anywhere] * 3,
        out_specs=[vm, anywhere, vm],
        scratch_shapes=[block(ring), block(ring + 1), block(2), low(2, experts, slots, width), low(2, experts, slots, width)]
        + [low(rows, width), low(2, rows, width)]
        + [dma((2,)), dma((2,)), dma((ring,)), chain, chain, dma((2, 2)), dma],
        compiler_params=pltpu.CompilerParams(collective_id=3, has_side_effects=True, vmem_limit_bytes=60 << 20),
        cost_estimate=pl.CostEstimate(flops=100_000_000_000, bytes_accessed=200_000_000, transcendentals=0),
        name="give_back",
    )(hot, logit, logit.transpose(0, 2, 1), router, pairs, mixed, n2)


def matmul(left, right):
    return jnp.dot(left, right, preferred_element_type=jnp.float32)


def times_transposed(left, right):
    return lax.dot_general(
        left, right, (((1,), (1,)), ((), ())), preferred_element_type=jnp.float32
    )


def transposed_times(left, right):
    return lax.dot_general(
        left, right, (((0,), (0,)), ((), ())), preferred_element_type=jnp.float32
    )


def corners():
    return ((0, 1), (1, 0), (1, 1))


def corner(da, db):
    pa, pb = turn("ca", da), turn("cb", db)
    return 2 * pa + pb, {"ca": pa, "cb": pb}


def rows_to_heads(src, dst, send, got, place):
    rows, width = src.shape[0], dst.shape[1]
    me, _ = corner(0, 0)
    there = dst.at[pl.ds(pl.multiple_of(me * rows, rows), rows), :]
    for i, (da, db) in enumerate(corners()):
        peer, to = corner(da, db)
        push(src.at[:, pl.ds(pl.multiple_of(peer * width, width), width)], there, send.at[i], got.at[i], to)
    pltpu.make_async_copy(src.at[:, pl.ds(pl.multiple_of(me * width, width), width)], there, place).start()


def wait_heads(src, dst, got, place):
    rows = src.shape[0]
    here = lambda at: dst.at[pl.ds(pl.multiple_of(at * rows, rows), rows), :]
    await_bytes(here(corner(0, 0)[0]), place)
    for i, (da, db) in enumerate(corners()):
        await_bytes(here(corner(da, db)[0]), got.at[i])


def swap_halves(v):
    return pltpu.roll(v, HD // 2, 1)


def norm_and_turn(raw, gain, cosine, sine, out):
    rows, width = raw.shape
    tile = 32

    def part(i, carry):
        at = pl.ds(pl.multiple_of(i * tile, tile), tile)
        value = raw[at, :]
        factor = lax.rsqrt(jnp.mean(value * value, axis=-1, keepdims=True) + EPSILON)
        for h in range(width // HD):
            lanes = pl.ds(h * HD, HD)
            v = raw[at, lanes] * factor * gain[:, lanes]
            out[at, lanes] = (v * cosine[at, :] + swap_halves(v) * sine[at, :]).astype(out.dtype)
        return carry

    lax.fori_loop(0, rows // tile, part, 0)


def norm_and_turn_back(grad, raw, gain, cosine, sine, out, gain_grad, turned):
    rows, width = raw.shape
    tile = 32
    gain_grad[...] = jnp.zeros_like(gain_grad)

    def part(i, carry):
        at = pl.ds(pl.multiple_of(i * tile, tile), tile)
        value = raw[at, :]
        factor = lax.rsqrt(jnp.mean(value * value, axis=-1, keepdims=True) + EPSILON)
        inner = jnp.zeros((tile, HD), jnp.float32)
        for h in range(width // HD):
            lanes = pl.ds(h * HD, HD)
            g = grad[at, lanes].astype(jnp.float32)
            g = g * cosine[at, :] - swap_halves(g) * sine[at, :]
            turned[:, lanes] = g
            inner = inner + g * gain[:, lanes] * raw[at, lanes]
        inner = jnp.sum(inner, axis=-1, keepdims=True) * (factor * factor * factor / width)
        for h in range(width // HD):
            lanes = pl.ds(h * HD, HD)
            g, v = turned[:, lanes], raw[at, lanes]
            out[at, lanes] = (factor * (g * gain[:, lanes]) - v * inner).astype(out.dtype)
            gained = g * v * factor
            gain_grad[:, lanes] += sum(gained[k : k + 8] for k in range(0, tile, 8))
        return carry

    lax.fori_loop(0, rows // tile, part, 0)


def attend_kernel(scale, q_raw, k_raw, v, q_gain, k_gain, cosine, sine, keep, o, qh, kh, vh, logs, q, k, oh, send, got, place, send_o, got_o, place_o):
    rows, width = v.shape[0], qh.shape[1]
    greet([corner(da, db)[1] for da, db in corners()])
    pairs = ((v, vh), (k, kh), (q, qh))
    rows_to_heads(v, vh, send.at[0], got.at[0], place.at[0])
    norm_and_turn(k_raw, k_gain, cosine, sine, k)
    rows_to_heads(k, kh, send.at[1], got.at[1], place.at[1])
    norm_and_turn(q_raw, q_gain, cosine, sine, q)
    rows_to_heads(q, qh, send.at[2], got.at[2], place.at[2])
    for i, (src, dst) in enumerate(pairs):
        wait_heads(src, dst, got.at[i], place.at[i])
    me, _ = corner(0, 0)
    tile = 128
    mine = pl.ds(pl.multiple_of(me * width, width), width)

    def block(at_block):
        def part(i, carry):
            at = pl.ds(pl.multiple_of(at_block * rows + i * tile, tile), tile)
            for h in range(width // HD):
                lanes = pl.ds(h * HD, HD)
                s = times_transposed(qh[at, lanes], kh[:, lanes]) * scale
                s = jnp.where(keep[...] > 0.0, s, NEG_FILL)
                peak = jnp.max(s, axis=-1, keepdims=True)
                p = jnp.exp(s - peak)
                total = jnp.sum(p, axis=-1, keepdims=True)
                logs[h, at, :] = peak + jnp.log(total)
                low = (p * (1.0 / total)).astype(jnp.bfloat16)
                oh[at, lanes] = matmul(low, vh[:, lanes]).astype(jnp.bfloat16)
            return carry

        lax.fori_loop(0, rows // tile, part, 0)

    for i, (da, db) in enumerate(corners()):
        peer, to = corner(da, db)
        block(peer)
        push(oh.at[pl.ds(pl.multiple_of(peer * rows, rows), rows), :], o.at[:, mine], send_o.at[i], got_o.at[i], to)
    block(me)
    pltpu.make_async_copy(oh.at[pl.ds(pl.multiple_of(me * rows, rows), rows), :], o.at[:, mine], place_o).start()
    pltpu.make_async_copy(oh.at[pl.ds(pl.multiple_of(me * rows, rows), rows), :], o.at[:, mine], place_o).wait()
    piece = o.at[:, mine]
    for i in range(3):
        await_bytes(piece, got_o.at[i])
        await_bytes(piece, send_o.at[i])
        for j in range(3):
            await_bytes(piece, send.at[j, i])


def attend(q_raw, k_raw, v, q_gain, k_gain, cosine, sine, keep, scale):
    rows, width = v.shape
    chips = lax.axis_size("ca") * lax.axis_size("cb")
    heads = jax.ShapeDtypeStruct((rows * chips, width // chips), v.dtype)
    vm, dma = pl.BlockSpec(memory_space=pltpu.VMEM), pltpu.SemaphoreType.DMA
    return pl.pallas_call(
        functools.partial(attend_kernel, scale),
        out_shape=[jax.ShapeDtypeStruct(v.shape, v.dtype), heads, heads, heads]
        + [jax.ShapeDtypeStruct((width // chips // HD, rows * chips, 1), jnp.float32)],
        in_specs=[vm] * 8,
        out_specs=[vm] * 5,
        scratch_shapes=[pltpu.VMEM(v.shape, v.dtype)] * 2 + [pltpu.VMEM(heads.shape, v.dtype)]
        + [dma((3, 3)), dma((3, 3)), dma((3,)), dma((3,)), dma((3,)), dma],
        compiler_params=pltpu.CompilerParams(collective_id=4, has_side_effects=True, vmem_limit_bytes=48 << 20),
        cost_estimate=pl.CostEstimate(flops=1_000_000, bytes_accessed=10_000, transcendentals=0),
        name="attend",
    )(q_raw, k_raw, v, q_gain, k_gain, cosine, sine, keep)


def attend_back_kernel(
    scale, do, qh, kh, vh, logs, keep, q_raw, k_raw, q_gain, k_gain, cosine, sine,
    dq_raw, dk_raw, dv, q_gain_grad, k_gain_grad,
    doh, dqh, dkh, dvh, dq, dk, turned, send, got, place, send_g, got_g, place_g,
):
    rows, width = do.shape[0], qh.shape[1]
    greet([corner(da, db)[1] for da, db in corners()])
    rows_to_heads(do, doh, send, got, place)
    wait_heads(do, doh, got, place)
    me, _ = corner(0, 0)
    tile, total_rows = 128, qh.shape[0]
    grads = ((dqh, dq), (dkh, dk), (dvh, dv))

    def one_head(h):
        lanes = pl.ds(h * HD, HD)

        def part(i, carry):
            dk_sum, dv_sum = carry
            at = pl.ds(pl.multiple_of(i * tile, tile), tile)
            qb, db, kb, vb = qh[at, lanes], doh[at, lanes], kh[:, lanes], vh[:, lanes]
            s = times_transposed(qb, kb) * scale
            s = jnp.where(keep[...] > 0.0, s, NEG_FILL)
            p = jnp.exp(s - logs[h, at, :])
            dp = times_transposed(db, vb)
            ds = (p * (dp - jnp.sum(dp * p, axis=-1, keepdims=True))).astype(jnp.bfloat16)
            dqh[at, lanes] = (matmul(ds, kb) * scale).astype(jnp.bfloat16)
            dk_sum = dk_sum + transposed_times(ds, qb)
            dv_sum = dv_sum + transposed_times(p.astype(jnp.bfloat16), db)
            return dk_sum, dv_sum

        zero = jnp.zeros((total_rows, HD), jnp.float32)
        dk_sum, dv_sum = lax.fori_loop(0, total_rows // tile, part, (zero, zero))
        dkh[:, lanes] = (dk_sum * scale).astype(jnp.bfloat16)
        dvh[:, lanes] = dv_sum.astype(jnp.bfloat16)

    for h in range(width // HD):
        one_head(h)
        lanes = pl.ds(h * HD, HD)
        here = pl.ds(pl.multiple_of(me * width + h * HD, HD), HD)
        for g, (src, dst) in enumerate(grads):
            for i, (da, db) in enumerate(corners()):
                peer, to = corner(da, db)
                push(src.at[pl.ds(pl.multiple_of(peer * rows, rows), rows), lanes], dst.at[:, here], send_g.at[g, i, h], got_g.at[g, i, h], to)
            own = src.at[pl.ds(pl.multiple_of(me * rows, rows), rows), lanes]
            pltpu.make_async_copy(own, dst.at[:, here], place_g.at[g, h]).start()
    piece = dq.at[:, pl.ds(0, HD)]
    for h in range(width // HD):
        for g in range(3):
            await_bytes(piece, place_g.at[g, h])
            for i in range(3):
                await_bytes(piece, send_g.at[g, i, h])
                await_bytes(piece, got_g.at[g, i, h])
    for i in range(3):
        await_bytes(do.at[:, pl.ds(0, width)], send.at[i])
    norm_and_turn_back(dk, k_raw, k_gain, cosine, sine, dk_raw, k_gain_grad, turned)
    norm_and_turn_back(dq, q_raw, q_gain, cosine, sine, dq_raw, q_gain_grad, turned)


def attend_back(do, qh, kh, vh, logs, keep, q_raw, k_raw, q_gain, k_gain, cosine, sine, scale):
    heads = qh.shape[1] // HD
    vm, dma = pl.BlockSpec(memory_space=pltpu.VMEM), pltpu.SemaphoreType.DMA
    return pl.pallas_call(
        functools.partial(attend_back_kernel, scale),
        out_shape=[jax.ShapeDtypeStruct(do.shape, do.dtype)] * 3 + [jax.ShapeDtypeStruct((8, do.shape[1]), jnp.float32)] * 2,
        in_specs=[vm] * 12,
        out_specs=[vm] * 5,
        scratch_shapes=[pltpu.VMEM(qh.shape, qh.dtype)] * 4
        + [pltpu.VMEM(do.shape, do.dtype)] * 2
        + [pltpu.VMEM((32, do.shape[1]), jnp.float32)]
        + [dma((3,)), dma((3,)), dma, dma((3, 3, heads)), dma((3, 3, heads)), dma((3, heads))],
        compiler_params=pltpu.CompilerParams(collective_id=5, has_side_effects=True, vmem_limit_bytes=56 << 20),
        cost_estimate=pl.CostEstimate(flops=50_000_000_000, bytes_accessed=10_000_000, transcendentals=0),
        name="attend_back",
    )(do, qh, kh, vh, logs, keep, q_raw, k_raw, q_gain, k_gain, cosine, sine)


def join_kernel(own, from_b, from_a, first, second, out, held, load, store):
    experts, units = own.shape[:2]
    a, b = lax.axis_index("ca"), lax.axis_index("cb")
    na, nb = turn("ca", 1), turn("cb", 1)
    loads, stores = [], []
    for piece, (p, q) in enumerate(((a, b), (a, nb), (na, b), (na, nb))):
        for e in range(experts):
            if piece < 3:
                src = (own, from_b, from_a)[piece].at[e]
            else:
                src = first.at[e] if e < experts // 2 else second.at[e - experts // 2]
            here = held.at[piece, e]
            loads.append(pltpu.make_async_copy(src, here, load.at[piece, e]))
            at = pl.ds(pl.multiple_of((2 * p + q) * units, units), units)
            stores.append(pltpu.make_async_copy(here, out.at[e, at, :], store.at[piece, e]))
    for copy in loads:
        copy.start()
    for fetch, copy in zip(loads, stores):
        fetch.wait()
        copy.start()
    for copy in stores:
        copy.wait()


def join(own, from_b, from_a, first, second):
    experts, units, width = own.shape
    anywhere, dma = pl.BlockSpec(memory_space=pl.ANY), pltpu.SemaphoreType.DMA((4, experts))
    return pl.pallas_call(
        join_kernel,
        out_shape=jax.ShapeDtypeStruct((experts, 4 * units, width), own.dtype),
        in_specs=[anywhere] * 5,
        out_specs=anywhere,
        scratch_shapes=[pltpu.VMEM((4, experts, units, width), own.dtype), dma, dma],
        cost_estimate=pl.CostEstimate(flops=0, bytes_accessed=8 * experts * units * width * 2, transcendentals=0),
        name="join",
    )(own, from_b, from_a, first, second)


def norm_rows(values, gain):
    factor = lax.rsqrt(jnp.mean(values * values, axis=-1, keepdims=True) + EPSILON)
    return (values * factor * gain, factor)


def norm_back(grad, values, factor, gain):
    weighted = grad * gain
    inner = jnp.mean(weighted * values, axis=-1, keepdims=True)
    return (factor * weighted - values * factor**3 * inner, jnp.sum(grad * values * factor, axis=0))


def rotary_tables(positions, head_dim):
    half_dim = head_dim // 2
    frequency = jnp.exp(-math.log(ROPE_THETA) * jnp.arange(half_dim, dtype=jnp.float32) / half_dim)
    angles = positions.astype(jnp.float32)[:, None] * frequency[None, :]
    return (jnp.cos(angles), jnp.sin(angles))


def local(
    tokens, cotangent, lengths, expert_ids, query_weight, key_weight, value_weight, out_weight,
    router_weight, first_gain, second_gain, query_gain, key_gain, gate_weight, up_weight, down_weight,
):
    token_count = tokens.shape[1]
    model_width = tokens.shape[2]
    head_dim = HD
    top_count = expert_ids.shape[2]
    experts = router_weight.shape[1]
    local_experts = gate_weight.shape[0]
    ctx_size = lax.axis_size(CTX)
    sources = lax.axis_size(EXP)
    capacity = max(2, -(-(token_count * top_count * 9) // (experts * 8)))
    score_scale = 1.0 / math.sqrt(head_dim)
    seq_len = token_count * ctx_size

    inputs = tokens[0].astype(jnp.float32)
    length = lengths[0]
    positions = lax.axis_index(CTX) * token_count + jnp.arange(token_count, dtype=jnp.int32)
    row_valid = positions < length
    row_valid = row_valid.astype(jnp.float32)[:, None]
    key_valid = jnp.arange(seq_len, dtype=jnp.int32) < length
    grad_total_low = (cotangent[0].astype(jnp.float32) * row_valid).astype(jnp.bfloat16)
    grad_total = grad_total_low.astype(jnp.float32)

    rows_each = query_weight.shape[0]
    packed = jnp.concatenate(
        [g.reshape(-1) for g in (first_gain, second_gain, query_gain, key_gain)] + [router_weight.reshape(-1)]
    )
    small = jnp.pad(packed, (0, -packed.size % 2048)).reshape(-1, 128)
    ids_low = expert_ids[0].astype(jnp.bfloat16).reshape(-1, 128)
    gathered, (ids_all, g_all) = spread([query_weight, key_weight, value_weight, out_weight, small], [ids_low, grad_total_low])
    full_query, full_key, full_value, full_out = (w.reshape(model_width, -1) for w in gathered[:4])
    smalls = gathered[4].reshape(-1, small.size)
    gains = [smalls[:, i * rows_each : (i + 1) * rows_each].reshape(-1).astype(jnp.float32) for i in range(4)]
    gain_first, gain_second, gain_queries, gain_keys = gains
    full_router = smalls[:, 4 * rows_each : packed.size].reshape(model_width, experts)
    ids_all = ids_all.reshape(sources, token_count, top_count).astype(jnp.int32)
    full_value, gate_weight, up_weight = lax.optimization_barrier((full_value, gate_weight, up_weight))
    gate_all, up_all = (lax.all_gather(w, CTX, axis=2, tiled=True) for w in (gate_weight, up_weight))
    cosine, sine = rotary_tables(positions, head_dim)
    normed_one, factor_one = norm_rows(inputs, gain_first)
    normed_one_low = normed_one.astype(jnp.bfloat16)
    query_raw = matmul(normed_one_low, full_query)
    key_raw = matmul(normed_one_low, full_key)
    value_low = matmul(normed_one_low, full_value).astype(jnp.bfloat16)
    keep = key_valid.astype(jnp.float32)[None, :]
    turns = (jnp.concatenate([cosine, cosine], axis=1), jnp.concatenate([-sine, sine], axis=1))
    row = lambda g: g.reshape(1, model_width)
    shared = (row(gain_queries), row(gain_keys), *turns)
    attended_low, *saved = attend(query_raw, key_raw, value_low, *shared, keep, score_scale)
    flip = lambda v, axis: lax.ppermute(v, axis, [(0, 1), (1, 0)])
    hidden_state = inputs + matmul(attended_low, full_out)
    normed_two, factor_two = norm_rows(hidden_state, gain_second)
    normed_two_low = normed_two.astype(jnp.bfloat16)

    first_expert = lax.axis_index(EXP) * local_experts
    own_experts = first_expert + jnp.arange(local_experts, dtype=jnp.int32)
    mask = jnp.any(ids_all[:, None, :, :] == own_experts[None, :, None, None], axis=-1)
    before = (jnp.arange(token_count)[:, None] < jnp.arange(token_count)[None, :]).astype(jnp.bfloat16)
    ranks = jnp.einsum("seu,ut->set", mask.astype(jnp.bfloat16), before, preferred_element_type=jnp.float32)
    slots = jnp.arange(capacity, dtype=jnp.float32)
    hot = (mask[:, :, None, :] & (ranks[:, :, None, :] == slots[None, None, :, None])).astype(jnp.bfloat16)
    router_turned = full_router.T
    n2_all, x, de, row_gate, probs = dispatch(normed_two_low, router_turned, hot, g_all)
    n2_all = n2_all.reshape(sources, token_count, model_width)
    probs = probs.transpose(0, 2, 1).reshape(-1, experts)
    hot32 = hot.astype(jnp.float32)
    x, gate_all, down_weight = lax.optimization_barrier((x, gate_all, down_weight))
    down_b, down_a = flip(down_weight, "cb"), flip(down_weight, "ca")
    first_half = local_experts // 2
    down_corner = [flip(down_b[:first_half], "ca"), flip(down_a[first_half:], "cb")]
    ee = lambda eq, a, b: jnp.einsum(eq, a, b, preferred_element_type=jnp.float32)
    gp = ee("escd,edf->escf", x, gate_all)
    up = ee("escd,edf->escf", x, up_all)
    sig = jax.nn.sigmoid(gp)
    hid = (gp * sig * up).astype(jnp.bfloat16)
    down_part = ee("escf,escd->efd", hid, de).astype(jnp.bfloat16)
    *down_corner, down_part = lax.optimization_barrier((*down_corner, down_part))
    down_all = join(down_weight, down_b, down_a, *down_corner)
    eo = ee("escf,efd->escd", hid, down_all).astype(jnp.bfloat16)
    gained = jnp.sum(de.astype(jnp.float32) * eo.astype(jnp.float32), axis=-1)
    mixed_rows = (row_gate * eo.astype(jnp.float32)).astype(jnp.bfloat16)
    dhid = ee("escd,efd->escf", de, down_all)
    dgp = (dhid * up * sig * (1.0 + gp * (1.0 - sig))).astype(jnp.bfloat16)
    dup = (dhid * gp * sig).astype(jnp.bfloat16)
    gate_part = ee("escd,escf->edf", x, dgp)
    up_part = ee("escd,escf->edf", x, dup)
    parts = [v.astype(jnp.bfloat16) for v in (down_part, gate_part, up_part)]
    dgp, dup, *_ = lax.optimization_barrier((dgp, dup, *parts))
    rs_ctx = lambda v, a: lax.psum_scatter(v, CTX, scatter_dimension=a, tiled=True)
    down_grad, gate_grad, up_grad = rs_ctx(parts[0], 1), rs_ctx(parts[1], 2), rs_ctx(parts[2], 2)
    dpair = (ee("escf,edf->escd", dgp, gate_all) + ee("escf,edf->escd", dup, up_all)).astype(jnp.bfloat16)

    gained = jnp.sum(hot32 * gained.transpose(1, 0, 2)[..., None], axis=2)
    gained = gained.transpose(0, 2, 1).reshape(-1, local_experts)
    onto = (jnp.arange(experts)[None, :] == own_experts[:, None]).astype(jnp.float32)
    weighed = jnp.sum(gained[:, :, None] * onto[None], axis=1)
    dlogit_low = (weighed - probs * jnp.sum(gained, axis=-1, keepdims=True)).astype(jnp.bfloat16)
    dpair, down_grad = lax.optimization_barrier((dpair, down_grad))
    dn2, mixed_part, router_part = give_back(
        hot.transpose(0, 1, 3, 2), dlogit_low.reshape(sources, token_count, experts), router_turned, dpair, mixed_rows, n2_all
    )
    router_part = router_part.T
    dn2, gate_grad = lax.optimization_barrier((dn2, gate_grad))
    mixed = lax.psum_scatter(mixed_part.reshape(-1, model_width), EXP, scatter_dimension=0, tiled=True)

    dh_norm, gain_second_part = norm_back(dn2, hidden_state, factor_two, gain_second)
    grad_hidden = grad_total + dh_norm
    dh_low = grad_hidden.astype(jnp.bfloat16)
    out_part = transposed_times(attended_low, dh_low)
    d_att = times_transposed(dh_low, full_out).astype(jnp.bfloat16)
    dq_low, dk_low, dv_low, *gain_parts = attend_back(d_att, *saved, keep, query_raw, key_raw, *shared, score_scale)
    dv_low, up_grad = lax.optimization_barrier((dv_low, up_grad))
    gain_queries_part, gain_keys_part = (jnp.sum(g, axis=0) for g in gain_parts)
    core = lax.axis_index("core")
    swap = lambda v: lax.ppermute(v, "core", [(0, 1), (1, 0)])

    def columns_of_core(v):
        width = model_width // 2
        mine = lax.dynamic_slice_in_dim(v, core * width, width, 1)
        other = lax.dynamic_slice_in_dim(v, (1 - core) * width, width, 1)
        return jnp.concatenate([mine, swap(other)], axis=0)

    both = lambda v: jnp.concatenate([v, swap(v)], axis=0)
    n1_both, att_both = both(normed_one_low), both(attended_low)
    rights = [columns_of_core(v) for v in (dh_low, dv_low, dq_low, dk_low)]
    split = lambda v: v.reshape(ctx_size * sources // 2, 2, -1)
    small_parts = jnp.concatenate(
        [split(v) for v in (gain_second_part, gain_queries_part, gain_keys_part, router_part)], axis=2
    )
    small_parts = jnp.pad(small_parts, ((0, 0), (0, 0), (0, -small_parts.shape[2] % 2048)))
    small_parts = lax.dynamic_index_in_dim(small_parts, core, 1, False) + swap(lax.dynamic_index_in_dim(small_parts, 1 - core, 1, False))
    weight_grads, small_grads, input_grad, gain_first_sums = collect(
        small_parts.reshape(ctx_size * sources // 2, -1, 128), (att_both, n1_both), rights, (dq_low, dk_low, dv_low),
        (full_query, full_key, full_value), tokens[0], row(gain_first), grad_hidden,
    )
    weight_grads, mixed, gate_grad, up_grad, down_grad = lax.optimization_barrier(
        (list(weight_grads), mixed, gate_grad, up_grad, down_grad)
    )
    layer_out = (row_valid * (hidden_state + mixed.astype(jnp.float32))).astype(jnp.bfloat16)
    gate_grad, up_grad, down_grad = (v.astype(jnp.float32) for v in (gate_grad, up_grad, down_grad))
    weight_grads = [weight_grads[k] for k in (2, 3, 1, 0)]
    small_grads = small_grads.reshape(-1)
    gain_grads = [lax.dynamic_slice_in_dim(jnp.sum(gain_first_sums, axis=0), lax.axis_index(ALL) * rows_each, rows_each)]
    gain_grads += [small_grads[i * rows_each : (i + 1) * rows_each] for i in range(3)]
    router_grad = small_grads[3 * rows_each : packed.size - rows_each].reshape(rows_each, experts)
    return (layer_out[None], input_grad[None], *weight_grads, router_grad, *gain_grads, gate_grad, up_grad, down_grad)


def solution(mesh):
    ctx, exp = mesh.devices.shape
    fine = Mesh(mesh.devices.reshape(2, ctx // 2, exp // 2, 2), ("ca", "cb", "ring", "core"))
    rows = P(EXP, CTX, None)
    flat2, flat1 = P(ALL, None), P(ALL)
    placed = (rows, rows, P(EXP), rows) + (flat2,) * 5 + (flat1,) * 4 + (P(EXP, None, CTX),) * 2 + (P(EXP, CTX, None),)
    outs = (rows, rows) + (flat2,) * 5 + (flat1,) * 4 + (P(EXP, None, CTX),) * 2 + (P(EXP, CTX, None),)
    return jax.shard_map(local, mesh=fine, in_specs=placed, out_specs=outs, check_vma=False)
```

```python
import functools
import math

import jax
import jax.numpy as jnp
from jax import lax
from jax.experimental import pallas as pl
from jax.experimental.pallas import tpu as pltpu
from jax.sharding import Mesh
from jax.sharding import PartitionSpec as P

HEADS = 16
HD = 128
EPSILON = 1e-06
ROPE_THETA = 10000.0
NEG_FILL = -1e30

CTX = ("ca", "cb")
EXP = ("ring", "core")
ALL = CTX + EXP


MESH = pl.DeviceIdType.MESH


def turn(name, by):
    size = lax.axis_size(name)
    return lax.rem(lax.axis_index(name) + by, size)


def await_bytes(ref, sem):
    pltpu.make_async_copy(ref, ref, sem).wait()


def greet(peers):
    barrier = pltpu.get_barrier_semaphore()
    for peer in peers:
        pl.semaphore_signal(barrier, inc=1, device_id=peer, device_id_type=MESH)
    pl.semaphore_wait(barrier, len(peers))


def push(src, dst, ssem, rsem, to):
    pltpu.make_async_remote_copy(
        src_ref=src, dst_ref=dst, send_sem=ssem, recv_sem=rsem, device_id=to, device_id_type=MESH
    ).start()


RING, SIDE_B, SIDE_A, FIRST, SECOND, CORE_OWN, CORE_B, CORE_A, CORE_FIRST, CORE_SECOND = range(10)


def along(step):
    ring, r = lax.axis_size("ring"), lax.axis_index("ring")
    to_next, to_last = {"ring": turn("ring", 1)}, {"ring": turn("ring", ring - 1)}
    return (
        ((r + 1 < ring) & (r >= step), r >= step + 1, lax.rem(r + ring - step, ring), lax.rem(r + ring - 1 - step, ring), to_next, 0),
        ((r >= 1) & (r + step < ring), r + 1 + step < ring, lax.rem(r + step, ring), lax.rem(r + 1 + step, ring), to_last, 1),
    )


def send_along(step, own, block_of, send, got):
    for sent, _, block, _, to, side in along(step):

        @pl.when(sent)
        def _(block=block, to=to, side=side):
            src = own if isinstance(step, int) and step == 0 else block_of(block)
            push(src, block_of(block), send.at[side, step], got.at[side, step], to)


def take_along(step, block_of, got, then):
    for _, comes, _, block, _, side in along(step):

        @pl.when(comes)
        def _(block=block, side=side):
            await_bytes(block_of(block), got.at[side, step])

    for _, comes, _, block, _, side in along(step):

        @pl.when(comes)
        def _(block=block):
            then(block)


def sent_along(own, send):
    ring = lax.axis_size("ring")
    for step in range(ring - 1):
        for sent, _, _, _, _, side in along(step):

            @pl.when(sent)
            def _(side=side):
                await_bytes(own, send.at[side, step])


def spread_kernel(count, tables, *refs):
    ring = lax.axis_size("ring")
    ins, refs = refs[: count + tables], refs[count + tables :]
    outs, sems = refs[: count + tables], refs[count + tables :]
    send, send_ring, got_ring, got_b, got_a, got, place, core_sem = sems
    a, b, r, c = (lax.axis_index(n) for n in ALL)
    na, nb, nc = turn("ca", 1), turn("cb", 1), turn("core", 1)
    to_a, to_b, to_core = {"ca": na}, {"cb": nb}, {"core": nc}
    greet([to_a, to_b, to_core] + [{"ring": turn("ring", k)} for k in range(1, ring)])

    def half(ref, which):
        rows, cols = ref.shape[-2:]
        if rows * 8 < cols:
            return ref.at[..., pl.ds(which * (cols // 2), cols // 2)]
        return ref.at[..., pl.ds(which * (rows // 2), rows // 2), :]

    def halves(ref, which):
        rows, cols = ref.shape[-2:]
        if rows * 8 < cols:
            return ref.at[:, :, pl.ds(which * (cols // 2), cols // 2)]
        return ref.at[:, pl.ds(which * (rows // 2), rows // 2), :]

    def place_of(w):
        return (lambda at: outs[w].at[a, b, at, c]) if w < count else (lambda at: outs[w].at[at, c])

    for w in range(count + tables):
        pltpu.make_async_copy(ins[w], place_of(w)(r), place.at[w]).start()
    for w in reversed(range(count)):
        send_along(0, ins[w], place_of(w), send_ring.at[w], got_ring.at[w])
        here = place_of(w)(r)
        push(ins[w], here, send.at[w, SIDE_B], got_b.at[w, r], to_b)
        push(ins[w], here, send.at[w, SIDE_A], got_a.at[w, r], to_a)
        push(ins[w], here, send.at[w, CORE_OWN], got.at[w, CORE_OWN], to_core)
    for t in range(tables):
        push(ins[count + t], place_of(count + t)(r), core_sem.at[t, 0], core_sem.at[t, 1], to_core)

    def sides(w):
        for step in range(ring - 1):

            def on(at):
                block = place_of(w)(at)
                push(block, block, send.at[w, SIDE_B], got_b.at[w, at], to_b)
                push(block, block, send.at[w, SIDE_A], got_a.at[w, at], to_a)
                push(block, block, send.at[w, CORE_OWN], got.at[w, CORE_OWN], to_core)

            take_along(step, place_of(w), got_ring.at[w], on)
            if step + 1 < ring - 1:
                send_along(step + 1, ins[w], place_of(w), send_ring.at[w], got_ring.at[w])

    def diagonal(w):
        out = outs[w]

        def one(k, carry):
            at = lax.rem(r + ring - k, ring)
            block = out.at[a, nb, at, c]
            await_bytes(block, got_b.at[w, at])
            push(half(block, 0), half(block, 0), send.at[w, FIRST], got.at[w, FIRST], to_a)
            push(block, block, send.at[w, CORE_B], got.at[w, CORE_B], to_core)
            block = out.at[na, b, at, c]
            await_bytes(block, got_a.at[w, at])
            push(half(block, 1), half(block, 1), send.at[w, SECOND], got.at[w, SECOND], to_b)
            push(block, block, send.at[w, CORE_A], got.at[w, CORE_A], to_core)
            return carry

        lax.fori_loop(0, ring, one, 0)

    def last(w):
        block = outs[w].at[na, nb, :, c]
        for which, kind, core_kind in ((0, FIRST, CORE_FIRST), (1, SECOND, CORE_SECOND)):
            part = halves(block, which)
            await_bytes(part, got.at[w, kind])
            push(part, part, send.at[w, core_kind], got.at[w, core_kind], to_core)

    def table_step(t, step):
        w = count + t

        def on(at):
            push(place_of(w)(at), place_of(w)(at), core_sem.at[t, 0], core_sem.at[t, 1], to_core)

        if step >= 0:
            take_along(step, place_of(w), got_ring.at[w], on)
        if step + 1 < ring - 1:
            send_along(step + 1, ins[w], place_of(w), send_ring.at[w], got_ring.at[w])

    order = list(reversed(range(count)))
    for step in range(count + 2):
        if step < count:
            sides(order[step])
        if step >= count - 1:
            for t in range(tables):
                table_step(t, step - count)
        if 0 <= step - 1 < count:
            diagonal(order[step - 1])
        if 0 <= step - 2 < count:
            last(order[step - 2])
    for step in range(2, ring - 1):
        for t in range(tables):
            table_step(t, step)

    for w in range(count):
        out = outs[w]
        mine = lambda p, q: out.at[p, q, :, c]
        await_bytes(ins[w], place.at[w])
        sent_along(ins[w], send_ring.at[w])
        for kind in (SIDE_B, SIDE_A, CORE_OWN, CORE_B, CORE_A):
            await_bytes(mine(a, b), send.at[w, kind])
        for which, kind in ((0, FIRST), (1, SECOND), (0, CORE_FIRST), (1, CORE_SECOND)):
            await_bytes(halves(mine(a, b), which), send.at[w, kind])
        for kind, p, q in ((CORE_OWN, a, b), (CORE_B, a, nb), (CORE_A, na, b)):
            await_bytes(out.at[p, q, :, nc], got.at[w, kind])
        for which, kind in ((0, CORE_FIRST), (1, CORE_SECOND)):
            await_bytes(halves(out.at[na, nb, :, nc], which), got.at[w, kind])
    for t in range(tables):
        w = count + t
        await_bytes(ins[w], place.at[w])
        sent_along(ins[w], send_ring.at[w])
        await_bytes(outs[w].at[:, c], core_sem.at[t, 0])
        await_bytes(outs[w].at[:, nc], core_sem.at[t, 1])


def spread(shards, tables):
    count, more, ring = len(shards), len(tables), lax.axis_size("ring")
    square = (lax.axis_size("ca"), lax.axis_size("cb"), ring, 2)
    dma = pltpu.SemaphoreType.DMA
    outs = pl.pallas_call(
        functools.partial(spread_kernel, count, more),
        out_shape=[jax.ShapeDtypeStruct(square + s.shape, s.dtype) for s in shards]
        + [jax.ShapeDtypeStruct((ring, 2) + t.shape, t.dtype) for t in tables],
        in_specs=[pl.BlockSpec(memory_space=pltpu.VMEM)] * (count + more),
        out_specs=[pl.BlockSpec(memory_space=pl.ANY)] * (count + more),
        scratch_shapes=[
            dma((count, 10)), dma((count + more, 2, ring)), dma((count + more, 2, ring)), dma((count, ring)), dma((count, ring)),
            dma((count, 10)), dma((count + more,)), dma((more, 2)),
        ],
        compiler_params=pltpu.CompilerParams(collective_id=0, has_side_effects=True),
        cost_estimate=pl.CostEstimate(flops=150_000_000_000, bytes_accessed=300_000_000, transcendentals=0),
        name="spread",
    )(*shards, *tables)
    return outs[:count], outs[count:]


def collect_kernel(count, *refs):
    ring = lax.axis_size("ring")
    whole = (count - 1) // 2
    small, lefts, rights, refs = refs[0], (refs[1],) + (refs[2],) * (whole - 1), refs[3 : whole + 3], refs[whole + 3 :]
    grads, matrices, (x, gain, passed), refs = refs[:3], refs[3:6], refs[6:9], refs[9:]
    outs, (input_grad, gain_out), refs = refs[: whole + 1], refs[whole + 1 : whole + 3], refs[whole + 3 :]
    scratch, (out_a, out_b), refs = refs[: 9 * count], refs[9 * count : 9 * count + 2], refs[9 * count + 2 :]
    send, got, ring_send, ring_got, load, chunks, dn1, sums, arrived, ring_arrived, fetch, gain_send, gain_got = refs
    a, b, r, c = (lax.axis_index(n) for n in ALL)
    na, nb, nc = turn("ca", 1), turn("cb", 1), turn("core", 1)
    to_a, to_b, to_core = {"ca": na}, {"cb": nb}, {"core": nc}
    bufs = [scratch[9 * w : 9 * w + 9] for w in range(count)]
    greet([to_a, to_b, to_core] + [{"ring": turn("ring", k)} for k in range(1, ring)])

    def chunk(i, slot, w):
        rows = chunks.shape[2]
        return pltpu.make_async_copy(
            matrices[w].at[pl.ds(pl.multiple_of(i * rows, rows), rows), :], chunks.at[slot, w], fetch.at[slot, w]
        )

    steps, chunk_rows = matrices[0].shape[0] // chunks.shape[2], chunks.shape[2]

    def input_part(begin, end):
        rows = chunk_rows

        def one(i, carry):
            slot = lax.rem(i, 2)

            @pl.when(i + 1 < steps)
            def _():
                for w in range(3):
                    chunk(i + 1, 1 - slot, w).start()

            value = jnp.zeros((x.shape[0], rows), jnp.float32)
            for w in range(3):
                chunk(i, slot, w).wait()
                value = value + times_transposed(grads[w][...], chunks[slot, w])
            dn1[:, pl.ds(pl.multiple_of(i * rows, rows), rows)] = value
            return carry

        lax.fori_loop(begin, end, one, 0)

    def input_end():
        tile = 32
        sums[0] = jnp.zeros(sums.shape[1:], jnp.float32)

        def back(i, carry):
            at = pl.ds(pl.multiple_of(i * tile, tile), tile)
            v, grad = x[at, :].astype(jnp.float32), dn1[at, :]
            factor = lax.rsqrt(jnp.mean(v * v, axis=-1, keepdims=True) + EPSILON)
            weighted = grad * gain[...]
            inner = jnp.mean(weighted * v, axis=-1, keepdims=True)
            total = passed[at, :] + factor * weighted - v * (factor * factor * factor * inner)
            input_grad[at, :] = total.astype(input_grad.dtype)
            gained = grad * v * factor
            sums[0] += sum(gained[k : k + 8] for k in range(0, tile, 8))
            return carry

        lax.fori_loop(0, x.shape[0] // tile, back, 0)
        push(sums.at[0], arrived.at[0], gain_send.at[0], gain_got.at[0], to_a)

    def gain_stage(stage):
        if stage < 3:
            await_bytes(arrived.at[stage], gain_got.at[stage])
            sums[stage + 1] = sums[stage] + arrived[stage]
            if stage < 2:
                push(sums.at[stage + 1], arrived.at[stage + 1], gain_send.at[stage + 1], gain_got.at[stage + 1], (to_b, to_core)[stage])
            else:
                for k in range(1, ring):
                    push(sums.at[3], ring_arrived.at[k - 1], gain_send.at[2 + k], gain_got.at[2 + k], {"ring": turn("ring", k)})
        else:
            total = sums[3]
            for k in range(1, ring):
                await_bytes(ring_arrived.at[k - 1], gain_got.at[2 + k])
                total = total + ring_arrived[k - 1]
            gain_out[...] = total
            for k in range(3 + ring - 1):
                await_bytes(sums.at[0], gain_send.at[k])

    def half(ref, which):
        rows, cols = ref.shape[-2:]
        lead = (slice(None),) * (len(ref.shape) - 2)
        if cols > 128:
            return ref.at[(*lead, slice(None), pl.ds(which * (cols // 2), cols // 2))]
        return ref.at[(*lead, pl.ds(which * (rows // 2), rows // 2), slice(None))]

    own_a, own_b = bufs[0][:2]
    loads = (
        pltpu.make_async_copy(half(small.at[a], 0), own_a, load.at[0, 0]),
        pltpu.make_async_copy(half(small.at[:, b], 1), own_b, load.at[0, 1]),
    )

    def product(w, block, which):
        own = bufs[w][0]
        rows, cols = own.shape[1] * own.shape[2], own.shape[3]
        at, part = divmod(w - 1, 2)
        left = lefts[at][:, pl.ds(pl.multiple_of(block * rows, rows), rows)]
        value = transposed_times(left, rights[at][:, pl.ds((2 * part + which) * cols, cols)])
        return value.reshape(own.shape[1:])

    def sent_first(w):
        await_bytes(bufs[w][2], send.at[w, 0])
        await_bytes(bufs[w][3], send.at[w, 1])

    def first(w):
        in_a, in_b = bufs[w][2:4]
        if w == 0:
            for copy in loads:
                copy.start()
            push(half(small.at[na], 0), in_a, send.at[w, 0], got.at[w, 0], to_a)
            push(half(small.at[:, nb], 1), in_b, send.at[w, 1], got.at[w, 1], to_b)
            return
        if w > 2:
            sent_first(w - 2)

        def one_a(i, carry):
            out_a[w % 2, i] = product(w, 2 * na + i, 0).astype(out_a.dtype)
            return carry

        def one_b(i, carry):
            out_b[w % 2, i] = product(w, 2 * i + nb, 1).astype(out_b.dtype)
            return carry

        lax.fori_loop(0, 2, one_a, 0)
        push(out_a.at[w % 2], in_a, send.at[w, 0], got.at[w, 0], to_a)
        lax.fori_loop(0, 2, one_b, 0)
        push(out_b.at[w % 2], in_b, send.at[w, 1], got.at[w, 1], to_b)

    def second(w):
        own_a, own_b, in_a, in_b, in_a2, in_b2 = bufs[w][:6]
        if w == 0:
            for copy in loads:
                copy.wait()

        def one_a(i, carry):
            mine = own_a[i] if w == 0 else product(w, 2 * a + i, 0)
            own_a[i] = (mine + in_a[i].astype(jnp.float32)).astype(own_a.dtype)
            return carry

        def one_b(i, carry):
            mine = own_b[i] if w == 0 else product(w, 2 * i + b, 1)
            own_b[i] = (mine + in_b[i].astype(jnp.float32)).astype(own_b.dtype)
            return carry

        await_bytes(in_a, got.at[w, 0])
        lax.fori_loop(0, 2, one_a, 0)
        push(own_a.at[nb], in_a2, send.at[w, 2], got.at[w, 2], to_b)
        await_bytes(in_b, got.at[w, 1])
        lax.fori_loop(0, 2, one_b, 0)
        push(own_b.at[na], in_b2, send.at[w, 3], got.at[w, 3], to_a)

    def third(w):
        own_a, own_b, _, _, in_a2, in_b2, total, in_ring = bufs[w][:8]
        await_bytes(in_a2, got.at[w, 2])
        await_bytes(in_b2, got.at[w, 3])

        def one(k, carry):
            sums = [
                own[own_at, k].astype(jnp.float32) + more[k].astype(jnp.float32)
                for own, own_at, more in ((own_a, b, in_a2), (own_b, a, in_b2))
            ]
            for which in range(2):
                half(total.at[k], which)[...] = sums[which].astype(total.dtype)
            return carry

        lax.fori_loop(0, ring, one, 0)
        for k in range(1, ring):
            at = turn("ring", k)
            push(total.at[at], in_ring.at[k - 1], ring_send.at[w, k - 1], ring_got.at[w, k - 1], {"ring": at})

    def fourth(w):
        total, in_ring, final = bufs[w][6:9]
        for k in range(1, ring):
            await_bytes(in_ring.at[k - 1], ring_got.at[w, k - 1])
        if final.shape[0] == 2:
            rows = final.shape[1]
            for core in range(2):
                at = pl.ds(core * rows, rows)
                value = total[r, at, :].astype(jnp.float32)
                for k in range(ring - 1):
                    value = value + in_ring[k, at, :].astype(jnp.float32)
                final[core] = value
            cols = final.shape[2]
            at, part = divmod(w - 1, 2)
            there = outs[at + 1].at[:, pl.ds(pl.multiple_of((2 * c + part) * cols, cols), cols)]
            push(final.at[nc], there, send.at[w, 4], got.at[w, 4], to_core)
            pltpu.make_async_copy(final.at[c], there, load.at[w, 2]).start()
        else:
            value = total[r].astype(jnp.float32)
            for k in range(ring - 1):
                value = value + in_ring[k].astype(jnp.float32)
            outs[w][...] = value

    def finish(w):
        own_a, own_b, in_a, in_b, in_a2, in_b2, total, in_ring, final = bufs[w]
        if w == 0 or w + 2 >= count:
            sent_first(w)
        await_bytes(in_a2, send.at[w, 2])
        await_bytes(in_b2, send.at[w, 3])
        for k in range(1, ring):
            await_bytes(in_ring.at[k - 1], ring_send.at[w, k - 1])
        if final.shape[0] == 2:
            await_bytes(final.at[0], send.at[w, 4])
            await_bytes(final.at[0], got.at[w, 4])
            await_bytes(final.at[0], load.at[w, 2])

    for w in range(3):
        chunk(0, 0, w).start()
    first(0)
    for step in range(max(count + 3, 9)):
        if step + 1 < count:
            first(step + 1)
        if step < count:
            second(step)
        if 0 <= step - 1 < count:
            third(step - 1)
        if 0 <= step - 2 < count:
            fourth(step - 2)
        if 1 <= step < 5:
            input_part((step - 1) * steps // 4, step * steps // 4)
        if step == 4:
            input_end()
        if 4 < step < 9:
            gain_stage(step - 5)
    for w in range(count):
        finish(w)


def collect(small, lefts, rights, grads, matrices, x, gain, passed):
    count, ring = 2 * len(rights) + 1, lax.axis_size("ring")
    chips = lax.axis_size("ca") * lax.axis_size("cb") * ring
    square = (lax.axis_size("ca"), lax.axis_size("cb"), ring)
    view = small.reshape(square + small.shape[1:])
    rows = lefts[0].shape[1] // chips
    forms = [(*view.shape[3:], view.dtype)] + [(rows, r.shape[1] // 2, r.dtype) for r in rights for _ in range(2)]
    shapes = [view.shape[3:]] + [(rows // 2, 2 * r.shape[1]) for r in rights]
    shapes, scratch = [jax.ShapeDtypeStruct(shape, jnp.float32) for shape in shapes], []
    for rows, cols, dtype in forms:
        piece = (rows, cols // 2) if cols > 128 else (rows // 2, cols)
        big = cols > 128
        vmem = lambda *shape: pltpu.VMEM(shape, dtype)
        scratch += [vmem(2, ring, *piece)] * 4 + [vmem(ring, *piece)] * 2
        scratch += [vmem(ring, rows, cols), vmem(ring - 1, rows, cols)]
        scratch += [pltpu.VMEM((2, rows // 2, cols) if big else (1, 8, 128), jnp.float32)]
    scratch += [vmem(2, 2, ring, *piece)] * 2
    dma = pltpu.SemaphoreType.DMA
    vm, anywhere = pl.BlockSpec(memory_space=pltpu.VMEM), pl.BlockSpec(memory_space=pl.ANY)
    wide = (8, gain.shape[1])
    f32 = lambda *shape: pltpu.VMEM(shape, jnp.float32)
    outs = pl.pallas_call(
        functools.partial(collect_kernel, count),
        out_shape=shapes + [jax.ShapeDtypeStruct(x.shape, x.dtype), jax.ShapeDtypeStruct(wide, jnp.float32)],
        in_specs=[anywhere] + [vm] * (len(rights) + 5) + [anywhere] * 3 + [vm] * 3,
        out_specs=[vm] * (len(rights) + 3),
        scratch_shapes=scratch
        + [dma((count, 5)), dma((count, 5)), dma((count, ring - 1)), dma((count, ring - 1)), dma((count, 3))]
        + [pltpu.VMEM((2, 3, 128, x.shape[1]), x.dtype), f32(*x.shape), f32(4, *wide), f32(3, *wide), f32(ring - 1, *wide)]
        + [dma((2, 3)), dma((2 + ring,)), dma((2 + ring,))],
        compiler_params=pltpu.CompilerParams(collective_id=1, has_side_effects=True, vmem_limit_bytes=62 << 20),
        cost_estimate=pl.CostEstimate(flops=160_000_000_000, bytes_accessed=320_000_000, transcendentals=0),
        name="collect",
    )(view, *lefts, *rights, *grads, *matrices, x, gain, passed)
    return outs[1:-2], outs[0], outs[-2], outs[-1]


def dispatch_kernel(
    rows, router, hot, g_all, out, picked, grads, gates, probs,
    rows_in, g_in, picked_low, grads_low, load, store, ring_send, ring_got, place, core_send, core_got,
):
    ring = lax.axis_size("ring")
    r, c, nc = lax.axis_index("ring"), lax.axis_index("core"), turn("core", 1)
    to_core, experts = {"core": nc}, hot.shape[1]
    greet([to_core] + [{"ring": turn("ring", k)} for k in range(1, ring)])
    block_of = lambda at: out.at[at, c]

    own = pltpu.make_async_copy(rows, block_of(r), place)
    own.start()
    push(rows, block_of(r), core_send, core_got.at[r], to_core)
    own.wait()
    send_along(0, block_of(r), block_of, ring_send, ring_got)
    first = (r * 2 + c) * experts
    width = rows.shape[1]
    cols = min(512, width)

    def pick(at, core):
        source = at * 2 + core
        copies = (
            pltpu.make_async_copy(out.at[at, core], rows_in, load.at[0]),
            pltpu.make_async_copy(g_all.at[at, core], g_in, load.at[1]),
        )
        for copy in copies:
            copy.start()
        copies[0].wait()
        logits = times_transposed(router[...], rows_in[...])
        likely = jnp.exp(logits - jnp.max(logits, axis=0, keepdims=True))
        probs[source] = likely / jnp.sum(likely, axis=0, keepdims=True)
        copies[1].wait()
        for e in range(experts):
            own_probs = probs[source, pl.ds(first + e, 1), :]
            gate = jnp.sum(hot[source, e].astype(jnp.float32) * own_probs, axis=-1, keepdims=True)
            gates[e, source] = gate

            def part(i, carry):
                lanes = pl.ds(pl.multiple_of(i * cols, cols), cols)
                chosen = hot[source, e]
                picked_low[e, :, lanes] = matmul(chosen, rows_in[:, lanes]).astype(picked_low.dtype)
                grads_low[e, :, lanes] = (matmul(chosen, g_in[:, lanes]) * gate).astype(grads_low.dtype)
                return carry

            lax.fori_loop(0, width // cols, part, 0)
        stores = (
            pltpu.make_async_copy(picked_low, picked.at[:, source], store.at[0]),
            pltpu.make_async_copy(grads_low, grads.at[:, source], store.at[1]),
        )
        for copy in stores:
            copy.start()
        for copy in stores:
            copy.wait()

    pick(r, c)
    await_bytes(out.at[r, nc], core_got.at[r])
    pick(r, nc)

    def step_on(step, carry):
        take_along(step, block_of, ring_got, lambda at: None)

        @pl.when(step + 1 < ring - 1)
        def _():
            send_along(step + 1, None, block_of, ring_send, ring_got)

        for _, comes, _, block, _, _ in along(step):

            @pl.when(comes)
            def _(block=block):
                push(block_of(block), block_of(block), core_send, core_got.at[block], to_core)

        def four(k, carry):
            side, other = k // 2, lax.rem(k, 2)
            (_, comes0, _, block0, _, _), (_, comes1, _, block1, _, _) = along(step)
            block = jnp.where(side == 0, block0, block1)
            comes = ((side == 0) & comes0) | ((side == 1) & comes1)
            core = lax.rem(c + other, 2)

            @pl.when(comes & (other == 1))
            def _():
                await_bytes(out.at[block, nc], core_got.at[block])

            @pl.when(comes)
            def _():
                pick(block, core)

            return carry

        lax.fori_loop(0, 4, four, 0)
        return carry

    lax.fori_loop(0, ring - 1, step_on, 0)
    sent_along(rows, ring_send)
    await_bytes(out.at[:, c], core_send)


def dispatch(rows, router, hot, g_all):
    ring, dma = lax.axis_size("ring"), pltpu.SemaphoreType.DMA
    sources, experts, slots, count = hot.shape
    width = rows.shape[1]
    low = lambda *shape: jax.ShapeDtypeStruct(shape, rows.dtype)
    f32 = lambda *shape: jax.ShapeDtypeStruct(shape, jnp.float32)
    vm, anywhere = pl.BlockSpec(memory_space=pltpu.VMEM), pl.BlockSpec(memory_space=pl.ANY)
    block = pltpu.VMEM((experts, slots, width), rows.dtype)
    chosen = (experts, sources, slots, width)
    return pl.pallas_call(
        dispatch_kernel,
        out_shape=[
            low(ring, 2, count, width), low(*chosen), low(*chosen), f32(experts, sources, slots, 1),
            f32(sources, router.shape[0], count),
        ],
        in_specs=[vm, vm, vm, anywhere],
        out_specs=[anywhere, anywhere, anywhere, vm, vm],
        scratch_shapes=[pltpu.VMEM(rows.shape, rows.dtype)] * 2
        + [block, block]
        + [dma((2,)), dma((2,)), dma((2, ring)), dma((2, ring)), dma, dma, dma((ring,))],
        compiler_params=pltpu.CompilerParams(collective_id=2, has_side_effects=True, vmem_limit_bytes=56 << 20),
        cost_estimate=pl.CostEstimate(flops=1_000_000, bytes_accessed=10_000, transcendentals=0),
        name="dispatch",
    )(rows, router, hot, g_all)


def give_back_kernel(
    hot, logit, logit_turned, router, pairs, mixed, n2, out, mixed_out, router_part,
    sums, chain_in, to_core, pair_in, mixed_in, mixed_low, n2_in,
    load, core_send, core_got, chain_send, chain_got, load_more, store,
):
    ring, pieces, rows, width = sums.shape
    sources, experts = hot.shape[:2]
    r, c, nc = lax.axis_index("ring"), lax.axis_index("core"), turn("core", 1)
    to_next, to_last = {"ring": turn("ring", 1)}, {"ring": turn("ring", ring - 1)}
    greet([{"core": nc}] + [{"ring": turn("ring", k)} for k in range(1, ring)])
    cols, tile = min(512, width), 32

    def whose(i):
        return (1 - i % 2) * (ring - 1 - i // 2) + (i % 2) * (i // 2)

    def fetch(i, j):
        return pltpu.make_async_copy(pairs.at[:, whose(i) * 2 + (nc, c)[j]], pair_in.at[j], load.at[j])

    def put_back(source, ref, lanes):
        return sum(matmul(hot[source, e], ref[e, :, lanes]) for e in range(experts))

    def block(source, j, into, more):
        def part(k, carry):
            lanes = pl.ds(pl.multiple_of(k * cols, cols), cols)
            value = put_back(source, pair_in.at[j], lanes) + matmul(logit[source], router[:, lanes])
            for piece in range(pieces):
                got = value[piece * rows : (piece + 1) * rows]
                if more is not None:
                    got = got + more[piece, :, lanes].astype(jnp.float32)
                into[piece, :, lanes] = got.astype(into.dtype)
            return carry

        lax.fori_loop(0, width // cols, part, 0)

    def fetch_beside(source):
        at = lax.rem(source, 2)
        return (
            pltpu.make_async_copy(mixed.at[:, source], mixed_in.at[at], load_more.at[at, 0]),
            pltpu.make_async_copy(n2.at[source], n2_in.at[at], load_more.at[at, 1]),
        )

    def beside(source):
        at = lax.rem(source, 2)

        @pl.when(source + 1 < sources)
        def _():
            for copy in fetch_beside(source + 1):
                copy.start()

        for copy in fetch_beside(source):
            copy.wait()

        @pl.when(source > 0)
        def _():
            await_bytes(mixed_low, store)

        def part(k, carry):
            lanes = pl.ds(pl.multiple_of(k * cols, cols), cols)
            mixed_low[:, lanes] = put_back(source, mixed_in.at[at], lanes).astype(mixed_low.dtype)
            router_part[:, lanes] += matmul(logit_turned[source], n2_in[at, :, lanes])
            return carry

        lax.fori_loop(0, width // cols, part, 0)
        pltpu.make_async_copy(mixed_low, mixed_out.at[source], store).start()

    def slot(side, d, at):
        return d if side == 0 else jnp.where(d == at, ring, d)

    def pass_on(side, step, d, piece, to):
        there = chain_in.at[slot(side, d, r - 1), piece]
        push(sums.at[d, piece], there, chain_send.at[side, step, piece], chain_got.at[side, step, piece], to)

    router_part[...] = jnp.zeros_like(router_part)
    fetch(0, 0).start()
    fetch(0, 1).start()
    for copy in fetch_beside(0):
        copy.start()

    def start(i, carry):
        d = whose(i)
        outgoing = to_core.at[lax.rem(i, 2)]
        fetch(i, 0).wait()

        @pl.when(i >= 2)
        def _():
            await_bytes(outgoing, core_send.at[lax.rem(i, 2)])

        block(d * 2 + nc, 0, outgoing, None)
        push(outgoing, sums.at[d], core_send.at[lax.rem(i, 2)], core_got.at[d], {"core": nc})
        fetch(i, 1).wait()
        await_bytes(sums.at[d], core_got.at[d])
        block(d * 2 + c, 1, sums.at[d], sums.at[d])
        for piece in range(pieces):

            @pl.when((r == 0) & (d != r))
            def _():
                pass_on(0, ring - 1 - d, d, piece, to_next)

            @pl.when((r == ring - 1) & (d != r))
            def _():
                pass_on(1, d, d, piece, to_last)

        @pl.when(i + 1 < ring)
        def _():
            fetch(i + 1, 0).start()
            fetch(i + 1, 1).start()

        beside(i)
        return carry

    lax.fori_loop(0, ring, start, 0)

    def sides(time):
        up, down = time - r, time - (ring - 1 - r)
        return (
            ((r >= 1) & (up >= 0), jnp.maximum(up, 0), ring - 1 - jnp.maximum(up, 0), to_next, 0),
            ((r + 1 < ring) & (down >= 0), jnp.maximum(down, 0), jnp.maximum(down, 0), to_last, 1),
        )

    def on(time, carry):
        for piece in range(pieces):
            for comes, step, d, to, side in sides(time):

                @pl.when(comes)
                def _(step=step, d=d, to=to, side=side):
                    arrived = chain_in.at[slot(side, d, r), piece]
                    await_bytes(arrived, chain_got.at[side, step, piece])

                    def one(k, carry):
                        at = pl.ds(pl.multiple_of(k * tile, tile), tile)
                        total = sums[d, piece, at].astype(jnp.float32) + arrived[at].astype(jnp.float32)
                        sums[d, piece, at] = total.astype(sums.dtype)
                        return carry

                    lax.fori_loop(0, rows // tile, one, 0)

                    @pl.when(time < ring - 1)
                    def _():
                        pass_on(side, step, d, piece, to)

        @pl.when(time < ring - 1)
        def _():
            beside(ring + time - 1)

        return carry

    def rest(source, carry):
        beside(source)
        return carry

    lax.fori_loop(1, ring - 1, on, 0)
    lax.fori_loop(2 * ring - 2, sources, rest, 0)
    on(ring - 1, 0)
    await_bytes(mixed_low, store)

    def total(k, carry):
        at = pl.ds(pl.multiple_of(k * tile, tile), tile)
        for piece in range(pieces):
            out[pl.ds(pl.multiple_of(piece * rows + k * tile, tile), tile), :] = sums[r, piece, at].astype(jnp.float32)
        return carry

    lax.fori_loop(0, rows // tile, total, 0)
    for k in range(2):
        await_bytes(to_core.at[k], core_send.at[k])
    for step in range(ring - 1):
        for piece in range(pieces):
            for sent, side in ((r + step < ring - 1, 0), (step < r, 1)):

                @pl.when(sent)
                def _(side=side):
                    await_bytes(sums.at[0, 0], chain_send.at[side, step, piece])


def give_back(hot, logit, router, pairs, mixed, n2):
    ring, dma, pieces = lax.axis_size("ring"), pltpu.SemaphoreType.DMA, 2
    experts, sources, slots, width = pairs.shape
    rows, all_experts = hot.shape[2], router.shape[0]
    vm, anywhere = pl.BlockSpec(memory_space=pltpu.VMEM), pl.BlockSpec(memory_space=pl.ANY)
    low = lambda *shape: pltpu.VMEM(shape, pairs.dtype)
    block = lambda n: low(n, pieces, rows // pieces, width)
    chain = dma((2, ring, pieces))
    return pl.pallas_call(
        give_back_kernel,
        out_shape=[
            jax.ShapeDtypeStruct((rows, width), jnp.float32),
            jax.ShapeDtypeStruct((sources, rows, width), pairs.dtype),
            jax.ShapeDtypeStruct((all_experts, width), jnp.float32),
        ],
        in_specs=[vm] * 4 + [anywhere] * 3,
        out_specs=[vm, anywhere, vm],
        scratch_shapes=[block(ring), block(ring + 1), block(2), low(2, experts, slots, width), low(2, experts, slots, width)]
        + [low(rows, width), low(2, rows, width)]
        + [dma((2,)), dma((2,)), dma((ring,)), chain, chain, dma((2, 2)), dma],
        compiler_params=pltpu.CompilerParams(collective_id=3, has_side_effects=True, vmem_limit_bytes=60 << 20),
        cost_estimate=pl.CostEstimate(flops=100_000_000_000, bytes_accessed=200_000_000, transcendentals=0),
        name="give_back",
    )(hot, logit, logit.transpose(0, 2, 1), router, pairs, mixed, n2)


def matmul(left, right):
    return jnp.dot(left, right, preferred_element_type=jnp.float32)


def times_transposed(left, right):
    return lax.dot_general(
        left, right, (((1,), (1,)), ((), ())), preferred_element_type=jnp.float32
    )


def transposed_times(left, right):
    return lax.dot_general(
        left, right, (((0,), (0,)), ((), ())), preferred_element_type=jnp.float32
    )


def corners():
    return ((0, 1), (1, 0), (1, 1))


def corner(da, db):
    pa, pb = turn("ca", da), turn("cb", db)
    return 2 * pa + pb, {"ca": pa, "cb": pb}


def rows_to_heads(src, dst, send, got, place):
    rows, width = src.shape[0], dst.shape[1]
    me, _ = corner(0, 0)
    there = dst.at[pl.ds(pl.multiple_of(me * rows, rows), rows), :]
    for i, (da, db) in enumerate(corners()):
        peer, to = corner(da, db)
        push(src.at[:, pl.ds(pl.multiple_of(peer * width, width), width)], there, send.at[i], got.at[i], to)
    pltpu.make_async_copy(src.at[:, pl.ds(pl.multiple_of(me * width, width), width)], there, place).start()


def wait_heads(src, dst, got, place):
    rows = src.shape[0]
    here = lambda at: dst.at[pl.ds(pl.multiple_of(at * rows, rows), rows), :]
    await_bytes(here(corner(0, 0)[0]), place)
    for i, (da, db) in enumerate(corners()):
        await_bytes(here(corner(da, db)[0]), got.at[i])


def swap_halves(v):
    return pltpu.roll(v, HD // 2, 1)


def norm_and_turn(raw, gain, cosine, sine, out):
    rows, width = raw.shape
    tile = 32

    def part(i, carry):
        at = pl.ds(pl.multiple_of(i * tile, tile), tile)
        value = raw[at, :]
        factor = lax.rsqrt(jnp.mean(value * value, axis=-1, keepdims=True) + EPSILON)
        for h in range(width // HD):
            lanes = pl.ds(h * HD, HD)
            v = raw[at, lanes] * factor * gain[:, lanes]
            out[at, lanes] = (v * cosine[at, :] + swap_halves(v) * sine[at, :]).astype(out.dtype)
        return carry

    lax.fori_loop(0, rows // tile, part, 0)


def norm_and_turn_back(grad, raw, gain, cosine, sine, out, gain_grad, turned):
    rows, width = raw.shape
    tile = 32
    gain_grad[...] = jnp.zeros_like(gain_grad)

    def part(i, carry):
        at = pl.ds(pl.multiple_of(i * tile, tile), tile)
        value = raw[at, :]
        factor = lax.rsqrt(jnp.mean(value * value, axis=-1, keepdims=True) + EPSILON)
        inner = jnp.zeros((tile, HD), jnp.float32)
        for h in range(width // HD):
            lanes = pl.ds(h * HD, HD)
            g = grad[at, lanes].astype(jnp.float32)
            g = g * cosine[at, :] - swap_halves(g) * sine[at, :]
            turned[:, lanes] = g
            inner = inner + g * gain[:, lanes] * raw[at, lanes]
        inner = jnp.sum(inner, axis=-1, keepdims=True) * (factor * factor * factor / width)
        for h in range(width // HD):
            lanes = pl.ds(h * HD, HD)
            g, v = turned[:, lanes], raw[at, lanes]
            out[at, lanes] = (factor * (g * gain[:, lanes]) - v * inner).astype(out.dtype)
            gained = g * v * factor
            gain_grad[:, lanes] += sum(gained[k : k + 8] for k in range(0, tile, 8))
        return carry

    lax.fori_loop(0, rows // tile, part, 0)


def attend_kernel(scale, q_raw, k_raw, v, q_gain, k_gain, cosine, sine, keep, o, qh, kh, vh, logs, q, k, oh, send, got, place, send_o, got_o, place_o):
    rows, width = v.shape[0], qh.shape[1]
    greet([corner(da, db)[1] for da, db in corners()])
    pairs = ((v, vh), (k, kh), (q, qh))
    rows_to_heads(v, vh, send.at[0], got.at[0], place.at[0])
    norm_and_turn(k_raw, k_gain, cosine, sine, k)
    rows_to_heads(k, kh, send.at[1], got.at[1], place.at[1])
    norm_and_turn(q_raw, q_gain, cosine, sine, q)
    rows_to_heads(q, qh, send.at[2], got.at[2], place.at[2])
    for i, (src, dst) in enumerate(pairs):
        wait_heads(src, dst, got.at[i], place.at[i])
    me, _ = corner(0, 0)
    tile = 128
    mine = pl.ds(pl.multiple_of(me * width, width), width)

    def block(at_block):
        def part(i, carry):
            at = pl.ds(pl.multiple_of(at_block * rows + i * tile, tile), tile)
            for h in range(width // HD):
                lanes = pl.ds(h * HD, HD)
                s = times_transposed(qh[at, lanes], kh[:, lanes]) * scale
                s = jnp.where(keep[...] > 0.0, s, NEG_FILL)
                peak = jnp.max(s, axis=-1, keepdims=True)
                p = jnp.exp(s - peak)
                total = jnp.sum(p, axis=-1, keepdims=True)
                logs[h, at, :] = peak + jnp.log(total)
                low = (p * (1.0 / total)).astype(jnp.bfloat16)
                oh[at, lanes] = matmul(low, vh[:, lanes]).astype(jnp.bfloat16)
            return carry

        lax.fori_loop(0, rows // tile, part, 0)

    for i, (da, db) in enumerate(corners()):
        peer, to = corner(da, db)
        block(peer)
        push(oh.at[pl.ds(pl.multiple_of(peer * rows, rows), rows), :], o.at[:, mine], send_o.at[i], got_o.at[i], to)
    block(me)
    pltpu.make_async_copy(oh.at[pl.ds(pl.multiple_of(me * rows, rows), rows), :], o.at[:, mine], place_o).start()
    pltpu.make_async_copy(oh.at[pl.ds(pl.multiple_of(me * rows, rows), rows), :], o.at[:, mine], place_o).wait()
    piece = o.at[:, mine]
    for i in range(3):
        await_bytes(piece, got_o.at[i])
        await_bytes(piece, send_o.at[i])
        for j in range(3):
            await_bytes(piece, send.at[j, i])


def attend(q_raw, k_raw, v, q_gain, k_gain, cosine, sine, keep, scale):
    rows, width = v.shape
    chips = lax.axis_size("ca") * lax.axis_size("cb")
    heads = jax.ShapeDtypeStruct((rows * chips, width // chips), v.dtype)
    vm, dma = pl.BlockSpec(memory_space=pltpu.VMEM), pltpu.SemaphoreType.DMA
    return pl.pallas_call(
        functools.partial(attend_kernel, scale),
        out_shape=[jax.ShapeDtypeStruct(v.shape, v.dtype), heads, heads, heads]
        + [jax.ShapeDtypeStruct((width // chips // HD, rows * chips, 1), jnp.float32)],
        in_specs=[vm] * 8,
        out_specs=[vm] * 5,
        scratch_shapes=[pltpu.VMEM(v.shape, v.dtype)] * 2 + [pltpu.VMEM(heads.shape, v.dtype)]
        + [dma((3, 3)), dma((3, 3)), dma((3,)), dma((3,)), dma((3,)), dma],
        compiler_params=pltpu.CompilerParams(collective_id=4, has_side_effects=True, vmem_limit_bytes=48 << 20),
        cost_estimate=pl.CostEstimate(flops=1_000_000, bytes_accessed=10_000, transcendentals=0),
        name="attend",
    )(q_raw, k_raw, v, q_gain, k_gain, cosine, sine, keep)


def attend_back_kernel(
    scale, do, qh, kh, vh, logs, keep, q_raw, k_raw, q_gain, k_gain, cosine, sine,
    dq_raw, dk_raw, dv, q_gain_grad, k_gain_grad,
    doh, dqh, dkh, dvh, dq, dk, turned, send, got, place, send_g, got_g, place_g,
):
    rows, width = do.shape[0], qh.shape[1]
    greet([corner(da, db)[1] for da, db in corners()])
    rows_to_heads(do, doh, send, got, place)
    wait_heads(do, doh, got, place)
    me, _ = corner(0, 0)
    tile, total_rows = 128, qh.shape[0]
    grads = ((dqh, dq), (dkh, dk), (dvh, dv))

    def one_head(h):
        lanes = pl.ds(h * HD, HD)

        def part(i, carry):
            dk_sum, dv_sum = carry
            at = pl.ds(pl.multiple_of(i * tile, tile), tile)
            qb, db, kb, vb = qh[at, lanes], doh[at, lanes], kh[:, lanes], vh[:, lanes]
            s = times_transposed(qb, kb) * scale
            s = jnp.where(keep[...] > 0.0, s, NEG_FILL)
            p = jnp.exp(s - logs[h, at, :])
            dp = times_transposed(db, vb)
            ds = (p * (dp - jnp.sum(dp * p, axis=-1, keepdims=True))).astype(jnp.bfloat16)
            dqh[at, lanes] = (matmul(ds, kb) * scale).astype(jnp.bfloat16)
            dk_sum = dk_sum + transposed_times(ds, qb)
            dv_sum = dv_sum + transposed_times(p.astype(jnp.bfloat16), db)
            return dk_sum, dv_sum

        zero = jnp.zeros((total_rows, HD), jnp.float32)
        dk_sum, dv_sum = lax.fori_loop(0, total_rows // tile, part, (zero, zero))
        dkh[:, lanes] = (dk_sum * scale).astype(jnp.bfloat16)
        dvh[:, lanes] = dv_sum.astype(jnp.bfloat16)

    for h in range(width // HD):
        one_head(h)
        lanes = pl.ds(h * HD, HD)
        here = pl.ds(pl.multiple_of(me * width + h * HD, HD), HD)
        for g, (src, dst) in enumerate(grads):
            for i, (da, db) in enumerate(corners()):
                peer, to = corner(da, db)
                push(src.at[pl.ds(pl.multiple_of(peer * rows, rows), rows), lanes], dst.at[:, here], send_g.at[g, i, h], got_g.at[g, i, h], to)
            own = src.at[pl.ds(pl.multiple_of(me * rows, rows), rows), lanes]
            pltpu.make_async_copy(own, dst.at[:, here], place_g.at[g, h]).start()
    piece = dq.at[:, pl.ds(0, HD)]
    for h in range(width // HD):
        for g in range(3):
            await_bytes(piece, place_g.at[g, h])
            for i in range(3):
                await_bytes(piece, send_g.at[g, i, h])
                await_bytes(piece, got_g.at[g, i, h])
    for i in range(3):
        await_bytes(do.at[:, pl.ds(0, width)], send.at[i])
    norm_and_turn_back(dk, k_raw, k_gain, cosine, sine, dk_raw, k_gain_grad, turned)
    norm_and_turn_back(dq, q_raw, q_gain, cosine, sine, dq_raw, q_gain_grad, turned)


def attend_back(do, qh, kh, vh, logs, keep, q_raw, k_raw, q_gain, k_gain, cosine, sine, scale):
    heads = qh.shape[1] // HD
    vm, dma = pl.BlockSpec(memory_space=pltpu.VMEM), pltpu.SemaphoreType.DMA
    return pl.pallas_call(
        functools.partial(attend_back_kernel, scale),
        out_shape=[jax.ShapeDtypeStruct(do.shape, do.dtype)] * 3 + [jax.ShapeDtypeStruct((8, do.shape[1]), jnp.float32)] * 2,
        in_specs=[vm] * 12,
        out_specs=[vm] * 5,
        scratch_shapes=[pltpu.VMEM(qh.shape, qh.dtype)] * 4
        + [pltpu.VMEM(do.shape, do.dtype)] * 2
        + [pltpu.VMEM((32, do.shape[1]), jnp.float32)]
        + [dma((3,)), dma((3,)), dma, dma((3, 3, heads)), dma((3, 3, heads)), dma((3, heads))],
        compiler_params=pltpu.CompilerParams(collective_id=5, has_side_effects=True, vmem_limit_bytes=56 << 20),
        cost_estimate=pl.CostEstimate(flops=50_000_000_000, bytes_accessed=10_000_000, transcendentals=0),
        name="attend_back",
    )(do, qh, kh, vh, logs, keep, q_raw, k_raw, q_gain, k_gain, cosine, sine)


def join_kernel(own, from_b, from_a, first, second, out, held, load, store):
    experts, units = own.shape[:2]
    a, b = lax.axis_index("ca"), lax.axis_index("cb")
    na, nb = turn("ca", 1), turn("cb", 1)
    loads, stores = [], []
    for piece, (p, q) in enumerate(((a, b), (a, nb), (na, b), (na, nb))):
        for e in range(experts):
            if piece < 3:
                src = (own, from_b, from_a)[piece].at[e]
            else:
                src = first.at[e] if e < experts // 2 else second.at[e - experts // 2]
            here = held.at[piece, e]
            loads.append(pltpu.make_async_copy(src, here, load.at[piece, e]))
            at = pl.ds(pl.multiple_of((2 * p + q) * units, units), units)
            stores.append(pltpu.make_async_copy(here, out.at[e, at, :], store.at[piece, e]))
    for copy in loads:
        copy.start()
    for fetch, copy in zip(loads, stores):
        fetch.wait()
        copy.start()
    for copy in stores:
        copy.wait()


def join(own, from_b, from_a, first, second):
    experts, units, width = own.shape
    anywhere, dma = pl.BlockSpec(memory_space=pl.ANY), pltpu.SemaphoreType.DMA((4, experts))
    return pl.pallas_call(
        join_kernel,
        out_shape=jax.ShapeDtypeStruct((experts, 4 * units, width), own.dtype),
        in_specs=[anywhere] * 5,
        out_specs=anywhere,
        scratch_shapes=[pltpu.VMEM((4, experts, units, width), own.dtype), dma, dma],
        cost_estimate=pl.CostEstimate(flops=0, bytes_accessed=8 * experts * units * width * 2, transcendentals=0),
        name="join",
    )(own, from_b, from_a, first, second)


def norm_rows(values, gain):
    factor = lax.rsqrt(jnp.mean(values * values, axis=-1, keepdims=True) + EPSILON)
    return (values * factor * gain, factor)


def norm_back(grad, values, factor, gain):
    weighted = grad * gain
    inner = jnp.mean(weighted * values, axis=-1, keepdims=True)
    return (factor * weighted - values * factor**3 * inner, jnp.sum(grad * values * factor, axis=0))


def rotary_tables(positions, head_dim):
    half_dim = head_dim // 2
    frequency = jnp.exp(-math.log(ROPE_THETA) * jnp.arange(half_dim, dtype=jnp.float32) / half_dim)
    angles = positions.astype(jnp.float32)[:, None] * frequency[None, :]
    return (jnp.cos(angles), jnp.sin(angles))


def local(
    tokens, cotangent, lengths, expert_ids, query_weight, key_weight, value_weight, out_weight,
    router_weight, first_gain, second_gain, query_gain, key_gain, gate_weight, up_weight, down_weight,
):
    token_count = tokens.shape[1]
    model_width = tokens.shape[2]
    head_dim = HD
    top_count = expert_ids.shape[2]
    experts = router_weight.shape[1]
    local_experts = gate_weight.shape[0]
    ctx_size = lax.axis_size(CTX)
    sources = lax.axis_size(EXP)
    capacity = max(2, -(-(token_count * top_count * 9) // (experts * 8)))
    score_scale = 1.0 / math.sqrt(head_dim)
    seq_len = token_count * ctx_size

    inputs = tokens[0].astype(jnp.float32)
    length = lengths[0]
    positions = lax.axis_index(CTX) * token_count + jnp.arange(token_count, dtype=jnp.int32)
    row_valid = positions < length
    row_valid = row_valid.astype(jnp.float32)[:, None]
    key_valid = jnp.arange(seq_len, dtype=jnp.int32) < length
    grad_total_low = (cotangent[0].astype(jnp.float32) * row_valid).astype(jnp.bfloat16)
    grad_total = grad_total_low.astype(jnp.float32)

    rows_each = query_weight.shape[0]
    packed = jnp.concatenate(
        [g.reshape(-1) for g in (first_gain, second_gain, query_gain, key_gain)] + [router_weight.reshape(-1)]
    )
    small = jnp.pad(packed, (0, -packed.size % 2048)).reshape(-1, 128)
    ids_low = expert_ids[0].astype(jnp.bfloat16).reshape(-1, 128)
    gathered, (ids_all, g_all) = spread([query_weight, key_weight, value_weight, out_weight, small], [ids_low, grad_total_low])
    full_query, full_key, full_value, full_out = (w.reshape(model_width, -1) for w in gathered[:4])
    smalls = gathered[4].reshape(-1, small.size)
    gains = [smalls[:, i * rows_each : (i + 1) * rows_each].reshape(-1).astype(jnp.float32) for i in range(4)]
    gain_first, gain_second, gain_queries, gain_keys = gains
    full_router = smalls[:, 4 * rows_each : packed.size].reshape(model_width, experts)
    ids_all = ids_all.reshape(sources, token_count, top_count).astype(jnp.int32)
    full_value, gate_weight, up_weight = lax.optimization_barrier((full_value, gate_weight, up_weight))
    gate_all, up_all = (lax.all_gather(w, CTX, axis=2, tiled=True) for w in (gate_weight, up_weight))
    cosine, sine = rotary_tables(positions, head_dim)
    normed_one, factor_one = norm_rows(inputs, gain_first)
    normed_one_low = normed_one.astype(jnp.bfloat16)
    query_raw = matmul(normed_one_low, full_query)
    key_raw = matmul(normed_one_low, full_key)
    value_low = matmul(normed_one_low, full_value).astype(jnp.bfloat16)
    keep = key_valid.astype(jnp.float32)[None, :]
    turns = (jnp.concatenate([cosine, cosine], axis=1), jnp.concatenate([-sine, sine], axis=1))
    row = lambda g: g.reshape(1, model_width)
    shared = (row(gain_queries), row(gain_keys), *turns)
    attended_low, *saved = attend(query_raw, key_raw, value_low, *shared, keep, score_scale)
    flip = lambda v, axis: lax.ppermute(v, axis, [(0, 1), (1, 0)])
    hidden_state = inputs + matmul(attended_low, full_out)
    normed_two, factor_two = norm_rows(hidden_state, gain_second)
    normed_two_low = normed_two.astype(jnp.bfloat16)

    first_expert = lax.axis_index(EXP) * local_experts
    own_experts = first_expert + jnp.arange(local_experts, dtype=jnp.int32)
    mask = jnp.any(ids_all[:, None, :, :] == own_experts[None, :, None, None], axis=-1)
    before = (jnp.arange(token_count)[:, None] < jnp.arange(token_count)[None, :]).astype(jnp.bfloat16)
    ranks = jnp.einsum("seu,ut->set", mask.astype(jnp.bfloat16), before, preferred_element_type=jnp.float32)
    slots = jnp.arange(capacity, dtype=jnp.float32)
    hot = (mask[:, :, None, :] & (ranks[:, :, None, :] == slots[None, None, :, None])).astype(jnp.bfloat16)
    router_turned = full_router.T
    n2_all, x, de, row_gate, probs = dispatch(normed_two_low, router_turned, hot, g_all)
    n2_all = n2_all.reshape(sources, token_count, model_width)
    probs = probs.transpose(0, 2, 1).reshape(-1, experts)
    hot32 = hot.astype(jnp.float32)
    x, gate_all, down_weight = lax.optimization_barrier((x, gate_all, down_weight))
    down_b, down_a = flip(down_weight, "cb"), flip(down_weight, "ca")
    first_half = local_experts // 2
    down_corner = [flip(down_b[:first_half], "ca"), flip(down_a[first_half:], "cb")]
    ee = lambda eq, a, b: jnp.einsum(eq, a, b, preferred_element_type=jnp.float32)
    gp = ee("escd,edf->escf", x, gate_all)
    up = ee("escd,edf->escf", x, up_all)
    sig = jax.nn.sigmoid(gp)
    hid = (gp * sig * up).astype(jnp.bfloat16)
    down_part = ee("escf,escd->efd", hid, de).astype(jnp.bfloat16)
    *down_corner, down_part = lax.optimization_barrier((*down_corner, down_part))
    down_all = join(down_weight, down_b, down_a, *down_corner)
    eo = ee("escf,efd->escd", hid, down_all).astype(jnp.bfloat16)
    gained = jnp.sum(de.astype(jnp.float32) * eo.astype(jnp.float32), axis=-1)
    mixed_rows = (row_gate * eo.astype(jnp.float32)).astype(jnp.bfloat16)
    dhid = ee("escd,efd->escf", de, down_all)
    dgp = (dhid * up * sig * (1.0 + gp * (1.0 - sig))).astype(jnp.bfloat16)
    dup = (dhid * gp * sig).astype(jnp.bfloat16)
    gate_part = ee("escd,escf->edf", x, dgp)
    up_part = ee("escd,escf->edf", x, dup)
    parts = [v.astype(jnp.bfloat16) for v in (down_part, gate_part, up_part)]
    dgp, dup, *_ = lax.optimization_barrier((dgp, dup, *parts))
    rs_ctx = lambda v, a: lax.psum_scatter(v, CTX, scatter_dimension=a, tiled=True)
    down_grad, gate_grad, up_grad = rs_ctx(parts[0], 1), rs_ctx(parts[1], 2), rs_ctx(parts[2], 2)
    dpair = (ee("escf,edf->escd", dgp, gate_all) + ee("escf,edf->escd", dup, up_all)).astype(jnp.bfloat16)

    gained = jnp.sum(hot32 * gained.transpose(1, 0, 2)[..., None], axis=2)
    gained = gained.transpose(0, 2, 1).reshape(-1, local_experts)
    onto = (jnp.arange(experts)[None, :] == own_experts[:, None]).astype(jnp.float32)
    weighed = jnp.sum(gained[:, :, None] * onto[None], axis=1)
    dlogit_low = (weighed - probs * jnp.sum(gained, axis=-1, keepdims=True)).astype(jnp.bfloat16)
    dpair, down_grad = lax.optimization_barrier((dpair, down_grad))
    dn2, mixed_part, router_part = give_back(
        hot.transpose(0, 1, 3, 2), dlogit_low.reshape(sources, token_count, experts), router_turned, dpair, mixed_rows, n2_all
    )
    router_part = router_part.T
    dn2, gate_grad = lax.optimization_barrier((dn2, gate_grad))
    mixed = lax.psum_scatter(mixed_part.reshape(-1, model_width), EXP, scatter_dimension=0, tiled=True)

    dh_norm, gain_second_part = norm_back(dn2, hidden_state, factor_two, gain_second)
    grad_hidden = grad_total + dh_norm
    dh_low = grad_hidden.astype(jnp.bfloat16)
    out_part = transposed_times(attended_low, dh_low)
    d_att = times_transposed(dh_low, full_out).astype(jnp.bfloat16)
    dq_low, dk_low, dv_low, *gain_parts = attend_back(d_att, *saved, keep, query_raw, key_raw, *shared, score_scale)
    dv_low, up_grad = lax.optimization_barrier((dv_low, up_grad))
    gain_queries_part, gain_keys_part = (jnp.sum(g, axis=0) for g in gain_parts)
    core = lax.axis_index("core")
    swap = lambda v: lax.ppermute(v, "core", [(0, 1), (1, 0)])

    def columns_of_core(v):
        width = model_width // 2
        mine = lax.dynamic_slice_in_dim(v, core * width, width, 1)
        other = lax.dynamic_slice_in_dim(v, (1 - core) * width, width, 1)
        return jnp.concatenate([mine, swap(other)], axis=0)

    both = lambda v: jnp.concatenate([v, swap(v)], axis=0)
    n1_both, att_both = both(normed_one_low), both(attended_low)
    rights = [columns_of_core(v) for v in (dh_low, dv_low, dq_low, dk_low)]
    split = lambda v: v.reshape(ctx_size * sources // 2, 2, -1)
    small_parts = jnp.concatenate(
        [split(v) for v in (gain_second_part, gain_queries_part, gain_keys_part, router_part)], axis=2
    )
    small_parts = jnp.pad(small_parts, ((0, 0), (0, 0), (0, -small_parts.shape[2] % 2048)))
    small_parts = lax.dynamic_index_in_dim(small_parts, core, 1, False) + swap(lax.dynamic_index_in_dim(small_parts, 1 - core, 1, False))
    weight_grads, small_grads, input_grad, gain_first_sums = collect(
        small_parts.reshape(ctx_size * sources // 2, -1, 128), (att_both, n1_both), rights, (dq_low, dk_low, dv_low),
        (full_query, full_key, full_value), tokens[0], row(gain_first), grad_hidden,
    )
    weight_grads, mixed, gate_grad, up_grad, down_grad = lax.optimization_barrier(
        (list(weight_grads), mixed, gate_grad, up_grad, down_grad)
    )
    layer_out = (row_valid * (hidden_state + mixed.astype(jnp.float32))).astype(jnp.bfloat16)
    gate_grad, up_grad, down_grad = (v.astype(jnp.float32) for v in (gate_grad, up_grad, down_grad))
    weight_grads = [weight_grads[k] for k in (2, 3, 1, 0)]
    small_grads = small_grads.reshape(-1)
    gain_grads = [lax.dynamic_slice_in_dim(jnp.sum(gain_first_sums, axis=0), lax.axis_index(ALL) * rows_each, rows_each)]
    gain_grads += [small_grads[i * rows_each : (i + 1) * rows_each] for i in range(3)]
    router_grad = small_grads[3 * rows_each : packed.size - rows_each].reshape(rows_each, experts)
    return (layer_out[None], input_grad[None], *weight_grads, router_grad, *gain_grads, gate_grad, up_grad, down_grad)


def solution(mesh):
    ctx, exp = mesh.devices.shape
    fine = Mesh(mesh.devices.reshape(2, ctx // 2, exp // 2, 2), ("ca", "cb", "ring", "core"))
    rows = P(EXP, CTX, None)
    flat2, flat1 = P(ALL, None), P(ALL)
    placed = (rows, rows, P(EXP), rows) + (flat2,) * 5 + (flat1,) * 4 + (P(EXP, None, CTX),) * 2 + (P(EXP, CTX, None),)
    outs = (rows, rows) + (flat2,) * 5 + (flat1,) * 4 + (P(EXP, None, CTX),) * 2 + (P(EXP, CTX, None),)
    return jax.shard_map(local, mesh=fine, in_specs=placed, out_specs=outs, check_vma=False)
```

```python
import functools
import math

import jax
import jax.numpy as jnp
from jax import lax
from jax.experimental import pallas as pl
from jax.experimental.pallas import tpu as pltpu
from jax.sharding import Mesh
from jax.sharding import PartitionSpec as P

HEADS = 16
HD = 128
EPSILON = 1e-06
ROPE_THETA = 10000.0
NEG_FILL = -1e30

CTX = ("ca", "cb")
EXP = ("ring", "core")
ALL = CTX + EXP


MESH = pl.DeviceIdType.MESH


def turn(name, by):
    size = lax.axis_size(name)
    return lax.rem(lax.axis_index(name) + by, size)


def await_bytes(ref, sem):
    pltpu.make_async_copy(ref, ref, sem).wait()


def greet(peers):
    barrier = pltpu.get_barrier_semaphore()
    for peer in peers:
        pl.semaphore_signal(barrier, inc=1, device_id=peer, device_id_type=MESH)
    pl.semaphore_wait(barrier, len(peers))


def push(src, dst, ssem, rsem, to):
    pltpu.make_async_remote_copy(
        src_ref=src, dst_ref=dst, send_sem=ssem, recv_sem=rsem, device_id=to, device_id_type=MESH
    ).start()


RING, SIDE_B, SIDE_A, FIRST, SECOND, CORE_OWN, CORE_B, CORE_A, CORE_FIRST, CORE_SECOND = range(10)


def along(step):
    ring, r = lax.axis_size("ring"), lax.axis_index("ring")
    to_next, to_last = {"ring": turn("ring", 1)}, {"ring": turn("ring", ring - 1)}
    return (
        ((r + 1 < ring) & (r >= step), r >= step + 1, lax.rem(r + ring - step, ring), lax.rem(r + ring - 1 - step, ring), to_next, 0),
        ((r >= 1) & (r + step < ring), r + 1 + step < ring, lax.rem(r + step, ring), lax.rem(r + 1 + step, ring), to_last, 1),
    )


def send_along(step, own, block_of, send, got):
    for sent, _, block, _, to, side in along(step):

        @pl.when(sent)
        def _(block=block, to=to, side=side):
            src = own if isinstance(step, int) and step == 0 else block_of(block)
            push(src, block_of(block), send.at[side, step], got.at[side, step], to)


def take_along(step, block_of, got, then):
    for _, comes, _, block, _, side in along(step):

        @pl.when(comes)
        def _(block=block, side=side):
            await_bytes(block_of(block), got.at[side, step])

    for _, comes, _, block, _, side in along(step):

        @pl.when(comes)
        def _(block=block):
            then(block)


def sent_along(own, send):
    ring = lax.axis_size("ring")
    for step in range(ring - 1):
        for sent, _, _, _, _, side in along(step):

            @pl.when(sent)
            def _(side=side):
                await_bytes(own, send.at[side, step])


def spread_kernel(count, tables, *refs):
    ring = lax.axis_size("ring")
    ins, refs = refs[: count + tables], refs[count + tables :]
    outs, sems = refs[: count + tables], refs[count + tables :]
    send, send_ring, got_ring, got_b, got_a, got, place, core_sem = sems
    a, b, r, c = (lax.axis_index(n) for n in ALL)
    na, nb, nc = turn("ca", 1), turn("cb", 1), turn("core", 1)
    to_a, to_b, to_core = {"ca": na}, {"cb": nb}, {"core": nc}
    greet([to_a, to_b, to_core] + [{"ring": turn("ring", k)} for k in range(1, ring)])

    def half(ref, which):
        rows, cols = ref.shape[-2:]
        if rows * 8 < cols:
            return ref.at[..., pl.ds(which * (cols // 2), cols // 2)]
        return ref.at[..., pl.ds(which * (rows // 2), rows // 2), :]

    def halves(ref, which):
        rows, cols = ref.shape[-2:]
        if rows * 8 < cols:
            return ref.at[:, :, pl.ds(which * (cols // 2), cols // 2)]
        return ref.at[:, pl.ds(which * (rows // 2), rows // 2), :]

    def place_of(w):
        return (lambda at: outs[w].at[a, b, at, c]) if w < count else (lambda at: outs[w].at[at, c])

    for w in range(count + tables):
        pltpu.make_async_copy(ins[w], place_of(w)(r), place.at[w]).start()
    for w in reversed(range(count)):
        send_along(0, ins[w], place_of(w), send_ring.at[w], got_ring.at[w])
        here = place_of(w)(r)
        push(ins[w], here, send.at[w, SIDE_B], got_b.at[w, r], to_b)
        push(ins[w], here, send.at[w, SIDE_A], got_a.at[w, r], to_a)
        push(ins[w], here, send.at[w, CORE_OWN], got.at[w, CORE_OWN], to_core)
    for t in range(tables):
        push(ins[count + t], place_of(count + t)(r), core_sem.at[t, 0], core_sem.at[t, 1], to_core)

    def sides(w):
        for step in range(ring - 1):

            def on(at):
                block = place_of(w)(at)
                push(block, block, send.at[w, SIDE_B], got_b.at[w, at], to_b)
                push(block, block, send.at[w, SIDE_A], got_a.at[w, at], to_a)
                push(block, block, send.at[w, CORE_OWN], got.at[w, CORE_OWN], to_core)

            take_along(step, place_of(w), got_ring.at[w], on)
            if step + 1 < ring - 1:
                send_along(step + 1, ins[w], place_of(w), send_ring.at[w], got_ring.at[w])

    def diagonal(w):
        out = outs[w]

        def one(k, carry):
            at = lax.rem(r + ring - k, ring)
            block = out.at[a, nb, at, c]
            await_bytes(block, got_b.at[w, at])
            push(half(block, 0), half(block, 0), send.at[w, FIRST], got.at[w, FIRST], to_a)
            push(block, block, send.at[w, CORE_B], got.at[w, CORE_B], to_core)
            block = out.at[na, b, at, c]
            await_bytes(block, got_a.at[w, at])
            push(half(block, 1), half(block, 1), send.at[w, SECOND], got.at[w, SECOND], to_b)
            push(block, block, send.at[w, CORE_A], got.at[w, CORE_A], to_core)
            return carry

        lax.fori_loop(0, ring, one, 0)

    def last(w):
        block = outs[w].at[na, nb, :, c]
        for which, kind, core_kind in ((0, FIRST, CORE_FIRST), (1, SECOND, CORE_SECOND)):
            part = halves(block, which)
            await_bytes(part, got.at[w, kind])
            push(part, part, send.at[w, core_kind], got.at[w, core_kind], to_core)

    def table_step(t, step):
        w = count + t

        def on(at):
            push(place_of(w)(at), place_of(w)(at), core_sem.at[t, 0], core_sem.at[t, 1], to_core)

        if step >= 0:
            take_along(step, place_of(w), got_ring.at[w], on)
        if step + 1 < ring - 1:
            send_along(step + 1, ins[w], place_of(w), send_ring.at[w], got_ring.at[w])

    order = list(reversed(range(count)))
    for step in range(count + 2):
        if step < count:
            sides(order[step])
        if step >= count - 1:
            for t in range(tables):
                table_step(t, step - count)
        if 0 <= step - 1 < count:
            diagonal(order[step - 1])
        if 0 <= step - 2 < count:
            last(order[step - 2])
    for step in range(2, ring - 1):
        for t in range(tables):
            table_step(t, step)

    for w in range(count):
        out = outs[w]
        mine = lambda p, q: out.at[p, q, :, c]
        await_bytes(ins[w], place.at[w])
        sent_along(ins[w], send_ring.at[w])
        for kind in (SIDE_B, SIDE_A, CORE_OWN, CORE_B, CORE_A):
            await_bytes(mine(a, b), send.at[w, kind])
        for which, kind in ((0, FIRST), (1, SECOND), (0, CORE_FIRST), (1, CORE_SECOND)):
            await_bytes(halves(mine(a, b), which), send.at[w, kind])
        for kind, p, q in ((CORE_OWN, a, b), (CORE_B, a, nb), (CORE_A, na, b)):
            await_bytes(out.at[p, q, :, nc], got.at[w, kind])
        for which, kind in ((0, CORE_FIRST), (1, CORE_SECOND)):
            await_bytes(halves(out.at[na, nb, :, nc], which), got.at[w, kind])
    for t in range(tables):
        w = count + t
        await_bytes(ins[w], place.at[w])
        sent_along(ins[w], send_ring.at[w])
        await_bytes(outs[w].at[:, c], core_sem.at[t, 0])
        await_bytes(outs[w].at[:, nc], core_sem.at[t, 1])


def spread(shards, tables):
    count, more, ring = len(shards), len(tables), lax.axis_size("ring")
    square = (lax.axis_size("ca"), lax.axis_size("cb"), ring, 2)
    dma = pltpu.SemaphoreType.DMA
    outs = pl.pallas_call(
        functools.partial(spread_kernel, count, more),
        out_shape=[jax.ShapeDtypeStruct(square + s.shape, s.dtype) for s in shards]
        + [jax.ShapeDtypeStruct((ring, 2) + t.shape, t.dtype) for t in tables],
        in_specs=[pl.BlockSpec(memory_space=pltpu.VMEM)] * (count + more),
        out_specs=[pl.BlockSpec(memory_space=pl.ANY)] * (count + more),
        scratch_shapes=[
            dma((count, 10)), dma((count + more, 2, ring)), dma((count + more, 2, ring)), dma((count, ring)), dma((count, ring)),
            dma((count, 10)), dma((count + more,)), dma((more, 2)),
        ],
        compiler_params=pltpu.CompilerParams(collective_id=0, has_side_effects=True),
        cost_estimate=pl.CostEstimate(flops=150_000_000_000, bytes_accessed=300_000_000, transcendentals=0),
        name="spread",
    )(*shards, *tables)
    return outs[:count], outs[count:]


def column_units(count, width):
    units = []
    for at in range(count):
        pieces = 4 if at == count - 1 else 2
        units += [(at, part * width // pieces, width // pieces) for part in range(pieces)]
    return units


def collect_kernel(whole, units, *refs):
    ring = lax.axis_size("ring")
    count = len(units) + 1
    small, lefts, rights, refs = refs[0], (refs[1],) + (refs[2],) * (whole - 1), refs[3 : whole + 3], refs[whole + 3 :]
    grads, matrices, (x, gain, passed), refs = refs[:3], refs[3:6], refs[6:9], refs[9:]
    outs, (input_grad, gain_out), refs = refs[: whole + 1], refs[whole + 1 : whole + 3], refs[whole + 3 :]
    scratch, (out_a, out_b), refs = refs[: 9 * count], refs[9 * count : 9 * count + 2], refs[9 * count + 2 :]
    send, got, ring_send, ring_got, load, chunks, dn1, sums, arrived, ring_arrived, fetch, gain_send, gain_got = refs
    a, b, r, c = (lax.axis_index(n) for n in ALL)
    na, nb, nc = turn("ca", 1), turn("cb", 1), turn("core", 1)
    to_a, to_b, to_core = {"ca": na}, {"cb": nb}, {"core": nc}
    bufs = [scratch[9 * w : 9 * w + 9] for w in range(count)]
    greet([to_a, to_b, to_core] + [{"ring": turn("ring", k)} for k in range(1, ring)])

    def chunk(i, slot, w):
        rows = chunks.shape[2]
        return pltpu.make_async_copy(
            matrices[w].at[pl.ds(pl.multiple_of(i * rows, rows), rows), :], chunks.at[slot, w], fetch.at[slot, w]
        )

    steps, chunk_rows = matrices[0].shape[0] // chunks.shape[2], chunks.shape[2]

    def input_part(begin, end):
        rows = chunk_rows

        def one(i, carry):
            slot = lax.rem(i, 2)

            @pl.when(i + 1 < steps)
            def _():
                for w in range(3):
                    chunk(i + 1, 1 - slot, w).start()

            value = jnp.zeros((x.shape[0], rows), jnp.float32)
            for w in range(3):
                chunk(i, slot, w).wait()
                value = value + times_transposed(grads[w][...], chunks[slot, w])
            dn1[:, pl.ds(pl.multiple_of(i * rows, rows), rows)] = value
            return carry

        lax.fori_loop(begin, end, one, 0)

    def input_end():
        tile = 32
        sums[0] = jnp.zeros(sums.shape[1:], jnp.float32)

        def back(i, carry):
            at = pl.ds(pl.multiple_of(i * tile, tile), tile)
            v, grad = x[at, :].astype(jnp.float32), dn1[at, :]
            factor = lax.rsqrt(jnp.mean(v * v, axis=-1, keepdims=True) + EPSILON)
            weighted = grad * gain[...]
            inner = jnp.mean(weighted * v, axis=-1, keepdims=True)
            total = passed[at, :] + factor * weighted - v * (factor * factor * factor * inner)
            input_grad[at, :] = total.astype(input_grad.dtype)
            gained = grad * v * factor
            sums[0] += sum(gained[k : k + 8] for k in range(0, tile, 8))
            return carry

        lax.fori_loop(0, x.shape[0] // tile, back, 0)
        push(sums.at[0], arrived.at[0], gain_send.at[0], gain_got.at[0], to_a)

    def gain_stage(stage):
        if stage < 3:
            await_bytes(arrived.at[stage], gain_got.at[stage])
            sums[stage + 1] = sums[stage] + arrived[stage]
            if stage < 2:
                push(sums.at[stage + 1], arrived.at[stage + 1], gain_send.at[stage + 1], gain_got.at[stage + 1], (to_b, to_core)[stage])
            else:
                for k in range(1, ring):
                    push(sums.at[3], ring_arrived.at[k - 1], gain_send.at[2 + k], gain_got.at[2 + k], {"ring": turn("ring", k)})
        else:
            total = sums[3]
            for k in range(1, ring):
                await_bytes(ring_arrived.at[k - 1], gain_got.at[2 + k])
                total = total + ring_arrived[k - 1]
            gain_out[...] = total
            for k in range(3 + ring - 1):
                await_bytes(sums.at[0], gain_send.at[k])

    def half(ref, which):
        rows, cols = ref.shape[-2:]
        lead = (slice(None),) * (len(ref.shape) - 2)
        if cols > 128:
            return ref.at[(*lead, slice(None), pl.ds(which * (cols // 2), cols // 2))]
        return ref.at[(*lead, pl.ds(which * (rows // 2), rows // 2), slice(None))]

    own_a, own_b = bufs[0][:2]
    loads = (
        pltpu.make_async_copy(half(small.at[a], 0), own_a, load.at[0, 0]),
        pltpu.make_async_copy(half(small.at[:, b], 1), own_b, load.at[0, 1]),
    )

    def product(w, block, which):
        own = bufs[w][0]
        rows, cols = own.shape[1] * own.shape[2], own.shape[3]
        at, begin, _ = units[w - 1]
        left = lefts[at][:, pl.ds(pl.multiple_of(block * rows, rows), rows)]
        value = transposed_times(left, rights[at][:, pl.ds(begin + which * cols, cols)])
        return value.reshape(own.shape[1:])

    def sent_first(w):
        await_bytes(bufs[w][2], send.at[w, 0])
        await_bytes(bufs[w][3], send.at[w, 1])

    def first(w):
        in_a, in_b = bufs[w][2:4]
        if w == 0:
            for copy in loads:
                copy.start()
            push(half(small.at[na], 0), in_a, send.at[w, 0], got.at[w, 0], to_a)
            push(half(small.at[:, nb], 1), in_b, send.at[w, 1], got.at[w, 1], to_b)
            return
        if w > 2:
            sent_first(w - 2)

        own_cols = pl.ds(0, bufs[w][0].shape[3])

        def one_a(i, carry):
            out_a[w % 2, i, :, :, own_cols] = product(w, 2 * na + i, 0).astype(out_a.dtype)
            return carry

        def one_b(i, carry):
            out_b[w % 2, i, :, :, own_cols] = product(w, 2 * i + nb, 1).astype(out_b.dtype)
            return carry

        lax.fori_loop(0, 2, one_a, 0)
        push(out_a.at[w % 2, :, :, :, own_cols], in_a, send.at[w, 0], got.at[w, 0], to_a)
        lax.fori_loop(0, 2, one_b, 0)
        push(out_b.at[w % 2, :, :, :, own_cols], in_b, send.at[w, 1], got.at[w, 1], to_b)

    def second(w):
        own_a, own_b, in_a, in_b, in_a2, in_b2 = bufs[w][:6]
        if w == 0:
            for copy in loads:
                copy.wait()

        def one_a(i, carry):
            mine = own_a[i] if w == 0 else product(w, 2 * a + i, 0)
            own_a[i] = (mine + in_a[i].astype(jnp.float32)).astype(own_a.dtype)
            return carry

        def one_b(i, carry):
            mine = own_b[i] if w == 0 else product(w, 2 * i + b, 1)
            own_b[i] = (mine + in_b[i].astype(jnp.float32)).astype(own_b.dtype)
            return carry

        await_bytes(in_a, got.at[w, 0])
        lax.fori_loop(0, 2, one_a, 0)
        push(own_a.at[nb], in_a2, send.at[w, 2], got.at[w, 2], to_b)
        await_bytes(in_b, got.at[w, 1])
        lax.fori_loop(0, 2, one_b, 0)
        push(own_b.at[na], in_b2, send.at[w, 3], got.at[w, 3], to_a)

    def third(w):
        own_a, own_b, _, _, in_a2, in_b2, total, in_ring = bufs[w][:8]
        await_bytes(in_a2, got.at[w, 2])
        await_bytes(in_b2, got.at[w, 3])

        def one(k, carry):
            sums = [
                own[own_at, k].astype(jnp.float32) + more[k].astype(jnp.float32)
                for own, own_at, more in ((own_a, b, in_a2), (own_b, a, in_b2))
            ]
            for which in range(2):
                half(total.at[k], which)[...] = sums[which].astype(total.dtype)
            return carry

        lax.fori_loop(0, ring, one, 0)
        for k in range(1, ring):
            at = turn("ring", k)
            push(total.at[at], in_ring.at[k - 1], ring_send.at[w, k - 1], ring_got.at[w, k - 1], {"ring": at})

    def fourth(w):
        total, in_ring, final = bufs[w][6:9]
        for k in range(1, ring):
            await_bytes(in_ring.at[k - 1], ring_got.at[w, k - 1])
        if final.shape[0] == 2:
            rows = final.shape[1]
            for core in range(2):
                at = pl.ds(core * rows, rows)
                value = total[r, at, :].astype(jnp.float32)
                for k in range(ring - 1):
                    value = value + in_ring[k, at, :].astype(jnp.float32)
                final[core] = value
            cols = final.shape[2]
            at, begin, _ = units[w - 1]
            there = outs[at + 1].at[:, pl.ds(pl.multiple_of(c * rights[at].shape[1] + begin, 128), cols)]
            push(final.at[nc], there, send.at[w, 4], got.at[w, 4], to_core)
            pltpu.make_async_copy(final.at[c], there, load.at[w, 2]).start()
        else:
            value = total[r].astype(jnp.float32)
            for k in range(ring - 1):
                value = value + in_ring[k].astype(jnp.float32)
            outs[w][...] = value

    def finish(w):
        own_a, own_b, in_a, in_b, in_a2, in_b2, total, in_ring, final = bufs[w]
        if w == 0 or w + 2 >= count:
            sent_first(w)
        await_bytes(in_a2, send.at[w, 2])
        await_bytes(in_b2, send.at[w, 3])
        for k in range(1, ring):
            await_bytes(in_ring.at[k - 1], ring_send.at[w, k - 1])
        if final.shape[0] == 2:
            await_bytes(final.at[0], send.at[w, 4])
            await_bytes(final.at[0], got.at[w, 4])
            await_bytes(final.at[0], load.at[w, 2])

    for w in range(3):
        chunk(0, 0, w).start()
    first(0)
    for step in range(max(count + 3, 9)):
        if step + 1 < count:
            first(step + 1)
        if step < count:
            second(step)
        if 0 <= step - 1 < count:
            third(step - 1)
        if 0 <= step - 2 < count:
            fourth(step - 2)
        if 1 <= step < 5:
            input_part((step - 1) * steps // 4, step * steps // 4)
        if step == 4:
            input_end()
        if 4 < step < 9:
            gain_stage(step - 5)
    for w in range(count):
        finish(w)


def collect(small, lefts, rights, grads, matrices, x, gain, passed):
    units, ring = column_units(len(rights), rights[0].shape[1]), lax.axis_size("ring")
    count = len(units) + 1
    chips = lax.axis_size("ca") * lax.axis_size("cb") * ring
    square = (lax.axis_size("ca"), lax.axis_size("cb"), ring)
    view = small.reshape(square + small.shape[1:])
    rows = lefts[0].shape[1] // chips
    forms = [(*view.shape[3:], view.dtype)] + [(rows, cols, lefts[0].dtype) for _, _, cols in units]
    shapes = [view.shape[3:]] + [(rows // 2, 2 * r.shape[1]) for r in rights]
    shapes, scratch = [jax.ShapeDtypeStruct(shape, jnp.float32) for shape in shapes], []
    for rows, cols, dtype in forms:
        piece = (rows, cols // 2) if cols > 128 else (rows // 2, cols)
        big = cols > 128
        vmem = lambda *shape: pltpu.VMEM(shape, dtype)
        scratch += [vmem(2, ring, *piece)] * 4 + [vmem(ring, *piece)] * 2
        scratch += [vmem(ring, rows, cols), vmem(ring - 1, rows, cols)]
        scratch += [pltpu.VMEM((2, rows // 2, cols) if big else (1, 8, 128), jnp.float32)]
    scratch += [vmem(2, 2, ring, lefts[0].shape[1] // chips, units[0][2] // 2)] * 2
    dma = pltpu.SemaphoreType.DMA
    vm, anywhere = pl.BlockSpec(memory_space=pltpu.VMEM), pl.BlockSpec(memory_space=pl.ANY)
    wide = (8, gain.shape[1])
    f32 = lambda *shape: pltpu.VMEM(shape, jnp.float32)
    outs = pl.pallas_call(
        functools.partial(collect_kernel, len(rights), units),
        out_shape=shapes + [jax.ShapeDtypeStruct(x.shape, x.dtype), jax.ShapeDtypeStruct(wide, jnp.float32)],
        in_specs=[anywhere] + [vm] * (len(rights) + 5) + [anywhere] * 3 + [vm] * 3,
        out_specs=[vm] * (len(rights) + 3),
        scratch_shapes=scratch
        + [dma((count, 5)), dma((count, 5)), dma((count, ring - 1)), dma((count, ring - 1)), dma((count, 3))]
        + [pltpu.VMEM((2, 3, 128, x.shape[1]), x.dtype), f32(*x.shape), f32(4, *wide), f32(3, *wide), f32(ring - 1, *wide)]
        + [dma((2, 3)), dma((2 + ring,)), dma((2 + ring,))],
        compiler_params=pltpu.CompilerParams(collective_id=1, has_side_effects=True, vmem_limit_bytes=62 << 20),
        cost_estimate=pl.CostEstimate(flops=160_000_000_000, bytes_accessed=320_000_000, transcendentals=0),
        name="collect",
    )(view, *lefts, *rights, *grads, *matrices, x, gain, passed)
    return outs[1:-2], outs[0], outs[-2], outs[-1]


def dispatch_kernel(
    rows, router, hot, g_all, out, picked, grads, gates, probs,
    rows_in, g_in, picked_low, grads_low, load, store, ring_send, ring_got, place, core_send, core_got,
):
    ring = lax.axis_size("ring")
    r, c, nc = lax.axis_index("ring"), lax.axis_index("core"), turn("core", 1)
    to_core, experts = {"core": nc}, hot.shape[1]
    greet([to_core] + [{"ring": turn("ring", k)} for k in range(1, ring)])
    block_of = lambda at: out.at[at, c]

    own = pltpu.make_async_copy(rows, block_of(r), place)
    own.start()
    push(rows, block_of(r), core_send, core_got.at[r], to_core)
    own.wait()
    send_along(0, block_of(r), block_of, ring_send, ring_got)
    first = (r * 2 + c) * experts
    width = rows.shape[1]
    cols = min(512, width)

    def pick(at, core):
        source = at * 2 + core
        copies = (
            pltpu.make_async_copy(out.at[at, core], rows_in, load.at[0]),
            pltpu.make_async_copy(g_all.at[at, core], g_in, load.at[1]),
        )
        for copy in copies:
            copy.start()
        copies[0].wait()
        logits = times_transposed(router[...], rows_in[...])
        likely = jnp.exp(logits - jnp.max(logits, axis=0, keepdims=True))
        probs[source] = likely / jnp.sum(likely, axis=0, keepdims=True)
        copies[1].wait()
        for e in range(experts):
            own_probs = probs[source, pl.ds(first + e, 1), :]
            gate = jnp.sum(hot[source, e].astype(jnp.float32) * own_probs, axis=-1, keepdims=True)
            gates[e, source] = gate

            def part(i, carry):
                lanes = pl.ds(pl.multiple_of(i * cols, cols), cols)
                chosen = hot[source, e]
                picked_low[e, :, lanes] = matmul(chosen, rows_in[:, lanes]).astype(picked_low.dtype)
                grads_low[e, :, lanes] = (matmul(chosen, g_in[:, lanes]) * gate).astype(grads_low.dtype)
                return carry

            lax.fori_loop(0, width // cols, part, 0)
        stores = (
            pltpu.make_async_copy(picked_low, picked.at[:, source], store.at[0]),
            pltpu.make_async_copy(grads_low, grads.at[:, source], store.at[1]),
        )
        for copy in stores:
            copy.start()
        for copy in stores:
            copy.wait()

    pick(r, c)
    await_bytes(out.at[r, nc], core_got.at[r])
    pick(r, nc)

    def step_on(step, carry):
        take_along(step, block_of, ring_got, lambda at: None)

        @pl.when(step + 1 < ring - 1)
        def _():
            send_along(step + 1, None, block_of, ring_send, ring_got)

        for _, comes, _, block, _, _ in along(step):

            @pl.when(comes)
            def _(block=block):
                push(block_of(block), block_of(block), core_send, core_got.at[block], to_core)

        def four(k, carry):
            side, other = k // 2, lax.rem(k, 2)
            (_, comes0, _, block0, _, _), (_, comes1, _, block1, _, _) = along(step)
            block = jnp.where(side == 0, block0, block1)
            comes = ((side == 0) & comes0) | ((side == 1) & comes1)
            core = lax.rem(c + other, 2)

            @pl.when(comes & (other == 1))
            def _():
                await_bytes(out.at[block, nc], core_got.at[block])

            @pl.when(comes)
            def _():
                pick(block, core)

            return carry

        lax.fori_loop(0, 4, four, 0)
        return carry

    lax.fori_loop(0, ring - 1, step_on, 0)
    sent_along(rows, ring_send)
    await_bytes(out.at[:, c], core_send)


def dispatch(rows, router, hot, g_all):
    ring, dma = lax.axis_size("ring"), pltpu.SemaphoreType.DMA
    sources, experts, slots, count = hot.shape
    width = rows.shape[1]
    low = lambda *shape: jax.ShapeDtypeStruct(shape, rows.dtype)
    f32 = lambda *shape: jax.ShapeDtypeStruct(shape, jnp.float32)
    vm, anywhere = pl.BlockSpec(memory_space=pltpu.VMEM), pl.BlockSpec(memory_space=pl.ANY)
    block = pltpu.VMEM((experts, slots, width), rows.dtype)
    chosen = (experts, sources, slots, width)
    return pl.pallas_call(
        dispatch_kernel,
        out_shape=[
            low(ring, 2, count, width), low(*chosen), low(*chosen), f32(experts, sources, slots, 1),
            f32(sources, router.shape[0], count),
        ],
        in_specs=[vm, vm, vm, anywhere],
        out_specs=[anywhere, anywhere, anywhere, vm, vm],
        scratch_shapes=[pltpu.VMEM(rows.shape, rows.dtype)] * 2
        + [block, block]
        + [dma((2,)), dma((2,)), dma((2, ring)), dma((2, ring)), dma, dma, dma((ring,))],
        compiler_params=pltpu.CompilerParams(collective_id=2, has_side_effects=True, vmem_limit_bytes=56 << 20),
        cost_estimate=pl.CostEstimate(flops=1_000_000, bytes_accessed=10_000, transcendentals=0),
        name="dispatch",
    )(rows, router, hot, g_all)


def give_back_kernel(
    hot, logit, logit_turned, router, pairs, mixed, n2, out, mixed_out, router_part,
    sums, chain_in, to_core, pair_in, mixed_in, mixed_low, n2_in,
    load, core_send, core_got, chain_send, chain_got, load_more, store,
):
    ring, pieces, rows, width = sums.shape
    sources, experts = hot.shape[:2]
    r, c, nc = lax.axis_index("ring"), lax.axis_index("core"), turn("core", 1)
    to_next, to_last = {"ring": turn("ring", 1)}, {"ring": turn("ring", ring - 1)}
    greet([{"core": nc}] + [{"ring": turn("ring", k)} for k in range(1, ring)])
    cols, tile = min(512, width), 32

    def whose(i):
        return (1 - i % 2) * (ring - 1 - i // 2) + (i % 2) * (i // 2)

    def fetch(i, j):
        return pltpu.make_async_copy(pairs.at[:, whose(i) * 2 + (nc, c)[j]], pair_in.at[j], load.at[j])

    def put_back(source, ref, lanes):
        return sum(matmul(hot[source, e], ref[e, :, lanes]) for e in range(experts))

    def block(source, j, into, more):
        def part(k, carry):
            lanes = pl.ds(pl.multiple_of(k * cols, cols), cols)
            value = put_back(source, pair_in.at[j], lanes) + matmul(logit[source], router[:, lanes])
            for piece in range(pieces):
                got = value[piece * rows : (piece + 1) * rows]
                if more is not None:
                    got = got + more[piece, :, lanes].astype(jnp.float32)
                into[piece, :, lanes] = got.astype(into.dtype)
            return carry

        lax.fori_loop(0, width // cols, part, 0)

    def fetch_beside(source):
        at = lax.rem(source, 2)
        return (
            pltpu.make_async_copy(mixed.at[:, source], mixed_in.at[at], load_more.at[at, 0]),
            pltpu.make_async_copy(n2.at[source], n2_in.at[at], load_more.at[at, 1]),
        )

    def beside(source):
        at = lax.rem(source, 2)

        @pl.when(source + 1 < sources)
        def _():
            for copy in fetch_beside(source + 1):
                copy.start()

        for copy in fetch_beside(source):
            copy.wait()

        @pl.when(source > 0)
        def _():
            await_bytes(mixed_low, store)

        def part(k, carry):
            lanes = pl.ds(pl.multiple_of(k * cols, cols), cols)
            mixed_low[:, lanes] = put_back(source, mixed_in.at[at], lanes).astype(mixed_low.dtype)
            router_part[:, lanes] += matmul(logit_turned[source], n2_in[at, :, lanes])
            return carry

        lax.fori_loop(0, width // cols, part, 0)
        pltpu.make_async_copy(mixed_low, mixed_out.at[source], store).start()

    def slot(side, d, at):
        return d if side == 0 else jnp.where(d == at, ring, d)

    def pass_on(side, step, d, piece, to):
        there = chain_in.at[slot(side, d, r - 1), piece]
        push(sums.at[d, piece], there, chain_send.at[side, step, piece], chain_got.at[side, step, piece], to)

    router_part[...] = jnp.zeros_like(router_part)
    fetch(0, 0).start()
    fetch(0, 1).start()
    for copy in fetch_beside(0):
        copy.start()

    def start(i, carry):
        d = whose(i)
        outgoing = to_core.at[lax.rem(i, 2)]
        fetch(i, 0).wait()

        @pl.when(i >= 2)
        def _():
            await_bytes(outgoing, core_send.at[lax.rem(i, 2)])

        block(d * 2 + nc, 0, outgoing, None)
        push(outgoing, sums.at[d], core_send.at[lax.rem(i, 2)], core_got.at[d], {"core": nc})
        fetch(i, 1).wait()
        await_bytes(sums.at[d], core_got.at[d])
        block(d * 2 + c, 1, sums.at[d], sums.at[d])
        for piece in range(pieces):

            @pl.when((r == 0) & (d != r))
            def _():
                pass_on(0, ring - 1 - d, d, piece, to_next)

            @pl.when((r == ring - 1) & (d != r))
            def _():
                pass_on(1, d, d, piece, to_last)

        @pl.when(i + 1 < ring)
        def _():
            fetch(i + 1, 0).start()
            fetch(i + 1, 1).start()

        beside(i)
        return carry

    lax.fori_loop(0, ring, start, 0)

    def sides(time):
        up, down = time - r, time - (ring - 1 - r)
        return (
            ((r >= 1) & (up >= 0), jnp.maximum(up, 0), ring - 1 - jnp.maximum(up, 0), to_next, 0),
            ((r + 1 < ring) & (down >= 0), jnp.maximum(down, 0), jnp.maximum(down, 0), to_last, 1),
        )

    def on(time, carry):
        for piece in range(pieces):
            for comes, step, d, to, side in sides(time):

                @pl.when(comes)
                def _(step=step, d=d, to=to, side=side):
                    arrived = chain_in.at[slot(side, d, r), piece]
                    await_bytes(arrived, chain_got.at[side, step, piece])

                    def one(k, carry):
                        at = pl.ds(pl.multiple_of(k * tile, tile), tile)
                        total = sums[d, piece, at].astype(jnp.float32) + arrived[at].astype(jnp.float32)
                        sums[d, piece, at] = total.astype(sums.dtype)
                        return carry

                    lax.fori_loop(0, rows // tile, one, 0)

                    @pl.when(time < ring - 1)
                    def _():
                        pass_on(side, step, d, piece, to)

        @pl.when(time < ring - 1)
        def _():
            beside(ring + time - 1)

        return carry

    def rest(source, carry):
        beside(source)
        return carry

    lax.fori_loop(1, ring - 1, on, 0)
    lax.fori_loop(2 * ring - 2, sources, rest, 0)
    on(ring - 1, 0)
    await_bytes(mixed_low, store)

    def total(k, carry):
        at = pl.ds(pl.multiple_of(k * tile, tile), tile)
        for piece in range(pieces):
            out[pl.ds(pl.multiple_of(piece * rows + k * tile, tile), tile), :] = sums[r, piece, at].astype(jnp.float32)
        return carry

    lax.fori_loop(0, rows // tile, total, 0)
    for k in range(2):
        await_bytes(to_core.at[k], core_send.at[k])
    for step in range(ring - 1):
        for piece in range(pieces):
            for sent, side in ((r + step < ring - 1, 0), (step < r, 1)):

                @pl.when(sent)
                def _(side=side):
                    await_bytes(sums.at[0, 0], chain_send.at[side, step, piece])


def give_back(hot, logit, router, pairs, mixed, n2):
    ring, dma, pieces = lax.axis_size("ring"), pltpu.SemaphoreType.DMA, 2
    experts, sources, slots, width = pairs.shape
    rows, all_experts = hot.shape[2], router.shape[0]
    vm, anywhere = pl.BlockSpec(memory_space=pltpu.VMEM), pl.BlockSpec(memory_space=pl.ANY)
    low = lambda *shape: pltpu.VMEM(shape, pairs.dtype)
    block = lambda n: low(n, pieces, rows // pieces, width)
    chain = dma((2, ring, pieces))
    return pl.pallas_call(
        give_back_kernel,
        out_shape=[
            jax.ShapeDtypeStruct((rows, width), jnp.float32),
            jax.ShapeDtypeStruct((sources, rows, width), pairs.dtype),
            jax.ShapeDtypeStruct((all_experts, width), jnp.float32),
        ],
        in_specs=[vm] * 4 + [anywhere] * 3,
        out_specs=[vm, anywhere, vm],
        scratch_shapes=[block(ring), block(ring + 1), block(2), low(2, experts, slots, width), low(2, experts, slots, width)]
        + [low(rows, width), low(2, rows, width)]
        + [dma((2,)), dma((2,)), dma((ring,)), chain, chain, dma((2, 2)), dma],
        compiler_params=pltpu.CompilerParams(collective_id=3, has_side_effects=True, vmem_limit_bytes=60 << 20),
        cost_estimate=pl.CostEstimate(flops=100_000_000_000, bytes_accessed=200_000_000, transcendentals=0),
        name="give_back",
    )(hot, logit, logit.transpose(0, 2, 1), router, pairs, mixed, n2)


def matmul(left, right):
    return jnp.dot(left, right, preferred_element_type=jnp.float32)


def times_transposed(left, right):
    return lax.dot_general(
        left, right, (((1,), (1,)), ((), ())), preferred_element_type=jnp.float32
    )


def transposed_times(left, right):
    return lax.dot_general(
        left, right, (((0,), (0,)), ((), ())), preferred_element_type=jnp.float32
    )


def corners():
    return ((0, 1), (1, 0), (1, 1))


def corner(da, db):
    pa, pb = turn("ca", da), turn("cb", db)
    return 2 * pa + pb, {"ca": pa, "cb": pb}


def rows_to_heads(src, dst, send, got, place):
    rows, width = src.shape[0], dst.shape[1]
    me, _ = corner(0, 0)
    there = dst.at[pl.ds(pl.multiple_of(me * rows, rows), rows), :]
    for i, (da, db) in enumerate(corners()):
        peer, to = corner(da, db)
        push(src.at[:, pl.ds(pl.multiple_of(peer * width, width), width)], there, send.at[i], got.at[i], to)
    pltpu.make_async_copy(src.at[:, pl.ds(pl.multiple_of(me * width, width), width)], there, place).start()


def wait_heads(src, dst, got, place):
    rows = src.shape[0]
    here = lambda at: dst.at[pl.ds(pl.multiple_of(at * rows, rows), rows), :]
    await_bytes(here(corner(0, 0)[0]), place)
    for i, (da, db) in enumerate(corners()):
        await_bytes(here(corner(da, db)[0]), got.at[i])


def swap_halves(v):
    return pltpu.roll(v, HD // 2, 1)


def norm_and_turn(raw, gain, cosine, sine, out):
    rows, width = raw.shape
    tile = 32

    def part(i, carry):
        at = pl.ds(pl.multiple_of(i * tile, tile), tile)
        value = raw[at, :]
        factor = lax.rsqrt(jnp.mean(value * value, axis=-1, keepdims=True) + EPSILON)
        for h in range(width // HD):
            lanes = pl.ds(h * HD, HD)
            v = raw[at, lanes] * factor * gain[:, lanes]
            out[at, lanes] = (v * cosine[at, :] + swap_halves(v) * sine[at, :]).astype(out.dtype)
        return carry

    lax.fori_loop(0, rows // tile, part, 0)


def norm_and_turn_back(grad, raw, gain, cosine, sine, out, gain_grad, turned):
    rows, width = raw.shape
    tile = 32
    gain_grad[...] = jnp.zeros_like(gain_grad)

    def part(i, carry):
        at = pl.ds(pl.multiple_of(i * tile, tile), tile)
        value = raw[at, :]
        factor = lax.rsqrt(jnp.mean(value * value, axis=-1, keepdims=True) + EPSILON)
        inner = jnp.zeros((tile, HD), jnp.float32)
        for h in range(width // HD):
            lanes = pl.ds(h * HD, HD)
            g = grad[at, lanes].astype(jnp.float32)
            g = g * cosine[at, :] - swap_halves(g) * sine[at, :]
            turned[:, lanes] = g
            inner = inner + g * gain[:, lanes] * raw[at, lanes]
        inner = jnp.sum(inner, axis=-1, keepdims=True) * (factor * factor * factor / width)
        for h in range(width // HD):
            lanes = pl.ds(h * HD, HD)
            g, v = turned[:, lanes], raw[at, lanes]
            out[at, lanes] = (factor * (g * gain[:, lanes]) - v * inner).astype(out.dtype)
            gained = g * v * factor
            gain_grad[:, lanes] += sum(gained[k : k + 8] for k in range(0, tile, 8))
        return carry

    lax.fori_loop(0, rows // tile, part, 0)


def attend_kernel(scale, q_raw, k_raw, v, q_gain, k_gain, cosine, sine, keep, o, qh, kh, vh, logs, q, k, oh, send, got, place, send_o, got_o, place_o):
    rows, width = v.shape[0], qh.shape[1]
    greet([corner(da, db)[1] for da, db in corners()])
    pairs = ((v, vh), (k, kh), (q, qh))
    rows_to_heads(v, vh, send.at[0], got.at[0], place.at[0])
    norm_and_turn(k_raw, k_gain, cosine, sine, k)
    rows_to_heads(k, kh, send.at[1], got.at[1], place.at[1])
    norm_and_turn(q_raw, q_gain, cosine, sine, q)
    rows_to_heads(q, qh, send.at[2], got.at[2], place.at[2])
    for i, (src, dst) in enumerate(pairs):
        wait_heads(src, dst, got.at[i], place.at[i])
    me, _ = corner(0, 0)
    tile = 128
    mine = pl.ds(pl.multiple_of(me * width, width), width)

    def block(at_block):
        def part(i, carry):
            at = pl.ds(pl.multiple_of(at_block * rows + i * tile, tile), tile)
            for h in range(width // HD):
                lanes = pl.ds(h * HD, HD)
                s = times_transposed(qh[at, lanes], kh[:, lanes]) * scale
                s = jnp.where(keep[...] > 0.0, s, NEG_FILL)
                peak = jnp.max(s, axis=-1, keepdims=True)
                p = jnp.exp(s - peak)
                total = jnp.sum(p, axis=-1, keepdims=True)
                logs[h, at, :] = peak + jnp.log(total)
                low = (p * (1.0 / total)).astype(jnp.bfloat16)
                oh[at, lanes] = matmul(low, vh[:, lanes]).astype(jnp.bfloat16)
            return carry

        lax.fori_loop(0, rows // tile, part, 0)

    for i, (da, db) in enumerate(corners()):
        peer, to = corner(da, db)
        block(peer)
        push(oh.at[pl.ds(pl.multiple_of(peer * rows, rows), rows), :], o.at[:, mine], send_o.at[i], got_o.at[i], to)
    block(me)
    pltpu.make_async_copy(oh.at[pl.ds(pl.multiple_of(me * rows, rows), rows), :], o.at[:, mine], place_o).start()
    pltpu.make_async_copy(oh.at[pl.ds(pl.multiple_of(me * rows, rows), rows), :], o.at[:, mine], place_o).wait()
    piece = o.at[:, mine]
    for i in range(3):
        await_bytes(piece, got_o.at[i])
        await_bytes(piece, send_o.at[i])
        for j in range(3):
            await_bytes(piece, send.at[j, i])


def attend(q_raw, k_raw, v, q_gain, k_gain, cosine, sine, keep, scale):
    rows, width = v.shape
    chips = lax.axis_size("ca") * lax.axis_size("cb")
    heads = jax.ShapeDtypeStruct((rows * chips, width // chips), v.dtype)
    vm, dma = pl.BlockSpec(memory_space=pltpu.VMEM), pltpu.SemaphoreType.DMA
    return pl.pallas_call(
        functools.partial(attend_kernel, scale),
        out_shape=[jax.ShapeDtypeStruct(v.shape, v.dtype), heads, heads, heads]
        + [jax.ShapeDtypeStruct((width // chips // HD, rows * chips, 1), jnp.float32)],
        in_specs=[vm] * 8,
        out_specs=[vm] * 5,
        scratch_shapes=[pltpu.VMEM(v.shape, v.dtype)] * 2 + [pltpu.VMEM(heads.shape, v.dtype)]
        + [dma((3, 3)), dma((3, 3)), dma((3,)), dma((3,)), dma((3,)), dma],
        compiler_params=pltpu.CompilerParams(collective_id=4, has_side_effects=True, vmem_limit_bytes=48 << 20),
        cost_estimate=pl.CostEstimate(flops=1_000_000, bytes_accessed=10_000, transcendentals=0),
        name="attend",
    )(q_raw, k_raw, v, q_gain, k_gain, cosine, sine, keep)


def attend_back_kernel(
    scale, do, qh, kh, vh, logs, keep, q_raw, k_raw, q_gain, k_gain, cosine, sine,
    dq_raw, dk_raw, dv, q_gain_grad, k_gain_grad,
    doh, dqh, dkh, dvh, dq, dk, turned, send, got, place, send_g, got_g, place_g,
):
    rows, width = do.shape[0], qh.shape[1]
    greet([corner(da, db)[1] for da, db in corners()])
    rows_to_heads(do, doh, send, got, place)
    wait_heads(do, doh, got, place)
    me, _ = corner(0, 0)
    tile, total_rows = 128, qh.shape[0]
    grads = ((dqh, dq), (dkh, dk), (dvh, dv))

    def one_head(h):
        lanes = pl.ds(h * HD, HD)

        def part(i, carry):
            dk_sum, dv_sum = carry
            at = pl.ds(pl.multiple_of(i * tile, tile), tile)
            qb, db, kb, vb = qh[at, lanes], doh[at, lanes], kh[:, lanes], vh[:, lanes]
            s = times_transposed(qb, kb) * scale
            s = jnp.where(keep[...] > 0.0, s, NEG_FILL)
            p = jnp.exp(s - logs[h, at, :])
            dp = times_transposed(db, vb)
            ds = (p * (dp - jnp.sum(dp * p, axis=-1, keepdims=True))).astype(jnp.bfloat16)
            dqh[at, lanes] = (matmul(ds, kb) * scale).astype(jnp.bfloat16)
            dk_sum = dk_sum + transposed_times(ds, qb)
            dv_sum = dv_sum + transposed_times(p.astype(jnp.bfloat16), db)
            return dk_sum, dv_sum

        zero = jnp.zeros((total_rows, HD), jnp.float32)
        dk_sum, dv_sum = lax.fori_loop(0, total_rows // tile, part, (zero, zero))
        dkh[:, lanes] = (dk_sum * scale).astype(jnp.bfloat16)
        dvh[:, lanes] = dv_sum.astype(jnp.bfloat16)

    for h in range(width // HD):
        one_head(h)
        lanes = pl.ds(h * HD, HD)
        here = pl.ds(pl.multiple_of(me * width + h * HD, HD), HD)
        for g, (src, dst) in enumerate(grads):
            for i, (da, db) in enumerate(corners()):
                peer, to = corner(da, db)
                push(src.at[pl.ds(pl.multiple_of(peer * rows, rows), rows), lanes], dst.at[:, here], send_g.at[g, i, h], got_g.at[g, i, h], to)
            own = src.at[pl.ds(pl.multiple_of(me * rows, rows), rows), lanes]
            pltpu.make_async_copy(own, dst.at[:, here], place_g.at[g, h]).start()
    piece = dq.at[:, pl.ds(0, HD)]
    for h in range(width // HD):
        for g in range(3):
            await_bytes(piece, place_g.at[g, h])
            for i in range(3):
                await_bytes(piece, send_g.at[g, i, h])
                await_bytes(piece, got_g.at[g, i, h])
    for i in range(3):
        await_bytes(do.at[:, pl.ds(0, width)], send.at[i])
    norm_and_turn_back(dk, k_raw, k_gain, cosine, sine, dk_raw, k_gain_grad, turned)
    norm_and_turn_back(dq, q_raw, q_gain, cosine, sine, dq_raw, q_gain_grad, turned)


def attend_back(do, qh, kh, vh, logs, keep, q_raw, k_raw, q_gain, k_gain, cosine, sine, scale):
    heads = qh.shape[1] // HD
    vm, dma = pl.BlockSpec(memory_space=pltpu.VMEM), pltpu.SemaphoreType.DMA
    return pl.pallas_call(
        functools.partial(attend_back_kernel, scale),
        out_shape=[jax.ShapeDtypeStruct(do.shape, do.dtype)] * 3 + [jax.ShapeDtypeStruct((8, do.shape[1]), jnp.float32)] * 2,
        in_specs=[vm] * 12,
        out_specs=[vm] * 5,
        scratch_shapes=[pltpu.VMEM(qh.shape, qh.dtype)] * 4
        + [pltpu.VMEM(do.shape, do.dtype)] * 2
        + [pltpu.VMEM((32, do.shape[1]), jnp.float32)]
        + [dma((3,)), dma((3,)), dma, dma((3, 3, heads)), dma((3, 3, heads)), dma((3, heads))],
        compiler_params=pltpu.CompilerParams(collective_id=5, has_side_effects=True, vmem_limit_bytes=56 << 20),
        cost_estimate=pl.CostEstimate(flops=50_000_000_000, bytes_accessed=10_000_000, transcendentals=0),
        name="attend_back",
    )(do, qh, kh, vh, logs, keep, q_raw, k_raw, q_gain, k_gain, cosine, sine)


def join_kernel(own, from_b, from_a, first, second, out, held, load, store):
    experts, units = own.shape[:2]
    a, b = lax.axis_index("ca"), lax.axis_index("cb")
    na, nb = turn("ca", 1), turn("cb", 1)
    loads, stores = [], []
    for piece, (p, q) in enumerate(((a, b), (a, nb), (na, b), (na, nb))):
        for e in range(experts):
            if piece < 3:
                src = (own, from_b, from_a)[piece].at[e]
            else:
                src = first.at[e] if e < experts // 2 else second.at[e - experts // 2]
            here = held.at[piece, e]
            loads.append(pltpu.make_async_copy(src, here, load.at[piece, e]))
            at = pl.ds(pl.multiple_of((2 * p + q) * units, units), units)
            stores.append(pltpu.make_async_copy(here, out.at[e, at, :], store.at[piece, e]))
    for copy in loads:
        copy.start()
    for fetch, copy in zip(loads, stores):
        fetch.wait()
        copy.start()
    for copy in stores:
        copy.wait()


def join(own, from_b, from_a, first, second):
    experts, units, width = own.shape
    anywhere, dma = pl.BlockSpec(memory_space=pl.ANY), pltpu.SemaphoreType.DMA((4, experts))
    return pl.pallas_call(
        join_kernel,
        out_shape=jax.ShapeDtypeStruct((experts, 4 * units, width), own.dtype),
        in_specs=[anywhere] * 5,
        out_specs=anywhere,
        scratch_shapes=[pltpu.VMEM((4, experts, units, width), own.dtype), dma, dma],
        cost_estimate=pl.CostEstimate(flops=0, bytes_accessed=8 * experts * units * width * 2, transcendentals=0),
        name="join",
    )(own, from_b, from_a, first, second)


def norm_rows(values, gain):
    factor = lax.rsqrt(jnp.mean(values * values, axis=-1, keepdims=True) + EPSILON)
    return (values * factor * gain, factor)


def norm_back(grad, values, factor, gain):
    weighted = grad * gain
    inner = jnp.mean(weighted * values, axis=-1, keepdims=True)
    return (factor * weighted - values * factor**3 * inner, jnp.sum(grad * values * factor, axis=0))


def rotary_tables(positions, head_dim):
    half_dim = head_dim // 2
    frequency = jnp.exp(-math.log(ROPE_THETA) * jnp.arange(half_dim, dtype=jnp.float32) / half_dim)
    angles = positions.astype(jnp.float32)[:, None] * frequency[None, :]
    return (jnp.cos(angles), jnp.sin(angles))


def local(
    tokens, cotangent, lengths, expert_ids, query_weight, key_weight, value_weight, out_weight,
    router_weight, first_gain, second_gain, query_gain, key_gain, gate_weight, up_weight, down_weight,
):
    token_count = tokens.shape[1]
    model_width = tokens.shape[2]
    head_dim = HD
    top_count = expert_ids.shape[2]
    experts = router_weight.shape[1]
    local_experts = gate_weight.shape[0]
    ctx_size = lax.axis_size(CTX)
    sources = lax.axis_size(EXP)
    capacity = max(2, -(-(token_count * top_count * 9) // (experts * 8)))
    score_scale = 1.0 / math.sqrt(head_dim)
    seq_len = token_count * ctx_size

    inputs = tokens[0].astype(jnp.float32)
    length = lengths[0]
    positions = lax.axis_index(CTX) * token_count + jnp.arange(token_count, dtype=jnp.int32)
    row_valid = positions < length
    row_valid = row_valid.astype(jnp.float32)[:, None]
    key_valid = jnp.arange(seq_len, dtype=jnp.int32) < length
    grad_total_low = (cotangent[0].astype(jnp.float32) * row_valid).astype(jnp.bfloat16)
    grad_total = grad_total_low.astype(jnp.float32)

    rows_each = query_weight.shape[0]
    packed = jnp.concatenate(
        [g.reshape(-1) for g in (first_gain, second_gain, query_gain, key_gain)] + [router_weight.reshape(-1)]
    )
    small = jnp.pad(packed, (0, -packed.size % 2048)).reshape(-1, 128)
    ids_low = expert_ids[0].astype(jnp.bfloat16).reshape(-1, 128)
    gathered, (ids_all, g_all) = spread([query_weight, key_weight, value_weight, out_weight, small], [ids_low, grad_total_low])
    full_query, full_key, full_value, full_out = (w.reshape(model_width, -1) for w in gathered[:4])
    smalls = gathered[4].reshape(-1, small.size)
    gains = [smalls[:, i * rows_each : (i + 1) * rows_each].reshape(-1).astype(jnp.float32) for i in range(4)]
    gain_first, gain_second, gain_queries, gain_keys = gains
    full_router = smalls[:, 4 * rows_each : packed.size].reshape(model_width, experts)
    ids_all = ids_all.reshape(sources, token_count, top_count).astype(jnp.int32)
    full_value, gate_weight, up_weight = lax.optimization_barrier((full_value, gate_weight, up_weight))
    gate_all, up_all = (lax.all_gather(w, CTX, axis=2, tiled=True) for w in (gate_weight, up_weight))
    cosine, sine = rotary_tables(positions, head_dim)
    normed_one, factor_one = norm_rows(inputs, gain_first)
    normed_one_low = normed_one.astype(jnp.bfloat16)
    query_raw = matmul(normed_one_low, full_query)
    key_raw = matmul(normed_one_low, full_key)
    value_low = matmul(normed_one_low, full_value).astype(jnp.bfloat16)
    keep = key_valid.astype(jnp.float32)[None, :]
    turns = (jnp.concatenate([cosine, cosine], axis=1), jnp.concatenate([-sine, sine], axis=1))
    row = lambda g: g.reshape(1, model_width)
    shared = (row(gain_queries), row(gain_keys), *turns)
    attended_low, *saved = attend(query_raw, key_raw, value_low, *shared, keep, score_scale)
    flip = lambda v, axis: lax.ppermute(v, axis, [(0, 1), (1, 0)])
    hidden_state = inputs + matmul(attended_low, full_out)
    normed_two, factor_two = norm_rows(hidden_state, gain_second)
    normed_two_low = normed_two.astype(jnp.bfloat16)

    first_expert = lax.axis_index(EXP) * local_experts
    own_experts = first_expert + jnp.arange(local_experts, dtype=jnp.int32)
    mask = jnp.any(ids_all[:, None, :, :] == own_experts[None, :, None, None], axis=-1)
    before = (jnp.arange(token_count)[:, None] < jnp.arange(token_count)[None, :]).astype(jnp.bfloat16)
    ranks = jnp.einsum("seu,ut->set", mask.astype(jnp.bfloat16), before, preferred_element_type=jnp.float32)
    slots = jnp.arange(capacity, dtype=jnp.float32)
    hot = (mask[:, :, None, :] & (ranks[:, :, None, :] == slots[None, None, :, None])).astype(jnp.bfloat16)
    router_turned = full_router.T
    n2_all, x, de, row_gate, probs = dispatch(normed_two_low, router_turned, hot, g_all)
    n2_all = n2_all.reshape(sources, token_count, model_width)
    probs = probs.transpose(0, 2, 1).reshape(-1, experts)
    hot32 = hot.astype(jnp.float32)
    x, gate_all, down_weight = lax.optimization_barrier((x, gate_all, down_weight))
    down_b, down_a = flip(down_weight, "cb"), flip(down_weight, "ca")
    first_half = local_experts // 2
    down_corner = [flip(down_b[:first_half], "ca"), flip(down_a[first_half:], "cb")]
    ee = lambda eq, a, b: jnp.einsum(eq, a, b, preferred_element_type=jnp.float32)
    gp = ee("escd,edf->escf", x, gate_all)
    up = ee("escd,edf->escf", x, up_all)
    sig = jax.nn.sigmoid(gp)
    hid = (gp * sig * up).astype(jnp.bfloat16)
    down_part = ee("escf,escd->efd", hid, de).astype(jnp.bfloat16)
    *down_corner, down_part = lax.optimization_barrier((*down_corner, down_part))
    down_all = join(down_weight, down_b, down_a, *down_corner)
    eo = ee("escf,efd->escd", hid, down_all).astype(jnp.bfloat16)
    gained = jnp.sum(de.astype(jnp.float32) * eo.astype(jnp.float32), axis=-1)
    mixed_rows = (row_gate * eo.astype(jnp.float32)).astype(jnp.bfloat16)
    dhid = ee("escd,efd->escf", de, down_all)
    dgp = (dhid * up * sig * (1.0 + gp * (1.0 - sig))).astype(jnp.bfloat16)
    dup = (dhid * gp * sig).astype(jnp.bfloat16)
    gate_part = ee("escd,escf->edf", x, dgp)
    up_part = ee("escd,escf->edf", x, dup)
    parts = [v.astype(jnp.bfloat16) for v in (down_part, gate_part, up_part)]
    dgp, dup, *_ = lax.optimization_barrier((dgp, dup, *parts))
    rs_ctx = lambda v, a: lax.psum_scatter(v, CTX, scatter_dimension=a, tiled=True)
    down_grad, gate_grad, up_grad = rs_ctx(parts[0], 1), rs_ctx(parts[1], 2), rs_ctx(parts[2], 2)
    dpair = (ee("escf,edf->escd", dgp, gate_all) + ee("escf,edf->escd", dup, up_all)).astype(jnp.bfloat16)

    gained = jnp.sum(hot32 * gained.transpose(1, 0, 2)[..., None], axis=2)
    gained = gained.transpose(0, 2, 1).reshape(-1, local_experts)
    onto = (jnp.arange(experts)[None, :] == own_experts[:, None]).astype(jnp.float32)
    weighed = jnp.sum(gained[:, :, None] * onto[None], axis=1)
    dlogit_low = (weighed - probs * jnp.sum(gained, axis=-1, keepdims=True)).astype(jnp.bfloat16)
    dpair, down_grad = lax.optimization_barrier((dpair, down_grad))
    dn2, mixed_part, router_part = give_back(
        hot.transpose(0, 1, 3, 2), dlogit_low.reshape(sources, token_count, experts), router_turned, dpair, mixed_rows, n2_all
    )
    router_part = router_part.T
    dn2, gate_grad = lax.optimization_barrier((dn2, gate_grad))
    mixed = lax.psum_scatter(mixed_part.reshape(-1, model_width), EXP, scatter_dimension=0, tiled=True)

    dh_norm, gain_second_part = norm_back(dn2, hidden_state, factor_two, gain_second)
    grad_hidden = grad_total + dh_norm
    dh_low = grad_hidden.astype(jnp.bfloat16)
    out_part = transposed_times(attended_low, dh_low)
    d_att = times_transposed(dh_low, full_out).astype(jnp.bfloat16)
    dq_low, dk_low, dv_low, *gain_parts = attend_back(d_att, *saved, keep, query_raw, key_raw, *shared, score_scale)
    dv_low, up_grad = lax.optimization_barrier((dv_low, up_grad))
    gain_queries_part, gain_keys_part = (jnp.sum(g, axis=0) for g in gain_parts)
    core = lax.axis_index("core")
    swap = lambda v: lax.ppermute(v, "core", [(0, 1), (1, 0)])

    def columns_of_core(v):
        width = model_width // 2
        mine = lax.dynamic_slice_in_dim(v, core * width, width, 1)
        other = lax.dynamic_slice_in_dim(v, (1 - core) * width, width, 1)
        return jnp.concatenate([mine, swap(other)], axis=0)

    both = lambda v: jnp.concatenate([v, swap(v)], axis=0)
    n1_both, att_both = both(normed_one_low), both(attended_low)
    rights = [columns_of_core(v) for v in (dh_low, dv_low, dq_low, dk_low)]
    split = lambda v: v.reshape(ctx_size * sources // 2, 2, -1)
    small_parts = jnp.concatenate(
        [split(v) for v in (gain_second_part, gain_queries_part, gain_keys_part, router_part)], axis=2
    )
    small_parts = jnp.pad(small_parts, ((0, 0), (0, 0), (0, -small_parts.shape[2] % 2048)))
    small_parts = lax.dynamic_index_in_dim(small_parts, core, 1, False) + swap(lax.dynamic_index_in_dim(small_parts, 1 - core, 1, False))
    weight_grads, small_grads, input_grad, gain_first_sums = collect(
        small_parts.reshape(ctx_size * sources // 2, -1, 128), (att_both, n1_both), rights, (dq_low, dk_low, dv_low),
        (full_query, full_key, full_value), tokens[0], row(gain_first), grad_hidden,
    )
    weight_grads, mixed, gate_grad, up_grad, down_grad = lax.optimization_barrier(
        (list(weight_grads), mixed, gate_grad, up_grad, down_grad)
    )
    layer_out = (row_valid * (hidden_state + mixed.astype(jnp.float32))).astype(jnp.bfloat16)
    gate_grad, up_grad, down_grad = (v.astype(jnp.float32) for v in (gate_grad, up_grad, down_grad))
    weight_grads = [weight_grads[k] for k in (2, 3, 1, 0)]
    small_grads = small_grads.reshape(-1)
    gain_grads = [lax.dynamic_slice_in_dim(jnp.sum(gain_first_sums, axis=0), lax.axis_index(ALL) * rows_each, rows_each)]
    gain_grads += [small_grads[i * rows_each : (i + 1) * rows_each] for i in range(3)]
    router_grad = small_grads[3 * rows_each : packed.size - rows_each].reshape(rows_each, experts)
    return (layer_out[None], input_grad[None], *weight_grads, router_grad, *gain_grads, gate_grad, up_grad, down_grad)


def solution(mesh):
    ctx, exp = mesh.devices.shape
    fine = Mesh(mesh.devices.reshape(2, ctx // 2, exp // 2, 2), ("ca", "cb", "ring", "core"))
    rows = P(EXP, CTX, None)
    flat2, flat1 = P(ALL, None), P(ALL)
    placed = (rows, rows, P(EXP), rows) + (flat2,) * 5 + (flat1,) * 4 + (P(EXP, None, CTX),) * 2 + (P(EXP, CTX, None),)
    outs = (rows, rows) + (flat2,) * 5 + (flat1,) * 4 + (P(EXP, None, CTX),) * 2 + (P(EXP, CTX, None),)
    return jax.shard_map(local, mesh=fine, in_specs=placed, out_specs=outs, check_vma=False)
```
